32 devices in a mesh: dp: 8 (over y, x, core), blk: 4 (over z).
Axes of the slice: x: 2, y: 2, z: 4, core: 2. Of those that a mesh axis runs over, the one named last changes fastest.
Arguments:
- tokens: bfloat16 [24, 1024, 1024], P('dp', 'blk'), may hold values from -6 to 6
- cotangent: bfloat16 [24, 1024, 1024], P('dp', 'blk'), may hold values from -6 to 6
- domain_ids: int32 [24, 1024], P('dp', 'blk'), may hold values from 0 to 21
- domain_weight: float32 [22], replicated, may hold values from 0.3 to 3
- frozen_input_weights: bfloat16 [1024, 8192], P('dp'), may hold values from -0.1875 to 0.1875
- bias_in: bfloat16 [8192], replicated, may hold values from -1.25 to 1.25
- frozen_down_weight: bfloat16 [4096, 1024], P('dp'), may hold values from -0.09375 to 0.09375
- bias_ff: bfloat16 [1024], replicated, may hold values from -1.25 to 1.25
- norm_gain: float32 [2, 1024], replicated, may hold values from 0.5 to 1.5
- norm_shift: float32 [2, 1024], replicated, may hold values from -1.25 to 1.25
- adapt_a: float32 [1024, 384], P('dp'), may hold values from -0.1875 to 0.1875
- adapt_a_ff: float32 [4096, 128], P('dp'), may hold values from -0.09375 to 0.09375
- adapt_b: float32 [128, 8192], P(None, 'dp'), may hold values from -0.5 to 0.5
- adapt_b_ff: float32 [128, 1024], P(None, 'dp'), may hold values from -0.5 to 0.5
- mean_a: float32 [1024, 384], P('dp'), may hold values from -192 to 192
- mean_a_ff: float32 [4096, 128], P('dp'), may hold values from -192 to 192
- mean_b: float32 [128, 8192], P(None, 'dp'), may hold values from -192 to 192
- mean_b_ff: float32 [128, 1024], P(None, 'dp'), may hold values from -192 to 192
- square_a: float32 [1024, 384], P('dp'), may hold values from 100 to 100000
- square_a_ff: float32 [4096, 128], P('dp'), may hold values from 100 to 100000
- square_b: float32 [128, 8192], P(None, 'dp'), may hold values from 100 to 100000
- square_b_ff: float32 [128, 1024], P(None, 'dp'), may hold values from 100 to 100000
- keep_a: int32 [1024, 384], P('dp'), may hold values 0 or 1
- keep_a_ff: int32 [4096, 128], P('dp'), may hold values 0 or 1
- keep_b: int32 [128, 8192], P(None, 'dp'), may hold values 0 or 1
- keep_b_ff: int32 [128, 1024], P(None, 'dp'), may hold values 0 or 1
Outputs:
- mixed: bfloat16 [24, 1024, 1024], P('dp', 'blk')
- grad_tokens: bfloat16 [24, 1024, 1024], P('dp', 'blk')
- grad_gain: float32 [2, 1024], replicated
- grad_shift: float32 [2, 1024], replicated
- grad_a: float32 [1024, 384], P('dp')
- grad_a_ff: float32 [4096, 128], P('dp')
- grad_b: float32 [128, 8192], P(None, 'dp')
- grad_b_ff: float32 [128, 1024], P(None, 'dp')
- new_mean_a: float32 [1024, 384], P('dp')
- new_square_a: float32 [1024, 384], P('dp')
- new_mean_a_ff: float32 [4096, 128], P('dp')
- new_square_a_ff: float32 [4096, 128], P('dp')
- new_mean_b: float32 [128, 8192], P(None, 'dp')
- new_square_b: float32 [128, 8192], P(None, 'dp')
- new_mean_b_ff: float32 [128, 1024], P(None, 'dp')
- new_square_b_ff: float32 [128, 1024], P(None, 'dp')
- folded_input_weights: bfloat16 [1024, 8192], P('dp')
- folded_down_weight: bfloat16 [4096, 1024], P('dp')
The draws below stay inside these ranges and needn't reach their ends.
All inputs are finite; a program needn't handle non-finite values. No bound on the sum of `keep_a` or of `keep_a_ff` or of `keep_b` or of `keep_b_ff` on one device may be relied on, other than what follows from the above.
Results may differ from the reference program's by a relative error of at most 0.025.
Values may be sent and summed in bfloat16 or wider, within the bound.
A program may use at most 320 MiB of HBM per device.

```python
import math
import jax
import jax.numpy as jnp
import numpy as np
from jax import lax

D = 1024
FF = 4096
HEADS = 16
ROTARY = 16
RANK = 128
SEQ_LEN = 1024
DOMAINS = 22
SEQS = 24
COLS = 8192


def with_ends(values, own_key, least, top_value):
    spot = [jax.random.randint(jax.random.fold_in(own_key, axis), (), 0, length) for axis, length in enumerate(values.shape)]
    longest = values.shape.index(max(values.shape))
    neighbour = spot[:longest] + [(spot[longest] + 1) % values.shape[longest]] + spot[longest + 1:]
    return values.at[tuple(spot)].set(least).at[tuple(neighbour)].set(top_value)


def block_scale(stream_key, extent, cuts, smallest, largest):
    def one(axis_at, shards_of):
        draws = jax.random.uniform(jax.random.fold_in(jax.random.fold_in(stream_key, 6), axis_at), (shards_of,), jnp.float32, smallest / len(cuts), largest / len(cuts))
        return jnp.repeat(jnp.exp(draws), extent[axis_at] // shards_of).reshape((-1,) + (1,) * (len(extent) - axis_at - 1))

    factor_of = one(*cuts[0])
    for cut in cuts[1:]:
        factor_of = factor_of * one(*cut)
    return factor_of


def cumulative_ranks(amount, slope):
    portions = [(1 << 20) // math.isqrt(rank ** slope) + 1 for rank in range(1, amount + 1)]
    deviation = 1 + sum(portions) // (1 << 30)
    return np.cumsum(np.array([max(1, weight // deviation) for weight in portions]))


def ranked(own_key, extent, number_of, slope):
    listing = cumulative_ranks(number_of, slope)
    ticket = jax.random.randint(jax.random.fold_in(own_key, 1), extent, 0, int(listing[number_of - 1]))
    standing = jnp.searchsorted(jnp.asarray(listing, jnp.int32), ticket, side="right")
    return jax.random.permutation(jax.random.fold_in(own_key, 2), number_of)[standing].astype(jnp.int32)


def centred(own_key, dims, deviation, bound, shards=(), held_as=jnp.bfloat16):
    values = jax.random.normal(own_key, dims, jnp.float32) * deviation
    if len(shards) > 0:
        values = block_scale(own_key, dims, shards, -0.22, 0.18) * values
    return jnp.clip(values, min=-bound, max=bound).astype(held_as)


def setup_inputs(seed: int = 0) -> dict:
    arg_keys = jax.random.split(jax.random.key(seed), 27)
    tokens = centred(arg_keys[0], (SEQS, SEQ_LEN, D), 1.0, 6.0, ((0, 8), (1, 4)))
    cotangent = centred(arg_keys[1], (SEQS, SEQ_LEN, D), 1.0, 6.0, ((0, 8), (1, 4)))
    domain_ids = with_ends(ranked(arg_keys[2], (SEQS, SEQ_LEN), DOMAINS, 2), jax.random.fold_in(arg_keys[2], 3), 0, DOMAINS - 1).astype(jnp.int32)
    domain_weight = jnp.clip(jnp.exp(jax.random.uniform(arg_keys[3], (DOMAINS,), jnp.float32, math.log(0.3), math.log(3.0))), 0.3, 3.0)
    frozen_input_weights = centred(arg_keys[4], (D, COLS), D ** -0.5, 0.1875, ((0, 8),))
    bias_in = centred(arg_keys[5], (COLS,), 0.2, 1.25)
    frozen_down_weight = centred(arg_keys[6], (FF, D), FF ** -0.5, 0.09375, ((0, 8),))
    bias_ff = centred(arg_keys[7], (D,), 0.2, 1.25)
    norm_gain = jnp.clip(1.0 + 0.1 * jax.random.normal(arg_keys[8], (2, D), jnp.float32), 0.5, 1.5)
    norm_shift = centred(arg_keys[9], (2, D), 0.2, 1.25, (), jnp.float32)
    adapt_a = centred(arg_keys[10], (D, 3 * RANK), D ** -0.5, 0.1875, ((0, 8),), jnp.float32)
    adapt_a_ff = centred(arg_keys[11], (FF, RANK), FF ** -0.5, 0.09375, ((0, 8),), jnp.float32)
    adapt_b = centred(arg_keys[12], (RANK, COLS), RANK ** -0.5, 0.5, ((1, 8),), jnp.float32)
    adapt_b_ff = centred(arg_keys[13], (RANK, D), RANK ** -0.5, 0.5, ((1, 8),), jnp.float32)
    mean_a = centred(arg_keys[14], (D, 3 * RANK), 30.0, 192.0, ((0, 8),), jnp.float32)
    mean_a_ff = centred(arg_keys[15], (FF, RANK), 30.0, 192.0, ((0, 8),), jnp.float32)
    mean_b = centred(arg_keys[16], (RANK, COLS), 30.0, 192.0, ((1, 8),), jnp.float32)
    mean_b_ff = centred(arg_keys[17], (RANK, D), 30.0, 192.0, ((1, 8),), jnp.float32)
    square_a = jnp.clip(jnp.exp(math.log(100000.0) - 6.9077553 * jax.random.uniform(arg_keys[18], (D, 3 * RANK), jnp.float32) ** block_scale(arg_keys[18], (D, 3 * RANK), ((0, 8),), -0.2, 0.2)), 100.0, 100000.0)
    square_a_ff = jnp.clip(jnp.exp(math.log(100000.0) - 6.9077553 * jax.random.uniform(arg_keys[19], (FF, RANK), jnp.float32) ** block_scale(arg_keys[19], (FF, RANK), ((0, 8),), -0.2, 0.2)), 100.0, 100000.0)
    square_b = jnp.clip(jnp.exp(math.log(100000.0) - 6.9077553 * jax.random.uniform(arg_keys[20], (RANK, COLS), jnp.float32) ** block_scale(arg_keys[20], (RANK, COLS), ((1, 8),), -0.2, 0.2)), 100.0, 100000.0)
    square_b_ff = jnp.clip(jnp.exp(math.log(100000.0) - 6.9077553 * jax.random.uniform(arg_keys[21], (RANK, D), jnp.float32) ** block_scale(arg_keys[21], (RANK, D), ((1, 8),), -0.2, 0.2)), 100.0, 100000.0)
    keep_a = with_ends((jax.random.randint(arg_keys[22], (D, 3 * RANK), 0, 2) < 1).astype(jnp.int32), jax.random.fold_in(arg_keys[22], 1), 0, 1)
    keep_a_ff = with_ends((jax.random.randint(arg_keys[23], (FF, RANK), 0, 2) < 1).astype(jnp.int32), jax.random.fold_in(arg_keys[23], 1), 0, 1)
    keep_b = with_ends((jax.random.randint(arg_keys[24], (RANK, COLS), 0, 2) < 1).astype(jnp.int32), jax.random.fold_in(arg_keys[24], 1), 0, 1)
    keep_b_ff = with_ends((jax.random.randint(arg_keys[25], (RANK, D), 0, 2) < 1).astype(jnp.int32), jax.random.fold_in(arg_keys[25], 1), 0, 1)
    return dict(tokens=tokens, cotangent=cotangent, domain_ids=domain_ids, domain_weight=domain_weight, frozen_input_weights=frozen_input_weights, bias_in=bias_in, frozen_down_weight=frozen_down_weight, bias_ff=bias_ff, norm_gain=norm_gain, norm_shift=norm_shift, adapt_a=adapt_a, adapt_a_ff=adapt_a_ff, adapt_b=adapt_b, adapt_b_ff=adapt_b_ff, mean_a=mean_a, mean_a_ff=mean_a_ff, mean_b=mean_b, mean_b_ff=mean_b_ff, square_a=square_a, square_a_ff=square_a_ff, square_b=square_b, square_b_ff=square_b_ff, keep_a=keep_a, keep_a_ff=keep_a_ff, keep_b=keep_b, keep_b_ff=keep_b_ff)


@jax.custom_vjp
def low(v):
    return lax.optimization_barrier(v.astype(jnp.bfloat16)).astype(jnp.float32)

@jax.custom_vjp
def low_back(v):
    return v

def low_keep(v):
    return (low(v), None)

def low_pass(kept, grad):
    return (grad,)

def back_keep(v):
    return (v, None)

def back_low(kept, grad):
    return (low(grad),)
low.defvjp(low_keep, low_pass)
low_back.defvjp(back_keep, back_low)
highest = lax.Precision.HIGHEST
adapter_scale = 0.25
rope_base = 10000.0
norm_eps = 1e-05
masked_score = -1e+30
first_fix = 1.0 - (0.9 ** 10) ** 10
second_fix = 1.0 - (0.999 ** 10) ** 10

def multiplier(left, right):
    return jnp.dot(left, right, precision=highest)

def layer_norm(values, gain, shift):
    centre = values - lax.optimization_barrier(jnp.mean(values, axis=-1, keepdims=True))
    spread = lax.optimization_barrier(jnp.mean(centre * centre, axis=-1, keepdims=True))
    return centre * lax.rsqrt(spread + norm_eps) * gain + shift

def rope_tables(positions, rotary):
    half = rotary // 2
    freqs = rope_base ** (-(jnp.arange(half, dtype=jnp.float32) * 2.0) / rotary)
    angles = positions.astype(jnp.float32)[:, None] * freqs[None, :]
    return (jnp.cos(angles), jnp.sin(angles))

def rotate(values, cosine, sine, rotary):
    half = rotary // 2
    front = values[..., :half]
    back = values[..., half:rotary]
    rest = values[..., rotary:]
    cos_b = cosine[:, None, :]
    sin_b = sine[:, None, :]
    return jnp.concatenate([front * cos_b - back * sin_b, back * cos_b + front * sin_b, rest], axis=-1)

def adapted(input_rows, weight_matrix, bias_vector, down, upper_factor):
    base_matrix = multiplier(input_rows, weight_matrix) + bias_vector
    middle_rows = low(low_back(multiplier(input_rows, down)))
    return base_matrix + adapter_scale * multiplier(middle_rows, upper_factor)

def attend_rows(query, keys, values, start, qrows, length):
    depth = query.shape[-1]
    scores = low_back(jnp.einsum('gqhe,gkhe->ghqk', query, keys, precision=highest) * (1.0 / jnp.sqrt(1.0 * depth)))
    qpos = start + jnp.arange(qrows, dtype=jnp.int32)
    kpos = jnp.arange(length, dtype=jnp.int32)
    allowed = qpos[:, None] >= kpos[None, :]
    scores = jnp.where(allowed, scores, masked_score)
    weights = low(jax.nn.softmax(scores, axis=-1))
    return jnp.einsum('ghqk,gkhe->gqhe', weights, values, precision=highest)

def layer(input_rows, frozen, gain, shift, adapt_a, adapt_a_ff, adapt_b, adapt_b_ff):
    frozen_input_weights, bias_in, frozen_down_weight, bias_ff = frozen
    groups, length, width = input_rows.shape
    depth = width // HEADS
    rank = adapt_b.shape[0]
    down_in = low(adapt_a)
    down_ff = low(adapt_a_ff)
    up_in = low(adapt_b)
    up_ff = low(adapt_b_ff)
    first = low(layer_norm(input_rows, gain[0], shift[0]))
    second = low(layer_norm(input_rows, gain[1], shift[1]))
    joint = low_back(adapted(first, frozen_input_weights[:, :3 * width], bias_in[:3 * width], down_in[:, :rank], up_in[:, :3 * width]))
    cosine, sine = rope_tables(jnp.arange(length, dtype=jnp.int32), ROTARY)
    query = low(rotate(joint[..., :width].reshape(groups, length, HEADS, depth), cosine, sine, ROTARY))
    keys = low(rotate(joint[..., width:2 * width].reshape(groups, length, HEADS, depth), cosine, sine, ROTARY))
    values = low(joint[..., 2 * width:].reshape(groups, length, HEADS, depth))
    qrows = min(512, length)

    def block(index):
        start = index * qrows
        part = lax.dynamic_slice_in_dim(query, start, qrows, 1)
        return attend_rows(part, keys, values, start, qrows, length)
    blocks = lax.map(jax.checkpoint(block), jnp.arange(length // qrows, dtype=jnp.int32))
    heads_out = jnp.moveaxis(blocks, 0, 1).reshape(groups, length, width)
    attended = low(low_back(heads_out))
    branch_att = low_back(adapted(attended, frozen_input_weights[:, 3 * width:4 * width], bias_in[3 * width:4 * width], down_in[:, rank:2 * rank], up_in[:, 3 * width:4 * width]))
    hidden_pre = low_back(adapted(second, frozen_input_weights[:, 4 * width:], bias_in[4 * width:], down_in[:, 2 * rank:], up_in[:, 4 * width:]))
    hidden = low(jax.nn.gelu(hidden_pre, approximate=False))
    branch_ff = low_back(adapted(hidden, frozen_down_weight, bias_ff, down_ff, up_ff))
    return input_rows + branch_att + branch_ff

def adam_update(param, grad, mean, square, keep):
    mean_new = 0.9 * mean + 0.1 * grad
    square_new = 0.999 * square + 0.001 * grad * grad
    fresh = param - 0.01 * (mean_new / first_fix) / (jnp.sqrt(square_new / second_fix) + 1e-08)
    kept = keep.astype(jnp.float32)
    return (fresh, mean_new * kept, square_new * kept)

def reference(tokens, cotangent, domain_ids, domain_weight, frozen_input_weights, bias_in, frozen_down_weight, bias_ff, norm_gain, norm_shift, adapt_a, adapt_a_ff, adapt_b, adapt_b_ff, mean_a, mean_a_ff, mean_b, mean_b_ff, square_a, square_a_ff, square_b, square_b_ff, keep_a, keep_a_ff, keep_b, keep_b_ff):
    frozen = (frozen_input_weights.astype(jnp.float32), bias_in.astype(jnp.float32), frozen_down_weight.astype(jnp.float32), bias_ff.astype(jnp.float32))
    seqs, length, width = tokens.shape
    rank = adapt_b.shape[0]
    per_step = 4
    input_rows = tokens.astype(jnp.float32).reshape(seqs // per_step, per_step, length, width)
    row_weight = domain_weight[domain_ids]
    row_grad = (cotangent.astype(jnp.float32) * row_weight[..., None]).reshape(seqs // per_step, per_step, length, width)
    params = (norm_gain, norm_shift, adapt_a, adapt_a_ff, adapt_b, adapt_b_ff)

    def step(totals, pair):
        block_in, block_grad = pair

        def apply(values, weights):
            return layer(values, frozen, *weights)
        result, pull = jax.vjp(apply, block_in, params)
        grad_in, grad_params = pull(block_grad)
        totals = jax.tree.map(lambda left, right: left + right, totals, grad_params)
        return (totals, (result.astype(jnp.bfloat16), grad_in.astype(jnp.bfloat16)))
    zeros = jax.tree.map(jnp.zeros_like, params)
    totals, (results, grad_ins) = lax.scan(step, zeros, (input_rows, row_grad))
    grad_gain, grad_shift, grad_a, grad_a_ff, grad_b, grad_b_ff = totals
    mixed = results.reshape(seqs, length, width)
    grad_tokens = grad_ins.reshape(seqs, length, width)
    fresh_a, new_mean_a, new_square_a = adam_update(adapt_a, grad_a, mean_a, square_a, keep_a)
    reset_down_adapter_left, new_mean_a_ff, new_square_a_ff = adam_update(adapt_a_ff, grad_a_ff, mean_a_ff, square_a_ff, keep_a_ff)
    fresh_b, new_mean_b, new_square_b = adam_update(adapt_b, grad_b, mean_b, square_b, keep_b)
    reset_down_adapter_right, new_mean_b_ff, new_square_b_ff = adam_update(adapt_b_ff, grad_b_ff, mean_b_ff, square_b_ff, keep_b_ff)
    input_weight_update = jnp.concatenate([multiplier(fresh_a[:, :rank], fresh_b[:, :3 * width]), multiplier(fresh_a[:, rank:2 * rank], fresh_b[:, 3 * width:4 * width]), multiplier(fresh_a[:, 2 * rank:], fresh_b[:, 4 * width:])], axis=1)
    folded_input_weights = (frozen_input_weights.astype(jnp.float32) + adapter_scale * input_weight_update).astype(jnp.bfloat16)
    folded_down_weight = (frozen_down_weight.astype(jnp.float32) + adapter_scale * multiplier(reset_down_adapter_left, reset_down_adapter_right)).astype(jnp.bfloat16)
    return (mixed, grad_tokens, grad_gain, grad_shift, grad_a, grad_a_ff, grad_b, grad_b_ff, new_mean_a, new_square_a, new_mean_a_ff, new_square_a_ff, new_mean_b, new_square_b, new_mean_b_ff, new_square_b_ff, folded_input_weights, folded_down_weight)
```

```python
import functools
import math

import jax
import jax.numpy as jnp
from jax import lax
from jax.experimental import pallas as pl
from jax.experimental.pallas import tpu as pltpu
from jax.sharding import PartitionSpec as P

HEADS = 16
ROTARY = 16
DOMAINS = 22

adapter_scale = 0.25
rope_base = 10000.0
norm_eps = 1e-05
masked_score = -1e30
first_fix = 1.0 - (0.9**10) ** 10
second_fix = 1.0 - (0.999**10) ** 10

f32 = jnp.float32
bf16 = jnp.bfloat16


def nn(left, right):
    return lax.dot_general(left, right, (((1,), (0,)), ((), ())), preferred_element_type=f32)


def nt(left, right):
    return lax.dot_general(left, right, (((1,), (1,)), ((), ())), preferred_element_type=f32)


def tn(left, right):
    return lax.dot_general(left, right, (((0,), (0,)), ((), ())), preferred_element_type=f32)


def rope_lane_tables(length, depth, lanes):
    half = ROTARY // 2
    freqs = rope_base ** (-(jnp.arange(half, dtype=f32) * 2.0) / ROTARY)
    angles = jnp.arange(length, dtype=f32)[:, None] * freqs[None, :]
    cosine, sine = jnp.cos(angles), jnp.sin(angles)
    rest = depth - ROTARY
    ones, zero_half = jnp.ones((length, rest), f32), jnp.zeros((length, half), f32)
    zero_rest = jnp.zeros((length, rest), f32)
    keep = jnp.concatenate([cosine, cosine, ones], axis=1)
    from_above = jnp.concatenate([-sine, zero_half, zero_rest], axis=1)
    from_below = jnp.concatenate([zero_half, sine, zero_rest], axis=1)
    times = lanes // depth
    return tuple(jnp.tile(table, (1, times)) for table in (keep, from_above, from_below))


def turn(values, keep, above, below, sign):
    lanes = values.shape[-1]
    half = ROTARY // 2
    up = pltpu.roll(values, lanes - half, 1)
    down = pltpu.roll(values, half, 1)
    return values * keep + sign * (up * above + down * below)


def qkv_kernel(
    z_ref, x_ref, gain_ref, shift_ref, wq_ref, wk_ref, wv_ref, a_ref, b_ref, bias_ref,
    keep_ref, above_ref, below_ref, q_ref, k_ref, v_ref, first_ref, mid_ref,
):
    cols = wq_ref.shape[1]
    x = x_ref[...].reshape(x_ref.shape[2:]).astype(f32)
    centre = x - jnp.mean(x, axis=-1, keepdims=True)
    spread = jnp.mean(centre * centre, axis=-1, keepdims=True)
    first = (centre * lax.rsqrt(spread + norm_eps) * gain_ref[...] + shift_ref[...]).astype(bf16)
    mid = nn(first, a_ref[...]).astype(bf16)
    first_ref[...] = first.reshape(first_ref.shape)
    mid_ref[...] = mid.reshape(mid_ref.shape)
    low = adapter_scale * nn(mid, b_ref[...]) + bias_ref[...]
    lanes = keep_ref.shape[1]
    tables = keep_ref[...], above_ref[...], below_ref[...]
    query = nn(first, wq_ref[...]) + low[:, :cols]
    keys = nn(first, wk_ref[...]) + low[:, cols : 2 * cols]
    values = nn(first, wv_ref[...]) + low[:, 2 * cols :]
    for at in range(0, cols, lanes):
        part = slice(at, at + lanes)
        q_ref[0, :, part] = turn(query[:, part], *tables, 1.0).astype(bf16)
        k_ref[0, :, part] = turn(keys[:, part], *tables, 1.0).astype(bf16)
    v_ref[0] = values.astype(bf16)


MESH = pl.DeviceIdType.MESH


def attend_pair(query, keys, values, grad, tables, dk_ref, dv_ref, depth, blocks, store):
    lanes = keys.shape[1]
    span = keys.shape[0] // blocks
    scale = 1.0 / math.sqrt(depth)
    lane = lax.broadcasted_iota(jnp.int32, (1, lanes), 1)
    masks = [jnp.where(lane // depth == h, 1.0, 0.0).astype(bf16) for h in range(lanes // depth)]
    diagonal = lax.broadcasted_iota(jnp.int32, (span, span), 0) <= lax.broadcasted_iota(
        jnp.int32, (span, span), 1
    )
    keys_t, values_t = keys.T, values.T
    dk_ref[...] = jnp.zeros_like(dk_ref)
    dv_ref[...] = jnp.zeros_like(dv_ref)
    for i in range(blocks):
        rows = slice(i * span, (i + 1) * span)
        end = (i + 1) * span
        q_i, g_i = query[rows], grad[rows]
        g_t = g_i.T
        outs, grads = [], []
        dk, dv = None, None
        for h, mask in enumerate(masks):
            part = slice(h * depth, (h + 1) * depth)
            q_h, g_h = q_i * mask, g_i * mask
            scores = nt(keys[:end], q_h) * scale
            last = jnp.where(diagonal, scores[i * span :], masked_score)
            scores = last if i == 0 else jnp.concatenate([scores[: i * span], last], axis=0)
            weights = jnp.exp(scores - jnp.max(scores, axis=0, keepdims=True))
            weights = weights * (1.0 / jnp.sum(weights, axis=0, keepdims=True))
            low = weights.astype(bf16)
            out_t = nn(values_t[part, :end], low)
            grad_p = nt(values[:end], g_h)
            delta = jnp.sum(out_t * g_t[part].astype(f32), axis=0, keepdims=True)
            grad_s = (weights * (grad_p - delta)).astype(bf16)
            outs.append(out_t)
            grads.append(nn(keys_t[part, :end], grad_s))
            dk_h, dv_h = nn(grad_s, q_h), nn(low, g_h)
            dk = dk_h if dk is None else dk + dk_h
            dv = dv_h if dv is None else dv + dv_h
        dk_ref[:end] += dk
        dv_ref[:end] += dv
        store(i, 0, jnp.concatenate(outs, axis=0).T.astype(bf16))
        dq = jnp.concatenate(grads, axis=0).T * scale
        store(i, 1, turn(dq, *[t[rows] for t in tables], -1.0).astype(bf16))
    for i in range(blocks):
        rows = slice(i * span, (i + 1) * span)
        dk = dk_ref[rows] * scale
        store(i, 2, turn(dk, *[t[rows] for t in tables], -1.0).astype(bf16))
        store(i, 3, dv_ref[rows].astype(bf16))


def middle_kernel(
    q_ref, k_ref, v_ref, g_ref, keep_ref, above_ref, below_ref, mid_qkv_t_ref,
    second_ref, low_ref, mid_ref, mid_t_ref, dmid_ref, dmid_t_ref,
    up_ref, down_ref, a_ref, b_ref, bias_ref,
    local_ref, own_ref, ff_ref, back_ref, mid_ff_ref, dmid_up_ref, ga_ref, gb_ref,
    buffer, dk_ref, dv_ref, mid_acc, dmid_acc, send_sem, recv_sem, own_sem,
    *, n, pairs, steps, depth,
):
    step = pl.program_id(0)
    z = lax.axis_index("blk")
    dp = lax.axis_index("dp")
    lanes = q_ref.shape[2]

    def copies(s):
        seq, pair = s // pairs, lax.rem(s, pairs)
        at = pl.ds(pl.multiple_of((z * pairs + pair) * lanes, lanes), lanes)
        target = local_ref.at[seq, :, :, at]
        own = pltpu.make_async_copy(buffer.at[s, z], target, own_sem.at[s])
        away = []
        for t in range(1, n):
            peer = lax.rem(z + t, n)
            away.append(
                pltpu.make_async_remote_copy(
                    src_ref=buffer.at[s, peer], dst_ref=target,
                    send_sem=send_sem.at[s, t], recv_sem=recv_sem.at[s, t],
                    device_id=(dp, peer), device_id_type=MESH,
                )
            )
        return own, away

    @pl.when(step == 0)
    def _():
        barrier = pltpu.get_barrier_semaphore()
        for t in range(1, n):
            pl.semaphore_signal(barrier, inc=1, device_id=(dp, lax.rem(z + t, n)), device_id_type=MESH)
        pl.semaphore_wait(barrier, n - 1)

    @pl.when(step < steps)
    def _():
        def store(i, kind, value):
            buffer[step, i, kind] = value
            if kind:
                own_ref[0, kind - 1, i * value.shape[0] : (i + 1) * value.shape[0], :] = value

        tables = keep_ref[...], above_ref[...], below_ref[...]
        attend_pair(q_ref[0], k_ref[0], v_ref[0], g_ref[0], tables, dk_ref, dv_ref, depth, n, store)
        own, away = copies(step)
        own.start()
        for copy in away:
            copy.start()

    @pl.when(step == steps)
    def _():
        ff_ref[...] = jnp.zeros_like(ff_ref)
        back_ref[...] = jnp.zeros_like(back_ref)
        mid_acc[...] = jnp.zeros_like(mid_acc)
        dmid_acc[...] = jnp.zeros_like(dmid_acc)

    @pl.when(step >= steps)
    def _():
        total = second_ref.shape[0]
        size = 256 if total % 256 == 0 else 128
        for at in range(0, total, size):
            rows = slice(at, at + size)
            pre = nn(second_ref[rows], up_ref[...]) + bias_ref[...] + adapter_scale * nn(mid_ref[rows], b_ref[...])
            cdf = 0.5 + 0.5 * lax.erf(pre * (1.0 / math.sqrt(2.0)))
            hidden = (pre * cdf).astype(bf16)
            slope = cdf + pre * (jnp.exp(-0.5 * pre * pre) * (1.0 / math.sqrt(2.0 * math.pi)))
            grad_hidden = nt(low_ref[rows], down_ref[...]) + nt(dmid_ref[rows], a_ref[...])
            dup = (slope * grad_hidden).astype(bf16)
            ff_ref[rows] += nn(hidden, down_ref[...])
            back_ref[rows] += nt(dup, up_ref[...])
            mid_acc[rows] += nn(hidden, a_ref[...])
            dmid_acc[rows] += nt(dup, b_ref[...])
            ga = nn(dmid_t_ref[:, rows], hidden)
            gb = nn(mid_t_ref[:, rows], dup)
            ga_ref[...] = ga if at == 0 else ga_ref[...] + ga
            gb_ref[...] = gb if at == 0 else gb_ref[...] + gb

    @pl.when(step == pl.num_programs(0) - 1)
    def _():
        mid_ff_ref[...] = mid_acc[...].astype(bf16)
        dmid_up_ref[...] = (adapter_scale * dmid_acc[...]).astype(bf16)
        for s in range(steps):
            own, away = copies(s)
            own.wait()
            for copy in away:
                copy.wait()


def finish_kernel(
    local_ref, wo_ref, wq_ref, wk_ref, wv_ref, a_out_ref, a_qkv_ref, b_out_ref, bq_ref, bk_ref, bv_ref,
    bias_ref, x_ref, cot_ref, weight_ref, ff_ref, bias_ff_ref, mid_ff_ref, b_ff_ref,
    second_ref, dmid_up_ref, a_up_ref, gain_ref, dmid_out_t_ref, low_ref,
    mixed_ref, tokens_ref, norm_ref, ga_ref, gb_ref,
    att_acc, mid_acc, first_acc, dmid_acc,
):
    t = pl.program_id(0)
    rows = x_ref.shape[0] * x_ref.shape[1]
    cols = wq_ref.shape[1]

    @pl.when(t == 0)
    def _():
        att_acc[...] = jnp.zeros_like(att_acc)
        mid_acc[...] = jnp.zeros_like(mid_acc)
        first_acc[...] = jnp.zeros_like(first_acc)
        dmid_acc[...] = jnp.zeros_like(dmid_acc)

    out, dq, dk, dv = (local_ref[:, i].reshape(rows, cols) for i in range(4))
    att_acc[...] += nn(out, wo_ref[...])
    mid_acc[...] += nn(out, a_out_ref[...])
    first_acc[...] += nt(dq, wq_ref[...]) + nt(dk, wk_ref[...]) + nt(dv, wv_ref[...])
    dmid_acc[...] += nt(dq, bq_ref[...]) + nt(dk, bk_ref[...]) + nt(dv, bv_ref[...])
    ga_ref[...] = nn(dmid_out_t_ref[...], out)

    @pl.when(t == pl.num_programs(0) - 1)
    def _():
        size = x_ref.shape[1]
        norm = [jnp.zeros((1, first_acc.shape[1]), f32) for _ in range(4)]
        for q in range(x_ref.shape[0]):
            part = slice(q * size, (q + 1) * size)
            x = x_ref[q].astype(f32)
            mid = mid_acc[part].astype(bf16)
            gb = tn(mid, low_ref[part])
            gb_ref[...] = gb if q == 0 else gb_ref[...] + gb
            att = att_acc[part] + bias_ref[...] + adapter_scale * nn(mid, b_out_ref[...])
            ff = ff_ref[part] + bias_ff_ref[...] + adapter_scale * nn(mid_ff_ref[part], b_ff_ref[...])
            mixed_ref[q] = (x + att + ff).astype(bf16)
            dmid = (adapter_scale * dmid_acc[part]).astype(bf16)
            grad_first = first_acc[part] + nt(dmid, a_qkv_ref[...])
            grad_second = second_ref[part] + nt(dmid_up_ref[part], a_up_ref[...])
            centre = x - jnp.mean(x, axis=-1, keepdims=True)
            inv = lax.rsqrt(jnp.mean(centre * centre, axis=-1, keepdims=True) + norm_eps)
            unit = centre * inv
            pulled = grad_first * gain_ref[0:1] + grad_second * gain_ref[1:2]
            back = inv * (
                pulled
                - jnp.mean(pulled, axis=-1, keepdims=True)
                - unit * jnp.mean(pulled * unit, axis=-1, keepdims=True)
            )
            row_grad = cot_ref[q].astype(f32) * weight_ref[part]
            tokens_ref[q] = (row_grad + back).astype(bf16)
            for k, value in enumerate((grad_first * unit, grad_second * unit, grad_first, grad_second)):
                norm[k] += jnp.sum(value, axis=0, keepdims=True)
        norm_ref[...] = jnp.concatenate(norm, axis=0)


def adam_update(param, grad, mean, square, keep):
    mean_new = 0.9 * mean + 0.1 * grad
    square_new = 0.999 * square + 0.001 * grad * grad
    fresh = param - 0.01 * (mean_new / first_fix) / (jnp.sqrt(square_new / second_fix) + 1e-08)
    kept = keep.astype(f32)
    return (fresh, mean_new * kept, square_new * kept)


def body(
    dp_n,
    n,
    tokens,
    cotangent,
    domain_ids,
    domain_weight,
    frozen_input_weights,
    bias_in,
    frozen_down_weight,
    bias_ff,
    norm_gain,
    norm_shift,
    adapt_a,
    adapt_a_ff,
    adapt_b,
    adapt_b_ff,
    mean_a,
    mean_a_ff,
    mean_b,
    mean_b_ff,
    square_a,
    square_a_ff,
    square_b,
    square_b_ff,
    keep_a,
    keep_a_ff,
    keep_b,
    keep_b_ff,
):
    seqs, span, width = tokens.shape
    rows = seqs * span
    rank = adapt_b.shape[0]
    depth = width // HEADS
    cz = width // n
    length = n * span
    z = lax.axis_index("blk")
    z_arr = jnp.full((1,), z, jnp.int32)
    kr = frozen_input_weights.shape[0]
    down_rows, inner = frozen_down_weight.shape[0], frozen_down_weight.shape[0] * dp_n
    lanes = 128

    def shift_by(values, s):
        return lax.ppermute(values, "blk", [(i, (i + s) % n) for i in range(n)])

    b_cols = adapt_b.shape[1] + adapt_b_ff.shape[1]
    b_shard = jnp.concatenate([adapt_b, adapt_b_ff], axis=1).astype(bf16)
    one = jnp.concatenate(
        [frozen_input_weights[:, : 4 * width], adapt_a.astype(bf16), b_shard.reshape(kr, -1)], axis=1
    )
    one = lax.all_gather(one, "dp", axis=0, tiled=True)
    two = lax.all_gather(frozen_input_weights[:, 4 * width :], "dp", axis=0, tiled=True)
    three = jnp.concatenate([frozen_down_weight, adapt_a_ff.astype(bf16)], axis=1)
    three = lax.all_gather(three, "dp", axis=0, tiled=True)
    a_at = 4 * width
    b_at = a_at + 3 * rank
    a_all = one[:, a_at:b_at]
    b_all = one[:, b_at:].reshape(dp_n, rank, b_cols)
    b_in = jnp.transpose(b_all[:, :, : adapt_b.shape[1]], (1, 0, 2)).reshape(rank, -1)
    b_ff = jnp.transpose(b_all[:, :, adapt_b.shape[1] :], (1, 0, 2)).reshape(rank, width)
    w_out = one[:, 3 * width : 4 * width]
    w_up = two
    w_down, a_ff = three[:, :width], three[:, width:]

    right, left = tokens, tokens
    rights, lefts = [None], [None]
    for s in range(1, n):
        right = lax.ppermute(right, "blk", [(i, i + 1) for i in range(n - 1)])
        left = lax.ppermute(left, "blk", [(i + 1, i) for i in range(n - 1)])
        rights.append(right)
        lefts.append(left)
    x_all = jnp.stack(
        [tokens] + [jnp.where(z >= s, rights[s], lefts[n - s]) for s in range(1, n)]
    )

    lookup = (domain_ids[..., None] == jnp.arange(DOMAINS, dtype=jnp.int32)).astype(f32)
    row_weight = jnp.sum(lookup * domain_weight, axis=-1).reshape(rows, 1)
    row_grad = cotangent.astype(f32).reshape(rows, width) * row_weight
    grad_low = row_grad.astype(bf16)
    b_out = b_in[:, 3 * width : 4 * width]
    a_out = a_all[:, rank : 2 * rank]
    dmid_out = (adapter_scale * nt(grad_low, b_out)).astype(bf16)
    grad_att = (nt(grad_low, w_out) + nt(dmid_out, a_out)).astype(bf16)
    grad_att = jnp.transpose(grad_att.reshape(seqs, span, n, cz), (2, 0, 1, 3))

    def piece(values, s):
        return lax.dynamic_index_in_dim(values, lax.rem(z + s, n), 0, keepdims=False)

    g_all = jnp.stack(
        [piece(grad_att, 0)] + [shift_by(piece(grad_att, s), s) for s in range(1, n)]
    )

    tables = rope_lane_tables(length, depth, lanes)
    own = [lax.dynamic_slice_in_dim(b_in[:, t * width : (t + 1) * width], z * cz, cz, 1) for t in range(3)]
    b_own = jnp.concatenate(own, axis=1)
    bias32 = bias_in.astype(f32)
    bias_own = jnp.concatenate(
        [lax.dynamic_slice_in_dim(bias32, t * width + z * cz, cz, 0) for t in range(3)]
    ).reshape(1, 3 * cz)

    def block_of(s, z_ref):
        return lax.rem(z_ref[0] - s + n, n)

    table_spec = pl.BlockSpec((span, lanes), lambda s, q, z_ref: (block_of(s, z_ref), 0))
    head_spec = pl.BlockSpec((1, span, cz), lambda s, q, z_ref: (q, block_of(s, z_ref), 0))
    query, keys, values, first_all, mid_all = pl.pallas_call(
        qkv_kernel,
        grid_spec=pltpu.PrefetchScalarGridSpec(
            num_scalar_prefetch=1,
            grid=(n, seqs),
            in_specs=[
                pl.BlockSpec((1, 1, span, width), lambda s, q, z_ref: (s, q, 0, 0)),
                pl.BlockSpec((1, width), lambda s, q, z_ref: (0, 0)),
                pl.BlockSpec((1, width), lambda s, q, z_ref: (0, 0)),
                pl.BlockSpec((width, cz), lambda s, q, z_ref: (0, z_ref[0])),
                pl.BlockSpec((width, cz), lambda s, q, z_ref: (0, n + z_ref[0])),
                pl.BlockSpec((width, cz), lambda s, q, z_ref: (0, 2 * n + z_ref[0])),
                pl.BlockSpec((width, rank), lambda s, q, z_ref: (0, a_at // rank)),
                pl.BlockSpec((rank, 3 * cz), lambda s, q, z_ref: (0, 0)),
                pl.BlockSpec((1, 3 * cz), lambda s, q, z_ref: (0, 0)),
                table_spec,
                table_spec,
                table_spec,
            ],
            out_specs=[
                head_spec,
                head_spec,
                head_spec,
                pl.BlockSpec((1, 1, span, width), lambda s, q, z_ref: (block_of(s, z_ref), q, 0, 0)),
                pl.BlockSpec((1, 1, span, rank), lambda s, q, z_ref: (block_of(s, z_ref), q, 0, 0)),
            ],
        ),
        out_shape=[jax.ShapeDtypeStruct((seqs, length, cz), bf16)] * 3
        + [
            jax.ShapeDtypeStruct((n, seqs, span, width), bf16),
            jax.ShapeDtypeStruct((n, seqs, span, rank), bf16),
        ],
        compiler_params=pltpu.CompilerParams(vmem_limit_bytes=48 << 20),
        cost_estimate=pl.CostEstimate(
            flops=2 * n * rows * width * 4 * cz, bytes_accessed=6 * n * rows * width, transcendentals=0
        ),
        name="qkv",
    )(
        z_arr, x_all, norm_gain[0:1], norm_shift[0:1], one, one, one, one, b_own, bias_own, *tables
    )

    input_rows = tokens.astype(f32).reshape(rows, width)
    centre = input_rows - jnp.mean(input_rows, axis=-1, keepdims=True)
    inv = lax.rsqrt(jnp.mean(centre * centre, axis=-1, keepdims=True) + norm_eps)
    second = (centre * inv * norm_gain[1] + norm_shift[1]).astype(bf16)
    a_up = a_all[:, 2 * rank :]
    mid_up = nn(second, a_up).astype(bf16)
    dmid_ff = (adapter_scale * nt(grad_low, b_ff)).astype(bf16)
    pairs = cz // lanes
    steps = seqs * pairs
    inner_block = min(512, inner)
    g_pos = jnp.concatenate([g_all, g_all])
    g_pos = lax.rev(g_pos, (0,))
    g_pos = lax.dynamic_slice_in_dim(g_pos, lax.rem(n - 1 - z + n, n), n, 0)
    g_pos = jnp.transpose(g_pos, (1, 0, 2, 3)).reshape(seqs, length, cz)

    def one_buffer(shape):
        zeros = (0,) * len(shape)
        return pl.BlockSpec(shape, lambda s: zeros, pipeline_mode=pl.Buffered(1))

    def seq_pair(s):
        s = jnp.minimum(s, steps - 1)
        return s // pairs, lax.rem(s, pairs)

    def head_map(s):
        seq, pair = seq_pair(s)
        return seq, 0, pair

    def inner_at(s):
        return jnp.maximum(s - steps, 0)

    head = pl.BlockSpec((1, length, lanes), head_map)
    local, own, ff, grad_second, mid_ff, dmid_up, grad_a_ff_t, grad_b_up = pl.pallas_call(
        functools.partial(middle_kernel, n=n, pairs=pairs, steps=steps, depth=depth),
        grid=(steps + inner // inner_block,),
        in_specs=[head] * 4
        + [one_buffer((length, lanes))] * 3
        + [one_buffer((8, lanes))]
        + [one_buffer((rows, width))] * 2
        + [one_buffer((rows, rank)), one_buffer((rank, rows))] * 2
        + [
            pl.BlockSpec((width, inner_block), lambda s: (0, inner_at(s))),
            pl.BlockSpec((inner_block, width), lambda s: (inner_at(s), 0)),
            pl.BlockSpec((inner_block, rank), lambda s: (inner_at(s), width // rank)),
            pl.BlockSpec((rank, inner_block), lambda s: (0, 4 * width // inner_block + inner_at(s))),
            pl.BlockSpec((1, inner_block), lambda s: (0, 4 * width // inner_block + inner_at(s))),
        ],
        out_specs=[
            pl.BlockSpec(memory_space=pl.ANY),
            pl.BlockSpec((1, 3, length, lanes), lambda s: (seq_pair(s)[0], 0, 0, seq_pair(s)[1])),
            one_buffer((rows, width)),
            one_buffer((rows, width)),
            one_buffer((rows, rank)),
            one_buffer((rows, rank)),
            pl.BlockSpec((rank, inner_block), lambda s: (0, inner_at(s))),
            pl.BlockSpec((rank, inner_block), lambda s: (0, inner_at(s))),
        ],
        out_shape=[
            jax.ShapeDtypeStruct((seqs, 4, span, width), bf16),
            jax.ShapeDtypeStruct((seqs, 3, length, cz), bf16),
            jax.ShapeDtypeStruct((rows, width), f32),
            jax.ShapeDtypeStruct((rows, width), f32),
            jax.ShapeDtypeStruct((rows, rank), bf16),
            jax.ShapeDtypeStruct((rows, rank), bf16),
            jax.ShapeDtypeStruct((rank, inner), f32),
            jax.ShapeDtypeStruct((rank, inner), f32),
        ],
        scratch_shapes=[
            pltpu.VMEM((steps, n, 4, span, lanes), bf16),
            pltpu.VMEM((length, lanes), f32),
            pltpu.VMEM((length, lanes), f32),
            pltpu.VMEM((rows, rank), f32),
            pltpu.VMEM((rows, rank), f32),
            pltpu.SemaphoreType.DMA((steps, n)),
            pltpu.SemaphoreType.DMA((steps, n)),
            pltpu.SemaphoreType.DMA((steps,)),
        ],
        compiler_params=pltpu.CompilerParams(
            collective_id=0, has_side_effects=True, vmem_limit_bytes=60 << 20
        ),
        name="middle",
    )(
        query, keys, values, g_pos, *tables, tables[0][:8], second, grad_low, mid_up, mid_up.T, dmid_ff, dmid_ff.T,
        w_up, three, three, b_in, bias32.reshape(1, -1),
    )
    grad_b_up = adapter_scale * grad_b_up

    first_pos = jnp.transpose(first_all, (1, 0, 2, 3)).reshape(seqs * length, width)
    mid_pos = jnp.transpose(mid_all, (1, 0, 2, 3)).reshape(seqs * length, rank)
    djoint_own = [own[:, t].reshape(seqs * length, cz) for t in range(3)]
    dmid_own = sum(nt(djoint_own[t], b_own[:, t * cz : (t + 1) * cz]) for t in range(3))
    dmid_own = (adapter_scale * dmid_own).astype(bf16)
    grad_a_qkv_t = tn(dmid_own, first_pos)
    mine = (jnp.arange(n, dtype=jnp.int32) == z)[None, :, None]
    grad_b_qkv = jnp.concatenate(
        [
            jnp.where(mine, adapter_scale * tn(mid_pos, part)[:, None, :], 0.0).reshape(rank, width)
            for part in djoint_own
        ],
        axis=1,
    )
    grad_a_up_t = tn(dmid_up, second)
    grad_b_ffp = adapter_scale * tn(mid_ff, grad_low)

    def fixed(shape, *at):
        return pl.BlockSpec(shape, lambda t: at, pipeline_mode=pl.Buffered(1))

    def column(at, height):
        return pl.BlockSpec((height, cz), lambda t: (0, at * n + t))

    mixed, grad_tokens, norm_part, grad_a_out_t, grad_b_out = pl.pallas_call(
        finish_kernel,
        grid=(n,),
        in_specs=[
            pl.BlockSpec((seqs, 4, span, cz), lambda t: (0, 0, 0, t)),
            pl.BlockSpec((cz, width), lambda t: (t, 3)),
            column(0, width), column(1, width), column(2, width),
            pl.BlockSpec((cz, rank), lambda t: (t, a_at // rank + 1)),
            fixed((width, rank), 0, a_at // rank),
            fixed((rank, width), 0, 3),
            column(0, rank), column(1, rank), column(2, rank),
            fixed((1, width), 0, 3),
            fixed((seqs, span, width), 0, 0, 0),
            fixed((seqs, span, width), 0, 0, 0),
            fixed((rows, 1), 0, 0),
            fixed((rows, width), 0, 0),
            fixed((1, width), 0, 0),
            fixed((rows, rank), 0, 0),
            fixed((rank, width), 0, 0),
            fixed((rows, width), 0, 0),
            fixed((rows, rank), 0, 0),
            fixed((width, rank), 0, a_at // rank + 2),
            fixed((2, width), 0, 0),
            fixed((rank, rows), 0, 0),
            fixed((rows, width), 0, 0),
        ],
        out_specs=[
            fixed((seqs, span, width), 0, 0, 0),
            fixed((seqs, span, width), 0, 0, 0),
            fixed((4, width), 0, 0),
            pl.BlockSpec((rank, cz), lambda t: (0, t)),
            fixed((rank, width), 0, 0),
        ],
        out_shape=[
            jax.ShapeDtypeStruct((seqs, span, width), bf16),
            jax.ShapeDtypeStruct((seqs, span, width), bf16),
            jax.ShapeDtypeStruct((4, width), f32),
            jax.ShapeDtypeStruct((rank, width), f32),
            jax.ShapeDtypeStruct((rank, width), f32),
        ],
        scratch_shapes=[
            pltpu.VMEM((rows, width), f32),
            pltpu.VMEM((rows, rank), f32),
            pltpu.VMEM((rows, width), f32),
            pltpu.VMEM((rows, rank), f32),
        ],
        compiler_params=pltpu.CompilerParams(vmem_limit_bytes=56 << 20),
        name="finish",
    )(
        local, one, one, one, one, one, one, b_in, b_in, b_in, b_in, bias32.reshape(1, -1),
        tokens, cotangent, row_weight, ff, bias_ff.astype(f32).reshape(1, -1), mid_ff, b_ff,
        grad_second, dmid_up, one, norm_gain, dmid_out.T, grad_low,
    )
    grad_b_out = adapter_scale * grad_b_out

    def by_owner(values):
        return values.reshape(rank, dp_n, -1)

    parts = [
        by_owner(grad_a_qkv_t), by_owner(grad_a_out_t), by_owner(grad_a_up_t), by_owner(grad_a_ff_t),
        by_owner(jnp.concatenate([grad_b_qkv, grad_b_out, grad_b_up], axis=1)), by_owner(grad_b_ffp),
    ]
    widths = [p.shape[2] for p in parts]
    owned = jnp.transpose(jnp.concatenate(parts, axis=2), (1, 0, 2))
    norm_rows = jnp.broadcast_to(norm_part.reshape(1, -1, owned.shape[2]), (dp_n, 4 * width // owned.shape[2], owned.shape[2]))
    owned = jnp.concatenate([owned, norm_rows], axis=1)
    owned = lax.psum_scatter(owned, "dp", scatter_dimension=0, tiled=True)
    owned = lax.psum(owned[0], "blk")
    norm_sum = owned[rank:].reshape(4, width)
    grad_gain, grad_shift = norm_sum[:2], norm_sum[2:]
    cuts = [sum(widths[:i]) for i in range(len(widths) + 1)]
    pieces = [owned[:rank, cuts[i] : cuts[i + 1]] for i in range(len(widths))]
    grad_a = jnp.concatenate([p.T for p in pieces[:3]], axis=1)
    grad_a_ff = pieces[3].T
    grad_b, grad_b_ff = pieces[4], pieces[5]

    fresh_a, new_mean_a, new_square_a = adam_update(adapt_a, grad_a, mean_a, square_a, keep_a)
    fresh_a_ff, new_mean_a_ff, new_square_a_ff = adam_update(
        adapt_a_ff, grad_a_ff, mean_a_ff, square_a_ff, keep_a_ff
    )
    fresh_b, new_mean_b, new_square_b = adam_update(adapt_b, grad_b, mean_b, square_b, keep_b)
    fresh_b_ff, new_mean_b_ff, new_square_b_ff = adam_update(
        adapt_b_ff, grad_b_ff, mean_b_ff, square_b_ff, keep_b_ff
    )
    fresh = jnp.concatenate([fresh_b, fresh_b_ff], axis=1).astype(bf16)
    fresh = lax.all_gather(fresh, "dp", axis=0, tiled=False)
    fresh_in = jnp.transpose(fresh[:, :, : adapt_b.shape[1]], (1, 0, 2)).reshape(rank, -1)
    fresh_ff = jnp.transpose(fresh[:, :, adapt_b.shape[1] :], (1, 0, 2)).reshape(rank, width)
    fa = fresh_a.astype(bf16)
    update = jnp.concatenate(
        [
            nn(fa[:, :rank], fresh_in[:, : 3 * width]),
            nn(fa[:, rank : 2 * rank], fresh_in[:, 3 * width : 4 * width]),
            nn(fa[:, 2 * rank :], fresh_in[:, 4 * width :]),
        ],
        axis=1,
    )
    folded_input_weights = (frozen_input_weights.astype(f32) + adapter_scale * update).astype(bf16)
    folded_down_weight = (
        frozen_down_weight.astype(f32) + adapter_scale * nn(fresh_a_ff.astype(bf16), fresh_ff)
    ).astype(bf16)
    return (
        mixed,
        grad_tokens,
        grad_gain,
        grad_shift,
        grad_a,
        grad_a_ff,
        grad_b,
        grad_b_ff,
        new_mean_a,
        new_square_a,
        new_mean_a_ff,
        new_square_a_ff,
        new_mean_b,
        new_square_b,
        new_mean_b_ff,
        new_square_b_ff,
        folded_input_weights,
        folded_down_weight,
    )


def solution(mesh):
    in_specs = (
        P("dp", "blk", None),
        P("dp", "blk", None),
        P("dp", "blk"),
        P(),
        P("dp", None),
        P(),
        P("dp", None),
        P(),
        P(),
        P(),
        P("dp", None),
        P("dp", None),
        P(None, "dp"),
        P(None, "dp"),
        P("dp", None),
        P("dp", None),
        P(None, "dp"),
        P(None, "dp"),
        P("dp", None),
        P("dp", None),
        P(None, "dp"),
        P(None, "dp"),
        P("dp", None),
        P("dp", None),
        P(None, "dp"),
        P(None, "dp"),
    )
    out_specs = (
        P("dp", "blk", None),
        P("dp", "blk", None),
        P(),
        P(),
        P("dp", None),
        P("dp", None),
        P(None, "dp"),
        P(None, "dp"),
        P("dp", None),
        P("dp", None),
        P("dp", None),
        P("dp", None),
        P(None, "dp"),
        P(None, "dp"),
        P(None, "dp"),
        P(None, "dp"),
        P("dp", None),
        P("dp", None),
    )
    return jax.shard_map(
        functools.partial(body, mesh.shape["dp"], mesh.shape["blk"]), mesh=mesh, in_specs=in_specs, out_specs=out_specs, check_vma=False)
```

```python
import functools
import math

import jax
import jax.numpy as jnp
from jax import lax
from jax.experimental import pallas as pl
from jax.experimental.pallas import tpu as pltpu
from jax.sharding import PartitionSpec as P

HEADS = 16
ROTARY = 16
DOMAINS = 22

adapter_scale = 0.25
rope_base = 10000.0
norm_eps = 1e-05
masked_score = -1e30
first_fix = 1.0 - (0.9**10) ** 10
second_fix = 1.0 - (0.999**10) ** 10

f32 = jnp.float32
bf16 = jnp.bfloat16


def nn(left, right):
    return lax.dot_general(left, right, (((1,), (0,)), ((), ())), preferred_element_type=f32)


def nt(left, right):
    return lax.dot_general(left, right, (((1,), (1,)), ((), ())), preferred_element_type=f32)


def tn(left, right):
    return lax.dot_general(left, right, (((0,), (0,)), ((), ())), preferred_element_type=f32)


def rope_lane_tables(length, depth, lanes):
    half = ROTARY // 2
    freqs = rope_base ** (-(jnp.arange(half, dtype=f32) * 2.0) / ROTARY)
    angles = jnp.arange(length, dtype=f32)[:, None] * freqs[None, :]
    cosine, sine = jnp.cos(angles), jnp.sin(angles)
    rest = depth - ROTARY
    ones, zero_half = jnp.ones((length, rest), f32), jnp.zeros((length, half), f32)
    zero_rest = jnp.zeros((length, rest), f32)
    keep = jnp.concatenate([cosine, cosine, ones], axis=1)
    from_above = jnp.concatenate([-sine, zero_half, zero_rest], axis=1)
    from_below = jnp.concatenate([zero_half, sine, zero_rest], axis=1)
    times = lanes // depth
    return tuple(jnp.tile(table, (1, times)) for table in (keep, from_above, from_below))


def turn(values, keep, above, below, sign):
    lanes = values.shape[-1]
    half = ROTARY // 2
    up = pltpu.roll(values, lanes - half, 1)
    down = pltpu.roll(values, half, 1)
    return values * keep + sign * (up * above + down * below)


def qkv_kernel(
    z_ref, x_ref, gain_ref, shift_ref, wq_ref, wk_ref, wv_ref, a_ref, b_ref, bias_ref,
    keep_ref, above_ref, below_ref, q_ref, k_ref, v_ref, first_ref, mid_ref,
):
    cols = wq_ref.shape[1]
    x = x_ref[...].reshape(x_ref.shape[2:]).astype(f32)
    centre = x - jnp.mean(x, axis=-1, keepdims=True)
    spread = jnp.mean(centre * centre, axis=-1, keepdims=True)
    first = (centre * lax.rsqrt(spread + norm_eps) * gain_ref[...] + shift_ref[...]).astype(bf16)
    mid = nn(first, a_ref[...]).astype(bf16)
    first_ref[...] = first.reshape(first_ref.shape)
    mid_ref[...] = mid.reshape(mid_ref.shape)
    low = adapter_scale * nn(mid, b_ref[...]) + bias_ref[...]
    lanes = keep_ref.shape[1]
    tables = keep_ref[...], above_ref[...], below_ref[...]
    query = nn(first, wq_ref[...]) + low[:, :cols]
    keys = nn(first, wk_ref[...]) + low[:, cols : 2 * cols]
    values = nn(first, wv_ref[...]) + low[:, 2 * cols :]
    for at in range(0, cols, lanes):
        part = slice(at, at + lanes)
        q_ref[0, :, part] = turn(query[:, part], *tables, 1.0).astype(bf16)
        k_ref[0, :, part] = turn(keys[:, part], *tables, 1.0).astype(bf16)
    v_ref[0] = values.astype(bf16)


MESH = pl.DeviceIdType.MESH


def attend_pair(query, keys, values, grad, tables, dk_ref, dv_ref, depth, blocks, store):
    lanes = keys.shape[1]
    span = keys.shape[0] // blocks
    scale = 1.0 / math.sqrt(depth)
    lane = lax.broadcasted_iota(jnp.int32, (1, lanes), 1)
    masks = [jnp.where(lane // depth == h, 1.0, 0.0).astype(bf16) for h in range(lanes // depth)]
    diagonal = lax.broadcasted_iota(jnp.int32, (span, span), 0) <= lax.broadcasted_iota(
        jnp.int32, (span, span), 1
    )
    keys_t, values_t = keys.T, values.T
    dk_ref[...] = jnp.zeros_like(dk_ref)
    dv_ref[...] = jnp.zeros_like(dv_ref)
    for i in range(blocks):
        rows = slice(i * span, (i + 1) * span)
        end = (i + 1) * span
        q_i, g_i = query[rows], grad[rows]
        g_t = g_i.T
        outs, grads = [], []
        dk, dv = None, None
        for h, mask in enumerate(masks):
            part = slice(h * depth, (h + 1) * depth)
            q_h, g_h = q_i * mask, g_i * mask
            scores = nt(keys[:end], q_h) * scale
            last = jnp.where(diagonal, scores[i * span :], masked_score)
            scores = last if i == 0 else jnp.concatenate([scores[: i * span], last], axis=0)
            weights = jnp.exp(scores - jnp.max(scores, axis=0, keepdims=True))
            weights = weights * (1.0 / jnp.sum(weights, axis=0, keepdims=True))
            low = weights.astype(bf16)
            out_t = nn(values_t[part, :end], low)
            grad_p = nt(values[:end], g_h)
            delta = jnp.sum(out_t * g_t[part].astype(f32), axis=0, keepdims=True)
            grad_s = (weights * (grad_p - delta)).astype(bf16)
            outs.append(out_t)
            grads.append(nn(keys_t[part, :end], grad_s))
            dk_h, dv_h = nn(grad_s, q_h), nn(low, g_h)
            dk = dk_h if dk is None else dk + dk_h
            dv = dv_h if dv is None else dv + dv_h
        dk_ref[:end] += dk
        dv_ref[:end] += dv
        store(i, 0, jnp.concatenate(outs, axis=0).T.astype(bf16))
        dq = jnp.concatenate(grads, axis=0).T * scale
        store(i, 1, turn(dq, *[t[rows] for t in tables], -1.0).astype(bf16))
    for i in range(blocks):
        rows = slice(i * span, (i + 1) * span)
        dk = dk_ref[rows] * scale
        store(i, 2, turn(dk, *[t[rows] for t in tables], -1.0).astype(bf16))
        store(i, 3, dv_ref[rows].astype(bf16))


def middle_kernel(
    q_ref, k_ref, v_ref, g_ref, keep_ref, above_ref, below_ref, mid_qkv_t_ref,
    second_ref, low_ref, mid_ref, mid_t_ref, dmid_ref, dmid_t_ref,
    up_ref, down_ref, a_ref, b_ref, bias_ref,
    local_ref, own_ref, ff_ref, back_ref, mid_ff_ref, dmid_up_ref, ga_ref, gb_ref,
    buffer, dk_ref, dv_ref, mid_acc, dmid_acc, send_sem, recv_sem, own_sem,
    *, n, pairs, steps, depth,
):
    step = pl.program_id(0)
    z = lax.axis_index("blk")
    dp = lax.axis_index("dp")
    lanes = q_ref.shape[2]

    def copies(s):
        seq, pair = s // pairs, lax.rem(s, pairs)
        at = pl.ds(pl.multiple_of((z * pairs + pair) * lanes, lanes), lanes)
        target = local_ref.at[seq, :, :, at]
        own = pltpu.make_async_copy(buffer.at[s, z], target, own_sem.at[s])
        away = []
        for t in range(1, n):
            peer = lax.rem(z + t, n)
            away.append(
                pltpu.make_async_remote_copy(
                    src_ref=buffer.at[s, peer], dst_ref=target,
                    send_sem=send_sem.at[s, t], recv_sem=recv_sem.at[s, t],
                    device_id=(dp, peer), device_id_type=MESH,
                )
            )
        return own, away

    @pl.when(step == 0)
    def _():
        barrier = pltpu.get_barrier_semaphore()
        for t in range(1, n):
            pl.semaphore_signal(barrier, inc=1, device_id=(dp, lax.rem(z + t, n)), device_id_type=MESH)
        pl.semaphore_wait(barrier, n - 1)

    @pl.when(step < steps)
    def _():
        def store(i, kind, value):
            buffer[step, i, kind] = value
            if kind:
                own_ref[0, kind - 1, i * value.shape[0] : (i + 1) * value.shape[0], :] = value

        tables = keep_ref[...], above_ref[...], below_ref[...]
        attend_pair(q_ref[0], k_ref[0], v_ref[0], g_ref[0], tables, dk_ref, dv_ref, depth, n, store)
        own, away = copies(step)
        own.start()
        for copy in away:
            copy.start()

    @pl.when(step == steps)
    def _():
        ff_ref[...] = jnp.zeros_like(ff_ref)
        back_ref[...] = jnp.zeros_like(back_ref)
        mid_acc[...] = jnp.zeros_like(mid_acc)
        dmid_acc[...] = jnp.zeros_like(dmid_acc)

    @pl.when(step >= steps)
    def _():
        total = second_ref.shape[0]
        size = 256 if total % 256 == 0 else 128
        for at in range(0, total, size):
            rows = slice(at, at + size)
            pre = nn(second_ref[rows], up_ref[...]) + bias_ref[...] + adapter_scale * nn(mid_ref[rows], b_ref[...])
            cdf = 0.5 + 0.5 * lax.erf(pre * (1.0 / math.sqrt(2.0)))
            hidden = (pre * cdf).astype(bf16)
            slope = cdf + pre * (jnp.exp(-0.5 * pre * pre) * (1.0 / math.sqrt(2.0 * math.pi)))
            grad_hidden = nt(low_ref[rows], down_ref[...]) + nt(dmid_ref[rows], a_ref[...])
            dup = (slope * grad_hidden).astype(bf16)
            ff_ref[rows] += nn(hidden, down_ref[...])
            back_ref[rows] += nt(dup, up_ref[...])
            mid_acc[rows] += nn(hidden, a_ref[...])
            dmid_acc[rows] += nt(dup, b_ref[...])
            ga = nn(dmid_t_ref[:, rows], hidden)
            gb = nn(mid_t_ref[:, rows], dup)
            ga_ref[...] = ga if at == 0 else ga_ref[...] + ga
            gb_ref[...] = gb if at == 0 else gb_ref[...] + gb

    @pl.when(step == pl.num_programs(0) - 1)
    def _():
        mid_ff_ref[...] = mid_acc[...].astype(bf16)
        dmid_up_ref[...] = (adapter_scale * dmid_acc[...]).astype(bf16)
        for s in range(steps):
            own, away = copies(s)
            own.wait()
            for copy in away:
                copy.wait()


def finish_kernel(
    local_ref, wo_ref, wq_ref, wk_ref, wv_ref, a_out_ref, a_qkv_ref, b_out_ref, bq_ref, bk_ref, bv_ref,
    bias_ref, x_ref, cot_ref, weight_ref, ff_ref, bias_ff_ref, mid_ff_ref, b_ff_ref,
    second_ref, dmid_up_ref, a_up_ref, gain_ref, dmid_out_t_ref, low_ref,
    mixed_ref, tokens_ref, norm_ref, ga_ref, gb_ref,
    att_acc, mid_acc, first_acc, dmid_acc,
):
    t = pl.program_id(0)
    rows = x_ref.shape[0] * x_ref.shape[1]
    cols = wq_ref.shape[1]

    @pl.when(t == 0)
    def _():
        att_acc[...] = jnp.zeros_like(att_acc)
        mid_acc[...] = jnp.zeros_like(mid_acc)
        first_acc[...] = jnp.zeros_like(first_acc)
        dmid_acc[...] = jnp.zeros_like(dmid_acc)

    out, dq, dk, dv = (local_ref[:, i].reshape(rows, cols) for i in range(4))
    att_acc[...] += nn(out, wo_ref[...])
    mid_acc[...] += nn(out, a_out_ref[...])
    first_acc[...] += nt(dq, wq_ref[...]) + nt(dk, wk_ref[...]) + nt(dv, wv_ref[...])
    dmid_acc[...] += nt(dq, bq_ref[...]) + nt(dk, bk_ref[...]) + nt(dv, bv_ref[...])
    ga_ref[...] = nn(dmid_out_t_ref[...], out)

    @pl.when(t == pl.num_programs(0) - 1)
    def _():
        size = x_ref.shape[1]
        norm = [jnp.zeros((1, first_acc.shape[1]), f32) for _ in range(4)]
        for q in range(x_ref.shape[0]):
            part = slice(q * size, (q + 1) * size)
            x = x_ref[q].astype(f32)
            mid = mid_acc[part].astype(bf16)
            gb = tn(mid, low_ref[part])
            gb_ref[...] = gb if q == 0 else gb_ref[...] + gb
            att = att_acc[part] + bias_ref[...] + adapter_scale * nn(mid, b_out_ref[...])
            ff = ff_ref[part] + bias_ff_ref[...] + adapter_scale * nn(mid_ff_ref[part], b_ff_ref[...])
            mixed_ref[q] = (x + att + ff).astype(bf16)
            dmid = (adapter_scale * dmid_acc[part]).astype(bf16)
            grad_first = first_acc[part] + nt(dmid, a_qkv_ref[...])
            grad_second = second_ref[part] + nt(dmid_up_ref[part], a_up_ref[...])
            centre = x - jnp.mean(x, axis=-1, keepdims=True)
            inv = lax.rsqrt(jnp.mean(centre * centre, axis=-1, keepdims=True) + norm_eps)
            unit = centre * inv
            pulled = grad_first * gain_ref[0:1] + grad_second * gain_ref[1:2]
            back = inv * (
                pulled
                - jnp.mean(pulled, axis=-1, keepdims=True)
                - unit * jnp.mean(pulled * unit, axis=-1, keepdims=True)
            )
            row_grad = cot_ref[q].astype(f32) * weight_ref[part]
            tokens_ref[q] = (row_grad + back).astype(bf16)
            for k, value in enumerate((grad_first * unit, grad_second * unit, grad_first, grad_second)):
                norm[k] += jnp.sum(value, axis=0, keepdims=True)
        norm_ref[...] = jnp.concatenate(norm, axis=0)


def reduce_kernel(
    g_ref, norm_in_ref, b_ref, mean_ref, square_ref, bf_ref, mean_f_ref, square_f_ref,
    out_ref, norm_ref, fresh_ref,
    r1, h, r2a, r2b, ia, ib, r3a, r3b, total, r4, nr, nsum,
    s1, q1, s2, q2, s3, q3, s4, q4, s5, q5, sn, qn, sg, qg,
    *, n, chunks, b_at,
):
    z = lax.axis_index("blk")
    dp = lax.axis_index("dp")
    y, x, c = dp // 4, lax.rem(dp // 2, 2), lax.rem(dp, 2)
    core = (dp + 1 - 2 * c, z)
    along_x = (dp + 2 - 4 * x, z)
    along_y = (dp + 4 - 8 * y, z)
    peers = [(dp, lax.rem(z + t, n)) for t in range(1, n)]
    half = g_ref.shape[2] // 2
    part = g_ref.shape[2] // n
    width = g_ref.shape[3] // chunks

    barrier = pltpu.get_barrier_semaphore()
    for peer in [core, along_x, along_y] + peers:
        pl.semaphore_signal(barrier, inc=1, device_id=peer, device_id_type=MESH)
    pl.semaphore_wait(barrier, 2 + n)

    def remote(src, dst, send, recv, peer):
        return pltpu.make_async_remote_copy(
            src_ref=src, dst_ref=dst, send_sem=send, recv_sem=recv, device_id=peer, device_id_type=MESH
        )

    def cols(k):
        return slice(k * width, (k + 1) * width)

    def mine(k=None):
        return pl.ds(pl.multiple_of(z * part, part), part)

    def first(k):
        return [remote(g_ref.at[:, 1 - c, :, cols(k)], r1.at[:, :, cols(k)], s1.at[k], q1.at[k], core)]

    def second(k):
        return [
            remote(h.at[:, 1 - x, 0:half, cols(k)], r2a.at[:, :, cols(k)], s2.at[0, k], q2.at[0, k], along_x),
            remote(h.at[1 - y, :, half:, cols(k)], r2b.at[:, :, cols(k)], s2.at[1, k], q2.at[1, k], along_y),
        ]

    def third(k):
        return [
            remote(ia.at[1 - y, :, cols(k)], r3a.at[:, cols(k)], s3.at[0, k], q3.at[0, k], along_y),
            remote(ib.at[1 - x, :, cols(k)], r3b.at[:, cols(k)], s3.at[1, k], q3.at[1, k], along_x),
        ]

    def fourth(k):
        found = []
        for t in range(1, n):
            to = lax.rem(z + t, n)
            rows = pl.ds(pl.multiple_of(to * part, part), part)
            found.append(
                remote(total.at[rows, cols(k)], r4.at[t, :, cols(k)], s4.at[t, k], q4.at[t, k], peers[t - 1])
            )
        return found

    def fifth(k):
        return [
            remote(out_ref.at[mine(), cols(k)], out_ref.at[mine(), cols(k)], s5.at[t, k], q5.at[t, k], peers[t - 1])
            for t in range(1, n)
        ]

    def add(a, b):
        return (a.astype(f32) + b.astype(f32)).astype(bf16)

    def norm_copy(i, peer):
        return remote(nsum.at[i], nr.at[i], sn.at[i], qn.at[i], peer)

    nsum[0] = norm_in_ref[...]
    norm_stages = [norm_copy(0, core), norm_copy(1, along_x), norm_copy(2, along_y)]
    norm_last = [
        remote(nsum.at[3], nr.at[2 + t], sn.at[2 + t], qn.at[2 + t], peers[t - 1]) for t in range(1, n)
    ]
    for k in range(chunks):
        first(k)[0].start()
    norm_stages[0].start()

    def after_first(k):
        for copy in first(k):
            copy.wait()
        for yy in range(2):
            for xx in range(2):
                h[yy, xx, :, cols(k)] = add(g_ref[2 * yy + xx, c, :, cols(k)], r1[2 * yy + xx, :, cols(k)])
        for copy in second(k):
            copy.start()

    def after_second(k):
        for copy in second(k):
            copy.wait()
        for i in range(2):
            ia[i, :, cols(k)] = add(h[i, x, 0:half, cols(k)], r2a[i, :, cols(k)])
            ib[i, :, cols(k)] = add(h[y, i, half:, cols(k)], r2b[i, :, cols(k)])
        for copy in third(k):
            copy.start()

    def after_third(k):
        for copy in third(k):
            copy.wait()
        total[0:half, cols(k)] = add(ia[y, :, cols(k)], r3a[:, cols(k)])
        total[half:, cols(k)] = add(ib[x, :, cols(k)], r3b[:, cols(k)])
        for copy in fourth(k):
            copy.start()

    def after_fourth(k):
        for copy in fourth(k):
            copy.wait()
        value = total[mine(), cols(k)].astype(f32)
        for t in range(1, n):
            value += r4[t, :, cols(k)].astype(f32)
        out_ref[mine(), cols(k)] = value.astype(bf16)
        for copy in fifth(k):
            copy.start()

    def after_fifth(k):
        for copy in fifth(k):
            copy.wait()

    stages = [after_first, after_second, after_third, after_fourth, after_fifth]
    for step in range(chunks + len(stages) - 1):
        for at in reversed(range(len(stages))):
            if 0 <= step - at < chunks:
                stages[at](step - at)
        if step < 3:
            norm_stages[step].wait()
            nsum[step + 1] = nsum[step] + nr[step]
            if step < 2:
                norm_stages[step + 1].start()
            else:
                for copy in norm_last:
                    copy.start()
    for copy in norm_last:
        copy.wait()
    value = jnp.zeros_like(nsum[3])
    for blk in range(n):
        there = lax.rem(z - blk + n, n)
        value += jnp.where(there == 0, nsum[3], nr[2 + jnp.maximum(there, 1)])
    norm_ref[...] = value

    cut = b_ref.shape[1]
    grads = out_ref[:, b_at:].astype(f32)
    new_b = adam_fresh(b_ref[...], grads[:, :cut], mean_ref[...], square_ref[...])
    new_f = adam_fresh(bf_ref[...], grads[:, cut:], mean_f_ref[...], square_f_ref[...])
    fresh_ref[dp] = jnp.concatenate([new_b, new_f], axis=1).astype(bf16)

    def gather(i, slot, peer):
        return remote(fresh_ref.at[slot], fresh_ref.at[slot], sg.at[i], qg.at[i], peer)

    from_x, from_y = dp + 2 - 4 * x, dp + 4 - 8 * y
    across = dp + 2 - 4 * x + 4 - 8 * y
    onward = jnp.where(c == 0, from_y, from_x)
    target = (jnp.where(c == 0, along_x[0], along_y[0]), z)
    direct = [gather(0, dp, along_x), gather(1, dp, along_y), gather(2, dp, core)]
    for copy in direct:
        copy.start()
    direct[0].wait()
    direct[1].wait()
    more = [gather(3, onward, target), gather(4, from_x, core), gather(5, from_y, core)]
    for copy in more:
        copy.start()
    more[0].wait()
    last = gather(6, across, core)
    last.start()
    direct[2].wait()
    more[1].wait()
    more[2].wait()
    last.wait()


def update_kernel(
    g_ref, fresh_ref, w_ref, wd_ref, *refs, rank, width,
):
    params, outs = refs[:16], refs[16:30]
    a_new, aff_new = refs[30:]
    j = pl.program_id(0)
    cols = w_ref.shape[1]

    @pl.when(j == 0)
    def _():
        rows, inner = params[0].shape[0], params[4].shape[0]
        got = g_ref[...].astype(f32)
        grads = [
            jnp.concatenate([got[:, i * rows : (i + 1) * rows].T for i in range(3)], axis=1),
            got[:, 3 * rows : 3 * rows + inner].T,
        ]
        at = 3 * rows + inner
        cut = params[8].shape[1]
        grads += [got[:, at : at + cut], got[:, at + cut :]]
        for i, grad in enumerate(grads):
            param, mean, square, keep = (r[...] for r in params[4 * i : 4 * i + 4])
            mean_new = 0.9 * mean + 0.1 * grad
            square_new = 0.999 * square + 0.001 * grad * grad
            kept = keep.astype(f32)
            outs[i][...] = grad
            outs[4 + 2 * i][...] = mean_new * kept
            outs[5 + 2 * i][...] = square_new * kept
            if i < 2:
                fresh = param - 0.01 * (mean_new / first_fix) / (jnp.sqrt(square_new / second_fix) + 1e-08)
                if i == 0:
                    for k in range(3):
                        a_new[k] = fresh[:, k * rank : (k + 1) * rank].astype(bf16)
                else:
                    aff_new[...] = fresh.astype(bf16)

    block = jnp.where(j * cols < 3 * width, 0, jnp.where(j * cols < 4 * width, 1, 2))
    cut = params[8].shape[1]
    fresh = [fresh_ref[i] for i in range(fresh_ref.shape[0])]
    update = nn(a_new[block], jnp.concatenate([f[:, :cut] for f in fresh], axis=1))
    outs[12][...] = (w_ref[...].astype(f32) + adapter_scale * update).astype(bf16)
    update = nn(aff_new[...], jnp.concatenate([f[:, cut:] for f in fresh], axis=1))
    outs[13][...] = (wd_ref[...].astype(f32) + adapter_scale * update).astype(bf16)


def adam_fresh(param, grad, mean, square):
    mean_new = 0.9 * mean + 0.1 * grad
    square_new = 0.999 * square + 0.001 * grad * grad
    return param - 0.01 * (mean_new / first_fix) / (jnp.sqrt(square_new / second_fix) + 1e-08)


def body(
    dp_n,
    n,
    tokens,
    cotangent,
    domain_ids,
    domain_weight,
    frozen_input_weights,
    bias_in,
    frozen_down_weight,
    bias_ff,
    norm_gain,
    norm_shift,
    adapt_a,
    adapt_a_ff,
    adapt_b,
    adapt_b_ff,
    mean_a,
    mean_a_ff,
    mean_b,
    mean_b_ff,
    square_a,
    square_a_ff,
    square_b,
    square_b_ff,
    keep_a,
    keep_a_ff,
    keep_b,
    keep_b_ff,
):
    seqs, span, width = tokens.shape
    rows = seqs * span
    rank = adapt_b.shape[0]
    depth = width // HEADS
    cz = width // n
    length = n * span
    z = lax.axis_index("blk")
    z_arr = jnp.full((1,), z, jnp.int32)
    kr = frozen_input_weights.shape[0]
    down_rows, inner = frozen_down_weight.shape[0], frozen_down_weight.shape[0] * dp_n
    lanes = 128

    def shift_by(values, s):
        return lax.ppermute(values, "blk", [(i, (i + s) % n) for i in range(n)])

    b_cols = adapt_b.shape[1] + adapt_b_ff.shape[1]
    b_shard = jnp.concatenate([adapt_b, adapt_b_ff], axis=1).astype(bf16)
    one = jnp.concatenate(
        [frozen_input_weights[:, : 4 * width], adapt_a.astype(bf16), b_shard.reshape(kr, -1)], axis=1
    )
    one = lax.all_gather(one, "dp", axis=0, tiled=True)
    two = lax.all_gather(frozen_input_weights[:, 4 * width :], "dp", axis=0, tiled=True)
    three = jnp.concatenate([frozen_down_weight, adapt_a_ff.astype(bf16)], axis=1)
    three = lax.all_gather(three, "dp", axis=0, tiled=True)
    a_at = 4 * width
    b_at = a_at + 3 * rank
    a_all = one[:, a_at:b_at]
    b_all = one[:, b_at:].reshape(dp_n, rank, b_cols)
    b_in = jnp.transpose(b_all[:, :, : adapt_b.shape[1]], (1, 0, 2)).reshape(rank, -1)
    b_ff = jnp.transpose(b_all[:, :, adapt_b.shape[1] :], (1, 0, 2)).reshape(rank, width)
    w_out = one[:, 3 * width : 4 * width]
    w_up = two
    w_down, a_ff = three[:, :width], three[:, width:]

    right, left = tokens, tokens
    rights, lefts = [None], [None]
    for s in range(1, n):
        right = lax.ppermute(right, "blk", [(i, i + 1) for i in range(n - 1)])
        left = lax.ppermute(left, "blk", [(i + 1, i) for i in range(n - 1)])
        rights.append(right)
        lefts.append(left)
    x_all = jnp.stack(
        [tokens] + [jnp.where(z >= s, rights[s], lefts[n - s]) for s in range(1, n)]
    )

    lookup = (domain_ids[..., None] == jnp.arange(DOMAINS, dtype=jnp.int32)).astype(f32)
    row_weight = jnp.sum(lookup * domain_weight, axis=-1).reshape(rows, 1)
    row_grad = cotangent.astype(f32).reshape(rows, width) * row_weight
    grad_low = row_grad.astype(bf16)
    b_out = b_in[:, 3 * width : 4 * width]
    a_out = a_all[:, rank : 2 * rank]
    dmid_out = (adapter_scale * nt(grad_low, b_out)).astype(bf16)
    grad_att = (nt(grad_low, w_out) + nt(dmid_out, a_out)).astype(bf16)
    grad_att = jnp.transpose(grad_att.reshape(seqs, span, n, cz), (2, 0, 1, 3))

    def piece(values, s):
        return lax.dynamic_index_in_dim(values, lax.rem(z + s, n), 0, keepdims=False)

    g_all = jnp.stack(
        [piece(grad_att, 0)] + [shift_by(piece(grad_att, s), s) for s in range(1, n)]
    )

    tables = rope_lane_tables(length, depth, lanes)
    own = [lax.dynamic_slice_in_dim(b_in[:, t * width : (t + 1) * width], z * cz, cz, 1) for t in range(3)]
    b_own = jnp.concatenate(own, axis=1)
    bias32 = bias_in.astype(f32)
    bias_own = jnp.concatenate(
        [lax.dynamic_slice_in_dim(bias32, t * width + z * cz, cz, 0) for t in range(3)]
    ).reshape(1, 3 * cz)

    def block_of(s, z_ref):
        return lax.rem(z_ref[0] - s + n, n)

    table_spec = pl.BlockSpec((span, lanes), lambda s, q, z_ref: (block_of(s, z_ref), 0))
    head_spec = pl.BlockSpec((1, span, cz), lambda s, q, z_ref: (q, block_of(s, z_ref), 0))
    query, keys, values, first_all, mid_all = pl.pallas_call(
        qkv_kernel,
        grid_spec=pltpu.PrefetchScalarGridSpec(
            num_scalar_prefetch=1,
            grid=(n, seqs),
            in_specs=[
                pl.BlockSpec((1, 1, span, width), lambda s, q, z_ref: (s, q, 0, 0)),
                pl.BlockSpec((1, width), lambda s, q, z_ref: (0, 0)),
                pl.BlockSpec((1, width), lambda s, q, z_ref: (0, 0)),
                pl.BlockSpec((width, cz), lambda s, q, z_ref: (0, z_ref[0])),
                pl.BlockSpec((width, cz), lambda s, q, z_ref: (0, n + z_ref[0])),
                pl.BlockSpec((width, cz), lambda s, q, z_ref: (0, 2 * n + z_ref[0])),
                pl.BlockSpec((width, rank), lambda s, q, z_ref: (0, a_at // rank)),
                pl.BlockSpec((rank, 3 * cz), lambda s, q, z_ref: (0, 0)),
                pl.BlockSpec((1, 3 * cz), lambda s, q, z_ref: (0, 0)),
                table_spec,
                table_spec,
                table_spec,
            ],
            out_specs=[
                head_spec,
                head_spec,
                head_spec,
                pl.BlockSpec((1, 1, span, width), lambda s, q, z_ref: (block_of(s, z_ref), q, 0, 0)),
                pl.BlockSpec((1, 1, span, rank), lambda s, q, z_ref: (block_of(s, z_ref), q, 0, 0)),
            ],
        ),
        out_shape=[jax.ShapeDtypeStruct((seqs, length, cz), bf16)] * 3
        + [
            jax.ShapeDtypeStruct((n, seqs, span, width), bf16),
            jax.ShapeDtypeStruct((n, seqs, span, rank), bf16),
        ],
        compiler_params=pltpu.CompilerParams(vmem_limit_bytes=48 << 20),
        cost_estimate=pl.CostEstimate(
            flops=2 * n * rows * width * 4 * cz, bytes_accessed=6 * n * rows * width, transcendentals=0
        ),
        name="qkv",
    )(
        z_arr, x_all, norm_gain[0:1], norm_shift[0:1], one, one, one, one, b_own, bias_own, *tables
    )

    input_rows = tokens.astype(f32).reshape(rows, width)
    centre = input_rows - jnp.mean(input_rows, axis=-1, keepdims=True)
    inv = lax.rsqrt(jnp.mean(centre * centre, axis=-1, keepdims=True) + norm_eps)
    second = (centre * inv * norm_gain[1] + norm_shift[1]).astype(bf16)
    a_up = a_all[:, 2 * rank :]
    mid_up = nn(second, a_up).astype(bf16)
    dmid_ff = (adapter_scale * nt(grad_low, b_ff)).astype(bf16)
    pairs = cz // lanes
    steps = seqs * pairs
    inner_block = min(512, inner)
    g_pos = jnp.concatenate([g_all, g_all])
    g_pos = lax.rev(g_pos, (0,))
    g_pos = lax.dynamic_slice_in_dim(g_pos, lax.rem(n - 1 - z + n, n), n, 0)
    g_pos = jnp.transpose(g_pos, (1, 0, 2, 3)).reshape(seqs, length, cz)

    def one_buffer(shape):
        zeros = (0,) * len(shape)
        return pl.BlockSpec(shape, lambda s: zeros, pipeline_mode=pl.Buffered(1))

    def seq_pair(s):
        s = jnp.minimum(s, steps - 1)
        return s // pairs, lax.rem(s, pairs)

    def head_map(s):
        seq, pair = seq_pair(s)
        return seq, 0, pair

    def inner_at(s):
        return jnp.maximum(s - steps, 0)

    head = pl.BlockSpec((1, length, lanes), head_map)
    local, own, ff, grad_second, mid_ff, dmid_up, grad_a_ff_t, grad_b_up = pl.pallas_call(
        functools.partial(middle_kernel, n=n, pairs=pairs, steps=steps, depth=depth),
        grid=(steps + inner // inner_block,),
        in_specs=[head] * 4
        + [one_buffer((length, lanes))] * 3
        + [one_buffer((8, lanes))]
        + [one_buffer((rows, width))] * 2
        + [one_buffer((rows, rank)), one_buffer((rank, rows))] * 2
        + [
            pl.BlockSpec((width, inner_block), lambda s: (0, inner_at(s))),
            pl.BlockSpec((inner_block, width), lambda s: (inner_at(s), 0)),
            pl.BlockSpec((inner_block, rank), lambda s: (inner_at(s), width // rank)),
            pl.BlockSpec((rank, inner_block), lambda s: (0, 4 * width // inner_block + inner_at(s))),
            pl.BlockSpec((1, inner_block), lambda s: (0, 4 * width // inner_block + inner_at(s))),
        ],
        out_specs=[
            pl.BlockSpec(memory_space=pl.ANY),
            pl.BlockSpec((1, 3, length, lanes), lambda s: (seq_pair(s)[0], 0, 0, seq_pair(s)[1])),
            one_buffer((rows, width)),
            one_buffer((rows, width)),
            one_buffer((rows, rank)),
            one_buffer((rows, rank)),
            pl.BlockSpec((rank, inner_block), lambda s: (0, inner_at(s))),
            pl.BlockSpec((rank, inner_block), lambda s: (0, inner_at(s))),
        ],
        out_shape=[
            jax.ShapeDtypeStruct((seqs, 4, span, width), bf16),
            jax.ShapeDtypeStruct((seqs, 3, length, cz), bf16),
            jax.ShapeDtypeStruct((rows, width), f32),
            jax.ShapeDtypeStruct((rows, width), f32),
            jax.ShapeDtypeStruct((rows, rank), bf16),
            jax.ShapeDtypeStruct((rows, rank), bf16),
            jax.ShapeDtypeStruct((rank, inner), f32),
            jax.ShapeDtypeStruct((rank, inner), f32),
        ],
        scratch_shapes=[
            pltpu.VMEM((steps, n, 4, span, lanes), bf16),
            pltpu.VMEM((length, lanes), f32),
            pltpu.VMEM((length, lanes), f32),
            pltpu.VMEM((rows, rank), f32),
            pltpu.VMEM((rows, rank), f32),
            pltpu.SemaphoreType.DMA((steps, n)),
            pltpu.SemaphoreType.DMA((steps, n)),
            pltpu.SemaphoreType.DMA((steps,)),
        ],
        compiler_params=pltpu.CompilerParams(
            collective_id=0, has_side_effects=True, vmem_limit_bytes=60 << 20
        ),
        name="middle",
    )(
        query, keys, values, g_pos, *tables, tables[0][:8], second, grad_low, mid_up, mid_up.T, dmid_ff, dmid_ff.T,
        w_up, three, three, b_in, bias32.reshape(1, -1),
    )
    grad_b_up = adapter_scale * grad_b_up

    first_pos = jnp.transpose(first_all, (1, 0, 2, 3)).reshape(seqs * length, width)
    mid_pos = jnp.transpose(mid_all, (1, 0, 2, 3)).reshape(seqs * length, rank)
    djoint_own = [own[:, t].reshape(seqs * length, cz) for t in range(3)]
    dmid_own = sum(nt(djoint_own[t], b_own[:, t * cz : (t + 1) * cz]) for t in range(3))
    dmid_own = (adapter_scale * dmid_own).astype(bf16)
    grad_a_qkv_t = tn(dmid_own, first_pos)
    mine = (jnp.arange(n, dtype=jnp.int32) == z)[None, :, None]
    grad_b_qkv = jnp.concatenate(
        [
            jnp.where(mine, adapter_scale * tn(mid_pos, part)[:, None, :], 0.0).reshape(rank, width)
            for part in djoint_own
        ],
        axis=1,
    )
    grad_a_up_t = tn(dmid_up, second)
    grad_b_ffp = adapter_scale * tn(mid_ff, grad_low)

    def fixed(shape, *at):
        return pl.BlockSpec(shape, lambda t: at, pipeline_mode=pl.Buffered(1))

    def column(at, height):
        return pl.BlockSpec((height, cz), lambda t: (0, at * n + t))

    mixed, grad_tokens, norm_part, grad_a_out_t, grad_b_out = pl.pallas_call(
        finish_kernel,
        grid=(n,),
        in_specs=[
            pl.BlockSpec((seqs, 4, span, cz), lambda t: (0, 0, 0, t)),
            pl.BlockSpec((cz, width), lambda t: (t, 3)),
            column(0, width), column(1, width), column(2, width),
            pl.BlockSpec((cz, rank), lambda t: (t, a_at // rank + 1)),
            fixed((width, rank), 0, a_at // rank),
            fixed((rank, width), 0, 3),
            column(0, rank), column(1, rank), column(2, rank),
            fixed((1, width), 0, 3),
            fixed((seqs, span, width), 0, 0, 0),
            fixed((seqs, span, width), 0, 0, 0),
            fixed((rows, 1), 0, 0),
            fixed((rows, width), 0, 0),
            fixed((1, width), 0, 0),
            fixed((rows, rank), 0, 0),
            fixed((rank, width), 0, 0),
            fixed((rows, width), 0, 0),
            fixed((rows, rank), 0, 0),
            fixed((width, rank), 0, a_at // rank + 2),
            fixed((2, width), 0, 0),
            fixed((rank, rows), 0, 0),
            fixed((rows, width), 0, 0),
        ],
        out_specs=[
            fixed((seqs, span, width), 0, 0, 0),
            fixed((seqs, span, width), 0, 0, 0),
            fixed((4, width), 0, 0),
            pl.BlockSpec((rank, cz), lambda t: (0, t)),
            fixed((rank, width), 0, 0),
        ],
        out_shape=[
            jax.ShapeDtypeStruct((seqs, span, width), bf16),
            jax.ShapeDtypeStruct((seqs, span, width), bf16),
            jax.ShapeDtypeStruct((4, width), f32),
            jax.ShapeDtypeStruct((rank, width), f32),
            jax.ShapeDtypeStruct((rank, width), f32),
        ],
        scratch_shapes=[
            pltpu.VMEM((rows, width), f32),
            pltpu.VMEM((rows, rank), f32),
            pltpu.VMEM((rows, width), f32),
            pltpu.VMEM((rows, rank), f32),
        ],
        compiler_params=pltpu.CompilerParams(vmem_limit_bytes=56 << 20),
        name="finish",
    )(
        local, one, one, one, one, one, one, b_in, b_in, b_in, b_in, bias32.reshape(1, -1),
        tokens, cotangent, row_weight, ff, bias_ff.astype(f32).reshape(1, -1), mid_ff, b_ff,
        grad_second, dmid_up, one, norm_gain, dmid_out.T, grad_low,
    )
    grad_b_out = adapter_scale * grad_b_out

    def by_owner(values):
        return values.reshape(rank, dp_n, -1)

    parts = [
        by_owner(grad_a_qkv_t), by_owner(grad_a_out_t), by_owner(grad_a_up_t), by_owner(grad_a_ff_t),
        by_owner(jnp.concatenate([grad_b_qkv, grad_b_out, grad_b_up], axis=1)), by_owner(grad_b_ffp),
    ]
    widths = [p.shape[2] for p in parts]
    owned = jnp.transpose(jnp.concatenate([p.astype(bf16) for p in parts], axis=2), (1, 0, 2))
    total_cols = owned.shape[2]
    b_at = sum(widths[:4])
    if dp_n == 8 and rank % (16 * n) == 0:
        chunks = 4
        half = rank // 2
        vmem = pl.BlockSpec(memory_space=pltpu.VMEM)
        dma = pltpu.SemaphoreType.DMA
        reduced, norm_sum, fresh = pl.pallas_call(
            functools.partial(reduce_kernel, n=n, chunks=chunks, b_at=b_at),
            in_specs=[vmem] * 8,
            out_specs=[vmem] * 3,
            out_shape=[
                jax.ShapeDtypeStruct((rank, total_cols), bf16),
                jax.ShapeDtypeStruct((4, width), f32),
                jax.ShapeDtypeStruct((dp_n, rank, b_cols), bf16),
            ],
            scratch_shapes=[
                pltpu.VMEM((4, rank, total_cols), bf16),
                pltpu.VMEM((2, 2, rank, total_cols), bf16),
                pltpu.VMEM((2, half, total_cols), bf16),
                pltpu.VMEM((2, half, total_cols), bf16),
                pltpu.VMEM((2, half, total_cols), bf16),
                pltpu.VMEM((2, half, total_cols), bf16),
                pltpu.VMEM((half, total_cols), bf16),
                pltpu.VMEM((half, total_cols), bf16),
                pltpu.VMEM((rank, total_cols), bf16),
                pltpu.VMEM((n, rank // n, total_cols), bf16),
                pltpu.VMEM((2 + n, 4, width), f32),
                pltpu.VMEM((4, 4, width), f32),
                dma((chunks,)), dma((chunks,)),
                dma((2, chunks)), dma((2, chunks)),
                dma((2, chunks)), dma((2, chunks)),
                dma((n, chunks)), dma((n, chunks)),
                dma((n, chunks)), dma((n, chunks)),
                dma((2 + n,)), dma((2 + n,)),
                dma((7,)), dma((7,)),
            ],
            compiler_params=pltpu.CompilerParams(
                collective_id=1, has_side_effects=True, vmem_limit_bytes=48 << 20
            ),
            name="reduce",
        )(
            owned.reshape(4, 2, rank, total_cols), norm_part,
            adapt_b, mean_b, square_b, adapt_b_ff, mean_b_ff, square_b_ff,
        )
    else:
        reduced = lax.psum_scatter(owned.astype(f32), "dp", scatter_dimension=0, tiled=True)
        reduced = lax.psum(reduced[0], "blk").astype(bf16)
        norm_sum = lax.psum(norm_part, ("dp", "blk"))
        grads_b = reduced[:, b_at:].astype(f32)
        cut = adapt_b.shape[1]
        fresh = jnp.concatenate(
            [
                adam_fresh(adapt_b, grads_b[:, :cut], mean_b, square_b),
                adam_fresh(adapt_b_ff, grads_b[:, cut:], mean_b_ff, square_b_ff),
            ],
            axis=1,
        ).astype(bf16)
        fresh = lax.all_gather(fresh, "dp", axis=0, tiled=False)
    grad_gain, grad_shift = norm_sum[:2], norm_sum[2:]

    state = [
        adapt_a, mean_a, square_a, keep_a,
        adapt_a_ff, mean_a_ff, square_a_ff, keep_a_ff,
        adapt_b, mean_b, square_b, keep_b,
        adapt_b_ff, mean_b_ff, square_b_ff, keep_b_ff,
    ]

    def all_of(value):
        zeros = (0,) * value.ndim
        return pl.BlockSpec(value.shape, lambda j: zeros, pipeline_mode=pl.Buffered(1))

    four = [adapt_a, adapt_a_ff, adapt_b, adapt_b_ff]
    results = [v for v in four] + [v for v in four for _ in range(2)]
    b_w, f_w = adapt_b.shape[1], adapt_b_ff.shape[1]
    owners = max(1, lanes // f_w)
    w_spec = pl.BlockSpec((kr, owners * b_w), lambda j: (0, j))
    wd_spec = pl.BlockSpec((down_rows, owners * f_w), lambda j: (0, j))
    updated = pl.pallas_call(
        functools.partial(update_kernel, rank=rank, width=width),
        grid=(dp_n // owners,),
        in_specs=[all_of(reduced), pl.BlockSpec((owners, rank, b_cols), lambda j: (j, 0, 0)), w_spec, wd_spec]
        + [all_of(v) for v in state],
        out_specs=[all_of(v) for v in results] + [w_spec, wd_spec],
        out_shape=[jax.ShapeDtypeStruct(v.shape, f32) for v in results]
        + [
            jax.ShapeDtypeStruct(frozen_input_weights.shape, bf16),
            jax.ShapeDtypeStruct(frozen_down_weight.shape, bf16),
        ],
        scratch_shapes=[pltpu.VMEM((3, kr, rank), bf16), pltpu.VMEM((down_rows, rank), bf16)],
        compiler_params=pltpu.CompilerParams(vmem_limit_bytes=48 << 20),
        name="update",
    )(reduced, fresh, frozen_input_weights, frozen_down_weight, *state)
    grad_a, grad_a_ff, grad_b, grad_b_ff = updated[:4]
    new_mean_a, new_square_a, new_mean_a_ff, new_square_a_ff = updated[4:8]
    new_mean_b, new_square_b, new_mean_b_ff, new_square_b_ff = updated[8:12]
    folded_input_weights, folded_down_weight = updated[12:]
    return (
        mixed,
        grad_tokens,
        grad_gain,
        grad_shift,
        grad_a,
        grad_a_ff,
        grad_b,
        grad_b_ff,
        new_mean_a,
        new_square_a,
        new_mean_a_ff,
        new_square_a_ff,
        new_mean_b,
        new_square_b,
        new_mean_b_ff,
        new_square_b_ff,
        folded_input_weights,
        folded_down_weight,
    )


def solution(mesh):
    in_specs = (
        P("dp", "blk", None),
        P("dp", "blk", None),
        P("dp", "blk"),
        P(),
        P("dp", None),
        P(),
        P("dp", None),
        P(),
        P(),
        P(),
        P("dp", None),
        P("dp", None),
        P(None, "dp"),
        P(None, "dp"),
        P("dp", None),
        P("dp", None),
        P(None, "dp"),
        P(None, "dp"),
        P("dp", None),
        P("dp", None),
        P(None, "dp"),
        P(None, "dp"),
        P("dp", None),
        P("dp", None),
        P(None, "dp"),
        P(None, "dp"),
    )
    out_specs = (
        P("dp", "blk", None),
        P("dp", "blk", None),
        P(),
        P(),
        P("dp", None),
        P("dp", None),
        P(None, "dp"),
        P(None, "dp"),
        P("dp", None),
        P("dp", None),
        P("dp", None),
        P("dp", None),
        P(None, "dp"),
        P(None, "dp"),
        P(None, "dp"),
        P(None, "dp"),
        P("dp", None),
        P("dp", None),
    )
    return jax.shard_map(
        functools.partial(body, mesh.shape["dp"], mesh.shape["blk"]), mesh=mesh, in_specs=in_specs, out_specs=out_specs, check_vma=False)
```

```python
import functools
import math

import jax
import jax.numpy as jnp
import numpy as np
from jax import lax
from jax.experimental import pallas as pl
from jax.experimental.pallas import tpu as pltpu
from jax.sharding import PartitionSpec as P

HEADS = 16
ROTARY = 16
DOMAINS = 22

adapter_scale = 0.25
rope_base = 10000.0
norm_eps = 1e-05
masked_score = -1e30
first_fix = 1.0 - (0.9**10) ** 10
second_fix = 1.0 - (0.999**10) ** 10

f32 = jnp.float32
bf16 = jnp.bfloat16


def nn(left, right):
    return lax.dot_general(left, right, (((1,), (0,)), ((), ())), preferred_element_type=f32)


def nt(left, right):
    return lax.dot_general(left, right, (((1,), (1,)), ((), ())), preferred_element_type=f32)


def tn(left, right):
    return lax.dot_general(left, right, (((0,), (0,)), ((), ())), preferred_element_type=f32)


def rope_lane_tables(length, depth, lanes):
    half = ROTARY // 2
    freqs = rope_base ** (-(jnp.arange(half, dtype=f32) * 2.0) / ROTARY)
    angles = jnp.arange(length, dtype=f32)[:, None] * freqs[None, :]
    cosine, sine = jnp.cos(angles), jnp.sin(angles)
    rest = depth - ROTARY
    ones, zero_half = jnp.ones((length, rest), f32), jnp.zeros((length, half), f32)
    zero_rest = jnp.zeros((length, rest), f32)
    keep = jnp.concatenate([cosine, cosine, ones], axis=1)
    from_above = jnp.concatenate([-sine, zero_half, zero_rest], axis=1)
    from_below = jnp.concatenate([zero_half, sine, zero_rest], axis=1)
    times = lanes // depth
    return tuple(jnp.tile(table, (1, times)) for table in (keep, from_above, from_below))


def turn(values, keep, above, below, sign):
    lanes = values.shape[-1]
    half = ROTARY // 2
    up = pltpu.roll(values, lanes - half, 1)
    down = pltpu.roll(values, half, 1)
    return values * keep + sign * (up * above + down * below)


def qkv_kernel(
    z_ref, x_ref, gain_ref, shift_ref, wq_ref, wk_ref, wv_ref, a_ref, b_ref, bias_ref,
    keep_ref, above_ref, below_ref, q_ref, k_ref, v_ref, first_ref, mid_ref,
):
    cols = wq_ref.shape[1]
    x = x_ref[...].reshape(x_ref.shape[2:]).astype(f32)
    centre = x - jnp.mean(x, axis=-1, keepdims=True)
    spread = jnp.mean(centre * centre, axis=-1, keepdims=True)
    first = (centre * lax.rsqrt(spread + norm_eps) * gain_ref[...] + shift_ref[...]).astype(bf16)
    mid = nn(first, a_ref[...]).astype(bf16)
    first_ref[...] = first.reshape(first_ref.shape)
    mid_ref[...] = mid.reshape(mid_ref.shape)
    low = adapter_scale * nn(mid, b_ref[...]) + bias_ref[...]
    lanes = keep_ref.shape[1]
    tables = keep_ref[...], above_ref[...], below_ref[...]
    query = nn(first, wq_ref[...]) + low[:, :cols]
    keys = nn(first, wk_ref[...]) + low[:, cols : 2 * cols]
    values = nn(first, wv_ref[...]) + low[:, 2 * cols :]
    for at in range(0, cols, lanes):
        part = slice(at, at + lanes)
        q_ref[0, :, part] = turn(query[:, part], *tables, 1.0).astype(bf16)
        k_ref[0, :, part] = turn(keys[:, part], *tables, 1.0).astype(bf16)
    v_ref[0] = values.astype(bf16)


MESH = pl.DeviceIdType.MESH


def attend_pair(query, keys, values, grad, tables, dk_ref, dv_ref, depth, blocks, store):
    lanes = keys.shape[1]
    span = keys.shape[0] // blocks
    scale = 1.0 / math.sqrt(depth)
    lane = lax.broadcasted_iota(jnp.int32, (1, lanes), 1)
    masks = [jnp.where(lane // depth == h, 1.0, 0.0).astype(bf16) for h in range(lanes // depth)]
    diagonal = lax.broadcasted_iota(jnp.int32, (span, span), 0) <= lax.broadcasted_iota(
        jnp.int32, (span, span), 1
    )
    keys_t, values_t = keys.T, values.T
    dk_ref[...] = jnp.zeros_like(dk_ref)
    dv_ref[...] = jnp.zeros_like(dv_ref)
    for i in range(blocks):
        rows = slice(i * span, (i + 1) * span)
        end = (i + 1) * span
        q_i, g_i = query[rows], grad[rows]
        g_t = g_i.T
        outs, grads = [], []
        dk, dv = None, None
        for h, mask in enumerate(masks):
            part = slice(h * depth, (h + 1) * depth)
            q_h, g_h = q_i * mask, g_i * mask
            scores = nt(keys[:end], q_h) * scale
            last = jnp.where(diagonal, scores[i * span :], masked_score)
            scores = last if i == 0 else jnp.concatenate([scores[: i * span], last], axis=0)
            weights = jnp.exp(scores - jnp.max(scores, axis=0, keepdims=True))
            weights = weights * (1.0 / jnp.sum(weights, axis=0, keepdims=True))
            low = weights.astype(bf16)
            out_t = nn(values_t[part, :end], low)
            grad_p = nt(values[:end], g_h)
            delta = jnp.sum(out_t * g_t[part].astype(f32), axis=0, keepdims=True)
            grad_s = (weights * (grad_p - delta)).astype(bf16)
            outs.append(out_t)
            grads.append(nn(keys_t[part, :end], grad_s))
            dk_h, dv_h = nn(grad_s, q_h), nn(low, g_h)
            dk = dk_h if dk is None else dk + dk_h
            dv = dv_h if dv is None else dv + dv_h
        dk_ref[:end] += dk
        dv_ref[:end] += dv
        store(i, 0, jnp.concatenate(outs, axis=0).T.astype(bf16))
        dq = jnp.concatenate(grads, axis=0).T * scale
        store(i, 1, turn(dq, *[t[rows] for t in tables], -1.0).astype(bf16))
    for i in range(blocks):
        rows = slice(i * span, (i + 1) * span)
        dk = dk_ref[rows] * scale
        store(i, 2, turn(dk, *[t[rows] for t in tables], -1.0).astype(bf16))
        store(i, 3, dv_ref[rows].astype(bf16))


def normal(x):
    centre = x - jnp.mean(x, axis=-1, keepdims=True)
    return centre * lax.rsqrt(jnp.mean(centre * centre, axis=-1, keepdims=True) + norm_eps)


def front_kernel(
    tokens_ref, win_ref, wdown_ref, a_ref, aff_ref, b_ref, bff_ref,
    cot_ref, weight_ref, gain_ref, shift_ref, bias_ref, freq_ref,
    win_out, wdown_out, a_out, aff_out, b_out, bff_out,
    q_out, k_out, v_out, first_out, mid_out, g_out,
    low_ref, second_ref, mid_up_ref, mid_up_t_ref, dmid_ff_ref, dmid_ff_t_ref, dmid_out_t_ref,
    keep_ref, above_ref, below_ref,
    x_all, q_s, k_s, v_s, first_s, mid_s, ga, wout_v, wqkv_v, a_v, b_v, bff_v,
    sx, qx, own_sem, sr, qr, sl, ql, sd, qd, load_sem, store_sem, token_sem,
    *, n, depth,
):
    z = lax.axis_index("blk")
    dp = lax.axis_index("dp")
    y, x, c = dp // 4, lax.rem(dp // 2, 2), lax.rem(dp, 2)
    core = (dp + 1 - 2 * c, z)
    along_x = (dp + 2 - 4 * x, z)
    along_y = (dp + 4 - 8 * y, z)
    peers = [(dp, lax.rem(z + t, n)) for t in range(1, n)]
    seqs, span, width = tokens_ref.shape
    kr, down_rows, rank = win_ref.shape[0], wdown_ref.shape[0], b_ref.shape[0]
    b_w, f_w = b_ref.shape[1], bff_ref.shape[1]
    cz = q_s.shape[2]
    lanes = keep_ref.shape[1]
    four = 4 * width

    barrier = pltpu.get_barrier_semaphore()
    for peer in [core, along_x, along_y] + peers:
        pl.semaphore_signal(barrier, inc=1, device_id=peer, device_id_type=MESH)
    pl.semaphore_wait(barrier, 2 + n)

    def remote(src, dst, send, recv, peer):
        return pltpu.make_async_remote_copy(
            src_ref=src, dst_ref=dst, send_sem=send, recv_sem=recv, device_id=peer, device_id_type=MESH
        )

    shards = [
        (win_ref.at[:, :four], lambda d: win_out.at[pl.ds(pl.multiple_of(d * kr, kr), kr), :four]),
        (a_ref, lambda d: a_out.at[pl.ds(pl.multiple_of(d * kr, kr), kr), :]),
        (b_ref, lambda d: b_out.at[:, pl.ds(pl.multiple_of(d * b_w, b_w), b_w)]),
        (bff_ref, lambda d: bff_out.at[:, pl.ds(pl.multiple_of(d * f_w, f_w), f_w)]),
        (win_ref.at[:, four:], lambda d: win_out.at[pl.ds(pl.multiple_of(d * kr, kr), kr), four:]),
        (wdown_ref, lambda d: wdown_out.at[pl.ds(pl.multiple_of(d * down_rows, down_rows), down_rows), :]),
        (aff_ref, lambda d: aff_out.at[pl.ds(pl.multiple_of(d * down_rows, down_rows), down_rows), :]),
    ]
    groups = [(0, 1, 2, 3), (4,), (5, 6)]
    from_x, from_y = dp + 2 - 4 * x, dp + 4 - 8 * y
    across = dp + 2 - 4 * x + 4 - 8 * y
    onward = jnp.where(c == 0, from_y, from_x)
    target = (jnp.where(c == 0, along_x[0], along_y[0]), z)

    def hop(i, kind):
        shard, there = shards[i]
        src, dst, peer = {
            0: (shard, there(dp), along_x),
            1: (shard, there(dp), along_y),
            2: (shard, there(dp), core),
            3: (there(onward), there(onward), target),
            4: (there(from_x), there(from_x), core),
            5: (there(from_y), there(from_y), core),
            6: (there(across), there(across), core),
        }[kind]
        return remote(src, dst, sx.at[i, kind], qx.at[i, kind], peer)

    def own_copy(i):
        return pltpu.make_async_copy(shards[i][0], shards[i][1](dp), own_sem.at[i])

    def start_own(group):
        for kind in (0, 1, 2):
            for i in groups[group]:
                hop(i, kind).start()
        for i in groups[group]:
            own_copy(i).start()

    def pass_on(group):
        for i in groups[group]:
            hop(i, 0).wait_recv()
            hop(i, 1).wait_recv()
        for kind in (3, 4, 5):
            for i in groups[group]:
                hop(i, kind).start()

    def close(group):
        for i in groups[group]:
            hop(i, 3).wait_recv()
            hop(i, 6).start()

    def arrived(group):
        for i in groups[group]:
            own_copy(i).wait()
            for kind in (2, 4, 5, 6):
                hop(i, kind).wait_recv()

    def rightward(s):
        return remote(x_all.at[z - s + 1], x_all.at[z - s + 1], sr.at[s], qr.at[s], (dp, z + 1))

    def leftward(s):
        return remote(x_all.at[z + s - 1], x_all.at[z + s - 1], sl.at[s], ql.at[s], (dp, z - 1))

    def from_left(s):
        return remote(x_all.at[z - s], x_all.at[z - s], sr.at[s], qr.at[s], (dp, z - 1))

    def from_right(s):
        return remote(x_all.at[z + s], x_all.at[z + s], sl.at[s], ql.at[s], (dp, z + 1))

    def ring_start(s):
        pl.when((z < n - 1) & (z - s + 1 >= 0))(lambda: rightward(s).start())
        pl.when((z > 0) & (z + s - 1 < n))(lambda: leftward(s).start())

    def ring_wait(s):
        pl.when(z - s >= 0)(lambda: from_left(s).wait_recv())
        pl.when(z + s < n)(lambda: from_right(s).wait_recv())

    def ring_end(s):
        pl.when((z < n - 1) & (z - s + 1 >= 0))(lambda: rightward(s).wait_send())
        pl.when((z > 0) & (z + s - 1 < n))(lambda: leftward(s).wait_send())

    token_copy = pltpu.make_async_copy(tokens_ref, x_all.at[z], token_sem.at[0])
    token_copy.start()
    start_own(0)
    token_copy.wait()
    ring_start(1)

    unit_lane = lax.rem(lax.broadcasted_iota(jnp.int32, (1, lanes), 1), depth)
    half = ROTARY // 2
    for b in range(n):
        rows = slice(b * span, (b + 1) * span)
        place = (lax.broadcasted_iota(jnp.int32, (span, lanes), 0) + b * span).astype(f32)
        angle = place * freq_ref[...]
        cosine, sine = jnp.cos(angle), jnp.sin(angle)
        keep_ref[rows] = jnp.where(unit_lane < ROTARY, cosine, 1.0)
        above_ref[rows] = jnp.where(unit_lane < half, -sine, 0.0)
        below_ref[rows] = jnp.where((unit_lane >= half) & (unit_lane < ROTARY), sine, 0.0)
    for q in range(seqs):
        part = slice(q * span, (q + 1) * span)
        low_ref[part] = (cot_ref[q].astype(f32) * weight_ref[part]).astype(bf16)
        unit = normal(x_all[z, q].astype(f32))
        second_ref[part] = (unit * gain_ref[1:2] + shift_ref[1:2]).astype(bf16)

    pass_on(0)
    start_own(1)
    ring_wait(1)
    if n > 2:
        ring_start(2)
    close(0)
    arrived(0)

    loads = [
        pltpu.make_async_copy(win_out.at[:, 3 * width : four], wout_v, load_sem.at[0]),
        pltpu.make_async_copy(a_out, a_v, load_sem.at[1]),
        pltpu.make_async_copy(b_out, b_v, load_sem.at[2]),
        pltpu.make_async_copy(bff_out, bff_v, load_sem.at[3]),
    ] + [
        pltpu.make_async_copy(
            win_out.at[:, pl.ds(pl.multiple_of(t * width + z * cz, cz), cz)], wqkv_v.at[t], load_sem.at[4 + t]
        )
        for t in range(3)
    ]
    for copy in loads:
        copy.start()
    for copy in loads:
        copy.wait()

    def grad_out(q, _):
        part = pl.ds(pl.multiple_of(q * span, span), span)
        low = low_ref[part, :]
        dmid = (adapter_scale * nt(low, b_v[:, 3 * width : four])).astype(bf16)
        dmid_out_t_ref[q] = dmid.T
        for g in range(n):
            rows = slice(g * cz, (g + 1) * cz)
            value = nt(low, wout_v[rows]) + nt(dmid, a_v[rows, rank : 2 * rank])
            ga[g, q] = value.astype(bf16)
        return 0

    lax.fori_loop(0, seqs, grad_out, 0)
    place_own = pl.ds(pl.multiple_of(z * span, span), span)

    def grad_send(t):
        return remote(ga.at[lax.rem(z + t, n)], g_out.at[:, place_own, :], sd.at[t], qd.at[t], peers[t - 1])

    grad_own = pltpu.make_async_copy(ga.at[z], g_out.at[:, place_own, :], token_sem.at[1])
    grad_own.start()
    for t in range(1, n):
        grad_send(t).start()

    def stores(b):
        rows = pl.ds(pl.multiple_of(b * span, span), span)
        return [
            pltpu.make_async_copy(src.at[:, rows, :], dst.at[:, rows, :], store_sem.at[i, b])
            for i, (src, dst) in enumerate(
                ((q_s, q_out), (k_s, k_out), (v_s, v_out), (first_s, first_out), (mid_s, mid_out))
            )
        ]

    def project_block(b):
        rows = pl.ds(pl.multiple_of(b * span, span), span)

        def one(q, _):
            first = (normal(x_all[b, q].astype(f32)) * gain_ref[0:1] + shift_ref[0:1]).astype(bf16)
            mid = nn(first, a_v[:, 0:rank]).astype(bf16)
            first_s[q, rows, :] = first
            mid_s[q, rows, :] = mid
            for t, kept in enumerate((q_s, k_s, v_s)):
                at = pl.ds(pl.multiple_of(t * width + z * cz, cz), cz)
                value = nn(first, wqkv_v[t]) + adapter_scale * nn(mid, b_v[:, at]) + bias_ref[:, at]
                if t < 2:
                    value = jnp.concatenate(
                        [
                            turn(value[:, i : i + lanes], keep_ref[rows, :], above_ref[rows, :], below_ref[rows, :], 1.0)
                            for i in range(0, cz, lanes)
                        ],
                        axis=1,
                    )
                kept[q, rows, :] = value.astype(bf16)
            return 0

        lax.fori_loop(0, seqs, one, 0)
        for copy in stores(b):
            copy.start()

    def project_near(s):
        def side(i, _):
            b = z + s * (2 * i - 1)
            pl.when((b >= 0) & (b < n))(lambda: project_block(b))
            return 0

        lax.fori_loop(0, 2 if s else 1, side, 0)

    def local_products(q, _):
        part = pl.ds(pl.multiple_of(q * span, span), span)
        mid = nn(second_ref[part, :], a_v[:, 2 * rank : 3 * rank]).astype(bf16)
        mid_up_ref[part, :] = mid
        mid_up_t_ref[q] = mid.T
        dmid = (adapter_scale * nt(low_ref[part, :], bff_v[...])).astype(bf16)
        dmid_ff_ref[part, :] = dmid
        dmid_ff_t_ref[q] = dmid.T
        return 0

    project_block(z)
    pass_on(1)
    start_own(2)
    for s in range(2, n):
        ring_wait(s)
        if s + 1 < n:
            ring_start(s + 1)
        project_near(s - 1)
        if s == 2:
            close(1)
            lax.fori_loop(0, seqs, local_products, 0)
            pass_on(2)
    project_near(n - 1)
    close(2)
    arrived(1)
    arrived(2)
    for i in range(len(shards)):
        for kind in range(7):
            hop(i, kind).wait_send()
    for s in range(1, n):
        ring_end(s)
    grad_own.wait()
    for t in range(1, n):
        grad_send(t).wait()
    for b in range(n):
        for copy in stores(b):
            copy.wait()


def middle_kernel(
    q_ref, k_ref, v_ref, g_ref, keep_ref, above_ref, below_ref, mid_qkv_t_ref,
    second_ref, low_ref, mid_ref, mid_t_ref, dmid_ref, dmid_t_ref,
    up_ref, down_ref, a_ref, b_ref, bias_ref,
    local_ref, own_ref, ff_ref, back_ref, mid_ff_ref, dmid_up_ref, ga_ref, gb_ref,
    buffer, dk_ref, dv_ref, mid_acc, dmid_acc, send_sem, recv_sem, own_sem,
    *, n, pairs, steps, depth,
):
    step = pl.program_id(0)
    z = lax.axis_index("blk")
    dp = lax.axis_index("dp")
    lanes = q_ref.shape[2]

    def copies(s):
        seq, pair = s // pairs, lax.rem(s, pairs)
        at = pl.ds(pl.multiple_of((z * pairs + pair) * lanes, lanes), lanes)
        target = local_ref.at[seq, :, :, at]
        own = pltpu.make_async_copy(buffer.at[s, z], target, own_sem.at[s])
        away = []
        for t in range(1, n):
            peer = lax.rem(z + t, n)
            away.append(
                pltpu.make_async_remote_copy(
                    src_ref=buffer.at[s, peer], dst_ref=target,
                    send_sem=send_sem.at[s, t], recv_sem=recv_sem.at[s, t],
                    device_id=(dp, peer), device_id_type=MESH,
                )
            )
        return own, away

    @pl.when(step == 0)
    def _():
        barrier = pltpu.get_barrier_semaphore()
        for t in range(1, n):
            pl.semaphore_signal(barrier, inc=1, device_id=(dp, lax.rem(z + t, n)), device_id_type=MESH)
        pl.semaphore_wait(barrier, n - 1)

    @pl.when(step < steps)
    def _():
        def store(i, kind, value):
            buffer[step, i, kind] = value
            if kind:
                own_ref[0, kind - 1, i * value.shape[0] : (i + 1) * value.shape[0], :] = value

        tables = keep_ref[...], above_ref[...], below_ref[...]
        attend_pair(q_ref[0], k_ref[0], v_ref[0], g_ref[0], tables, dk_ref, dv_ref, depth, n, store)
        own, away = copies(step)
        own.start()
        for copy in away:
            copy.start()

    @pl.when(step == steps)
    def _():
        ff_ref[...] = jnp.zeros_like(ff_ref)
        back_ref[...] = jnp.zeros_like(back_ref)
        mid_acc[...] = jnp.zeros_like(mid_acc)
        dmid_acc[...] = jnp.zeros_like(dmid_acc)

    @pl.when(step >= steps)
    def _():
        count, size = mid_t_ref.shape[0], mid_t_ref.shape[2]
        for at in range(count):
            rows = slice(at * size, (at + 1) * size)
            pre = nn(second_ref[rows], up_ref[...]) + bias_ref[...] + adapter_scale * nn(mid_ref[rows], b_ref[...])
            cdf = 0.5 + 0.5 * lax.erf(pre * (1.0 / math.sqrt(2.0)))
            hidden = (pre * cdf).astype(bf16)
            slope = cdf + pre * (jnp.exp(-0.5 * pre * pre) * (1.0 / math.sqrt(2.0 * math.pi)))
            grad_hidden = nt(low_ref[rows], down_ref[...]) + nt(dmid_ref[rows], a_ref[...])
            dup = (slope * grad_hidden).astype(bf16)
            ff_ref[rows] += nn(hidden, down_ref[...])
            back_ref[rows] += nt(dup, up_ref[...])
            mid_acc[rows] += nn(hidden, a_ref[...])
            dmid_acc[rows] += nt(dup, b_ref[...])
            ga = nn(dmid_t_ref[at], hidden)
            gb = nn(mid_t_ref[at], dup)
            ga_ref[...] = ga if at == 0 else ga_ref[...] + ga
            gb_ref[...] = gb if at == 0 else gb_ref[...] + gb

    @pl.when(step == pl.num_programs(0) - 1)
    def _():
        mid_ff_ref[...] = mid_acc[...].astype(bf16)
        dmid_up_ref[...] = (adapter_scale * dmid_acc[...]).astype(bf16)
        for s in range(steps):
            own, away = copies(s)
            own.wait()
            for copy in away:
                copy.wait()


def finish_kernel(
    local_ref, wo_ref, wq_ref, wk_ref, wv_ref, a_out_ref, a_qkv_ref, b_out_ref, bq_ref, bk_ref, bv_ref,
    bias_ref, x_ref, cot_ref, weight_ref, ff_ref, bias_ff_ref, mid_ff_ref, b_ff_ref,
    second_ref, dmid_up_ref, a_up_ref, gain_ref, dmid_out_t_ref, low_ref,
    mixed_ref, tokens_ref, norm_ref, ga_ref, gb_ref,
    att_acc, mid_acc, first_acc, dmid_acc,
):
    t = pl.program_id(0)
    rows = x_ref.shape[0] * x_ref.shape[1]
    cols = wq_ref.shape[1]

    @pl.when(t == 0)
    def _():
        att_acc[...] = jnp.zeros_like(att_acc)
        mid_acc[...] = jnp.zeros_like(mid_acc)
        first_acc[...] = jnp.zeros_like(first_acc)
        dmid_acc[...] = jnp.zeros_like(dmid_acc)

    out, dq, dk, dv = (local_ref[:, i].reshape(rows, cols) for i in range(4))
    att_acc[...] += nn(out, wo_ref[...])
    mid_acc[...] += nn(out, a_out_ref[...])
    first_acc[...] += nt(dq, wq_ref[...]) + nt(dk, wk_ref[...]) + nt(dv, wv_ref[...])
    dmid_acc[...] += nt(dq, bq_ref[...]) + nt(dk, bk_ref[...]) + nt(dv, bv_ref[...])
    size = x_ref.shape[1]
    ga_ref[...] = sum(nn(dmid_out_t_ref[q], out[q * size : (q + 1) * size]) for q in range(x_ref.shape[0]))

    @pl.when(t == pl.num_programs(0) - 1)
    def _():
        size = x_ref.shape[1]
        norm = [jnp.zeros((1, first_acc.shape[1]), f32) for _ in range(4)]
        for q in range(x_ref.shape[0]):
            part = slice(q * size, (q + 1) * size)
            x = x_ref[q].astype(f32)
            mid = mid_acc[part].astype(bf16)
            gb = tn(mid, low_ref[part])
            gb_ref[...] = gb if q == 0 else gb_ref[...] + gb
            att = att_acc[part] + bias_ref[...] + adapter_scale * nn(mid, b_out_ref[...])
            ff = ff_ref[part] + bias_ff_ref[...] + adapter_scale * nn(mid_ff_ref[part], b_ff_ref[...])
            mixed_ref[q] = (x + att + ff).astype(bf16)
            dmid = (adapter_scale * dmid_acc[part]).astype(bf16)
            grad_first = first_acc[part] + nt(dmid, a_qkv_ref[...])
            grad_second = second_ref[part] + nt(dmid_up_ref[part], a_up_ref[...])
            centre = x - jnp.mean(x, axis=-1, keepdims=True)
            inv = lax.rsqrt(jnp.mean(centre * centre, axis=-1, keepdims=True) + norm_eps)
            unit = centre * inv
            pulled = grad_first * gain_ref[0:1] + grad_second * gain_ref[1:2]
            back = inv * (
                pulled
                - jnp.mean(pulled, axis=-1, keepdims=True)
                - unit * jnp.mean(pulled * unit, axis=-1, keepdims=True)
            )
            row_grad = cot_ref[q].astype(f32) * weight_ref[part]
            tokens_ref[q] = (row_grad + back).astype(bf16)
            for k, value in enumerate((grad_first * unit, grad_second * unit, grad_first, grad_second)):
                norm[k] += jnp.sum(value, axis=0, keepdims=True)
        norm_ref[...] = jnp.concatenate(norm, axis=0)


def reduce_kernel(
    g_ref, norm_in_ref, b_ref, mean_ref, square_ref, bf_ref, mean_f_ref, square_f_ref,
    out_ref, norm_ref, fresh_ref,
    r1, h, r2a, r2b, ia, ib, r3a, r3b, total, r4, nr, nsum,
    s1, q1, s2, q2, s3, q3, s4, q4, s5, q5, sn, qn, sg, qg,
    *, n, chunks, b_at,
):
    z = lax.axis_index("blk")
    dp = lax.axis_index("dp")
    y, x, c = dp // 4, lax.rem(dp // 2, 2), lax.rem(dp, 2)
    core = (dp + 1 - 2 * c, z)
    along_x = (dp + 2 - 4 * x, z)
    along_y = (dp + 4 - 8 * y, z)
    peers = [(dp, lax.rem(z + t, n)) for t in range(1, n)]
    half = g_ref.shape[2] // 2
    part = g_ref.shape[2] // n
    width = g_ref.shape[3] // chunks

    barrier = pltpu.get_barrier_semaphore()
    for peer in [core, along_x, along_y] + peers:
        pl.semaphore_signal(barrier, inc=1, device_id=peer, device_id_type=MESH)
    pl.semaphore_wait(barrier, 2 + n)

    def remote(src, dst, send, recv, peer):
        return pltpu.make_async_remote_copy(
            src_ref=src, dst_ref=dst, send_sem=send, recv_sem=recv, device_id=peer, device_id_type=MESH
        )

    def cols(k):
        return slice(k * width, (k + 1) * width)

    def mine(k=None):
        return pl.ds(pl.multiple_of(z * part, part), part)

    def first(k):
        return [remote(g_ref.at[:, 1 - c, :, cols(k)], r1.at[:, :, cols(k)], s1.at[k], q1.at[k], core)]

    def second(k):
        return [
            remote(h.at[:, 1 - x, 0:half, cols(k)], r2a.at[:, :, cols(k)], s2.at[0, k], q2.at[0, k], along_x),
            remote(h.at[1 - y, :, half:, cols(k)], r2b.at[:, :, cols(k)], s2.at[1, k], q2.at[1, k], along_y),
        ]

    def third(k):
        return [
            remote(ia.at[1 - y, :, cols(k)], r3a.at[:, cols(k)], s3.at[0, k], q3.at[0, k], along_y),
            remote(ib.at[1 - x, :, cols(k)], r3b.at[:, cols(k)], s3.at[1, k], q3.at[1, k], along_x),
        ]

    def fourth(k):
        found = []
        for t in range(1, n):
            to = lax.rem(z + t, n)
            rows = pl.ds(pl.multiple_of(to * part, part), part)
            found.append(
                remote(total.at[rows, cols(k)], r4.at[t, :, cols(k)], s4.at[t, k], q4.at[t, k], peers[t - 1])
            )
        return found

    def fifth(k):
        return [
            remote(out_ref.at[mine(), cols(k)], out_ref.at[mine(), cols(k)], s5.at[t, k], q5.at[t, k], peers[t - 1])
            for t in range(1, n)
        ]

    def add(a, b):
        return (a.astype(f32) + b.astype(f32)).astype(bf16)

    def norm_copy(i, peer):
        return remote(nsum.at[i], nr.at[i], sn.at[i], qn.at[i], peer)

    nsum[0] = norm_in_ref[...]
    norm_stages = [norm_copy(0, core), norm_copy(1, along_x), norm_copy(2, along_y)]
    norm_last = [
        remote(nsum.at[3], nr.at[2 + t], sn.at[2 + t], qn.at[2 + t], peers[t - 1]) for t in range(1, n)
    ]
    for k in range(chunks):
        first(k)[0].start()
    norm_stages[0].start()

    def after_first(k):
        for copy in first(k):
            copy.wait()
        for yy in range(2):
            for xx in range(2):
                h[yy, xx, :, cols(k)] = add(g_ref[2 * yy + xx, c, :, cols(k)], r1[2 * yy + xx, :, cols(k)])
        for copy in second(k):
            copy.start()

    def after_second(k):
        for copy in second(k):
            copy.wait()
        for i in range(2):
            ia[i, :, cols(k)] = add(h[i, x, 0:half, cols(k)], r2a[i, :, cols(k)])
            ib[i, :, cols(k)] = add(h[y, i, half:, cols(k)], r2b[i, :, cols(k)])
        for copy in third(k):
            copy.start()

    def after_third(k):
        for copy in third(k):
            copy.wait()
        total[0:half, cols(k)] = add(ia[y, :, cols(k)], r3a[:, cols(k)])
        total[half:, cols(k)] = add(ib[x, :, cols(k)], r3b[:, cols(k)])
        for copy in fourth(k):
            copy.start()

    def after_fourth(k):
        for copy in fourth(k):
            copy.wait()
        value = total[mine(), cols(k)].astype(f32)
        for t in range(1, n):
            value += r4[t, :, cols(k)].astype(f32)
        out_ref[mine(), cols(k)] = value.astype(bf16)
        for copy in fifth(k):
            copy.start()

    def after_fifth(k):
        for copy in fifth(k):
            copy.wait()

    stages = [after_first, after_second, after_third, after_fourth, after_fifth]
    for step in range(chunks + len(stages) - 1):
        for at in reversed(range(len(stages))):
            if 0 <= step - at < chunks:
                stages[at](step - at)
        if step < 3:
            norm_stages[step].wait()
            nsum[step + 1] = nsum[step] + nr[step]
            if step < 2:
                norm_stages[step + 1].start()
            else:
                for copy in norm_last:
                    copy.start()
    for copy in norm_last:
        copy.wait()
    value = jnp.zeros_like(nsum[3])
    for blk in range(n):
        there = lax.rem(z - blk + n, n)
        value += jnp.where(there == 0, nsum[3], nr[2 + jnp.maximum(there, 1)])
    norm_ref[...] = value

    cut = b_ref.shape[1]
    grads = out_ref[:, b_at:].astype(f32)
    new_b = adam_fresh(b_ref[...], grads[:, :cut], mean_ref[...], square_ref[...])
    new_f = adam_fresh(bf_ref[...], grads[:, cut:], mean_f_ref[...], square_f_ref[...])
    fresh_ref[dp] = jnp.concatenate([new_b, new_f], axis=1).astype(bf16)

    def gather(i, slot, peer):
        return remote(fresh_ref.at[slot], fresh_ref.at[slot], sg.at[i], qg.at[i], peer)

    from_x, from_y = dp + 2 - 4 * x, dp + 4 - 8 * y
    across = dp + 2 - 4 * x + 4 - 8 * y
    onward = jnp.where(c == 0, from_y, from_x)
    target = (jnp.where(c == 0, along_x[0], along_y[0]), z)
    direct = [gather(0, dp, along_x), gather(1, dp, along_y), gather(2, dp, core)]
    for copy in direct:
        copy.start()
    direct[0].wait()
    direct[1].wait()
    more = [gather(3, onward, target), gather(4, from_x, core), gather(5, from_y, core)]
    for copy in more:
        copy.start()
    more[0].wait()
    last = gather(6, across, core)
    last.start()
    direct[2].wait()
    more[1].wait()
    more[2].wait()
    last.wait()


def update_kernel(
    g_ref, fresh_ref, w_ref, wd_ref, *refs, rank, width,
):
    params, outs = refs[:16], refs[16:30]
    a_new, aff_new = refs[30:]
    j = pl.program_id(0)
    cols = w_ref.shape[1]

    @pl.when(j == 0)
    def _():
        rows, inner = params[0].shape[0], params[4].shape[0]
        got = g_ref[...].astype(f32)
        grads = [
            jnp.concatenate([got[:, i * rows : (i + 1) * rows].T for i in range(3)], axis=1),
            got[:, 3 * rows : 3 * rows + inner].T,
        ]
        at = 3 * rows + inner
        cut = params[8].shape[1]
        grads += [got[:, at : at + cut], got[:, at + cut :]]
        for i, grad in enumerate(grads):
            param, mean, square, keep = (r[...] for r in params[4 * i : 4 * i + 4])
            mean_new = 0.9 * mean + 0.1 * grad
            square_new = 0.999 * square + 0.001 * grad * grad
            kept = keep.astype(f32)
            outs[i][...] = grad
            outs[4 + 2 * i][...] = mean_new * kept
            outs[5 + 2 * i][...] = square_new * kept
            if i < 2:
                fresh = param - 0.01 * (mean_new / first_fix) / (jnp.sqrt(square_new / second_fix) + 1e-08)
                if i == 0:
                    for k in range(3):
                        a_new[k] = fresh[:, k * rank : (k + 1) * rank].astype(bf16)
                else:
                    aff_new[...] = fresh.astype(bf16)

    block = jnp.where(j * cols < 3 * width, 0, jnp.where(j * cols < 4 * width, 1, 2))
    cut = params[8].shape[1]
    fresh = [fresh_ref[i] for i in range(fresh_ref.shape[0])]
    update = nn(a_new[block], jnp.concatenate([f[:, :cut] for f in fresh], axis=1))
    outs[12][...] = (w_ref[...].astype(f32) + adapter_scale * update).astype(bf16)
    update = nn(aff_new[...], jnp.concatenate([f[:, cut:] for f in fresh], axis=1))
    outs[13][...] = (wd_ref[...].astype(f32) + adapter_scale * update).astype(bf16)


def adam_fresh(param, grad, mean, square):
    mean_new = 0.9 * mean + 0.1 * grad
    square_new = 0.999 * square + 0.001 * grad * grad
    return param - 0.01 * (mean_new / first_fix) / (jnp.sqrt(square_new / second_fix) + 1e-08)


def body(
    dp_n,
    n,
    tokens,
    cotangent,
    domain_ids,
    domain_weight,
    frozen_input_weights,
    bias_in,
    frozen_down_weight,
    bias_ff,
    norm_gain,
    norm_shift,
    adapt_a,
    adapt_a_ff,
    adapt_b,
    adapt_b_ff,
    mean_a,
    mean_a_ff,
    mean_b,
    mean_b_ff,
    square_a,
    square_a_ff,
    square_b,
    square_b_ff,
    keep_a,
    keep_a_ff,
    keep_b,
    keep_b_ff,
):
    seqs, span, width = tokens.shape
    rows = seqs * span
    rank = adapt_b.shape[0]
    depth = width // HEADS
    cz = width // n
    length = n * span
    z = lax.axis_index("blk")
    z_arr = jnp.full((1,), z, jnp.int32)
    kr = frozen_input_weights.shape[0]
    down_rows, inner = frozen_down_weight.shape[0], frozen_down_weight.shape[0] * dp_n
    lanes = 128

    def shift_by(values, s):
        return lax.ppermute(values, "blk", [(i, (i + s) % n) for i in range(n)])

    b_cols = adapt_b.shape[1] + adapt_b_ff.shape[1]
    bias32 = bias_in.astype(f32)
    lookup = (domain_ids[..., None] == jnp.arange(DOMAINS, dtype=jnp.int32)).astype(f32)
    row_weight = jnp.sum(lookup * domain_weight, axis=-1).reshape(rows, 1)
    whole_front = dp_n == 8 and rank % (16 * n) == 0
    if whole_front:
        vmem = pl.BlockSpec(memory_space=pltpu.VMEM)
        hbm = pl.BlockSpec(memory_space=pl.ANY)
        dma = pltpu.SemaphoreType.DMA
        half = ROTARY // 2
        freq = [rope_base ** (-(k * 2.0) / ROTARY) for k in range(half)]
        freq = np.tile(np.array(freq + freq + [0.0] * (depth - ROTARY), np.float32), lanes // depth)

        def shape(*dims, dtype=bf16):
            return jax.ShapeDtypeStruct(dims, dtype)

        (
            w_in, w_down, a_all, a_ff, b_in, b_ff, query, keys, values, first_pos, mid_pos, g_pos,
            grad_low, second, mid_up, mid_up_t, dmid_ff, dmid_ff_t, dmid_out_t, *tables,
        ) = pl.pallas_call(
            functools.partial(front_kernel, n=n, depth=depth),
            in_specs=[hbm] * 7 + [vmem] * 6,
            out_specs=[hbm] * 12 + [vmem] * 10,
            out_shape=[
                shape(width, 8 * width), shape(inner, width), shape(width, 3 * rank), shape(inner, rank),
                shape(rank, 8 * width), shape(rank, width),
                shape(seqs, length, cz), shape(seqs, length, cz), shape(seqs, length, cz),
                shape(seqs, length, width), shape(seqs, length, rank), shape(seqs, length, cz),
                shape(rows, width), shape(rows, width),
                shape(rows, rank), shape(seqs, rank, span), shape(rows, rank), shape(seqs, rank, span),
                shape(seqs, rank, span),
                shape(length, lanes, dtype=f32), shape(length, lanes, dtype=f32), shape(length, lanes, dtype=f32),
            ],
            scratch_shapes=[
                pltpu.VMEM((n, seqs, span, width), bf16),
                pltpu.VMEM((seqs, length, cz), bf16),
                pltpu.VMEM((seqs, length, cz), bf16),
                pltpu.VMEM((seqs, length, cz), bf16),
                pltpu.VMEM((seqs, length, width), bf16),
                pltpu.VMEM((seqs, length, rank), bf16),
                pltpu.VMEM((n, seqs, span, cz), bf16),
                pltpu.VMEM((width, width), bf16),
                pltpu.VMEM((3, width, cz), bf16),
                pltpu.VMEM((width, 3 * rank), bf16),
                pltpu.VMEM((rank, 8 * width), bf16),
                pltpu.VMEM((rank, width), bf16),
                dma((7, 7)), dma((7, 7)), dma((7,)),
                dma((n,)), dma((n,)), dma((n,)), dma((n,)), dma((n,)), dma((n,)),
                dma((7,)), dma((5, n)), dma((2,)),
            ],
            compiler_params=pltpu.CompilerParams(
                collective_id=2, has_side_effects=True, vmem_limit_bytes=58 << 20
            ),
            name="front",
        )(
            tokens, frozen_input_weights, frozen_down_weight,
            adapt_a.astype(bf16), adapt_a_ff.astype(bf16), adapt_b.astype(bf16), adapt_b_ff.astype(bf16),
            cotangent, row_weight, norm_gain, norm_shift, bias32.reshape(1, -1), freq.reshape(1, -1),
        )
    else:
        row_grad = cotangent.astype(f32).reshape(rows, width) * row_weight
        grad_low = row_grad.astype(bf16)
        b_shard = jnp.concatenate([adapt_b, adapt_b_ff], axis=1).astype(bf16)
        one = jnp.concatenate(
            [frozen_input_weights[:, : 4 * width], adapt_a.astype(bf16), b_shard.reshape(kr, -1)], axis=1
        )
        one = lax.all_gather(one, "dp", axis=0, tiled=True)
        two = lax.all_gather(frozen_input_weights[:, 4 * width :], "dp", axis=0, tiled=True)
        three = jnp.concatenate([frozen_down_weight, adapt_a_ff.astype(bf16)], axis=1)
        three = lax.all_gather(three, "dp", axis=0, tiled=True)
        a_at = 4 * width
        b_at = a_at + 3 * rank
        a_all = one[:, a_at:b_at]
        b_all = one[:, b_at:].reshape(dp_n, rank, b_cols)
        b_in = jnp.transpose(b_all[:, :, : adapt_b.shape[1]], (1, 0, 2)).reshape(rank, -1)
        b_ff = jnp.transpose(b_all[:, :, adapt_b.shape[1] :], (1, 0, 2)).reshape(rank, width)
        w_out = one[:, 3 * width : 4 * width]
        w_up = two
        w_down, a_ff = three[:, :width], three[:, width:]

        right, left = tokens, tokens
        rights, lefts = [None], [None]
        for s in range(1, n):
            right = lax.ppermute(right, "blk", [(i, i + 1) for i in range(n - 1)])
            left = lax.ppermute(left, "blk", [(i + 1, i) for i in range(n - 1)])
            rights.append(right)
            lefts.append(left)
        x_all = jnp.stack(
            [tokens] + [jnp.where(z >= s, rights[s], lefts[n - s]) for s in range(1, n)]
        )

        b_out = b_in[:, 3 * width : 4 * width]
        a_out = a_all[:, rank : 2 * rank]
        dmid_out = (adapter_scale * nt(grad_low, b_out)).astype(bf16)
        grad_att = (nt(grad_low, w_out) + nt(dmid_out, a_out)).astype(bf16)
        grad_att = jnp.transpose(grad_att.reshape(seqs, span, n, cz), (2, 0, 1, 3))

        def piece(values, s):
            return lax.dynamic_index_in_dim(values, lax.rem(z + s, n), 0, keepdims=False)

        g_all = jnp.stack(
            [piece(grad_att, 0)] + [shift_by(piece(grad_att, s), s) for s in range(1, n)]
        )

        tables = rope_lane_tables(length, depth, lanes)
        own = [lax.dynamic_slice_in_dim(b_in[:, t * width : (t + 1) * width], z * cz, cz, 1) for t in range(3)]
        b_own = jnp.concatenate(own, axis=1)
        bias_own = jnp.concatenate(
            [lax.dynamic_slice_in_dim(bias32, t * width + z * cz, cz, 0) for t in range(3)]
        ).reshape(1, 3 * cz)

        def block_of(s, z_ref):
            return lax.rem(z_ref[0] - s + n, n)

        table_spec = pl.BlockSpec((span, lanes), lambda s, q, z_ref: (block_of(s, z_ref), 0))
        head_spec = pl.BlockSpec((1, span, cz), lambda s, q, z_ref: (q, block_of(s, z_ref), 0))
        query, keys, values, first_all, mid_all = pl.pallas_call(
            qkv_kernel,
            grid_spec=pltpu.PrefetchScalarGridSpec(
                num_scalar_prefetch=1,
                grid=(n, seqs),
                in_specs=[
                    pl.BlockSpec((1, 1, span, width), lambda s, q, z_ref: (s, q, 0, 0)),
                    pl.BlockSpec((1, width), lambda s, q, z_ref: (0, 0)),
                    pl.BlockSpec((1, width), lambda s, q, z_ref: (0, 0)),
                    pl.BlockSpec((width, cz), lambda s, q, z_ref: (0, z_ref[0])),
                    pl.BlockSpec((width, cz), lambda s, q, z_ref: (0, n + z_ref[0])),
                    pl.BlockSpec((width, cz), lambda s, q, z_ref: (0, 2 * n + z_ref[0])),
                    pl.BlockSpec((width, rank), lambda s, q, z_ref: (0, a_at // rank)),
                    pl.BlockSpec((rank, 3 * cz), lambda s, q, z_ref: (0, 0)),
                    pl.BlockSpec((1, 3 * cz), lambda s, q, z_ref: (0, 0)),
                    table_spec,
                    table_spec,
                    table_spec,
                ],
                out_specs=[
                    head_spec,
                    head_spec,
                    head_spec,
                    pl.BlockSpec((1, 1, span, width), lambda s, q, z_ref: (block_of(s, z_ref), q, 0, 0)),
                    pl.BlockSpec((1, 1, span, rank), lambda s, q, z_ref: (block_of(s, z_ref), q, 0, 0)),
                ],
            ),
            out_shape=[jax.ShapeDtypeStruct((seqs, length, cz), bf16)] * 3
            + [
                jax.ShapeDtypeStruct((n, seqs, span, width), bf16),
                jax.ShapeDtypeStruct((n, seqs, span, rank), bf16),
            ],
            compiler_params=pltpu.CompilerParams(vmem_limit_bytes=48 << 20),
            cost_estimate=pl.CostEstimate(
                flops=2 * n * rows * width * 4 * cz, bytes_accessed=6 * n * rows * width, transcendentals=0
            ),
            name="qkv",
        )(
            z_arr, x_all, norm_gain[0:1], norm_shift[0:1], one, one, one, one, b_own, bias_own, *tables
        )

        input_rows = tokens.astype(f32).reshape(rows, width)
        centre = input_rows - jnp.mean(input_rows, axis=-1, keepdims=True)
        inv = lax.rsqrt(jnp.mean(centre * centre, axis=-1, keepdims=True) + norm_eps)
        second = (centre * inv * norm_gain[1] + norm_shift[1]).astype(bf16)
        a_up = a_all[:, 2 * rank :]
        mid_up = nn(second, a_up).astype(bf16)
        dmid_ff = (adapter_scale * nt(grad_low, b_ff)).astype(bf16)
        g_pos = jnp.concatenate([g_all, g_all])
        g_pos = lax.rev(g_pos, (0,))
        g_pos = lax.dynamic_slice_in_dim(g_pos, lax.rem(n - 1 - z + n, n), n, 0)
        g_pos = jnp.transpose(g_pos, (1, 0, 2, 3)).reshape(seqs, length, cz)

        first_pos = jnp.transpose(first_all, (1, 0, 2, 3))
        mid_pos = jnp.transpose(mid_all, (1, 0, 2, 3))
        w_in = jnp.concatenate([one[:, :a_at], two], axis=1)
        mid_up_t, dmid_ff_t, dmid_out_t = (
            jnp.transpose(v.reshape(seqs, span, rank), (0, 2, 1)) for v in (mid_up, dmid_ff, dmid_out)
        )

    pairs = cz // lanes
    steps = seqs * pairs
    inner_block = min(512, inner)
    def one_buffer(shape):
        zeros = (0,) * len(shape)
        return pl.BlockSpec(shape, lambda s: zeros, pipeline_mode=pl.Buffered(1))

    def seq_pair(s):
        s = jnp.minimum(s, steps - 1)
        return s // pairs, lax.rem(s, pairs)

    def head_map(s):
        seq, pair = seq_pair(s)
        return seq, 0, pair

    def inner_at(s):
        return jnp.maximum(s - steps, 0)

    head = pl.BlockSpec((1, length, lanes), head_map)
    local, own, ff, grad_second, mid_ff, dmid_up, grad_a_ff_t, grad_b_up = pl.pallas_call(
        functools.partial(middle_kernel, n=n, pairs=pairs, steps=steps, depth=depth),
        grid=(steps + inner // inner_block,),
        in_specs=[head] * 4
        + [one_buffer((length, lanes))] * 3
        + [one_buffer((8, lanes))]
        + [one_buffer((rows, width))] * 2
        + [one_buffer((rows, rank)), one_buffer((seqs, rank, span))] * 2
        + [
            pl.BlockSpec((width, inner_block), lambda s: (0, 4 * width // inner_block + inner_at(s))),
            pl.BlockSpec((inner_block, width), lambda s: (inner_at(s), 0)),
            pl.BlockSpec((inner_block, rank), lambda s: (inner_at(s), 0)),
            pl.BlockSpec((rank, inner_block), lambda s: (0, 4 * width // inner_block + inner_at(s))),
            pl.BlockSpec((1, inner_block), lambda s: (0, 4 * width // inner_block + inner_at(s))),
        ],
        out_specs=[
            pl.BlockSpec(memory_space=pl.ANY),
            pl.BlockSpec((1, 3, length, lanes), lambda s: (seq_pair(s)[0], 0, 0, seq_pair(s)[1])),
            one_buffer((rows, width)),
            one_buffer((rows, width)),
            one_buffer((rows, rank)),
            one_buffer((rows, rank)),
            pl.BlockSpec((rank, inner_block), lambda s: (0, inner_at(s))),
            pl.BlockSpec((rank, inner_block), lambda s: (0, inner_at(s))),
        ],
        out_shape=[
            jax.ShapeDtypeStruct((seqs, 4, span, width), bf16),
            jax.ShapeDtypeStruct((seqs, 3, length, cz), bf16),
            jax.ShapeDtypeStruct((rows, width), f32),
            jax.ShapeDtypeStruct((rows, width), f32),
            jax.ShapeDtypeStruct((rows, rank), bf16),
            jax.ShapeDtypeStruct((rows, rank), bf16),
            jax.ShapeDtypeStruct((rank, inner), f32),
            jax.ShapeDtypeStruct((rank, inner), f32),
        ],
        scratch_shapes=[
            pltpu.VMEM((steps, n, 4, span, lanes), bf16),
            pltpu.VMEM((length, lanes), f32),
            pltpu.VMEM((length, lanes), f32),
            pltpu.VMEM((rows, rank), f32),
            pltpu.VMEM((rows, rank), f32),
            pltpu.SemaphoreType.DMA((steps, n)),
            pltpu.SemaphoreType.DMA((steps, n)),
            pltpu.SemaphoreType.DMA((steps,)),
        ],
        compiler_params=pltpu.CompilerParams(
            collective_id=0, has_side_effects=True, vmem_limit_bytes=60 << 20
        ),
        name="middle",
    )(
        query, keys, values, g_pos, *tables, tables[0][:8], second, grad_low, mid_up, mid_up_t, dmid_ff, dmid_ff_t,
        w_in, w_down, a_ff, b_in, bias32.reshape(1, -1),
    )
    grad_b_up = adapter_scale * grad_b_up

    first_pos = first_pos.reshape(seqs * length, width)
    mid_pos = mid_pos.reshape(seqs * length, rank)
    b_own = jnp.concatenate(
        [lax.dynamic_slice_in_dim(b_in[:, t * width : (t + 1) * width], z * cz, cz, 1) for t in range(3)], axis=1
    )
    djoint_own = [own[:, t].reshape(seqs * length, cz) for t in range(3)]
    dmid_own = sum(nt(djoint_own[t], b_own[:, t * cz : (t + 1) * cz]) for t in range(3))
    dmid_own = (adapter_scale * dmid_own).astype(bf16)
    grad_a_qkv_t = tn(dmid_own, first_pos)
    mine = (jnp.arange(n, dtype=jnp.int32) == z)[None, :, None]
    grad_b_qkv = jnp.concatenate(
        [
            jnp.where(mine, adapter_scale * tn(mid_pos, part)[:, None, :], 0.0).reshape(rank, width)
            for part in djoint_own
        ],
        axis=1,
    )
    grad_a_up_t = tn(dmid_up, second)
    grad_b_ffp = adapter_scale * tn(mid_ff, grad_low)

    def fixed(shape, *at):
        return pl.BlockSpec(shape, lambda t: at, pipeline_mode=pl.Buffered(1))

    def column(at, height):
        return pl.BlockSpec((height, cz), lambda t: (0, at * n + t))

    mixed, grad_tokens, norm_part, grad_a_out_t, grad_b_out = pl.pallas_call(
        finish_kernel,
        grid=(n,),
        in_specs=[
            pl.BlockSpec((seqs, 4, span, cz), lambda t: (0, 0, 0, t)),
            pl.BlockSpec((cz, width), lambda t: (t, 3)),
            column(0, width), column(1, width), column(2, width),
            pl.BlockSpec((cz, rank), lambda t: (t, 1)),
            fixed((width, rank), 0, 0),
            fixed((rank, width), 0, 3),
            column(0, rank), column(1, rank), column(2, rank),
            fixed((1, width), 0, 3),
            fixed((seqs, span, width), 0, 0, 0),
            fixed((seqs, span, width), 0, 0, 0),
            fixed((rows, 1), 0, 0),
            fixed((rows, width), 0, 0),
            fixed((1, width), 0, 0),
            fixed((rows, rank), 0, 0),
            fixed((rank, width), 0, 0),
            fixed((rows, width), 0, 0),
            fixed((rows, rank), 0, 0),
            fixed((width, rank), 0, 2),
            fixed((2, width), 0, 0),
            fixed((seqs, rank, span), 0, 0, 0),
            fixed((rows, width), 0, 0),
        ],
        out_specs=[
            fixed((seqs, span, width), 0, 0, 0),
            fixed((seqs, span, width), 0, 0, 0),
            fixed((4, width), 0, 0),
            pl.BlockSpec((rank, cz), lambda t: (0, t)),
            fixed((rank, width), 0, 0),
        ],
        out_shape=[
            jax.ShapeDtypeStruct((seqs, span, width), bf16),
            jax.ShapeDtypeStruct((seqs, span, width), bf16),
            jax.ShapeDtypeStruct((4, width), f32),
            jax.ShapeDtypeStruct((rank, width), f32),
            jax.ShapeDtypeStruct((rank, width), f32),
        ],
        scratch_shapes=[
            pltpu.VMEM((rows, width), f32),
            pltpu.VMEM((rows, rank), f32),
            pltpu.VMEM((rows, width), f32),
            pltpu.VMEM((rows, rank), f32),
        ],
        compiler_params=pltpu.CompilerParams(vmem_limit_bytes=56 << 20),
        name="finish",
    )(
        local, w_in, w_in, w_in, w_in, a_all, a_all, b_in, b_in, b_in, b_in, bias32.reshape(1, -1),
        tokens, cotangent, row_weight, ff, bias_ff.astype(f32).reshape(1, -1), mid_ff, b_ff,
        grad_second, dmid_up, a_all, norm_gain, dmid_out_t, grad_low,
    )
    grad_b_out = adapter_scale * grad_b_out

    def by_owner(values):
        return values.reshape(rank, dp_n, -1)

    parts = [
        by_owner(grad_a_qkv_t), by_owner(grad_a_out_t), by_owner(grad_a_up_t), by_owner(grad_a_ff_t),
        by_owner(jnp.concatenate([grad_b_qkv, grad_b_out, grad_b_up], axis=1)), by_owner(grad_b_ffp),
    ]
    widths = [p.shape[2] for p in parts]
    owned = jnp.transpose(jnp.concatenate([p.astype(bf16) for p in parts], axis=2), (1, 0, 2))
    total_cols = owned.shape[2]
    b_at = sum(widths[:4])
    if dp_n == 8 and rank % (16 * n) == 0:
        chunks = 4
        half = rank // 2
        vmem = pl.BlockSpec(memory_space=pltpu.VMEM)
        dma = pltpu.SemaphoreType.DMA
        reduced, norm_sum, fresh = pl.pallas_call(
            functools.partial(reduce_kernel, n=n, chunks=chunks, b_at=b_at),
            in_specs=[vmem] * 8,
            out_specs=[vmem] * 3,
            out_shape=[
                jax.ShapeDtypeStruct((rank, total_cols), bf16),
                jax.ShapeDtypeStruct((4, width), f32),
                jax.ShapeDtypeStruct((dp_n, rank, b_cols), bf16),
            ],
            scratch_shapes=[
                pltpu.VMEM((4, rank, total_cols), bf16),
                pltpu.VMEM((2, 2, rank, total_cols), bf16),
                pltpu.VMEM((2, half, total_cols), bf16),
                pltpu.VMEM((2, half, total_cols), bf16),
                pltpu.VMEM((2, half, total_cols), bf16),
                pltpu.VMEM((2, half, total_cols), bf16),
                pltpu.VMEM((half, total_cols), bf16),
                pltpu.VMEM((half, total_cols), bf16),
                pltpu.VMEM((rank, total_cols), bf16),
                pltpu.VMEM((n, rank // n, total_cols), bf16),
                pltpu.VMEM((2 + n, 4, width), f32),
                pltpu.VMEM((4, 4, width), f32),
                dma((chunks,)), dma((chunks,)),
                dma((2, chunks)), dma((2, chunks)),
                dma((2, chunks)), dma((2, chunks)),
                dma((n, chunks)), dma((n, chunks)),
                dma((n, chunks)), dma((n, chunks)),
                dma((2 + n,)), dma((2 + n,)),
                dma((7,)), dma((7,)),
            ],
            compiler_params=pltpu.CompilerParams(
                collective_id=1, has_side_effects=True, vmem_limit_bytes=48 << 20
            ),
            name="reduce",
        )(
            owned.reshape(4, 2, rank, total_cols), norm_part,
            adapt_b, mean_b, square_b, adapt_b_ff, mean_b_ff, square_b_ff,
        )
    else:
        reduced = lax.psum_scatter(owned.astype(f32), "dp", scatter_dimension=0, tiled=True)
        reduced = lax.psum(reduced[0], "blk").astype(bf16)
        norm_sum = lax.psum(norm_part, ("dp", "blk"))
        grads_b = reduced[:, b_at:].astype(f32)
        cut = adapt_b.shape[1]
        fresh = jnp.concatenate(
            [
                adam_fresh(adapt_b, grads_b[:, :cut], mean_b, square_b),
                adam_fresh(adapt_b_ff, grads_b[:, cut:], mean_b_ff, square_b_ff),
            ],
            axis=1,
        ).astype(bf16)
        fresh = lax.all_gather(fresh, "dp", axis=0, tiled=False)
    grad_gain, grad_shift = norm_sum[:2], norm_sum[2:]

    state = [
        adapt_a, mean_a, square_a, keep_a,
        adapt_a_ff, mean_a_ff, square_a_ff, keep_a_ff,
        adapt_b, mean_b, square_b, keep_b,
        adapt_b_ff, mean_b_ff, square_b_ff, keep_b_ff,
    ]

    def all_of(value):
        zeros = (0,) * value.ndim
        return pl.BlockSpec(value.shape, lambda j: zeros, pipeline_mode=pl.Buffered(1))

    four = [adapt_a, adapt_a_ff, adapt_b, adapt_b_ff]
    results = [v for v in four] + [v for v in four for _ in range(2)]
    b_w, f_w = adapt_b.shape[1], adapt_b_ff.shape[1]
    owners = max(1, lanes // f_w)
    w_spec = pl.BlockSpec((kr, owners * b_w), lambda j: (0, j))
    wd_spec = pl.BlockSpec((down_rows, owners * f_w), lambda j: (0, j))
    updated = pl.pallas_call(
        functools.partial(update_kernel, rank=rank, width=width),
        grid=(dp_n // owners,),
        in_specs=[all_of(reduced), pl.BlockSpec((owners, rank, b_cols), lambda j: (j, 0, 0)), w_spec, wd_spec]
        + [all_of(v) for v in state],
        out_specs=[all_of(v) for v in results] + [w_spec, wd_spec],
        out_shape=[jax.ShapeDtypeStruct(v.shape, f32) for v in results]
        + [
            jax.ShapeDtypeStruct(frozen_input_weights.shape, bf16),
            jax.ShapeDtypeStruct(frozen_down_weight.shape, bf16),
        ],
        scratch_shapes=[pltpu.VMEM((3, kr, rank), bf16), pltpu.VMEM((down_rows, rank), bf16)],
        compiler_params=pltpu.CompilerParams(vmem_limit_bytes=48 << 20),
        name="update",
    )(reduced, fresh, frozen_input_weights, frozen_down_weight, *state)
    grad_a, grad_a_ff, grad_b, grad_b_ff = updated[:4]
    new_mean_a, new_square_a, new_mean_a_ff, new_square_a_ff = updated[4:8]
    new_mean_b, new_square_b, new_mean_b_ff, new_square_b_ff = updated[8:12]
    folded_input_weights, folded_down_weight = updated[12:]
    return (
        mixed,
        grad_tokens,
        grad_gain,
        grad_shift,
        grad_a,
        grad_a_ff,
        grad_b,
        grad_b_ff,
        new_mean_a,
        new_square_a,
        new_mean_a_ff,
        new_square_a_ff,
        new_mean_b,
        new_square_b,
        new_mean_b_ff,
        new_square_b_ff,
        folded_input_weights,
        folded_down_weight,
    )


def solution(mesh):
    in_specs = (
        P("dp", "blk", None),
        P("dp", "blk", None),
        P("dp", "blk"),
        P(),
        P("dp", None),
        P(),
        P("dp", None),
        P(),
        P(),
        P(),
        P("dp", None),
        P("dp", None),
        P(None, "dp"),
        P(None, "dp"),
        P("dp", None),
        P("dp", None),
        P(None, "dp"),
        P(None, "dp"),
        P("dp", None),
        P("dp", None),
        P(None, "dp"),
        P(None, "dp"),
        P("dp", None),
        P("dp", None),
        P(None, "dp"),
        P(None, "dp"),
    )
    out_specs = (
        P("dp", "blk", None),
        P("dp", "blk", None),
        P(),
        P(),
        P("dp", None),
        P("dp", None),
        P(None, "dp"),
        P(None, "dp"),
        P("dp", None),
        P("dp", None),
        P("dp", None),
        P("dp", None),
        P(None, "dp"),
        P(None, "dp"),
        P(None, "dp"),
        P(None, "dp"),
        P("dp", None),
        P("dp", None),
    )
    return jax.shard_map(
        functools.partial(body, mesh.shape["dp"], mesh.shape["blk"]), mesh=mesh, in_specs=in_specs, out_specs=out_specs, check_vma=False)
```

```python
import functools
import math

import jax
import jax.numpy as jnp
import numpy as np
from jax import lax
from jax.experimental import pallas as pl
from jax.experimental.pallas import tpu as pltpu
from jax.sharding import PartitionSpec as P

HEADS = 16
ROTARY = 16
DOMAINS = 22

adapter_scale = 0.25
rope_base = 10000.0
norm_eps = 1e-05
masked_score = -1e30
first_fix = 1.0 - (0.9**10) ** 10
second_fix = 1.0 - (0.999**10) ** 10

f32 = jnp.float32
bf16 = jnp.bfloat16


def nn(left, right):
    return lax.dot_general(left, right, (((1,), (0,)), ((), ())), preferred_element_type=f32)


def nt(left, right):
    return lax.dot_general(left, right, (((1,), (1,)), ((), ())), preferred_element_type=f32)


def tn(left, right):
    return lax.dot_general(left, right, (((0,), (0,)), ((), ())), preferred_element_type=f32)


def rope_lane_tables(length, depth, lanes):
    half = ROTARY // 2
    freqs = rope_base ** (-(jnp.arange(half, dtype=f32) * 2.0) / ROTARY)
    angles = jnp.arange(length, dtype=f32)[:, None] * freqs[None, :]
    cosine, sine = jnp.cos(angles), jnp.sin(angles)
    rest = depth - ROTARY
    ones, zero_half = jnp.ones((length, rest), f32), jnp.zeros((length, half), f32)
    zero_rest = jnp.zeros((length, rest), f32)
    keep = jnp.concatenate([cosine, cosine, ones], axis=1)
    from_above = jnp.concatenate([-sine, zero_half, zero_rest], axis=1)
    from_below = jnp.concatenate([zero_half, sine, zero_rest], axis=1)
    times = lanes // depth
    return tuple(jnp.tile(table, (1, times)) for table in (keep, from_above, from_below))


def turn(values, keep, above, below, sign):
    lanes = values.shape[-1]
    half = ROTARY // 2
    up = pltpu.roll(values, lanes - half, 1)
    down = pltpu.roll(values, half, 1)
    return values * keep + sign * (up * above + down * below)


def qkv_kernel(
    z_ref, x_ref, gain_ref, shift_ref, wq_ref, wk_ref, wv_ref, a_ref, b_ref, bias_ref,
    keep_ref, above_ref, below_ref, q_ref, k_ref, v_ref, first_ref, mid_ref,
):
    cols = wq_ref.shape[1]
    x = x_ref[...].reshape(x_ref.shape[2:]).astype(f32)
    centre = x - jnp.mean(x, axis=-1, keepdims=True)
    spread = jnp.mean(centre * centre, axis=-1, keepdims=True)
    first = (centre * lax.rsqrt(spread + norm_eps) * gain_ref[...] + shift_ref[...]).astype(bf16)
    mid = nn(first, a_ref[...]).astype(bf16)
    first_ref[...] = first.reshape(first_ref.shape)
    mid_ref[...] = mid.reshape(mid_ref.shape)
    low = adapter_scale * nn(mid, b_ref[...]) + bias_ref[...]
    lanes = keep_ref.shape[1]
    tables = keep_ref[...], above_ref[...], below_ref[...]
    query = nn(first, wq_ref[...]) + low[:, :cols]
    keys = nn(first, wk_ref[...]) + low[:, cols : 2 * cols]
    values = nn(first, wv_ref[...]) + low[:, 2 * cols :]
    for at in range(0, cols, lanes):
        part = slice(at, at + lanes)
        q_ref[0, :, part] = turn(query[:, part], *tables, 1.0).astype(bf16)
        k_ref[0, :, part] = turn(keys[:, part], *tables, 1.0).astype(bf16)
    v_ref[0] = values.astype(bf16)


MESH = pl.DeviceIdType.MESH


def attend_pair(query, keys, values, grad, tables, dk_ref, dv_ref, depth, blocks, store):
    lanes = keys.shape[1]
    span = keys.shape[0] // blocks
    scale = 1.0 / math.sqrt(depth)
    lane = lax.broadcasted_iota(jnp.int32, (1, lanes), 1)
    heads = lanes // depth
    masks = [jnp.where(lane // depth == h, 1.0, 0.0).astype(bf16) for h in range(heads)]
    scaled = [jnp.where(lane // depth == h, scale, 0.0).astype(bf16) for h in range(heads)]
    diagonal = lax.broadcasted_iota(jnp.int32, (span, span), 0) <= lax.broadcasted_iota(
        jnp.int32, (span, span), 1
    )
    keys_t, values_t = keys.T, values.T
    for i in range(blocks):
        done, end = i * span, (i + 1) * span
        rows = slice(done, end)
        q_i, g_i = query[rows], grad[rows]
        g_t = g_i.T
        outs, grads, lows, grads_s, q_parts, g_parts = [], [], [], [], [], []
        for h in range(heads):
            part = slice(h * depth, (h + 1) * depth)
            q_h, g_h = q_i * scaled[h], g_i * masks[h]
            last = jnp.where(diagonal, nt(keys[rows], q_h), masked_score)
            top = jnp.max(last, axis=0, keepdims=True)
            if i:
                scores = nt(keys[:done], q_h)
                top = jnp.maximum(top, jnp.max(scores, axis=0, keepdims=True))
            weights = jnp.exp(last - top)
            total = jnp.sum(weights, axis=0, keepdims=True)
            if i:
                before = jnp.exp(scores - top)
                total += jnp.sum(before, axis=0, keepdims=True)
                weights = jnp.concatenate([before, weights], axis=0)
            weights = weights * (1.0 / total)
            low = weights.astype(bf16)
            out_t = nn(values_t[part, :end], low)
            grad_p = nt(values[:end], g_h)
            delta = jnp.sum(out_t * g_t[part].astype(f32), axis=0, keepdims=True)
            grad_s = (weights * (grad_p - delta)).astype(bf16)
            outs.append(out_t)
            grads.append(nn(keys_t[part, :end], grad_s))
            lows.append(low)
            grads_s.append(grad_s)
            q_parts.append(q_h)
            g_parts.append(g_h)
        dk = nn(jnp.concatenate(grads_s, axis=1), jnp.concatenate(q_parts, axis=0))
        dv = nn(jnp.concatenate(lows, axis=1), jnp.concatenate(g_parts, axis=0))
        if i:
            dk_ref[:done] += dk[:done]
            dv_ref[:done] += dv[:done]
        dk_ref[rows] = dk[done:]
        dv_ref[rows] = dv[done:]
        store(i, 0, jnp.concatenate(outs, axis=0).T.astype(bf16))
        dq = jnp.concatenate(grads, axis=0).T * scale
        store(i, 1, turn(dq, *[t[rows] for t in tables], -1.0).astype(bf16))
    for i in range(blocks):
        rows = slice(i * span, (i + 1) * span)
        store(i, 2, turn(dk_ref[rows], *[t[rows] for t in tables], -1.0).astype(bf16))
        store(i, 3, dv_ref[rows].astype(bf16))


def normal(x):
    centre = x - jnp.mean(x, axis=-1, keepdims=True)
    return centre * lax.rsqrt(jnp.mean(centre * centre, axis=-1, keepdims=True) + norm_eps)


def front_kernel(
    tokens_ref, win_ref, wdown_ref, a_wide, aff_wide, b_wide, bff_wide,
    cot_ref, ids_ref, domain_ref, gain_ref, shift_ref, bias_ref, freq_ref,
    win_out, wdown_out, a_out, aff_out, b_out, bff_out,
    q_out, k_out, v_out, first_out, mid_out, g_out,
    low_ref, second_ref, mid_up_ref, mid_up_t_ref, dmid_ff_ref, dmid_ff_t_ref, dmid_out_t_ref,
    keep_ref, above_ref, below_ref, weight_ref,
    a_ref, aff_ref, b_ref, bff_ref, x_all, q_s, k_s, v_s, first_s, mid_s, ga, wout_v, wqkv_v, a_v, b_v, bff_v,
    sx, qx, own_sem, sr, qr, sl, ql, sd, qd, load_sem, store_sem, token_sem,
    *, n, depth,
):
    z = lax.axis_index("blk")
    dp = lax.axis_index("dp")
    y, x, c = dp // 4, lax.rem(dp // 2, 2), lax.rem(dp, 2)
    core = (dp + 1 - 2 * c, z)
    along_x = (dp + 2 - 4 * x, z)
    along_y = (dp + 4 - 8 * y, z)
    peers = [(dp, lax.rem(z + t, n)) for t in range(1, n)]
    seqs, span, width = tokens_ref.shape
    kr, down_rows, rank = win_ref.shape[0], wdown_ref.shape[0], b_ref.shape[0]
    b_w, f_w = b_ref.shape[1], bff_ref.shape[1]
    cz = q_s.shape[2]
    lanes = keep_ref.shape[1]
    four = 4 * width

    barrier = pltpu.get_barrier_semaphore()
    for peer in [core, along_x, along_y] + peers:
        pl.semaphore_signal(barrier, inc=1, device_id=peer, device_id_type=MESH)
    pl.semaphore_wait(barrier, 2 + n)

    def remote(src, dst, send, recv, peer):
        return pltpu.make_async_remote_copy(
            src_ref=src, dst_ref=dst, send_sem=send, recv_sem=recv, device_id=peer, device_id_type=MESH
        )

    shards = [
        (win_ref.at[:, :four], lambda d: win_out.at[pl.ds(pl.multiple_of(d * kr, kr), kr), :four]),
        (a_ref, lambda d: a_out.at[pl.ds(pl.multiple_of(d * kr, kr), kr), :]),
        (b_ref, lambda d: b_out.at[:, pl.ds(pl.multiple_of(d * b_w, b_w), b_w)]),
        (bff_ref, lambda d: bff_out.at[:, pl.ds(pl.multiple_of(d * f_w, f_w), f_w)]),
        (win_ref.at[:, four:], lambda d: win_out.at[pl.ds(pl.multiple_of(d * kr, kr), kr), four:]),
        (wdown_ref, lambda d: wdown_out.at[pl.ds(pl.multiple_of(d * down_rows, down_rows), down_rows), :]),
        (aff_ref, lambda d: aff_out.at[pl.ds(pl.multiple_of(d * down_rows, down_rows), down_rows), :]),
    ]
    groups = [(0, 1, 2, 3), (4,), (5, 6)]
    from_x, from_y = dp + 2 - 4 * x, dp + 4 - 8 * y
    across = dp + 2 - 4 * x + 4 - 8 * y
    onward = jnp.where(c == 0, from_y, from_x)
    target = (jnp.where(c == 0, along_x[0], along_y[0]), z)

    def hop(i, kind):
        shard, there = shards[i]
        src, dst, peer = {
            0: (shard, there(dp), along_x),
            1: (shard, there(dp), along_y),
            2: (shard, there(dp), core),
            3: (there(onward), there(onward), target),
            4: (there(from_x), there(from_x), core),
            5: (there(from_y), there(from_y), core),
            6: (there(across), there(across), core),
        }[kind]
        return remote(src, dst, sx.at[i, kind], qx.at[i, kind], peer)

    def own_copy(i):
        return pltpu.make_async_copy(shards[i][0], shards[i][1](dp), own_sem.at[i])

    def start_own(group):
        for kind in (0, 1, 2):
            for i in groups[group]:
                hop(i, kind).start()
        for i in groups[group]:
            own_copy(i).start()

    def pass_on(group):
        for i in groups[group]:
            hop(i, 0).wait_recv()
            hop(i, 1).wait_recv()
        for kind in (3, 4, 5):
            for i in groups[group]:
                hop(i, kind).start()

    def close(group):
        for i in groups[group]:
            hop(i, 3).wait_recv()
            hop(i, 6).start()

    def arrived(group):
        for i in groups[group]:
            own_copy(i).wait()
            for kind in (2, 4, 5, 6):
                hop(i, kind).wait_recv()

    def rightward(s):
        return remote(x_all.at[z - s + 1], x_all.at[z - s + 1], sr.at[s], qr.at[s], (dp, z + 1))

    def leftward(s):
        return remote(x_all.at[z + s - 1], x_all.at[z + s - 1], sl.at[s], ql.at[s], (dp, z - 1))

    def from_left(s):
        return remote(x_all.at[z - s], x_all.at[z - s], sr.at[s], qr.at[s], (dp, z - 1))

    def from_right(s):
        return remote(x_all.at[z + s], x_all.at[z + s], sl.at[s], ql.at[s], (dp, z + 1))

    def ring_start(s):
        pl.when((z < n - 1) & (z - s + 1 >= 0))(lambda: rightward(s).start())
        pl.when((z > 0) & (z + s - 1 < n))(lambda: leftward(s).start())

    def ring_wait(s):
        pl.when(z - s >= 0)(lambda: from_left(s).wait_recv())
        pl.when(z + s < n)(lambda: from_right(s).wait_recv())

    def ring_end(s):
        pl.when((z < n - 1) & (z - s + 1 >= 0))(lambda: rightward(s).wait_send())
        pl.when((z > 0) & (z + s - 1 < n))(lambda: leftward(s).wait_send())

    for low, values in ((a_ref, a_wide), (aff_ref, aff_wide), (b_ref, b_wide), (bff_ref, bff_wide)):
        low[...] = values[...].astype(bf16)
    token_copy = pltpu.make_async_copy(tokens_ref, x_all.at[z], token_sem.at[0])
    token_copy.start()
    start_own(0)
    token_copy.wait()
    ring_start(1)

    unit_lane = lax.rem(lax.broadcasted_iota(jnp.int32, (1, lanes), 1), depth)
    half = ROTARY // 2
    for b in range(n):
        rows = slice(b * span, (b + 1) * span)
        place = (lax.broadcasted_iota(jnp.int32, (span, lanes), 0) + b * span).astype(f32)
        angle = place * freq_ref[...]
        cosine, sine = jnp.cos(angle), jnp.sin(angle)
        keep_ref[rows] = jnp.where(unit_lane < ROTARY, cosine, 1.0)
        above_ref[rows] = jnp.where(unit_lane < half, -sine, 0.0)
        below_ref[rows] = jnp.where((unit_lane >= half) & (unit_lane < ROTARY), sine, 0.0)
    for q in range(seqs):
        part = slice(q * span, (q + 1) * span)
        ids = ids_ref[q : q + 1, :]
        found = jnp.zeros((1, span), f32)
        for k in range(DOMAINS):
            found = jnp.where(ids == k, domain_ref[k], found)
        weight = jnp.broadcast_to(found, (8, span)).T[:, :1]
        weight_ref[part] = weight
        low_ref[part] = (cot_ref[q].astype(f32) * weight).astype(bf16)
        unit = normal(x_all[z, q].astype(f32))
        second_ref[part] = (unit * gain_ref[1:2] + shift_ref[1:2]).astype(bf16)

    pass_on(0)
    start_own(1)
    ring_wait(1)
    if n > 2:
        ring_start(2)
    close(0)
    arrived(0)

    loads = [
        pltpu.make_async_copy(win_out.at[:, 3 * width : four], wout_v, load_sem.at[0]),
        pltpu.make_async_copy(a_out, a_v, load_sem.at[1]),
        pltpu.make_async_copy(b_out, b_v, load_sem.at[2]),
        pltpu.make_async_copy(bff_out, bff_v, load_sem.at[3]),
    ] + [
        pltpu.make_async_copy(
            win_out.at[:, pl.ds(pl.multiple_of(t * width + z * cz, cz), cz)], wqkv_v.at[t], load_sem.at[4 + t]
        )
        for t in range(3)
    ]
    for copy in loads:
        copy.start()
    for copy in loads:
        copy.wait()

    def grad_out(q, _):
        part = pl.ds(pl.multiple_of(q * span, span), span)
        low = low_ref[part, :]
        dmid = (adapter_scale * nt(low, b_v[:, 3 * width : four])).astype(bf16)
        dmid_out_t_ref[q] = dmid.T
        for g in range(n):
            rows = slice(g * cz, (g + 1) * cz)
            value = nt(low, wout_v[rows]) + nt(dmid, a_v[rows, rank : 2 * rank])
            ga[g, q] = value.astype(bf16)
        return 0

    lax.fori_loop(0, seqs, grad_out, 0)
    place_own = pl.ds(pl.multiple_of(z * span, span), span)

    def grad_send(t):
        return remote(ga.at[lax.rem(z + t, n)], g_out.at[:, place_own, :], sd.at[t], qd.at[t], peers[t - 1])

    grad_own = pltpu.make_async_copy(ga.at[z], g_out.at[:, place_own, :], token_sem.at[1])
    grad_own.start()
    for t in range(1, n):
        grad_send(t).start()

    def stores(b):
        rows = pl.ds(pl.multiple_of(b * span, span), span)
        return [
            pltpu.make_async_copy(src.at[:, rows, :], dst.at[:, rows, :], store_sem.at[i, b])
            for i, (src, dst) in enumerate(
                ((q_s, q_out), (k_s, k_out), (v_s, v_out), (first_s, first_out), (mid_s, mid_out))
            )
        ]

    def project_block(b):
        rows = pl.ds(pl.multiple_of(b * span, span), span)

        def one(q, _):
            first = (normal(x_all[b, q].astype(f32)) * gain_ref[0:1] + shift_ref[0:1]).astype(bf16)
            mid = nn(first, a_v[:, 0:rank]).astype(bf16)
            first_s[q, rows, :] = first
            mid_s[q, rows, :] = mid
            for t, kept in enumerate((q_s, k_s, v_s)):
                at = pl.ds(pl.multiple_of(t * width + z * cz, cz), cz)
                value = nn(first, wqkv_v[t]) + adapter_scale * nn(mid, b_v[:, at]) + bias_ref[:, at]
                if t < 2:
                    value = jnp.concatenate(
                        [
                            turn(value[:, i : i + lanes], keep_ref[rows, :], above_ref[rows, :], below_ref[rows, :], 1.0)
                            for i in range(0, cz, lanes)
                        ],
                        axis=1,
                    )
                kept[q, rows, :] = value.astype(bf16)
            return 0

        lax.fori_loop(0, seqs, one, 0)
        for copy in stores(b):
            copy.start()

    def project_near(s):
        def side(i, _):
            b = z + s * (2 * i - 1)
            pl.when((b >= 0) & (b < n))(lambda: project_block(b))
            return 0

        lax.fori_loop(0, 2 if s else 1, side, 0)

    def local_products(q, _):
        part = pl.ds(pl.multiple_of(q * span, span), span)
        mid = nn(second_ref[part, :], a_v[:, 2 * rank : 3 * rank]).astype(bf16)
        mid_up_ref[part, :] = mid
        mid_up_t_ref[q] = mid.T
        dmid = (adapter_scale * nt(low_ref[part, :], bff_v[...])).astype(bf16)
        dmid_ff_ref[part, :] = dmid
        dmid_ff_t_ref[q] = dmid.T
        return 0

    project_block(z)
    pass_on(1)
    start_own(2)
    for s in range(2, n):
        ring_wait(s)
        if s + 1 < n:
            ring_start(s + 1)
        project_near(s - 1)
        if s == 2:
            close(1)
            lax.fori_loop(0, seqs, local_products, 0)
            pass_on(2)
    project_near(n - 1)
    close(2)
    arrived(1)
    arrived(2)
    for i in range(len(shards)):
        for kind in range(7):
            hop(i, kind).wait_send()
    for s in range(1, n):
        ring_end(s)
    grad_own.wait()
    for t in range(1, n):
        grad_send(t).wait()
    for b in range(n):
        for copy in stores(b):
            copy.wait()


def remote(src, dst, send, recv, peer):
    return pltpu.make_async_remote_copy(
        src_ref=src, dst_ref=dst, send_sem=send, recv_sem=recv, device_id=peer, device_id_type=MESH
    )


def add_low(a, b):
    return (a.astype(f32) + b.astype(f32)).astype(bf16)


def plane():
    dp, z = lax.axis_index("dp"), lax.axis_index("blk")
    y, x, c = dp // 4, lax.rem(dp // 2, 2), lax.rem(dp, 2)
    return dp, z, y, x, c, (dp + 1 - 2 * c, z), (dp + 2 - 4 * x, z), (dp + 4 - 8 * y, z)


def greet(peers):
    barrier = pltpu.get_barrier_semaphore()
    for peer in peers:
        pl.semaphore_signal(barrier, inc=1, device_id=peer, device_id_type=MESH)
    pl.semaphore_wait(barrier, len(peers))


early_cuts = ((0, 512), (512, 1024), (1024, 1536), (1536, 1920))
late_end, a_ff_at, b_at_col, early_end = 256, 384, 896, 1920


class PlaneSum:
    def __init__(self, e, r1, r2a, r2b, r3a, r3b, s1, q1, s2, q2, s3, q3):
        self.refs = e, r1, r2a, r2b, r3a, r3b
        self.sems = s1, q1, s2, q2, s3, q3
        self.at = plane()
        self.half = e.shape[3] // 2

    def first(self, m):
        e, r1 = self.refs[:2]
        c, core = self.at[4], self.at[5]
        s1, q1 = self.sems[:2]
        if m < 4:
            cut = slice(late_end, early_end)
            return remote(e.at[m // 2, m % 2, 1 - c, :, cut], r1.at[m // 2, m % 2, :, cut], s1.at[m], q1.at[m], core)
        cut = slice(0, late_end)
        return remote(e.at[:, :, 1 - c, :, cut], r1.at[:, :, :, cut], s1.at[m], q1.at[m], core)

    def take_first(self, m):
        e, r1 = self.refs[:2]
        c = self.at[4]
        self.first(m).wait()
        for i in (m,) if m < 4 else range(4):
            yy, xx = i // 2, i % 2
            cut = slice(late_end, early_end) if m < 4 else slice(0, late_end)
            e[yy, xx, c, :, cut] = add_low(e[yy, xx, c, :, cut], r1[yy, xx, :, cut])

    def finish(self, out):
        e, r1, r2a, r2b, r3a, r3b = self.refs
        dp, z, y, x, c, core, along_x, along_y = self.at
        s1, q1, s2, q2, s3, q3 = self.sems
        half = self.half

        def second(k):
            cut = slice(*early_cuts[k])
            return [
                remote(e.at[:, 1 - x, c, 0:half, cut], r2a.at[:, :, cut], s2.at[0, k], q2.at[0, k], along_x),
                remote(e.at[1 - y, :, c, half:, cut], r2b.at[:, :, cut], s2.at[1, k], q2.at[1, k], along_y),
            ]

        def third(k):
            cut = slice(*early_cuts[k])
            return [
                remote(e.at[1 - y, x, c, 0:half, cut], r3a.at[:, cut], s3.at[0, k], q3.at[0, k], along_y),
                remote(e.at[y, 1 - x, c, half:, cut], r3b.at[:, cut], s3.at[1, k], q3.at[1, k], along_x),
            ]

        def after_second(k):
            cut = slice(*early_cuts[k])
            for copy in second(k):
                copy.wait()
            for i in range(2):
                e[i, x, c, 0:half, cut] = add_low(e[i, x, c, 0:half, cut], r2a[i, :, cut])
                e[y, i, c, half:, cut] = add_low(e[y, i, c, half:, cut], r2b[i, :, cut])
            for copy in third(k):
                copy.start()

        def after_third(k):
            cut = slice(*early_cuts[k])
            for copy in third(k):
                copy.wait()
            out[0:half, cut] = add_low(e[y, x, c, 0:half, cut], r3a[:, cut])
            out[half:, cut] = add_low(e[y, x, c, half:, cut], r3b[:, cut])

        count = len(early_cuts)
        for k in range(count):
            for copy in second(k):
                copy.start()
        for k in range(count + 1):
            if k < count:
                after_second(k)
            if k:
                after_third(k - 1)


def middle_kernel(
    q_ref, k_ref, v_ref, g_ref, keep_ref, above_ref, below_ref,
    second_ref, low_ref, mid_ref, mid_t_ref, dmid_ref, dmid_t_ref,
    up_ref, down_ref, a_ref, b_ref, bias_ref, *refs,
    n, pairs, steps, depth, early,
):
    if early:
        first_ref, mid_qkv_ref, local_ref, ff_ref, back_ref, mid_ff_ref, dmid_up_ref, sum_ref = refs[:8]
        buffer, dk_ref, dv_ref, mid_acc, dmid_acc, send_sem, recv_sem, own_sem = refs[8:16]
        e_ref, dmid_seq, gb_acc, ga_acc = refs[16:20]
        plane_refs = refs[20:]
    else:
        local_ref, own_ref, ff_ref, back_ref, mid_ff_ref, dmid_up_ref, ga_ref, gb_ref = refs[:8]
        buffer, dk_ref, dv_ref, mid_acc, dmid_acc, send_sem, recv_sem, own_sem = refs[8:]
    step = pl.program_id(0)
    z = lax.axis_index("blk")
    dp = lax.axis_index("dp")
    lanes = q_ref.shape[2]
    length = q_ref.shape[1]
    inner_block = up_ref.shape[1]
    width = up_ref.shape[0]
    cz = pairs * lanes
    if early:
        plane_sum = PlaneSum(e_ref, *plane_refs)

    def copies(s):
        seq, pair = s // pairs, lax.rem(s, pairs)
        at = pl.ds(pl.multiple_of((z * pairs + pair) * lanes, lanes), lanes)
        target = local_ref.at[seq, :, :, at]
        own = pltpu.make_async_copy(buffer.at[s, z], target, own_sem.at[s])
        away = []
        for t in range(1, n):
            peer = lax.rem(z + t, n)
            away.append(
                remote(buffer.at[s, peer], target, send_sem.at[s, t], recv_sem.at[s, t], (dp, peer))
            )
        return own, away

    @pl.when(step == 0)
    def _():
        peers = [(dp, lax.rem(z + t, n)) for t in range(1, n)]
        greet((list(plane()[5:]) if early else []) + peers)

    @pl.when(step < steps)
    def _():
        def store(i, kind, value):
            buffer[step, i, kind] = value
            if kind and not early:
                own_ref[0, kind - 1, i * value.shape[0] : (i + 1) * value.shape[0], :] = value

        tables = keep_ref[...], above_ref[...], below_ref[...]
        attend_pair(q_ref[0], k_ref[0], v_ref[0], g_ref[0], tables, dk_ref, dv_ref, depth, n, store)
        own, away = copies(step)
        own.start()
        for copy in away:
            copy.start()
        if early:
            seq, pair = step // pairs, lax.rem(step, pairs)
            mid_t = mid_qkv_ref[0].T
            dmid = jnp.zeros((length, lanes), f32)
            for t in range(3):
                grad = buffer[step, :, t + 1].reshape(length, lanes)
                at = pl.ds(pl.multiple_of(t * width + z * cz + pair * lanes, lanes), lanes)
                dmid += nt(grad, b_ref[:, at])
                product = nn(mid_t, grad)
                gb_acc[t, pair] = jnp.where(seq == 0, product, gb_acc[t, pair] + product)
            dmid = jnp.where(pair == 0, dmid, dmid_seq[...] + dmid)
            dmid_seq[...] = dmid

            @pl.when(pair == pairs - 1)
            def _():
                product = nn((adapter_scale * dmid_seq[...]).astype(bf16).T, first_ref[0])
                ga_acc[...] = jnp.where(seq == 0, product, ga_acc[...] + product)

    @pl.when(step == steps)
    def _():
        ff_ref[...] = jnp.zeros_like(ff_ref)
        back_ref[...] = jnp.zeros_like(back_ref)
        mid_acc[...] = jnp.zeros_like(mid_acc)
        dmid_acc[...] = jnp.zeros_like(dmid_acc)
        if early:
            for owner in range(8):
                place = (owner // 4, owner // 2 % 2, owner % 2)
                e_ref[place + (slice(None), slice(late_end, a_ff_at))] = ga_acc[
                    :, owner * lanes : (owner + 1) * lanes
                ].astype(bf16)
                if owner < 4:
                    e_ref[place + (slice(None), slice(b_at_col, early_end))] = jnp.zeros((lanes, 1024), bf16)
            for t in range(3):
                for pair in range(pairs):
                    at = pl.ds(pl.multiple_of(b_at_col + z * cz + pair * lanes, lanes), lanes)
                    e_ref[0, t // 2, t % 2, :, at] = (adapter_scale * gb_acc[t, pair]).astype(bf16)

    @pl.when(step >= steps)
    def _():
        count, size = mid_t_ref.shape[0], mid_t_ref.shape[2]
        j = step - steps
        if early:
            up_b = b_ref[:, pl.ds(pl.multiple_of(4 * width + j * inner_block, inner_block), inner_block)]
        else:
            up_b = b_ref[...]
        ga, gb = None, None
        for at in range(count):
            rows = slice(at * size, (at + 1) * size)
            pre = nn(second_ref[rows], up_ref[...]) + bias_ref[...] + adapter_scale * nn(mid_ref[rows], up_b)
            cdf = 0.5 + 0.5 * lax.erf(pre * (1.0 / math.sqrt(2.0)))
            hidden = (pre * cdf).astype(bf16)
            slope = cdf + pre * (jnp.exp(-0.5 * pre * pre) * (1.0 / math.sqrt(2.0 * math.pi)))
            grad_hidden = nt(low_ref[rows], down_ref[...]) + nt(dmid_ref[rows], a_ref[...])
            dup = (slope * grad_hidden).astype(bf16)
            ff_ref[rows] += nn(hidden, down_ref[...])
            back_ref[rows] += nt(dup, up_ref[...])
            mid_acc[rows] += nn(hidden, a_ref[...])
            dmid_acc[rows] += nt(dup, up_b)
            ga_part = nn(dmid_t_ref[at], hidden)
            gb_part = nn(mid_t_ref[at], dup)
            ga = ga_part if ga is None else ga + ga_part
            gb = gb_part if gb is None else gb + gb_part
        if early:
            e_ref[j // 4, lax.rem(j // 2, 2), lax.rem(j, 2), :, a_ff_at:b_at_col] = ga.astype(bf16)
            at = pl.ds(pl.multiple_of(b_at_col + lax.rem(j, 2) * inner_block, lanes), inner_block)
            e_ref[1, j // 4, lax.rem(j // 2, 2), :, at] = (adapter_scale * gb).astype(bf16)
            for m in range(3):

                @pl.when(j == 2 * m + 3)
                def _(m=m):
                    plane_sum.take_first(m)

            for m in range(4):
                pl.when(j == 2 * m + 1)(lambda m=m: plane_sum.first(m).start())
        else:
            ga_ref[...] = ga
            gb_ref[...] = gb

    @pl.when(step == pl.num_programs(0) - 1)
    def _():
        mid_ff_ref[...] = mid_acc[...].astype(bf16)
        dmid_up_ref[...] = (adapter_scale * dmid_acc[...]).astype(bf16)
        if early:
            count, size = mid_t_ref.shape[0], mid_t_ref.shape[2]
            ga, gb = None, None
            for at in range(count):
                rows = slice(at * size, (at + 1) * size)
                ga_part = nn(dmid_up_ref[rows].T, second_ref[rows])
                gb_part = nn(mid_ff_ref[rows].T, low_ref[rows])
                ga = ga_part if ga is None else ga + ga_part
                gb = gb_part if gb is None else gb + gb_part
            for owner in range(8):
                place = (owner // 4, owner // 2 % 2, owner % 2, slice(None))
                at = slice(owner * lanes, (owner + 1) * lanes)
                e_ref[place + (slice(0, lanes),)] = ga[:, at].astype(bf16)
                e_ref[place + (slice(lanes, late_end),)] = (adapter_scale * gb[:, at]).astype(bf16)
            plane_sum.first(4).start()
            plane_sum.take_first(3)
            plane_sum.take_first(4)
            plane_sum.finish(sum_ref)
        for s in range(steps):
            own, away = copies(s)
            own.wait()
            for copy in away:
                copy.wait()


def finish_kernel(
    local_ref, wo_ref, wq_ref, wk_ref, wv_ref, a_out_ref, a_qkv_ref, b_out_ref, bq_ref, bk_ref, bv_ref,
    bias_ref, x_ref, cot_ref, weight_ref, ff_ref, bias_ff_ref, mid_ff_ref, b_ff_ref,
    second_ref, dmid_up_ref, a_up_ref, gain_ref, dmid_out_t_ref, low_ref,
    mixed_ref, tokens_ref, norm_ref, ga_ref, gb_ref,
    att_acc, mid_acc, first_acc, dmid_acc,
):
    t = pl.program_id(0)
    rows = x_ref.shape[0] * x_ref.shape[1]
    cols = wq_ref.shape[1]

    @pl.when(t == 0)
    def _():
        att_acc[...] = jnp.zeros_like(att_acc)
        mid_acc[...] = jnp.zeros_like(mid_acc)
        first_acc[...] = jnp.zeros_like(first_acc)
        dmid_acc[...] = jnp.zeros_like(dmid_acc)

    out, dq, dk, dv = (local_ref[:, i].reshape(rows, cols) for i in range(4))
    att_acc[...] += nn(out, wo_ref[...])
    mid_acc[...] += nn(out, a_out_ref[...])
    first_acc[...] += nt(dq, wq_ref[...]) + nt(dk, wk_ref[...]) + nt(dv, wv_ref[...])
    dmid_acc[...] += nt(dq, bq_ref[...]) + nt(dk, bk_ref[...]) + nt(dv, bv_ref[...])
    size = x_ref.shape[1]
    ga_ref[...] = sum(nn(dmid_out_t_ref[q], out[q * size : (q + 1) * size]) for q in range(x_ref.shape[0]))

    @pl.when(t == pl.num_programs(0) - 1)
    def _():
        size = x_ref.shape[1]
        norm = [jnp.zeros((1, first_acc.shape[1]), f32) for _ in range(4)]
        for q in range(x_ref.shape[0]):
            part = slice(q * size, (q + 1) * size)
            x = x_ref[q].astype(f32)
            mid = mid_acc[part].astype(bf16)
            gb = tn(mid, low_ref[part])
            gb_ref[...] = gb if q == 0 else gb_ref[...] + gb
            att = att_acc[part] + bias_ref[...] + adapter_scale * nn(mid, b_out_ref[...])
            ff = ff_ref[part] + bias_ff_ref[...] + adapter_scale * nn(mid_ff_ref[part], b_ff_ref[...])
            mixed_ref[q] = (x + att + ff).astype(bf16)
            dmid = (adapter_scale * dmid_acc[part]).astype(bf16)
            grad_first = first_acc[part] + nt(dmid, a_qkv_ref[...])
            grad_second = second_ref[part] + nt(dmid_up_ref[part], a_up_ref[...])
            centre = x - jnp.mean(x, axis=-1, keepdims=True)
            inv = lax.rsqrt(jnp.mean(centre * centre, axis=-1, keepdims=True) + norm_eps)
            unit = centre * inv
            pulled = grad_first * gain_ref[0:1] + grad_second * gain_ref[1:2]
            back = inv * (
                pulled
                - jnp.mean(pulled, axis=-1, keepdims=True)
                - unit * jnp.mean(pulled * unit, axis=-1, keepdims=True)
            )
            row_grad = cot_ref[q].astype(f32) * weight_ref[part]
            tokens_ref[q] = (row_grad + back).astype(bf16)
            for k, value in enumerate((grad_first * unit, grad_second * unit, grad_first, grad_second)):
                norm[k] += jnp.sum(value, axis=0, keepdims=True)
        norm_ref[...] = jnp.concatenate(norm, axis=0)


def tail_kernel(
    o_ref, dq_ref, dk_ref, dv_ref, wo_ref, wq_ref, wk_ref, wv_ref, a_out_ref, a_qkv_ref, b_out_ref,
    bq_ref, bk_ref, bv_ref, bias_ref, x_ref, cot_ref, weight_ref, ff_ref, bias_ff_ref, mid_ff_ref, b_ff_ref,
    second_ref, dmid_up_ref, a_up_ref, gain_ref, dmid_out_t_ref, low_ref,
    e_ref, b_ref, mean_ref, square_ref, bf_ref, mean_f_ref, square_f_ref,
    mixed_ref, tokens_ref, out_hbm, norm_ref, fresh_hbm,
    out_ref, fresh_ref, att_acc, mid_acc, first_acc, dmid_acc,
    r4, la, lb, lr1, lr2, lr3, lbr, lj, lr4, lbr4, lbt, nr, nsum,
    s4, q4, s5, q5, sl, ql, sl4, ql4, sl5, ql5, sn, qn, sg, qg, done_sem,
    *, n,
):
    step = pl.program_id(0)
    dp, z, y, x, c, core, along_x, along_y = plane()
    peers = [(dp, lax.rem(z + t, n)) for t in range(1, n)]
    seqs, size, width = x_ref.shape
    rows, cols = seqs * size, o_ref.shape[3]
    rank = e_ref.shape[0]
    part = rank // n
    lanes = 128
    mine = pl.ds(pl.multiple_of(z * part, part), part)
    late = slice(early_end, early_end + lanes)

    def to_part(t):
        return pl.ds(pl.multiple_of(lax.rem(z + t, n) * part, part), part)

    def e_out(k, t):
        cut = slice(*early_cuts[k])
        return remote(e_ref.at[to_part(t), cut], r4.at[t, :, cut], s4.at[t, k], q4.at[t, k], peers[t - 1])

    def e_back(k, t):
        cut = slice(*early_cuts[k])
        return remote(out_ref.at[mine, cut], out_ref.at[mine, cut], s5.at[t, k], q5.at[t, k], peers[t - 1])

    count = len(early_cuts)

    has_b = (c == 1, (c == 1) & (x == 1), dp == 3)
    gives_b = (c == 0, (c == 1) & (x == 0), (c == 1) & (x == 1) & (y == 1))

    def late_a(i):
        src, dst, peer = [
            (la.at[:, :, 1 - c], lr1, core),
            (la.at[:, 1 - x, c], lr2, along_x),
            (la.at[1 - y, x, c], lr3, along_y),
        ][i]
        return remote(src, dst, sl.at[0, i], ql.at[0, i], peer)

    def late_b(i):
        return remote(lb, lbr.at[i], sl.at[1, i], ql.at[1, i], (core, along_x, along_y)[i])

    def late_start(i):
        late_a(i).start()
        pl.when(gives_b[i])(lambda: late_b(i).start())

    def late_take(i):
        late_a(i).wait()
        pl.when(gives_b[i])(lambda: late_b(i).wait_send())

        @pl.when(has_b[i])
        def _():
            late_b(i).wait_recv()
            lb[...] = add_low(lb[...], lbr[i])

        if i == 0:
            for yy in range(2):
                for xx in range(2):
                    la[yy, xx, c] = add_low(la[yy, xx, c], lr1[yy, xx])
        elif i == 1:
            for yy in range(2):
                la[yy, x, c] = add_low(la[yy, x, c], lr2[yy])
        else:
            lj[...] = add_low(la[y, x, c], lr3[...])

    def late_out(t):
        return (
            remote(lj.at[to_part(t), :], lr4.at[t], sl4.at[0, t], ql4.at[0, t], peers[t - 1]),
            remote(lb.at[to_part(t), :], lbr4.at[t], sl4.at[1, t], ql4.at[1, t], peers[t - 1]),
        )

    def late_back(t):
        return (
            remote(out_ref.at[mine, late], out_ref.at[mine, late], sl5.at[0, t], ql5.at[0, t], peers[t - 1]),
            remote(lbt.at[mine, :], lbt.at[mine, :], sl5.at[1, t], ql5.at[1, t], peers[t - 1]),
        )

    def both(make, act):
        for t in range(1, n):
            a, b = make(t)
            act(a)
            pl.when(dp == 3)(lambda b=b: act(b))

    from_x, from_y, from_c = along_x[0], along_y[0], core[0]
    across = from_x + from_y - dp
    onward = jnp.where(c == 0, from_y, from_x)
    target = (jnp.where(c == 0, from_x, from_y), z)
    other = 1 - 2 * c
    hops = [
        (dp, from_x, along_x), (dp, from_y, along_y), (dp, from_c, core), (onward, across, target),
        (from_x, from_x + other, core), (from_y, from_y + other, core), (across, across + other, core),
    ]

    def gather(kind):
        slot, _, peer = hops[kind]
        return remote(fresh_ref.at[slot], fresh_ref.at[slot], sg.at[kind], qg.at[kind], peer)

    def make_fresh():
        cut = b_ref.shape[1]
        grads = out_ref[:, b_at_col:early_end].astype(f32)
        new_b = adam_fresh(b_ref[...], grads, mean_ref[...], square_ref[...])
        grads = out_ref[:, lanes:late_end].astype(f32)
        new_f = adam_fresh(bf_ref[...], grads, mean_f_ref[...], square_f_ref[...])
        fresh_ref[dp] = jnp.concatenate([new_b, new_f], axis=1).astype(bf16)

    def norm_copy(i, peer):
        return remote(nsum.at[i], nr.at[i], sn.at[i], qn.at[i], peer)

    norm_stages = [norm_copy(0, core), norm_copy(1, along_x), norm_copy(2, along_y)]
    norm_last = [
        remote(nsum.at[3], nr.at[2 + t], sn.at[2 + t], qn.at[2 + t], peers[t - 1]) for t in range(1, n)
    ]

    def norm_take(i):
        norm_stages[i].wait()
        nsum[i + 1] = nsum[i] + nr[i]

    @pl.when(step == 0)
    def _():
        greet([core, along_x, along_y] + peers)
        for k in range(count):
            for t in range(1, n):
                e_out(k, t).start()
        att_acc[...] = jnp.zeros_like(att_acc)
        mid_acc[...] = jnp.zeros_like(mid_acc)
        first_acc[...] = jnp.zeros_like(first_acc)
        dmid_acc[...] = jnp.zeros_like(dmid_acc)

    @pl.when(step < n)
    def _():
        out = o_ref[...].reshape(rows, cols)
        att_acc[...] += nn(out, wo_ref[...])
        mid_acc[...] += nn(out, a_out_ref[...])
        ga = sum(nn(dmid_out_t_ref[q], out[q * size : (q + 1) * size]) for q in range(seqs)).astype(bf16)
        for i in range(cols // lanes):
            owner = step * (cols // lanes) + i
            la[owner // 4, lax.rem(owner // 2, 2), lax.rem(owner, 2)] = ga[:, i * lanes : (i + 1) * lanes]

    @pl.when(step == n - 1)
    def _():
        gb = None
        for q in range(seqs):
            at = slice(q * size, (q + 1) * size)
            product = nn(mid_acc[at].astype(bf16).T, low_ref[at])
            gb = product if gb is None else gb + product
        lb[...] = (adapter_scale * gb).astype(bf16)
        late_start(0)

    @pl.when(step >= n)
    def _():
        dq, dk, dv = (r[...].reshape(rows, cols) for r in (dq_ref, dk_ref, dv_ref))
        first_acc[...] += nt(dq, wq_ref[...]) + nt(dk, wk_ref[...]) + nt(dv, wv_ref[...])
        dmid_acc[...] += nt(dq, bq_ref[...]) + nt(dk, bk_ref[...]) + nt(dv, bv_ref[...])

    @pl.when(step == n + 1)
    def _():
        late_take(0)
        late_start(1)

    @pl.when(step == 2 * n - 1)
    def _():
        late_take(1)
        late_start(2)
        for k in range(count):
            cut = slice(*early_cuts[k])
            for t in range(1, n):
                e_out(k, t).wait()
            value = e_ref[mine, cut].astype(f32)
            for t in range(1, n):
                value += r4[t, :, cut].astype(f32)
            out_ref[mine, cut] = value.astype(bf16)
            for t in range(1, n):
                e_back(k, t).start()

    @pl.when(step == pl.num_programs(0) - 1)
    def _():
        norm = [jnp.zeros((1, width), f32) for _ in range(4)]

        def sequence(q):
            at = slice(q * size, (q + 1) * size)
            x_in = x_ref[q].astype(f32)
            mid = mid_acc[at].astype(bf16)
            att = att_acc[at] + bias_ref[...] + adapter_scale * nn(mid, b_out_ref[...])
            ff = ff_ref[at] + bias_ff_ref[...] + adapter_scale * nn(mid_ff_ref[at], b_ff_ref[...])
            mixed_ref[q] = (x_in + att + ff).astype(bf16)
            dmid = (adapter_scale * dmid_acc[at]).astype(bf16)
            grad_first = first_acc[at] + nt(dmid, a_qkv_ref[...])
            grad_second = second_ref[at] + nt(dmid_up_ref[at], a_up_ref[...])
            centre = x_in - jnp.mean(x_in, axis=-1, keepdims=True)
            inv = lax.rsqrt(jnp.mean(centre * centre, axis=-1, keepdims=True) + norm_eps)
            unit = centre * inv
            pulled = grad_first * gain_ref[0:1] + grad_second * gain_ref[1:2]
            back = inv * (
                pulled
                - jnp.mean(pulled, axis=-1, keepdims=True)
                - unit * jnp.mean(pulled * unit, axis=-1, keepdims=True)
            )
            row_grad = cot_ref[q].astype(f32) * weight_ref[at]
            tokens_ref[q] = (row_grad + back).astype(bf16)
            for k, value in enumerate((grad_first * unit, grad_second * unit, grad_first, grad_second)):
                norm[k] += jnp.sum(value, axis=0, keepdims=True)

        sequence(0)
        late_take(2)
        both(late_out, lambda copy: copy.start())
        for q in range(1, seqs - 1):
            sequence(q)
        both(late_out, lambda copy: copy.wait())
        value = lj[mine, :].astype(f32)
        for t in range(1, n):
            value += lr4[t].astype(f32)
        out_ref[mine, late] = value.astype(bf16)

        @pl.when(dp == 3)
        def _():
            value = lb[mine, :].astype(f32)
            for t in range(1, n):
                value += lbr4[t].astype(f32)
            lbt[mine, :] = value.astype(bf16)

        both(late_back, lambda copy: copy.start())
        sequence(seqs - 1)
        nsum[0] = jnp.concatenate(norm, axis=0)
        norm_stages[0].start()
        both(late_back, lambda copy: copy.wait())
        for k in range(count):
            for t in range(1, n):
                e_back(k, t).wait()

        @pl.when(dp == 3)
        def _():
            out_ref[:, b_at_col:early_end] = lbt[...]

        make_fresh()
        for kind in (0, 1, 2):
            gather(kind).start()
        keep_out = pltpu.make_async_copy(out_ref, out_hbm, done_sem.at[0])
        keep_out.start()
        norm_take(0)
        norm_stages[1].start()
        gather(0).wait_recv()
        gather(1).wait_recv()
        for kind in (3, 4, 5):
            gather(kind).start()
        norm_take(1)
        norm_stages[2].start()
        gather(3).wait_recv()
        gather(6).start()
        norm_take(2)
        for copy in norm_last:
            copy.start()
        for kind in (2, 4, 5, 6):
            gather(kind).wait_recv()
        keep_fresh = pltpu.make_async_copy(fresh_ref, fresh_hbm, done_sem.at[1])
        keep_fresh.start()
        for kind in range(7):
            gather(kind).wait_send()
        for copy in norm_last:
            copy.wait()
        keep_out.wait()
        keep_fresh.wait()
        value = jnp.zeros_like(nsum[3])
        for blk in range(n):
            there = lax.rem(z - blk + n, n)
            value += jnp.where(there == 0, nsum[3], nr[2 + jnp.maximum(there, 1)])
        norm_ref[...] = value


def update_kernel(
    g_ref, fresh_ref, w_ref, wd_ref, *refs, rank, width,
):
    params, outs = refs[:16], refs[16:30]
    a_new, aff_new = refs[30:]
    j = pl.program_id(0)
    cols = w_ref.shape[1]

    @pl.when(j == 0)
    def _():
        rows, inner = params[0].shape[0], params[4].shape[0]
        got = g_ref[...].astype(f32)
        cut, cut_f = params[8].shape[1], params[12].shape[1]
        up = got[:, :rows]
        qkv = got[:, rows + cut_f : 2 * rows + cut_f]
        out = got[:, 2 * rows + cut_f + inner + cut :]
        at = 2 * rows + cut_f
        grads = [
            jnp.concatenate([part.T for part in (qkv, out, up)], axis=1),
            got[:, at : at + inner].T,
            got[:, at + inner : at + inner + cut],
            got[:, rows : rows + cut_f],
        ]
        for i, grad in enumerate(grads):
            param, mean, square, keep = (r[...] for r in params[4 * i : 4 * i + 4])
            mean_new = 0.9 * mean + 0.1 * grad
            square_new = 0.999 * square + 0.001 * grad * grad
            kept = keep.astype(f32)
            outs[i][...] = grad
            outs[4 + 2 * i][...] = mean_new * kept
            outs[5 + 2 * i][...] = square_new * kept
            if i < 2:
                fresh = param - 0.01 * (mean_new / first_fix) / (jnp.sqrt(square_new / second_fix) + 1e-08)
                if i == 0:
                    for k in range(3):
                        a_new[k] = fresh[:, k * rank : (k + 1) * rank].astype(bf16)
                else:
                    aff_new[...] = fresh.astype(bf16)

    block = jnp.where(j * cols < 3 * width, 0, jnp.where(j * cols < 4 * width, 1, 2))
    cut = params[8].shape[1]
    fresh = [fresh_ref[i] for i in range(fresh_ref.shape[0])]
    update = nn(a_new[block], jnp.concatenate([f[:, :cut] for f in fresh], axis=1))
    outs[12][...] = (w_ref[...].astype(f32) + adapter_scale * update).astype(bf16)
    update = nn(aff_new[...], jnp.concatenate([f[:, cut:] for f in fresh], axis=1))
    outs[13][...] = (wd_ref[...].astype(f32) + adapter_scale * update).astype(bf16)


def adam_fresh(param, grad, mean, square):
    mean_new = 0.9 * mean + 0.1 * grad
    square_new = 0.999 * square + 0.001 * grad * grad
    return param - 0.01 * (mean_new / first_fix) / (jnp.sqrt(square_new / second_fix) + 1e-08)


def body(
    dp_n,
    n,
    tokens,
    cotangent,
    domain_ids,
    domain_weight,
    frozen_input_weights,
    bias_in,
    frozen_down_weight,
    bias_ff,
    norm_gain,
    norm_shift,
    adapt_a,
    adapt_a_ff,
    adapt_b,
    adapt_b_ff,
    mean_a,
    mean_a_ff,
    mean_b,
    mean_b_ff,
    square_a,
    square_a_ff,
    square_b,
    square_b_ff,
    keep_a,
    keep_a_ff,
    keep_b,
    keep_b_ff,
):
    seqs, span, width = tokens.shape
    rows = seqs * span
    rank = adapt_b.shape[0]
    depth = width // HEADS
    cz = width // n
    length = n * span
    z = lax.axis_index("blk")
    z_arr = jnp.full((1,), z, jnp.int32)
    kr = frozen_input_weights.shape[0]
    down_rows, inner = frozen_down_weight.shape[0], frozen_down_weight.shape[0] * dp_n
    lanes = 128

    def shift_by(values, s):
        return lax.ppermute(values, "blk", [(i, (i + s) % n) for i in range(n)])

    b_cols = adapt_b.shape[1] + adapt_b_ff.shape[1]
    bias32 = bias_in.astype(f32)
    whole_front = dp_n == 8 and n == 4 and seqs > 1 and (rank, width, inner) == (128, 1024, 4096)
    if whole_front:
        vmem = pl.BlockSpec(memory_space=pltpu.VMEM)
        hbm = pl.BlockSpec(memory_space=pl.ANY)
        dma = pltpu.SemaphoreType.DMA
        half = ROTARY // 2
        freq = [rope_base ** (-(k * 2.0) / ROTARY) for k in range(half)]
        freq = np.tile(np.array(freq + freq + [0.0] * (depth - ROTARY), np.float32), lanes // depth)

        def shape(*dims, dtype=bf16):
            return jax.ShapeDtypeStruct(dims, dtype)

        (
            w_in, w_down, a_all, a_ff, b_in, b_ff, query, keys, values, first_pos, mid_pos, g_pos,
            grad_low, second, mid_up, mid_up_t, dmid_ff, dmid_ff_t, dmid_out_t, *tables, row_weight,
        ) = pl.pallas_call(
            functools.partial(front_kernel, n=n, depth=depth),
            in_specs=[hbm] * 3 + [vmem] * 6 + [pl.BlockSpec(memory_space=pltpu.SMEM)] + [vmem] * 4,
            out_specs=[hbm] * 12 + [vmem] * 11,
            out_shape=[
                shape(width, 8 * width), shape(inner, width), shape(width, 3 * rank), shape(inner, rank),
                shape(rank, 8 * width), shape(rank, width),
                shape(seqs, length, cz), shape(seqs, length, cz), shape(seqs, length, cz),
                shape(seqs, length, width), shape(seqs, length, rank), shape(seqs, length, cz),
                shape(rows, width), shape(rows, width),
                shape(rows, rank), shape(seqs, rank, span), shape(rows, rank), shape(seqs, rank, span),
                shape(seqs, rank, span),
                shape(length, lanes, dtype=f32), shape(length, lanes, dtype=f32), shape(length, lanes, dtype=f32),
                shape(rows, 1, dtype=f32),
            ],
            scratch_shapes=[
                pltpu.VMEM(adapt_a.shape, bf16),
                pltpu.VMEM(adapt_a_ff.shape, bf16),
                pltpu.VMEM(adapt_b.shape, bf16),
                pltpu.VMEM(adapt_b_ff.shape, bf16),
                pltpu.VMEM((n, seqs, span, width), bf16),
                pltpu.VMEM((seqs, length, cz), bf16),
                pltpu.VMEM((seqs, length, cz), bf16),
                pltpu.VMEM((seqs, length, cz), bf16),
                pltpu.VMEM((seqs, length, width), bf16),
                pltpu.VMEM((seqs, length, rank), bf16),
                pltpu.VMEM((n, seqs, span, cz), bf16),
                pltpu.VMEM((width, width), bf16),
                pltpu.VMEM((3, width, cz), bf16),
                pltpu.VMEM((width, 3 * rank), bf16),
                pltpu.VMEM((rank, 8 * width), bf16),
                pltpu.VMEM((rank, width), bf16),
                dma((7, 7)), dma((7, 7)), dma((7,)),
                dma((n,)), dma((n,)), dma((n,)), dma((n,)), dma((n,)), dma((n,)),
                dma((7,)), dma((5, n)), dma((2,)),
            ],
            compiler_params=pltpu.CompilerParams(
                collective_id=2, has_side_effects=True, vmem_limit_bytes=58 << 20
            ),
            name="front",
        )(
            tokens, frozen_input_weights, frozen_down_weight,
            adapt_a, adapt_a_ff, adapt_b, adapt_b_ff,
            cotangent, domain_ids, domain_weight, norm_gain, norm_shift, bias32.reshape(1, -1), freq.reshape(1, -1),
        )
    else:
        lookup = (domain_ids[..., None] == jnp.arange(DOMAINS, dtype=jnp.int32)).astype(f32)
        row_weight = jnp.sum(lookup * domain_weight, axis=-1).reshape(rows, 1)
        row_grad = cotangent.astype(f32).reshape(rows, width) * row_weight
        grad_low = row_grad.astype(bf16)
        b_shard = jnp.concatenate([adapt_b, adapt_b_ff], axis=1).astype(bf16)
        one = jnp.concatenate(
            [frozen_input_weights[:, : 4 * width], adapt_a.astype(bf16), b_shard.reshape(kr, -1)], axis=1
        )
        one = lax.all_gather(one, "dp", axis=0, tiled=True)
        two = lax.all_gather(frozen_input_weights[:, 4 * width :], "dp", axis=0, tiled=True)
        three = jnp.concatenate([frozen_down_weight, adapt_a_ff.astype(bf16)], axis=1)
        three = lax.all_gather(three, "dp", axis=0, tiled=True)
        a_at = 4 * width
        b_at = a_at + 3 * rank
        a_all = one[:, a_at:b_at]
        b_all = one[:, b_at:].reshape(dp_n, rank, b_cols)
        b_in = jnp.transpose(b_all[:, :, : adapt_b.shape[1]], (1, 0, 2)).reshape(rank, -1)
        b_ff = jnp.transpose(b_all[:, :, adapt_b.shape[1] :], (1, 0, 2)).reshape(rank, width)
        w_out = one[:, 3 * width : 4 * width]
        w_up = two
        w_down, a_ff = three[:, :width], three[:, width:]

        right, left = tokens, tokens
        rights, lefts = [None], [None]
        for s in range(1, n):
            right = lax.ppermute(right, "blk", [(i, i + 1) for i in range(n - 1)])
            left = lax.ppermute(left, "blk", [(i + 1, i) for i in range(n - 1)])
            rights.append(right)
            lefts.append(left)
        x_all = jnp.stack(
            [tokens] + [jnp.where(z >= s, rights[s], lefts[n - s]) for s in range(1, n)]
        )

        b_out = b_in[:, 3 * width : 4 * width]
        a_out = a_all[:, rank : 2 * rank]
        dmid_out = (adapter_scale * nt(grad_low, b_out)).astype(bf16)
        grad_att = (nt(grad_low, w_out) + nt(dmid_out, a_out)).astype(bf16)
        grad_att = jnp.transpose(grad_att.reshape(seqs, span, n, cz), (2, 0, 1, 3))

        def piece(values, s):
            return lax.dynamic_index_in_dim(values, lax.rem(z + s, n), 0, keepdims=False)

        g_all = jnp.stack(
            [piece(grad_att, 0)] + [shift_by(piece(grad_att, s), s) for s in range(1, n)]
        )

        tables = rope_lane_tables(length, depth, lanes)
        own = [lax.dynamic_slice_in_dim(b_in[:, t * width : (t + 1) * width], z * cz, cz, 1) for t in range(3)]
        b_own = jnp.concatenate(own, axis=1)
        bias_own = jnp.concatenate(
            [lax.dynamic_slice_in_dim(bias32, t * width + z * cz, cz, 0) for t in range(3)]
        ).reshape(1, 3 * cz)

        def block_of(s, z_ref):
            return lax.rem(z_ref[0] - s + n, n)

        table_spec = pl.BlockSpec((span, lanes), lambda s, q, z_ref: (block_of(s, z_ref), 0))
        head_spec = pl.BlockSpec((1, span, cz), lambda s, q, z_ref: (q, block_of(s, z_ref), 0))
        query, keys, values, first_all, mid_all = pl.pallas_call(
            qkv_kernel,
            grid_spec=pltpu.PrefetchScalarGridSpec(
                num_scalar_prefetch=1,
                grid=(n, seqs),
                in_specs=[
                    pl.BlockSpec((1, 1, span, width), lambda s, q, z_ref: (s, q, 0, 0)),
                    pl.BlockSpec((1, width), lambda s, q, z_ref: (0, 0)),
                    pl.BlockSpec((1, width), lambda s, q, z_ref: (0, 0)),
                    pl.BlockSpec((width, cz), lambda s, q, z_ref: (0, z_ref[0])),
                    pl.BlockSpec((width, cz), lambda s, q, z_ref: (0, n + z_ref[0])),
                    pl.BlockSpec((width, cz), lambda s, q, z_ref: (0, 2 * n + z_ref[0])),
                    pl.BlockSpec((width, rank), lambda s, q, z_ref: (0, a_at // rank)),
                    pl.BlockSpec((rank, 3 * cz), lambda s, q, z_ref: (0, 0)),
                    pl.BlockSpec((1, 3 * cz), lambda s, q, z_ref: (0, 0)),
                    table_spec,
                    table_spec,
                    table_spec,
                ],
                out_specs=[
                    head_spec,
                    head_spec,
                    head_spec,
                    pl.BlockSpec((1, 1, span, width), lambda s, q, z_ref: (block_of(s, z_ref), q, 0, 0)),
                    pl.BlockSpec((1, 1, span, rank), lambda s, q, z_ref: (block_of(s, z_ref), q, 0, 0)),
                ],
            ),
            out_shape=[jax.ShapeDtypeStruct((seqs, length, cz), bf16)] * 3
            + [
                jax.ShapeDtypeStruct((n, seqs, span, width), bf16),
                jax.ShapeDtypeStruct((n, seqs, span, rank), bf16),
            ],
            compiler_params=pltpu.CompilerParams(vmem_limit_bytes=48 << 20),
            cost_estimate=pl.CostEstimate(
                flops=2 * n * rows * width * 4 * cz, bytes_accessed=6 * n * rows * width, transcendentals=0
            ),
            name="qkv",
        )(
            z_arr, x_all, norm_gain[0:1], norm_shift[0:1], one, one, one, one, b_own, bias_own, *tables
        )

        input_rows = tokens.astype(f32).reshape(rows, width)
        centre = input_rows - jnp.mean(input_rows, axis=-1, keepdims=True)
        inv = lax.rsqrt(jnp.mean(centre * centre, axis=-1, keepdims=True) + norm_eps)
        second = (centre * inv * norm_gain[1] + norm_shift[1]).astype(bf16)
        a_up = a_all[:, 2 * rank :]
        mid_up = nn(second, a_up).astype(bf16)
        dmid_ff = (adapter_scale * nt(grad_low, b_ff)).astype(bf16)
        g_pos = jnp.concatenate([g_all, g_all])
        g_pos = lax.rev(g_pos, (0,))
        g_pos = lax.dynamic_slice_in_dim(g_pos, lax.rem(n - 1 - z + n, n), n, 0)
        g_pos = jnp.transpose(g_pos, (1, 0, 2, 3)).reshape(seqs, length, cz)

        first_pos = jnp.transpose(first_all, (1, 0, 2, 3))
        mid_pos = jnp.transpose(mid_all, (1, 0, 2, 3))
        w_in = jnp.concatenate([one[:, :a_at], two], axis=1)
        mid_up_t, dmid_ff_t, dmid_out_t = (
            jnp.transpose(v.reshape(seqs, span, rank), (0, 2, 1)) for v in (mid_up, dmid_ff, dmid_out)
        )

    pairs = cz // lanes
    steps = seqs * pairs
    inner_block = min(512, inner)
    def one_buffer(shape):
        zeros = (0,) * len(shape)
        return pl.BlockSpec(shape, lambda s: zeros, pipeline_mode=pl.Buffered(1))

    def seq_pair(s):
        s = jnp.minimum(s, steps - 1)
        return s // pairs, lax.rem(s, pairs)

    def head_map(s):
        seq, pair = seq_pair(s)
        return seq, 0, pair

    def inner_at(s):
        return jnp.maximum(s - steps, 0)

    head = pl.BlockSpec((1, length, lanes), head_map)
    early = whole_front
    dma = pltpu.SemaphoreType.DMA
    half_rank = rank // 2

    def wide(*dims, dtype=bf16):
        return jax.ShapeDtypeStruct(dims, dtype)

    in_specs = (
        [head] * 4
        + [one_buffer((length, lanes))] * 3
        + [one_buffer((rows, width))] * 2
        + [one_buffer((rows, rank)), one_buffer((seqs, rank, span))] * 2
        + [
            pl.BlockSpec((width, inner_block), lambda s: (0, 4 * width // inner_block + inner_at(s))),
            pl.BlockSpec((inner_block, width), lambda s: (inner_at(s), 0)),
            pl.BlockSpec((inner_block, rank), lambda s: (inner_at(s), 0)),
            one_buffer((rank, 8 * width))
            if early
            else pl.BlockSpec((rank, inner_block), lambda s: (0, 4 * width // inner_block + inner_at(s))),
            pl.BlockSpec((1, inner_block), lambda s: (0, 4 * width // inner_block + inner_at(s))),
        ]
    )
    operands = [
        query, keys, values, g_pos, *tables, second, grad_low, mid_up, mid_up_t, dmid_ff, dmid_ff_t,
        w_in, w_down, a_ff, b_in, bias32.reshape(1, -1),
    ]
    partial_specs = [one_buffer((rows, width))] * 2 + [one_buffer((rows, rank))] * 2
    partial_shapes = [wide(rows, width, dtype=f32)] * 2 + [wide(rows, rank)] * 2
    local_spec, local_shape = pl.BlockSpec(memory_space=pl.ANY), wide(seqs, 4, span, width)
    scratch = [
        pltpu.VMEM((steps, n, 4, span, lanes), bf16),
        pltpu.VMEM((length, lanes), f32),
        pltpu.VMEM((length, lanes), f32),
        pltpu.VMEM((rows, rank), f32),
        pltpu.VMEM((rows, rank), f32),
        dma((steps, n)),
        dma((steps, n)),
        dma((steps,)),
    ]
    if early:
        in_specs += [
            pl.BlockSpec((1, length, width), lambda s: (seq_pair(s)[0], 0, 0)),
            pl.BlockSpec((1, length, rank), lambda s: (seq_pair(s)[0], 0, 0)),
        ]
        operands += [first_pos, mid_pos]
        out_specs = [local_spec] + partial_specs + [one_buffer((rank, early_end))]
        out_shapes = [local_shape] + partial_shapes + [wide(rank, early_end)]
        cuts = len(early_cuts)
        scratch += [
            pltpu.VMEM((2, 2, 2, rank, early_end), bf16),
            pltpu.VMEM((length, rank), f32),
            pltpu.VMEM((3, pairs, rank, lanes), f32),
            pltpu.VMEM((rank, width), f32),
            pltpu.VMEM((2, 2, rank, early_end), bf16),
            pltpu.VMEM((2, half_rank, early_end), bf16),
            pltpu.VMEM((2, half_rank, early_end), bf16),
            pltpu.VMEM((half_rank, early_end), bf16),
            pltpu.VMEM((half_rank, early_end), bf16),
            dma((5,)), dma((5,)), dma((2, cuts)), dma((2, cuts)), dma((2, cuts)), dma((2, cuts)),
        ]
    else:
        out_specs = (
            [local_spec, pl.BlockSpec((1, 3, length, lanes), lambda s: (seq_pair(s)[0], 0, 0, seq_pair(s)[1]))]
            + partial_specs
            + [pl.BlockSpec((rank, inner_block), lambda s: (0, inner_at(s)))] * 2
        )
        out_shapes = (
            [local_shape, wide(seqs, 3, length, cz)] + partial_shapes + [wide(rank, inner, dtype=f32)] * 2
        )
    middle = pl.pallas_call(
        functools.partial(middle_kernel, n=n, pairs=pairs, steps=steps, depth=depth, early=early),
        grid=(steps + inner // inner_block,),
        in_specs=in_specs,
        out_specs=out_specs,
        out_shape=out_shapes,
        scratch_shapes=scratch,
        compiler_params=pltpu.CompilerParams(
            collective_id=0, has_side_effects=True, vmem_limit_bytes=60 << 20
        ),
        name="middle",
    )(*operands)

    if early:
        local, ff, grad_second, mid_ff, dmid_up, summed = middle
        part = rank // n

        def single(shape, *at):
            return pl.BlockSpec(shape, lambda s: at, pipeline_mode=pl.Buffered(1))

        def of_out(s):
            return jnp.minimum(s, n - 1)

        def of_grad(s):
            return jnp.maximum(s - n, 0)

        def piece_spec(kind, at):
            return pl.BlockSpec((seqs, 1, span, cz), lambda s: (0, kind, 0, at(s)))

        def columns(kind, height):
            return pl.BlockSpec((height, cz), lambda s: (0, kind * n + of_grad(s)))

        full = single((seqs, span, width), 0, 0, 0)
        cuts = len(early_cuts)
        b_here = [adapt_b, mean_b, square_b, adapt_b_ff, mean_b_ff, square_b_ff]
        mixed, grad_tokens, reduced, norm_sum, fresh = pl.pallas_call(
            functools.partial(tail_kernel, n=n),
            grid=(2 * n,),
            in_specs=[
                piece_spec(0, of_out), piece_spec(1, of_grad), piece_spec(2, of_grad), piece_spec(3, of_grad),
                pl.BlockSpec((cz, width), lambda s: (of_out(s), 3)),
                columns(0, width), columns(1, width), columns(2, width),
                pl.BlockSpec((cz, rank), lambda s: (of_out(s), 1)),
                single((width, rank), 0, 0),
                single((rank, width), 0, 3),
                columns(0, rank), columns(1, rank), columns(2, rank),
                single((1, width), 0, 3),
                full, full,
                single((rows, 1), 0, 0),
                single((rows, width), 0, 0),
                single((1, width), 0, 0),
                single((rows, rank), 0, 0),
                single((rank, width), 0, 0),
                single((rows, width), 0, 0),
                single((rows, rank), 0, 0),
                single((width, rank), 0, 2),
                single((2, width), 0, 0),
                single((seqs, rank, span), 0, 0, 0),
                single((rows, width), 0, 0),
                single((rank, early_end), 0, 0),
            ]
            + [single(v.shape, 0, 0) for v in b_here],
            out_specs=[
                full, full, pl.BlockSpec(memory_space=pl.ANY), single((4, width), 0, 0),
                pl.BlockSpec(memory_space=pl.ANY),
            ],
            out_shape=[
                wide(seqs, span, width), wide(seqs, span, width), wide(rank, 2048), wide(4, width, dtype=f32),
                wide(dp_n, rank, b_cols),
            ],
            scratch_shapes=[
                pltpu.VMEM((rank, 2048), bf16),
                pltpu.VMEM((dp_n, rank, b_cols), bf16),
                pltpu.VMEM((rows, width), f32),
                pltpu.VMEM((rows, rank), f32),
                pltpu.VMEM((rows, width), f32),
                pltpu.VMEM((rows, rank), f32),
                pltpu.VMEM((n, part, early_end), bf16),
                pltpu.VMEM((2, 2, 2, rank, lanes), bf16),
                pltpu.VMEM((rank, width), bf16),
                pltpu.VMEM((2, 2, rank, lanes), bf16),
                pltpu.VMEM((2, rank, lanes), bf16),
                pltpu.VMEM((rank, lanes), bf16),
                pltpu.VMEM((3, rank, width), bf16),
                pltpu.VMEM((rank, lanes), bf16),
                pltpu.VMEM((n, part, lanes), bf16),
                pltpu.VMEM((n, part, width), bf16),
                pltpu.VMEM((rank, width), bf16),
                pltpu.VMEM((2 + n, 4, width), f32),
                pltpu.VMEM((4, 4, width), f32),
                dma((n, cuts)), dma((n, cuts)), dma((n, cuts)), dma((n, cuts)),
                dma((2, 3)), dma((2, 3)), dma((2, n)), dma((2, n)), dma((2, n)), dma((2, n)),
                dma((2 + n,)), dma((2 + n,)), dma((7,)), dma((7,)), dma((2,)),
            ],
            compiler_params=pltpu.CompilerParams(
                collective_id=1, has_side_effects=True, vmem_limit_bytes=58 << 20
            ),
            name="tail",
        )(
            local, local, local, local, w_in, w_in, w_in, w_in, a_all, a_all, b_in, b_in, b_in, b_in,
            bias32.reshape(1, -1), tokens, cotangent, row_weight, ff, bias_ff.astype(f32).reshape(1, -1), mid_ff, b_ff,
            grad_second, dmid_up, a_all, norm_gain, dmid_out_t, grad_low, summed, *b_here,
        )
    else:
        local, own, ff, grad_second, mid_ff, dmid_up, grad_a_ff_t, grad_b_up = middle
        grad_b_up = adapter_scale * grad_b_up
        first_pos = first_pos.reshape(seqs * length, width)
        mid_pos = mid_pos.reshape(seqs * length, rank)
        b_own = jnp.concatenate(
            [lax.dynamic_slice_in_dim(b_in[:, t * width : (t + 1) * width], z * cz, cz, 1) for t in range(3)], axis=1
        )
        djoint_own = [own[:, t].reshape(seqs * length, cz) for t in range(3)]
        dmid_own = sum(nt(djoint_own[t], b_own[:, t * cz : (t + 1) * cz]) for t in range(3))
        dmid_own = (adapter_scale * dmid_own).astype(bf16)
        grad_a_qkv_t = tn(dmid_own, first_pos)
        mine = (jnp.arange(n, dtype=jnp.int32) == z)[None, :, None]
        grad_b_qkv = jnp.concatenate(
            [
                jnp.where(mine, adapter_scale * tn(mid_pos, part)[:, None, :], 0.0).reshape(rank, width)
                for part in djoint_own
            ],
            axis=1,
        )
        grad_a_up_t = tn(dmid_up, second)
        grad_b_ffp = adapter_scale * tn(mid_ff, grad_low)

        def fixed(shape, *at):
            return pl.BlockSpec(shape, lambda t: at, pipeline_mode=pl.Buffered(1))

        def column(at, height):
            return pl.BlockSpec((height, cz), lambda t: (0, at * n + t))

        mixed, grad_tokens, norm_part, grad_a_out_t, grad_b_out = pl.pallas_call(
            finish_kernel,
            grid=(n,),
            in_specs=[
                pl.BlockSpec((seqs, 4, span, cz), lambda t: (0, 0, 0, t)),
                pl.BlockSpec((cz, width), lambda t: (t, 3)),
                column(0, width), column(1, width), column(2, width),
                pl.BlockSpec((cz, rank), lambda t: (t, 1)),
                fixed((width, rank), 0, 0),
                fixed((rank, width), 0, 3),
                column(0, rank), column(1, rank), column(2, rank),
                fixed((1, width), 0, 3),
                fixed((seqs, span, width), 0, 0, 0),
                fixed((seqs, span, width), 0, 0, 0),
                fixed((rows, 1), 0, 0),
                fixed((rows, width), 0, 0),
                fixed((1, width), 0, 0),
                fixed((rows, rank), 0, 0),
                fixed((rank, width), 0, 0),
                fixed((rows, width), 0, 0),
                fixed((rows, rank), 0, 0),
                fixed((width, rank), 0, 2),
                fixed((2, width), 0, 0),
                fixed((seqs, rank, span), 0, 0, 0),
                fixed((rows, width), 0, 0),
            ],
            out_specs=[
                fixed((seqs, span, width), 0, 0, 0),
                fixed((seqs, span, width), 0, 0, 0),
                fixed((4, width), 0, 0),
                pl.BlockSpec((rank, cz), lambda t: (0, t)),
                fixed((rank, width), 0, 0),
            ],
            out_shape=[
                jax.ShapeDtypeStruct((seqs, span, width), bf16),
                jax.ShapeDtypeStruct((seqs, span, width), bf16),
                jax.ShapeDtypeStruct((4, width), f32),
                jax.ShapeDtypeStruct((rank, width), f32),
                jax.ShapeDtypeStruct((rank, width), f32),
            ],
            scratch_shapes=[
                pltpu.VMEM((rows, width), f32),
                pltpu.VMEM((rows, rank), f32),
                pltpu.VMEM((rows, width), f32),
                pltpu.VMEM((rows, rank), f32),
            ],
            compiler_params=pltpu.CompilerParams(vmem_limit_bytes=56 << 20),
            name="finish",
        )(
            local, w_in, w_in, w_in, w_in, a_all, a_all, b_in, b_in, b_in, b_in, bias32.reshape(1, -1),
            tokens, cotangent, row_weight, ff, bias_ff.astype(f32).reshape(1, -1), mid_ff, b_ff,
            grad_second, dmid_up, a_all, norm_gain, dmid_out_t, grad_low,
        )
        grad_b_out = adapter_scale * grad_b_out

        def by_owner(values):
            return values.reshape(rank, dp_n, -1)

        parts = [
            by_owner(grad_a_up_t), by_owner(grad_b_ffp), by_owner(grad_a_qkv_t), by_owner(grad_a_ff_t),
            by_owner(jnp.concatenate([grad_b_qkv, grad_b_out, grad_b_up], axis=1)), by_owner(grad_a_out_t),
        ]
        widths = [p.shape[2] for p in parts]
        owned = jnp.transpose(jnp.concatenate([p.astype(bf16) for p in parts], axis=2), (1, 0, 2))
        b_at = sum(widths[:4])
        reduced = lax.psum_scatter(owned.astype(f32), "dp", scatter_dimension=0, tiled=True)
        reduced = lax.psum(reduced[0], "blk").astype(bf16)
        norm_sum = lax.psum(norm_part, ("dp", "blk"))
        grads_b = reduced[:, b_at : b_at + adapt_b.shape[1]].astype(f32)
        grads_f = reduced[:, widths[0] : widths[0] + widths[1]].astype(f32)
        fresh = jnp.concatenate(
            [
                adam_fresh(adapt_b, grads_b, mean_b, square_b),
                adam_fresh(adapt_b_ff, grads_f, mean_b_ff, square_b_ff),
            ],
            axis=1,
        ).astype(bf16)
        fresh = lax.all_gather(fresh, "dp", axis=0, tiled=False)
    grad_gain, grad_shift = norm_sum[:2], norm_sum[2:]

    state = [
        adapt_a, mean_a, square_a, keep_a,
        adapt_a_ff, mean_a_ff, square_a_ff, keep_a_ff,
        adapt_b, mean_b, square_b, keep_b,
        adapt_b_ff, mean_b_ff, square_b_ff, keep_b_ff,
    ]

    def all_of(value):
        zeros = (0,) * value.ndim
        return pl.BlockSpec(value.shape, lambda j: zeros, pipeline_mode=pl.Buffered(1))

    four = [adapt_a, adapt_a_ff, adapt_b, adapt_b_ff]
    results = [v for v in four] + [v for v in four for _ in range(2)]
    b_w, f_w = adapt_b.shape[1], adapt_b_ff.shape[1]
    owners = max(1, lanes // f_w)
    w_spec = pl.BlockSpec((kr, owners * b_w), lambda j: (0, j))
    wd_spec = pl.BlockSpec((down_rows, owners * f_w), lambda j: (0, j))
    updated = pl.pallas_call(
        functools.partial(update_kernel, rank=rank, width=width),
        grid=(dp_n // owners,),
        in_specs=[all_of(reduced), pl.BlockSpec((owners, rank, b_cols), lambda j: (j, 0, 0)), w_spec, wd_spec]
        + [all_of(v) for v in state],
        out_specs=[all_of(v) for v in results] + [w_spec, wd_spec],
        out_shape=[jax.ShapeDtypeStruct(v.shape, f32) for v in results]
        + [
            jax.ShapeDtypeStruct(frozen_input_weights.shape, bf16),
            jax.ShapeDtypeStruct(frozen_down_weight.shape, bf16),
        ],
        scratch_shapes=[pltpu.VMEM((3, kr, rank), bf16), pltpu.VMEM((down_rows, rank), bf16)],
        compiler_params=pltpu.CompilerParams(vmem_limit_bytes=48 << 20),
        name="update",
    )(reduced, fresh, frozen_input_weights, frozen_down_weight, *state)
    grad_a, grad_a_ff, grad_b, grad_b_ff = updated[:4]
    new_mean_a, new_square_a, new_mean_a_ff, new_square_a_ff = updated[4:8]
    new_mean_b, new_square_b, new_mean_b_ff, new_square_b_ff = updated[8:12]
    folded_input_weights, folded_down_weight = updated[12:]
    return (
        mixed,
        grad_tokens,
        grad_gain,
        grad_shift,
        grad_a,
        grad_a_ff,
        grad_b,
        grad_b_ff,
        new_mean_a,
        new_square_a,
        new_mean_a_ff,
        new_square_a_ff,
        new_mean_b,
        new_square_b,
        new_mean_b_ff,
        new_square_b_ff,
        folded_input_weights,
        folded_down_weight,
    )


def solution(mesh):
    in_specs = (
        P("dp", "blk", None),
        P("dp", "blk", None),
        P("dp", "blk"),
        P(),
        P("dp", None),
        P(),
        P("dp", None),
        P(),
        P(),
        P(),
        P("dp", None),
        P("dp", None),
        P(None, "dp"),
        P(None, "dp"),
        P("dp", None),
        P("dp", None),
        P(None, "dp"),
        P(None, "dp"),
        P("dp", None),
        P("dp", None),
        P(None, "dp"),
        P(None, "dp"),
        P("dp", None),
        P("dp", None),
        P(None, "dp"),
        P(None, "dp"),
    )
    out_specs = (
        P("dp", "blk", None),
        P("dp", "blk", None),
        P(),
        P(),
        P("dp", None),
        P("dp", None),
        P(None, "dp"),
        P(None, "dp"),
        P("dp", None),
        P("dp", None),
        P("dp", None),
        P("dp", None),
        P(None, "dp"),
        P(None, "dp"),
        P(None, "dp"),
        P(None, "dp"),
        P("dp", None),
        P("dp", None),
    )
    return jax.shard_map(
        functools.partial(body, mesh.shape["dp"], mesh.shape["blk"]), mesh=mesh, in_specs=in_specs, out_specs=out_specs, check_vma=False)
```

```python
import functools
import math

import jax
import jax.numpy as jnp
import numpy as np
from jax import lax
from jax.experimental import pallas as pl
from jax.experimental.pallas import tpu as pltpu
from jax.sharding import PartitionSpec as P

HEADS = 16
ROTARY = 16
DOMAINS = 22

adapter_scale = 0.25
rope_base = 10000.0
norm_eps = 1e-05
masked_score = -1e30
first_fix = 1.0 - (0.9**10) ** 10
second_fix = 1.0 - (0.999**10) ** 10

f32 = jnp.float32
bf16 = jnp.bfloat16


def nn(left, right):
    return lax.dot_general(left, right, (((1,), (0,)), ((), ())), preferred_element_type=f32)


def nt(left, right):
    return lax.dot_general(left, right, (((1,), (1,)), ((), ())), preferred_element_type=f32)


def tn(left, right):
    return lax.dot_general(left, right, (((0,), (0,)), ((), ())), preferred_element_type=f32)


def rope_lane_tables(length, depth, lanes):
    half = ROTARY // 2
    freqs = rope_base ** (-(jnp.arange(half, dtype=f32) * 2.0) / ROTARY)
    angles = jnp.arange(length, dtype=f32)[:, None] * freqs[None, :]
    cosine, sine = jnp.cos(angles), jnp.sin(angles)
    rest = depth - ROTARY
    ones, zero_half = jnp.ones((length, rest), f32), jnp.zeros((length, half), f32)
    zero_rest = jnp.zeros((length, rest), f32)
    keep = jnp.concatenate([cosine, cosine, ones], axis=1)
    from_above = jnp.concatenate([-sine, zero_half, zero_rest], axis=1)
    from_below = jnp.concatenate([zero_half, sine, zero_rest], axis=1)
    times = lanes // depth
    return tuple(jnp.tile(table, (1, times)) for table in (keep, from_above, from_below))


def turn(values, keep, above, below, sign):
    lanes = values.shape[-1]
    half = ROTARY // 2
    up = pltpu.roll(values, lanes - half, 1)
    down = pltpu.roll(values, half, 1)
    return values * keep + sign * (up * above + down * below)


def qkv_kernel(
    z_ref, x_ref, gain_ref, shift_ref, wq_ref, wk_ref, wv_ref, a_ref, b_ref, bias_ref,
    keep_ref, above_ref, below_ref, q_ref, k_ref, v_ref, first_ref, mid_ref,
):
    cols = wq_ref.shape[1]
    x = x_ref[...].reshape(x_ref.shape[2:]).astype(f32)
    centre = x - jnp.mean(x, axis=-1, keepdims=True)
    spread = jnp.mean(centre * centre, axis=-1, keepdims=True)
    first = (centre * lax.rsqrt(spread + norm_eps) * gain_ref[...] + shift_ref[...]).astype(bf16)
    mid = nn(first, a_ref[...]).astype(bf16)
    first_ref[...] = first.reshape(first_ref.shape)
    mid_ref[...] = mid.reshape(mid_ref.shape)
    low = adapter_scale * nn(mid, b_ref[...]) + bias_ref[...]
    lanes = keep_ref.shape[1]
    tables = keep_ref[...], above_ref[...], below_ref[...]
    query = nn(first, wq_ref[...]) + low[:, :cols]
    keys = nn(first, wk_ref[...]) + low[:, cols : 2 * cols]
    values = nn(first, wv_ref[...]) + low[:, 2 * cols :]
    for at in range(0, cols, lanes):
        part = slice(at, at + lanes)
        q_ref[0, :, part] = turn(query[:, part], *tables, 1.0).astype(bf16)
        k_ref[0, :, part] = turn(keys[:, part], *tables, 1.0).astype(bf16)
    v_ref[0] = values.astype(bf16)


MESH = pl.DeviceIdType.MESH


def attend_pair(query, keys, values, grad, tables, dk_ref, dv_ref, depth, blocks, store):
    lanes = keys.shape[1]
    span = keys.shape[0] // blocks
    scale = 1.0 / math.sqrt(depth)
    lane = lax.broadcasted_iota(jnp.int32, (1, lanes), 1)
    heads = lanes // depth
    masks = [jnp.where(lane // depth == h, 1.0, 0.0).astype(bf16) for h in range(heads)]
    scaled = [jnp.where(lane // depth == h, scale, 0.0).astype(bf16) for h in range(heads)]
    diagonal = lax.broadcasted_iota(jnp.int32, (span, span), 0) <= lax.broadcasted_iota(
        jnp.int32, (span, span), 1
    )
    keys_t, values_t = keys.T, values.T
    for i in range(blocks):
        done, end = i * span, (i + 1) * span
        rows = slice(done, end)
        q_i, g_i = query[rows], grad[rows]
        g_t = g_i.T
        outs, grads, lows, grads_s, q_parts, g_parts = [], [], [], [], [], []
        for h in range(heads):
            part = slice(h * depth, (h + 1) * depth)
            q_h, g_h = q_i * scaled[h], g_i * masks[h]
            last = jnp.where(diagonal, nt(keys[rows], q_h), masked_score)
            top = jnp.max(last, axis=0, keepdims=True)
            if i:
                scores = nt(keys[:done], q_h)
                top = jnp.maximum(top, jnp.max(scores, axis=0, keepdims=True))
            weights = jnp.exp(last - top)
            total = jnp.sum(weights, axis=0, keepdims=True)
            if i:
                before = jnp.exp(scores - top)
                total += jnp.sum(before, axis=0, keepdims=True)
                weights = jnp.concatenate([before, weights], axis=0)
            weights = weights * (1.0 / total)
            low = weights.astype(bf16)
            out_t = nn(values_t[part, :end], low)
            grad_p = nt(values[:end], g_h)
            delta = jnp.sum(out_t * g_t[part].astype(f32), axis=0, keepdims=True)
            grad_s = (weights * (grad_p - delta)).astype(bf16)
            outs.append(out_t)
            grads.append(nn(keys_t[part, :end], grad_s))
            lows.append(low)
            grads_s.append(grad_s)
            q_parts.append(q_h)
            g_parts.append(g_h)
        dk = nn(jnp.concatenate(grads_s, axis=1), jnp.concatenate(q_parts, axis=0))
        dv = nn(jnp.concatenate(lows, axis=1), jnp.concatenate(g_parts, axis=0))
        if i:
            dk_ref[:done] += dk[:done]
            dv_ref[:done] += dv[:done]
        dk_ref[rows] = dk[done:]
        dv_ref[rows] = dv[done:]
        store(i, 0, jnp.concatenate(outs, axis=0).T.astype(bf16))
        dq = jnp.concatenate(grads, axis=0).T * scale
        store(i, 1, turn(dq, *[t[rows] for t in tables], -1.0).astype(bf16))
    for i in range(blocks):
        rows = slice(i * span, (i + 1) * span)
        store(i, 2, turn(dk_ref[rows], *[t[rows] for t in tables], -1.0).astype(bf16))
        store(i, 3, dv_ref[rows].astype(bf16))


def normal(x):
    centre = x - jnp.mean(x, axis=-1, keepdims=True)
    return centre * lax.rsqrt(jnp.mean(centre * centre, axis=-1, keepdims=True) + norm_eps)


def front_kernel(
    tokens_ref, win_ref, wdown_ref, a_wide, aff_wide, b_wide, bff_wide,
    cot_ref, ids_ref, domain_ref, gain_ref, shift_ref, bias_ref, freq_ref,
    win_out, wdown_out, a_out, aff_out, b_out, bff_out,
    q_out, k_out, v_out, first_out, mid_out, g_out,
    low_ref, second_ref, mid_up_ref, mid_up_t_ref, dmid_ff_ref, dmid_ff_t_ref, dmid_out_t_ref,
    keep_ref, above_ref, below_ref, weight_ref,
    a_ref, aff_ref, b_ref, bff_ref, x_all, q_s, k_s, v_s, first_s, mid_s, ga, wout_v, wqkv_v, a_v, b_v, bff_v,
    sx, qx, own_sem, sr, qr, sl, ql, sd, qd, load_sem, store_sem, token_sem,
    *, n, depth,
):
    z = lax.axis_index("blk")
    dp = lax.axis_index("dp")
    y, x, c = dp // 4, lax.rem(dp // 2, 2), lax.rem(dp, 2)
    core = (dp + 1 - 2 * c, z)
    along_x = (dp + 2 - 4 * x, z)
    along_y = (dp + 4 - 8 * y, z)
    peers = [(dp, lax.rem(z + t, n)) for t in range(1, n)]
    seqs, span, width = tokens_ref.shape
    kr, down_rows, rank = win_ref.shape[0], wdown_ref.shape[0], b_ref.shape[0]
    b_w, f_w = b_ref.shape[1], bff_ref.shape[1]
    cz = q_s.shape[2]
    lanes = keep_ref.shape[1]
    four = 4 * width

    barrier = pltpu.get_barrier_semaphore()
    for peer in [core, along_x, along_y] + peers:
        pl.semaphore_signal(barrier, inc=1, device_id=peer, device_id_type=MESH)
    pl.semaphore_wait(barrier, 2 + n)

    def remote(src, dst, send, recv, peer):
        return pltpu.make_async_remote_copy(
            src_ref=src, dst_ref=dst, send_sem=send, recv_sem=recv, device_id=peer, device_id_type=MESH
        )

    shards = [
        (win_ref.at[:, :four], lambda d: win_out.at[pl.ds(pl.multiple_of(d * kr, kr), kr), :four]),
        (a_ref, lambda d: a_out.at[pl.ds(pl.multiple_of(d * kr, kr), kr), :]),
        (b_ref, lambda d: b_out.at[:, pl.ds(pl.multiple_of(d * b_w, b_w), b_w)]),
        (bff_ref, lambda d: bff_out.at[:, pl.ds(pl.multiple_of(d * f_w, f_w), f_w)]),
        (win_ref.at[:, four:], lambda d: win_out.at[pl.ds(pl.multiple_of(d * kr, kr), kr), four:]),
        (wdown_ref, lambda d: wdown_out.at[pl.ds(pl.multiple_of(d * down_rows, down_rows), down_rows), :]),
        (aff_ref, lambda d: aff_out.at[pl.ds(pl.multiple_of(d * down_rows, down_rows), down_rows), :]),
    ]
    groups = [(0, 1, 2, 3), (4,), (5, 6)]
    from_x, from_y = dp + 2 - 4 * x, dp + 4 - 8 * y
    across = dp + 2 - 4 * x + 4 - 8 * y
    onward = jnp.where(c == 0, from_y, from_x)
    target = (jnp.where(c == 0, along_x[0], along_y[0]), z)

    def hop(i, kind):
        shard, there = shards[i]
        src, dst, peer = {
            0: (shard, there(dp), along_x),
            1: (shard, there(dp), along_y),
            2: (shard, there(dp), core),
            3: (there(onward), there(onward), target),
            4: (there(from_x), there(from_x), core),
            5: (there(from_y), there(from_y), core),
            6: (there(across), there(across), core),
        }[kind]
        return remote(src, dst, sx.at[i, kind], qx.at[i, kind], peer)

    def own_copy(i):
        return pltpu.make_async_copy(shards[i][0], shards[i][1](dp), own_sem.at[i])

    def start_own(group):
        for kind in (0, 1, 2):
            for i in groups[group]:
                hop(i, kind).start()
        for i in groups[group]:
            own_copy(i).start()

    def pass_on(group):
        for i in groups[group]:
            hop(i, 0).wait_recv()
            hop(i, 1).wait_recv()
        for kind in (3, 4, 5):
            for i in groups[group]:
                hop(i, kind).start()

    def close(group):
        for i in groups[group]:
            hop(i, 3).wait_recv()
            hop(i, 6).start()

    def arrived(group):
        for i in groups[group]:
            own_copy(i).wait()
            for kind in (2, 4, 5, 6):
                hop(i, kind).wait_recv()

    def rightward(s):
        return remote(x_all.at[z - s + 1], x_all.at[z - s + 1], sr.at[s], qr.at[s], (dp, z + 1))

    def leftward(s):
        return remote(x_all.at[z + s - 1], x_all.at[z + s - 1], sl.at[s], ql.at[s], (dp, z - 1))

    def from_left(s):
        return remote(x_all.at[z - s], x_all.at[z - s], sr.at[s], qr.at[s], (dp, z - 1))

    def from_right(s):
        return remote(x_all.at[z + s], x_all.at[z + s], sl.at[s], ql.at[s], (dp, z + 1))

    def ring_start(s):
        pl.when((z < n - 1) & (z - s + 1 >= 0))(lambda: rightward(s).start())
        pl.when((z > 0) & (z + s - 1 < n))(lambda: leftward(s).start())

    def ring_wait(s):
        pl.when(z - s >= 0)(lambda: from_left(s).wait_recv())
        pl.when(z + s < n)(lambda: from_right(s).wait_recv())

    def ring_end(s):
        pl.when((z < n - 1) & (z - s + 1 >= 0))(lambda: rightward(s).wait_send())
        pl.when((z > 0) & (z + s - 1 < n))(lambda: leftward(s).wait_send())

    for low, values in ((a_ref, a_wide), (aff_ref, aff_wide), (b_ref, b_wide), (bff_ref, bff_wide)):
        low[...] = values[...].astype(bf16)
    token_copy = pltpu.make_async_copy(tokens_ref, x_all.at[z], token_sem.at[0])
    token_copy.start()
    start_own(0)
    token_copy.wait()
    ring_start(1)

    unit_lane = lax.rem(lax.broadcasted_iota(jnp.int32, (1, lanes), 1), depth)
    half = ROTARY // 2
    for b in range(n):
        rows = slice(b * span, (b + 1) * span)
        place = (lax.broadcasted_iota(jnp.int32, (span, lanes), 0) + b * span).astype(f32)
        angle = place * freq_ref[...]
        cosine, sine = jnp.cos(angle), jnp.sin(angle)
        keep_ref[rows] = jnp.where(unit_lane < ROTARY, cosine, 1.0)
        above_ref[rows] = jnp.where(unit_lane < half, -sine, 0.0)
        below_ref[rows] = jnp.where((unit_lane >= half) & (unit_lane < ROTARY), sine, 0.0)
    for q in range(seqs):
        part = slice(q * span, (q + 1) * span)
        ids = ids_ref[q : q + 1, :]
        found = jnp.zeros((1, span), f32)
        for k in range(DOMAINS):
            found = jnp.where(ids == k, domain_ref[k], found)
        weight = jnp.broadcast_to(found, (8, span)).T[:, :1]
        weight_ref[part] = weight
        low_ref[part] = (cot_ref[q].astype(f32) * weight).astype(bf16)
        unit = normal(x_all[z, q].astype(f32))
        second_ref[part] = (unit * gain_ref[1:2] + shift_ref[1:2]).astype(bf16)

    pass_on(0)
    start_own(1)
    ring_wait(1)
    if n > 2:
        ring_start(2)
    close(0)
    arrived(0)

    loads = [
        pltpu.make_async_copy(win_out.at[:, 3 * width : four], wout_v, load_sem.at[0]),
        pltpu.make_async_copy(a_out, a_v, load_sem.at[1]),
        pltpu.make_async_copy(b_out, b_v, load_sem.at[2]),
        pltpu.make_async_copy(bff_out, bff_v, load_sem.at[3]),
    ] + [
        pltpu.make_async_copy(
            win_out.at[:, pl.ds(pl.multiple_of(t * width + z * cz, cz), cz)], wqkv_v.at[t], load_sem.at[4 + t]
        )
        for t in range(3)
    ]
    for copy in loads:
        copy.start()
    for copy in loads:
        copy.wait()

    def grad_out(q, _):
        part = pl.ds(pl.multiple_of(q * span, span), span)
        low = low_ref[part, :]
        dmid = (adapter_scale * nt(low, b_v[:, 3 * width : four])).astype(bf16)
        dmid_out_t_ref[q] = dmid.T
        for g in range(n):
            rows = slice(g * cz, (g + 1) * cz)
            value = nt(low, wout_v[rows]) + nt(dmid, a_v[rows, rank : 2 * rank])
            ga[g, q] = value.astype(bf16)
        return 0

    lax.fori_loop(0, seqs, grad_out, 0)
    place_own = pl.ds(pl.multiple_of(z * span, span), span)

    def grad_send(t):
        return remote(ga.at[lax.rem(z + t, n)], g_out.at[:, place_own, :], sd.at[t], qd.at[t], peers[t - 1])

    grad_own = pltpu.make_async_copy(ga.at[z], g_out.at[:, place_own, :], token_sem.at[1])
    grad_own.start()
    for t in range(1, n):
        grad_send(t).start()

    def stores(b):
        rows = pl.ds(pl.multiple_of(b * span, span), span)
        return [
            pltpu.make_async_copy(src.at[:, rows, :], dst.at[:, rows, :], store_sem.at[i, b])
            for i, (src, dst) in enumerate(
                ((q_s, q_out), (k_s, k_out), (v_s, v_out), (first_s, first_out), (mid_s, mid_out))
            )
        ]

    def project_block(b):
        rows = pl.ds(pl.multiple_of(b * span, span), span)

        def one(q, _):
            first = (normal(x_all[b, q].astype(f32)) * gain_ref[0:1] + shift_ref[0:1]).astype(bf16)
            mid = nn(first, a_v[:, 0:rank]).astype(bf16)
            first_s[q, rows, :] = first
            mid_s[q, rows, :] = mid
            for t, kept in enumerate((q_s, k_s, v_s)):
                at = pl.ds(pl.multiple_of(t * width + z * cz, cz), cz)
                value = nn(first, wqkv_v[t]) + adapter_scale * nn(mid, b_v[:, at]) + bias_ref[:, at]
                if t < 2:
                    value = jnp.concatenate(
                        [
                            turn(value[:, i : i + lanes], keep_ref[rows, :], above_ref[rows, :], below_ref[rows, :], 1.0)
                            for i in range(0, cz, lanes)
                        ],
                        axis=1,
                    )
                kept[q, rows, :] = value.astype(bf16)
            return 0

        lax.fori_loop(0, seqs, one, 0)
        for copy in stores(b):
            copy.start()

    def project_near(s):
        def side(i, _):
            b = z + s * (2 * i - 1)
            pl.when((b >= 0) & (b < n) & ((s > 0) | (i == 0)))(lambda: project_block(b))
            return 0

        lax.fori_loop(0, 2, side, 0)

    def local_products(q, _):
        part = pl.ds(pl.multiple_of(q * span, span), span)
        mid = nn(second_ref[part, :], a_v[:, 2 * rank : 3 * rank]).astype(bf16)
        mid_up_ref[part, :] = mid
        mid_up_t_ref[q] = mid.T
        dmid = (adapter_scale * nt(low_ref[part, :], bff_v[...])).astype(bf16)
        dmid_ff_ref[part, :] = dmid
        dmid_ff_t_ref[q] = dmid.T
        return 0

    def walk(s, _):
        @pl.when(s == 1)
        def _():
            pass_on(1)
            start_own(2)

        @pl.when((s > 1) & (s < n))
        def _():
            ring_wait(s)
            pl.when(s + 1 < n)(lambda: ring_start(s + 1))

        project_near(s - 1)

        @pl.when(s == 2)
        def _():
            close(1)
            lax.fori_loop(0, seqs, local_products, 0)
            pass_on(2)

        return 0

    lax.fori_loop(1, n + 1, walk, 0)
    close(2)
    arrived(1)
    arrived(2)
    for i in range(len(shards)):
        for kind in range(7):
            hop(i, kind).wait_send()
    for s in range(1, n):
        ring_end(s)
    grad_own.wait()
    for t in range(1, n):
        grad_send(t).wait()
    for b in range(n):
        for copy in stores(b):
            copy.wait()


def remote(src, dst, send, recv, peer):
    return pltpu.make_async_remote_copy(
        src_ref=src, dst_ref=dst, send_sem=send, recv_sem=recv, device_id=peer, device_id_type=MESH
    )


def add_low(a, b):
    return (a.astype(f32) + b.astype(f32)).astype(bf16)


def plane():
    dp, z = lax.axis_index("dp"), lax.axis_index("blk")
    y, x, c = dp // 4, lax.rem(dp // 2, 2), lax.rem(dp, 2)
    return dp, z, y, x, c, (dp + 1 - 2 * c, z), (dp + 2 - 4 * x, z), (dp + 4 - 8 * y, z)


def greet(peers):
    barrier = pltpu.get_barrier_semaphore()
    for peer in peers:
        pl.semaphore_signal(barrier, inc=1, device_id=peer, device_id_type=MESH)
    pl.semaphore_wait(barrier, len(peers))


early_cuts = ((0, 512), (512, 1024), (1024, 1536), (1536, 1920))
late_end, a_ff_at, b_at_col, early_end = 256, 384, 896, 1920


class PlaneSum:
    def __init__(self, e, r1, r2a, r2b, r3a, r3b, s1, q1, s2, q2, s3, q3):
        self.refs = e, r1, r2a, r2b, r3a, r3b
        self.sems = s1, q1, s2, q2, s3, q3
        self.at = plane()
        self.half = e.shape[3] // 2

    def first(self, m):
        e, r1 = self.refs[:2]
        c, core = self.at[4], self.at[5]
        s1, q1 = self.sems[:2]
        if m < 4:
            cut = slice(late_end, early_end)
            return remote(e.at[m // 2, m % 2, 1 - c, :, cut], r1.at[m // 2, m % 2, :, cut], s1.at[m], q1.at[m], core)
        cut = slice(0, late_end)
        return remote(e.at[:, :, 1 - c, :, cut], r1.at[:, :, :, cut], s1.at[m], q1.at[m], core)

    def take_first(self, m):
        e, r1 = self.refs[:2]
        c = self.at[4]
        self.first(m).wait()
        for i in (m,) if m < 4 else range(4):
            yy, xx = i // 2, i % 2
            cut = slice(late_end, early_end) if m < 4 else slice(0, late_end)
            e[yy, xx, c, :, cut] = add_low(e[yy, xx, c, :, cut], r1[yy, xx, :, cut])

    def finish(self, out):
        e, r1, r2a, r2b, r3a, r3b = self.refs
        dp, z, y, x, c, core, along_x, along_y = self.at
        s1, q1, s2, q2, s3, q3 = self.sems
        half = self.half

        def second(k):
            cut = slice(*early_cuts[k])
            return [
                remote(e.at[:, 1 - x, c, 0:half, cut], r2a.at[:, :, cut], s2.at[0, k], q2.at[0, k], along_x),
                remote(e.at[1 - y, :, c, half:, cut], r2b.at[:, :, cut], s2.at[1, k], q2.at[1, k], along_y),
            ]

        def third(k):
            cut = slice(*early_cuts[k])
            return [
                remote(e.at[1 - y, x, c, 0:half, cut], r3a.at[:, cut], s3.at[0, k], q3.at[0, k], along_y),
                remote(e.at[y, 1 - x, c, half:, cut], r3b.at[:, cut], s3.at[1, k], q3.at[1, k], along_x),
            ]

        def after_second(k):
            cut = slice(*early_cuts[k])
            for copy in second(k):
                copy.wait()
            for i in range(2):
                e[i, x, c, 0:half, cut] = add_low(e[i, x, c, 0:half, cut], r2a[i, :, cut])
                e[y, i, c, half:, cut] = add_low(e[y, i, c, half:, cut], r2b[i, :, cut])
            for copy in third(k):
                copy.start()

        def after_third(k):
            cut = slice(*early_cuts[k])
            for copy in third(k):
                copy.wait()
            out[0:half, cut] = add_low(e[y, x, c, 0:half, cut], r3a[:, cut])
            out[half:, cut] = add_low(e[y, x, c, half:, cut], r3b[:, cut])

        count = len(early_cuts)
        for k in range(count):
            for copy in second(k):
                copy.start()
        for k in range(count + 1):
            if k < count:
                after_second(k)
            if k:
                after_third(k - 1)


def middle_kernel(
    q_ref, k_ref, v_ref, g_ref, keep_ref, above_ref, below_ref,
    second_ref, low_ref, mid_ref, mid_t_ref, dmid_ref, dmid_t_ref,
    up_ref, down_ref, a_ref, b_ref, bias_ref, *refs,
    n, pairs, steps, depth, early,
):
    if early:
        first_ref, mid_qkv_ref, local_ref, ff_ref, back_ref, mid_ff_ref, dmid_up_ref, sum_ref = refs[:8]
        buffer, dk_ref, dv_ref, mid_acc, dmid_acc, send_sem, recv_sem, own_sem = refs[8:16]
        e_ref, dmid_seq, gb_acc, ga_acc = refs[16:20]
        plane_refs = refs[20:]
    else:
        local_ref, own_ref, ff_ref, back_ref, mid_ff_ref, dmid_up_ref, ga_ref, gb_ref = refs[:8]
        buffer, dk_ref, dv_ref, mid_acc, dmid_acc, send_sem, recv_sem, own_sem = refs[8:]
    step = pl.program_id(0)
    z = lax.axis_index("blk")
    dp = lax.axis_index("dp")
    lanes = q_ref.shape[2]
    length = q_ref.shape[1]
    inner_block = up_ref.shape[1]
    width = up_ref.shape[0]
    cz = pairs * lanes
    if early:
        plane_sum = PlaneSum(e_ref, *plane_refs)

    def copies(s):
        seq, pair = s // pairs, lax.rem(s, pairs)
        at = pl.ds(pl.multiple_of((z * pairs + pair) * lanes, lanes), lanes)
        target = local_ref.at[seq, :, :, at]
        own = pltpu.make_async_copy(buffer.at[s, z], target, own_sem.at[s])
        away = []
        for t in range(1, n):
            peer = lax.rem(z + t, n)
            away.append(
                remote(buffer.at[s, peer], target, send_sem.at[s, t], recv_sem.at[s, t], (dp, peer))
            )
        return own, away

    @pl.when(step == 0)
    def _():
        peers = [(dp, lax.rem(z + t, n)) for t in range(1, n)]
        greet((list(plane()[5:]) if early else []) + peers)

    @pl.when(step < steps)
    def _():
        def store(i, kind, value):
            buffer[step, i, kind] = value
            if kind and not early:
                own_ref[0, kind - 1, i * value.shape[0] : (i + 1) * value.shape[0], :] = value

        tables = keep_ref[...], above_ref[...], below_ref[...]
        attend_pair(q_ref[0], k_ref[0], v_ref[0], g_ref[0], tables, dk_ref, dv_ref, depth, n, store)
        own, away = copies(step)
        own.start()
        for copy in away:
            copy.start()
        if early:
            seq, pair = step // pairs, lax.rem(step, pairs)
            mid_t = mid_qkv_ref[0].T
            dmid = jnp.zeros((length, lanes), f32)
            for t in range(3):
                grad = buffer[step, :, t + 1].reshape(length, lanes)
                at = pl.ds(pl.multiple_of(t * width + z * cz + pair * lanes, lanes), lanes)
                dmid += nt(grad, b_ref[:, at])
                product = nn(mid_t, grad)
                gb_acc[t, pair] = jnp.where(seq == 0, product, gb_acc[t, pair] + product)
            dmid = jnp.where(pair == 0, dmid, dmid_seq[...] + dmid)
            dmid_seq[...] = dmid

            @pl.when(pair == pairs - 1)
            def _():
                product = nn((adapter_scale * dmid_seq[...]).astype(bf16).T, first_ref[0])
                ga_acc[...] = jnp.where(seq == 0, product, ga_acc[...] + product)

    @pl.when(step == steps)
    def _():
        ff_ref[...] = jnp.zeros_like(ff_ref)
        back_ref[...] = jnp.zeros_like(back_ref)
        mid_acc[...] = jnp.zeros_like(mid_acc)
        dmid_acc[...] = jnp.zeros_like(dmid_acc)
        if early:
            for owner in range(8):
                place = (owner // 4, owner // 2 % 2, owner % 2)
                e_ref[place + (slice(None), slice(late_end, a_ff_at))] = ga_acc[
                    :, owner * lanes : (owner + 1) * lanes
                ].astype(bf16)
                if owner < 4:
                    e_ref[place + (slice(None), slice(b_at_col, early_end))] = jnp.zeros((lanes, 1024), bf16)
            for t in range(3):
                for pair in range(pairs):
                    at = pl.ds(pl.multiple_of(b_at_col + z * cz + pair * lanes, lanes), lanes)
                    e_ref[0, t // 2, t % 2, :, at] = (adapter_scale * gb_acc[t, pair]).astype(bf16)

    @pl.when(step >= steps)
    def _():
        count, size = mid_t_ref.shape[0], mid_t_ref.shape[2]
        j = step - steps
        if early:
            up_b = b_ref[:, pl.ds(pl.multiple_of(4 * width + j * inner_block, inner_block), inner_block)]
        else:
            up_b = b_ref[...]
        ga, gb = None, None
        for at in range(count):
            rows = slice(at * size, (at + 1) * size)
            pre = nn(second_ref[rows], up_ref[...]) + bias_ref[...] + adapter_scale * nn(mid_ref[rows], up_b)
            cdf = 0.5 + 0.5 * lax.erf(pre * (1.0 / math.sqrt(2.0)))
            hidden = (pre * cdf).astype(bf16)
            slope = cdf + pre * (jnp.exp(-0.5 * pre * pre) * (1.0 / math.sqrt(2.0 * math.pi)))
            grad_hidden = nt(low_ref[rows], down_ref[...]) + nt(dmid_ref[rows], a_ref[...])
            dup = (slope * grad_hidden).astype(bf16)
            ff_ref[rows] += nn(hidden, down_ref[...])
            back_ref[rows] += nt(dup, up_ref[...])
            mid_acc[rows] += nn(hidden, a_ref[...])
            dmid_acc[rows] += nt(dup, up_b)
            ga_part = nn(dmid_t_ref[at], hidden)
            gb_part = nn(mid_t_ref[at], dup)
            ga = ga_part if ga is None else ga + ga_part
            gb = gb_part if gb is None else gb + gb_part
        if early:
            e_ref[j // 4, lax.rem(j // 2, 2), lax.rem(j, 2), :, a_ff_at:b_at_col] = ga.astype(bf16)
            at = pl.ds(pl.multiple_of(b_at_col + lax.rem(j, 2) * inner_block, lanes), inner_block)
            e_ref[1, j // 4, lax.rem(j // 2, 2), :, at] = (adapter_scale * gb).astype(bf16)
            for m in range(3):

                @pl.when(j == 2 * m + 3)
                def _(m=m):
                    plane_sum.take_first(m)

            for m in range(4):
                pl.when(j == 2 * m + 1)(lambda m=m: plane_sum.first(m).start())
        else:
            ga_ref[...] = ga
            gb_ref[...] = gb

    @pl.when(step == pl.num_programs(0) - 1)
    def _():
        mid_ff_ref[...] = mid_acc[...].astype(bf16)
        dmid_up_ref[...] = (adapter_scale * dmid_acc[...]).astype(bf16)
        if early:
            count, size = mid_t_ref.shape[0], mid_t_ref.shape[2]
            ga, gb = None, None
            for at in range(count):
                rows = slice(at * size, (at + 1) * size)
                ga_part = nn(dmid_up_ref[rows].T, second_ref[rows])
                gb_part = nn(mid_ff_ref[rows].T, low_ref[rows])
                ga = ga_part if ga is None else ga + ga_part
                gb = gb_part if gb is None else gb + gb_part
            for owner in range(8):
                place = (owner // 4, owner // 2 % 2, owner % 2, slice(None))
                at = slice(owner * lanes, (owner + 1) * lanes)
                e_ref[place + (slice(0, lanes),)] = ga[:, at].astype(bf16)
                e_ref[place + (slice(lanes, late_end),)] = (adapter_scale * gb[:, at]).astype(bf16)
            plane_sum.first(4).start()
            plane_sum.take_first(3)
            plane_sum.take_first(4)
            plane_sum.finish(sum_ref)
        for s in range(steps):
            own, away = copies(s)
            own.wait()
            for copy in away:
                copy.wait()


def finish_kernel(
    local_ref, wo_ref, wq_ref, wk_ref, wv_ref, a_out_ref, a_qkv_ref, b_out_ref, bq_ref, bk_ref, bv_ref,
    bias_ref, x_ref, cot_ref, weight_ref, ff_ref, bias_ff_ref, mid_ff_ref, b_ff_ref,
    second_ref, dmid_up_ref, a_up_ref, gain_ref, dmid_out_t_ref, low_ref,
    mixed_ref, tokens_ref, norm_ref, ga_ref, gb_ref,
    att_acc, mid_acc, first_acc, dmid_acc,
):
    t = pl.program_id(0)
    rows = x_ref.shape[0] * x_ref.shape[1]
    cols = wq_ref.shape[1]

    @pl.when(t == 0)
    def _():
        att_acc[...] = jnp.zeros_like(att_acc)
        mid_acc[...] = jnp.zeros_like(mid_acc)
        first_acc[...] = jnp.zeros_like(first_acc)
        dmid_acc[...] = jnp.zeros_like(dmid_acc)

    out, dq, dk, dv = (local_ref[:, i].reshape(rows, cols) for i in range(4))
    att_acc[...] += nn(out, wo_ref[...])
    mid_acc[...] += nn(out, a_out_ref[...])
    first_acc[...] += nt(dq, wq_ref[...]) + nt(dk, wk_ref[...]) + nt(dv, wv_ref[...])
    dmid_acc[...] += nt(dq, bq_ref[...]) + nt(dk, bk_ref[...]) + nt(dv, bv_ref[...])
    size = x_ref.shape[1]
    ga_ref[...] = sum(nn(dmid_out_t_ref[q], out[q * size : (q + 1) * size]) for q in range(x_ref.shape[0]))

    @pl.when(t == pl.num_programs(0) - 1)
    def _():
        size = x_ref.shape[1]
        norm = [jnp.zeros((1, first_acc.shape[1]), f32) for _ in range(4)]
        for q in range(x_ref.shape[0]):
            part = slice(q * size, (q + 1) * size)
            x = x_ref[q].astype(f32)
            mid = mid_acc[part].astype(bf16)
            gb = tn(mid, low_ref[part])
            gb_ref[...] = gb if q == 0 else gb_ref[...] + gb
            att = att_acc[part] + bias_ref[...] + adapter_scale * nn(mid, b_out_ref[...])
            ff = ff_ref[part] + bias_ff_ref[...] + adapter_scale * nn(mid_ff_ref[part], b_ff_ref[...])
            mixed_ref[q] = (x + att + ff).astype(bf16)
            dmid = (adapter_scale * dmid_acc[part]).astype(bf16)
            grad_first = first_acc[part] + nt(dmid, a_qkv_ref[...])
            grad_second = second_ref[part] + nt(dmid_up_ref[part], a_up_ref[...])
            centre = x - jnp.mean(x, axis=-1, keepdims=True)
            inv = lax.rsqrt(jnp.mean(centre * centre, axis=-1, keepdims=True) + norm_eps)
            unit = centre * inv
            pulled = grad_first * gain_ref[0:1] + grad_second * gain_ref[1:2]
            back = inv * (
                pulled
                - jnp.mean(pulled, axis=-1, keepdims=True)
                - unit * jnp.mean(pulled * unit, axis=-1, keepdims=True)
            )
            row_grad = cot_ref[q].astype(f32) * weight_ref[part]
            tokens_ref[q] = (row_grad + back).astype(bf16)
            for k, value in enumerate((grad_first * unit, grad_second * unit, grad_first, grad_second)):
                norm[k] += jnp.sum(value, axis=0, keepdims=True)
        norm_ref[...] = jnp.concatenate(norm, axis=0)


def tail_kernel(
    o_ref, dq_ref, dk_ref, dv_ref, wo_ref, wq_ref, wk_ref, wv_ref, a_out_ref, a_qkv_ref, b_out_ref,
    bq_ref, bk_ref, bv_ref, bias_ref, x_ref, cot_ref, weight_ref, ff_ref, bias_ff_ref, mid_ff_ref, b_ff_ref,
    second_ref, dmid_up_ref, a_up_ref, gain_ref, dmid_out_t_ref, low_ref,
    e_ref, b_ref, mean_ref, square_ref, bf_ref, mean_f_ref, square_f_ref,
    mixed_ref, tokens_ref, out_hbm, norm_ref, fresh_hbm,
    out_ref, fresh_ref, att_acc, mid_acc, first_acc, dmid_acc,
    r4, la, lb, lr1, lr2, lr3, lbr, lj, lr4, lbr4, lbt, nr, nsum,
    s4, q4, s5, q5, sl, ql, sl4, ql4, sl5, ql5, sn, qn, sg, qg, done_sem,
    *, n,
):
    step = pl.program_id(0)
    dp, z, y, x, c, core, along_x, along_y = plane()
    peers = [(dp, lax.rem(z + t, n)) for t in range(1, n)]
    seqs, size, width = o_ref.shape[0], o_ref.shape[2], x_ref.shape[2]
    rows, cols = seqs * size, o_ref.shape[3]
    blocks = width // cols
    rank = e_ref.shape[0]
    part = rank // n
    lanes = 128
    mine = pl.ds(pl.multiple_of(z * part, part), part)
    late = slice(early_end, early_end + lanes)

    def to_part(t):
        return pl.ds(pl.multiple_of(lax.rem(z + t, n) * part, part), part)

    def e_out(k, t):
        cut = slice(*early_cuts[k])
        return remote(e_ref.at[to_part(t), cut], r4.at[t, :, cut], s4.at[t, k], q4.at[t, k], peers[t - 1])

    def e_back(k, t):
        cut = slice(*early_cuts[k])
        return remote(out_ref.at[mine, cut], out_ref.at[mine, cut], s5.at[t, k], q5.at[t, k], peers[t - 1])

    count = len(early_cuts)

    has_b = (c == 1, (c == 1) & (x == 1), dp == 3)
    gives_b = (c == 0, (c == 1) & (x == 0), (c == 1) & (x == 1) & (y == 1))

    def late_a(i):
        src, dst, peer = [
            (la.at[:, :, 1 - c], lr1, core),
            (la.at[:, 1 - x, c], lr2, along_x),
            (la.at[1 - y, x, c], lr3, along_y),
        ][i]
        return remote(src, dst, sl.at[0, i], ql.at[0, i], peer)

    def late_b(i):
        return remote(lb, lbr.at[i], sl.at[1, i], ql.at[1, i], (core, along_x, along_y)[i])

    def late_start(i):
        late_a(i).start()
        pl.when(gives_b[i])(lambda: late_b(i).start())

    def late_take(i):
        late_a(i).wait()
        pl.when(gives_b[i])(lambda: late_b(i).wait_send())

        @pl.when(has_b[i])
        def _():
            late_b(i).wait_recv()
            lb[...] = add_low(lb[...], lbr[i])

        if i == 0:
            for yy in range(2):
                for xx in range(2):
                    la[yy, xx, c] = add_low(la[yy, xx, c], lr1[yy, xx])
        elif i == 1:
            for yy in range(2):
                la[yy, x, c] = add_low(la[yy, x, c], lr2[yy])
        else:
            lj[...] = add_low(la[y, x, c], lr3[...])

    def late_out(t):
        return (
            remote(lj.at[to_part(t), :], lr4.at[t], sl4.at[0, t], ql4.at[0, t], peers[t - 1]),
            remote(lb.at[to_part(t), :], lbr4.at[t], sl4.at[1, t], ql4.at[1, t], peers[t - 1]),
        )

    def late_back(t):
        return (
            remote(out_ref.at[mine, late], out_ref.at[mine, late], sl5.at[0, t], ql5.at[0, t], peers[t - 1]),
            remote(lbt.at[mine, :], lbt.at[mine, :], sl5.at[1, t], ql5.at[1, t], peers[t - 1]),
        )

    def both(make, act):
        for t in range(1, n):
            a, b = make(t)
            act(a)
            pl.when(dp == 3)(lambda b=b: act(b))

    from_x, from_y, from_c = along_x[0], along_y[0], core[0]
    across = from_x + from_y - dp
    onward = jnp.where(c == 0, from_y, from_x)
    target = (jnp.where(c == 0, from_x, from_y), z)
    other = 1 - 2 * c
    hops = [
        (dp, from_x, along_x), (dp, from_y, along_y), (dp, from_c, core), (onward, across, target),
        (from_x, from_x + other, core), (from_y, from_y + other, core), (across, across + other, core),
    ]

    def gather(kind):
        slot, _, peer = hops[kind]
        return remote(fresh_ref.at[slot], fresh_ref.at[slot], sg.at[kind], qg.at[kind], peer)

    def make_fresh():
        cut = b_ref.shape[1]
        grads = out_ref[:, b_at_col:early_end].astype(f32)
        new_b = adam_fresh(b_ref[...], grads, mean_ref[...], square_ref[...])
        grads = out_ref[:, lanes:late_end].astype(f32)
        new_f = adam_fresh(bf_ref[...], grads, mean_f_ref[...], square_f_ref[...])
        fresh_ref[dp] = jnp.concatenate([new_b, new_f], axis=1).astype(bf16)

    def norm_copy(i, peer):
        return remote(nsum.at[i], nr.at[i], sn.at[i], qn.at[i], peer)

    norm_stages = [norm_copy(0, core), norm_copy(1, along_x), norm_copy(2, along_y)]
    norm_last = [
        remote(nsum.at[3], nr.at[2 + t], sn.at[2 + t], qn.at[2 + t], peers[t - 1]) for t in range(1, n)
    ]

    def norm_take(i):
        norm_stages[i].wait()
        nsum[i + 1] = nsum[i] + nr[i]

    @pl.when(step == 0)
    def _():
        greet([core, along_x, along_y] + peers)
        for k in range(count):
            for t in range(1, n):
                e_out(k, t).start()
        att_acc[...] = jnp.zeros_like(att_acc)
        mid_acc[...] = jnp.zeros_like(mid_acc)
        first_acc[...] = jnp.zeros_like(first_acc)
        dmid_acc[...] = jnp.zeros_like(dmid_acc)

    @pl.when(step < blocks)
    def _():
        out = o_ref[...].reshape(rows, cols)
        att_acc[...] += nn(out, wo_ref[...])
        mid_acc[...] += nn(out, a_out_ref[...])
        ga = sum(nn(dmid_out_t_ref[q], out[q * size : (q + 1) * size]) for q in range(seqs)).astype(bf16)
        for i in range(cols // lanes):
            owner = step * (cols // lanes) + i
            la[owner // 4, lax.rem(owner // 2, 2), lax.rem(owner, 2)] = ga[:, i * lanes : (i + 1) * lanes]

    @pl.when(step == blocks - 1)
    def _():
        gb = None
        for q in range(seqs):
            at = slice(q * size, (q + 1) * size)
            product = nn(mid_acc[at].astype(bf16).T, low_ref[at])
            gb = product if gb is None else gb + product
        lb[...] = (adapter_scale * gb).astype(bf16)
        late_start(0)

    @pl.when((step >= blocks) & (step < 2 * blocks))
    def _():
        dq, dk, dv = (r[...].reshape(rows, cols) for r in (dq_ref, dk_ref, dv_ref))
        first_acc[...] += nt(dq, wq_ref[...]) + nt(dk, wk_ref[...]) + nt(dv, wv_ref[...])
        dmid_acc[...] += nt(dq, bq_ref[...]) + nt(dk, bk_ref[...]) + nt(dv, bv_ref[...])

    @pl.when(step == blocks)
    def _():
        late_take(0)
        late_start(1)

    @pl.when(step == 2 * blocks - 1)
    def _():
        late_take(1)
        late_start(2)
        for k in range(count):
            cut = slice(*early_cuts[k])
            for t in range(1, n):
                e_out(k, t).wait()
            value = e_ref[mine, cut].astype(f32)
            for t in range(1, n):
                value += r4[t, :, cut].astype(f32)
            out_ref[mine, cut] = value.astype(bf16)
            for t in range(1, n):
                e_back(k, t).start()

    @pl.when(step >= 2 * blocks)
    def _():
        q = step - 2 * blocks
        at = pl.ds(pl.multiple_of(q * size, size), size)
        x_in = x_ref[0].astype(f32)
        mid = mid_acc[at, :].astype(bf16)
        att = att_acc[at, :] + bias_ref[...] + adapter_scale * nn(mid, b_out_ref[...])
        ff = ff_ref[...] + bias_ff_ref[...] + adapter_scale * nn(mid_ff_ref[at, :], b_ff_ref[...])
        mixed_ref[0] = (x_in + att + ff).astype(bf16)
        dmid = (adapter_scale * dmid_acc[at, :]).astype(bf16)
        grad_first = first_acc[at, :] + nt(dmid, a_qkv_ref[...])
        grad_second = second_ref[...] + nt(dmid_up_ref[at, :], a_up_ref[...])
        centre = x_in - jnp.mean(x_in, axis=-1, keepdims=True)
        inv = lax.rsqrt(jnp.mean(centre * centre, axis=-1, keepdims=True) + norm_eps)
        unit = centre * inv
        pulled = grad_first * gain_ref[0:1] + grad_second * gain_ref[1:2]
        back = inv * (
            pulled
            - jnp.mean(pulled, axis=-1, keepdims=True)
            - unit * jnp.mean(pulled * unit, axis=-1, keepdims=True)
        )
        row_grad = cot_ref[0].astype(f32) * weight_ref[at, :]
        tokens_ref[0] = (row_grad + back).astype(bf16)
        norm = [
            jnp.sum(value, axis=0, keepdims=True)
            for value in (grad_first * unit, grad_second * unit, grad_first, grad_second)
        ]
        norm = jnp.concatenate(norm, axis=0)
        nsum[0] = jnp.where(q == 0, norm, nsum[0] + norm)

    @pl.when(step == 2 * blocks)
    def _():
        late_take(2)
        both(late_out, lambda copy: copy.start())

    @pl.when(step == 2 * blocks + 1)
    def _():
        both(late_out, lambda copy: copy.wait())
        value = lj[mine, :].astype(f32)
        for t in range(1, n):
            value += lr4[t].astype(f32)
        out_ref[mine, late] = value.astype(bf16)

        @pl.when(dp == 3)
        def _():
            value = lb[mine, :].astype(f32)
            for t in range(1, n):
                value += lbr4[t].astype(f32)
            lbt[mine, :] = value.astype(bf16)

        both(late_back, lambda copy: copy.start())

    @pl.when(step == pl.num_programs(0) - 1)
    def _():
        norm_stages[0].start()
        both(late_back, lambda copy: copy.wait())
        for k in range(count):
            for t in range(1, n):
                e_back(k, t).wait()

        @pl.when(dp == 3)
        def _():
            out_ref[:, b_at_col:early_end] = lbt[...]

        make_fresh()
        for kind in (0, 1, 2):
            gather(kind).start()
        keep_out = pltpu.make_async_copy(out_ref, out_hbm, done_sem.at[0])
        keep_out.start()
        norm_take(0)
        norm_stages[1].start()
        gather(0).wait_recv()
        gather(1).wait_recv()
        for kind in (3, 4, 5):
            gather(kind).start()
        norm_take(1)
        norm_stages[2].start()
        gather(3).wait_recv()
        gather(6).start()
        norm_take(2)
        for copy in norm_last:
            copy.start()
        for kind in (2, 4, 5, 6):
            gather(kind).wait_recv()
        keep_fresh = pltpu.make_async_copy(fresh_ref, fresh_hbm, done_sem.at[1])
        keep_fresh.start()
        for kind in range(7):
            gather(kind).wait_send()
        for copy in norm_last:
            copy.wait()
        keep_out.wait()
        keep_fresh.wait()
        value = jnp.zeros_like(nsum[3])
        for blk in range(n):
            there = lax.rem(z - blk + n, n)
            value += jnp.where(there == 0, nsum[3], nr[2 + jnp.maximum(there, 1)])
        norm_ref[...] = value


def update_kernel(
    g_ref, fresh_ref, w_ref, wd_ref, *refs, rank, width,
):
    params, outs = refs[:16], refs[16:30]
    a_new, aff_new = refs[30:]
    j = pl.program_id(0)
    cols = w_ref.shape[1]

    @pl.when(j == 0)
    def _():
        rows, inner = params[0].shape[0], params[4].shape[0]
        got = g_ref[...].astype(f32)
        cut, cut_f = params[8].shape[1], params[12].shape[1]
        up = got[:, :rows]
        qkv = got[:, rows + cut_f : 2 * rows + cut_f]
        out = got[:, 2 * rows + cut_f + inner + cut :]
        at = 2 * rows + cut_f
        grads = [
            jnp.concatenate([part.T for part in (qkv, out, up)], axis=1),
            got[:, at : at + inner].T,
            got[:, at + inner : at + inner + cut],
            got[:, rows : rows + cut_f],
        ]
        for i, grad in enumerate(grads):
            param, mean, square, keep = (r[...] for r in params[4 * i : 4 * i + 4])
            mean_new = 0.9 * mean + 0.1 * grad
            square_new = 0.999 * square + 0.001 * grad * grad
            kept = keep.astype(f32)
            outs[i][...] = grad
            outs[4 + 2 * i][...] = mean_new * kept
            outs[5 + 2 * i][...] = square_new * kept
            if i < 2:
                fresh = param - 0.01 * (mean_new / first_fix) / (jnp.sqrt(square_new / second_fix) + 1e-08)
                if i == 0:
                    for k in range(3):
                        a_new[k] = fresh[:, k * rank : (k + 1) * rank].astype(bf16)
                else:
                    aff_new[...] = fresh.astype(bf16)

    block = jnp.where(j * cols < 3 * width, 0, jnp.where(j * cols < 4 * width, 1, 2))
    cut = params[8].shape[1]
    fresh = [fresh_ref[i] for i in range(fresh_ref.shape[0])]
    update = nn(a_new[block], jnp.concatenate([f[:, :cut] for f in fresh], axis=1))
    outs[12][...] = (w_ref[...].astype(f32) + adapter_scale * update).astype(bf16)
    update = nn(aff_new[...], jnp.concatenate([f[:, cut:] for f in fresh], axis=1))
    outs[13][...] = (wd_ref[...].astype(f32) + adapter_scale * update).astype(bf16)


def adam_fresh(param, grad, mean, square):
    mean_new = 0.9 * mean + 0.1 * grad
    square_new = 0.999 * square + 0.001 * grad * grad
    return param - 0.01 * (mean_new / first_fix) / (jnp.sqrt(square_new / second_fix) + 1e-08)


def body(
    dp_n,
    n,
    tokens,
    cotangent,
    domain_ids,
    domain_weight,
    frozen_input_weights,
    bias_in,
    frozen_down_weight,
    bias_ff,
    norm_gain,
    norm_shift,
    adapt_a,
    adapt_a_ff,
    adapt_b,
    adapt_b_ff,
    mean_a,
    mean_a_ff,
    mean_b,
    mean_b_ff,
    square_a,
    square_a_ff,
    square_b,
    square_b_ff,
    keep_a,
    keep_a_ff,
    keep_b,
    keep_b_ff,
):
    seqs, span, width = tokens.shape
    rows = seqs * span
    rank = adapt_b.shape[0]
    depth = width // HEADS
    cz = width // n
    length = n * span
    z = lax.axis_index("blk")
    z_arr = jnp.full((1,), z, jnp.int32)
    kr = frozen_input_weights.shape[0]
    down_rows, inner = frozen_down_weight.shape[0], frozen_down_weight.shape[0] * dp_n
    lanes = 128

    def shift_by(values, s):
        return lax.ppermute(values, "blk", [(i, (i + s) % n) for i in range(n)])

    b_cols = adapt_b.shape[1] + adapt_b_ff.shape[1]
    bias32 = bias_in.astype(f32)
    whole_front = dp_n == 8 and n == 4 and seqs > 1 and (rank, width, inner) == (128, 1024, 4096)
    if whole_front:
        vmem = pl.BlockSpec(memory_space=pltpu.VMEM)
        hbm = pl.BlockSpec(memory_space=pl.ANY)
        dma = pltpu.SemaphoreType.DMA
        half = ROTARY // 2
        freq = [rope_base ** (-(k * 2.0) / ROTARY) for k in range(half)]
        freq = np.tile(np.array(freq + freq + [0.0] * (depth - ROTARY), np.float32), lanes // depth)

        def shape(*dims, dtype=bf16):
            return jax.ShapeDtypeStruct(dims, dtype)

        (
            w_in, w_down, a_all, a_ff, b_in, b_ff, query, keys, values, first_pos, mid_pos, g_pos,
            grad_low, second, mid_up, mid_up_t, dmid_ff, dmid_ff_t, dmid_out_t, *tables, row_weight,
        ) = pl.pallas_call(
            functools.partial(front_kernel, n=n, depth=depth),
            in_specs=[hbm] * 3 + [vmem] * 6 + [pl.BlockSpec(memory_space=pltpu.SMEM)] + [vmem] * 4,
            out_specs=[hbm] * 12 + [vmem] * 11,
            out_shape=[
                shape(width, 8 * width), shape(inner, width), shape(width, 3 * rank), shape(inner, rank),
                shape(rank, 8 * width), shape(rank, width),
                shape(seqs, length, cz), shape(seqs, length, cz), shape(seqs, length, cz),
                shape(seqs, length, width), shape(seqs, length, rank), shape(seqs, length, cz),
                shape(rows, width), shape(rows, width),
                shape(rows, rank), shape(seqs, rank, span), shape(rows, rank), shape(seqs, rank, span),
                shape(seqs, rank, span),
                shape(length, lanes, dtype=f32), shape(length, lanes, dtype=f32), shape(length, lanes, dtype=f32),
                shape(rows, 1, dtype=f32),
            ],
            scratch_shapes=[
                pltpu.VMEM(adapt_a.shape, bf16),
                pltpu.VMEM(adapt_a_ff.shape, bf16),
                pltpu.VMEM(adapt_b.shape, bf16),
                pltpu.VMEM(adapt_b_ff.shape, bf16),
                pltpu.VMEM((n, seqs, span, width), bf16),
                pltpu.VMEM((seqs, length, cz), bf16),
                pltpu.VMEM((seqs, length, cz), bf16),
                pltpu.VMEM((seqs, length, cz), bf16),
                pltpu.VMEM((seqs, length, width), bf16),
                pltpu.VMEM((seqs, length, rank), bf16),
                pltpu.VMEM((n, seqs, span, cz), bf16),
                pltpu.VMEM((width, width), bf16),
                pltpu.VMEM((3, width, cz), bf16),
                pltpu.VMEM((width, 3 * rank), bf16),
                pltpu.VMEM((rank, 8 * width), bf16),
                pltpu.VMEM((rank, width), bf16),
                dma((7, 7)), dma((7, 7)), dma((7,)),
                dma((n,)), dma((n,)), dma((n,)), dma((n,)), dma((n,)), dma((n,)),
                dma((7,)), dma((5, n)), dma((2,)),
            ],
            compiler_params=pltpu.CompilerParams(
                collective_id=2, has_side_effects=True, vmem_limit_bytes=58 << 20
            ),
            name="front",
        )(
            tokens, frozen_input_weights, frozen_down_weight,
            adapt_a, adapt_a_ff, adapt_b, adapt_b_ff,
            cotangent, domain_ids, domain_weight, norm_gain, norm_shift, bias32.reshape(1, -1), freq.reshape(1, -1),
        )
    else:
        lookup = (domain_ids[..., None] == jnp.arange(DOMAINS, dtype=jnp.int32)).astype(f32)
        row_weight = jnp.sum(lookup * domain_weight, axis=-1).reshape(rows, 1)
        row_grad = cotangent.astype(f32).reshape(rows, width) * row_weight
        grad_low = row_grad.astype(bf16)
        b_shard = jnp.concatenate([adapt_b, adapt_b_ff], axis=1).astype(bf16)
        one = jnp.concatenate(
            [frozen_input_weights[:, : 4 * width], adapt_a.astype(bf16), b_shard.reshape(kr, -1)], axis=1
        )
        one = lax.all_gather(one, "dp", axis=0, tiled=True)
        two = lax.all_gather(frozen_input_weights[:, 4 * width :], "dp", axis=0, tiled=True)
        three = jnp.concatenate([frozen_down_weight, adapt_a_ff.astype(bf16)], axis=1)
        three = lax.all_gather(three, "dp", axis=0, tiled=True)
        a_at = 4 * width
        b_at = a_at + 3 * rank
        a_all = one[:, a_at:b_at]
        b_all = one[:, b_at:].reshape(dp_n, rank, b_cols)
        b_in = jnp.transpose(b_all[:, :, : adapt_b.shape[1]], (1, 0, 2)).reshape(rank, -1)
        b_ff = jnp.transpose(b_all[:, :, adapt_b.shape[1] :], (1, 0, 2)).reshape(rank, width)
        w_out = one[:, 3 * width : 4 * width]
        w_up = two
        w_down, a_ff = three[:, :width], three[:, width:]

        right, left = tokens, tokens
        rights, lefts = [None], [None]
        for s in range(1, n):
            right = lax.ppermute(right, "blk", [(i, i + 1) for i in range(n - 1)])
            left = lax.ppermute(left, "blk", [(i + 1, i) for i in range(n - 1)])
            rights.append(right)
            lefts.append(left)
        x_all = jnp.stack(
            [tokens] + [jnp.where(z >= s, rights[s], lefts[n - s]) for s in range(1, n)]
        )

        b_out = b_in[:, 3 * width : 4 * width]
        a_out = a_all[:, rank : 2 * rank]
        dmid_out = (adapter_scale * nt(grad_low, b_out)).astype(bf16)
        grad_att = (nt(grad_low, w_out) + nt(dmid_out, a_out)).astype(bf16)
        grad_att = jnp.transpose(grad_att.reshape(seqs, span, n, cz), (2, 0, 1, 3))

        def piece(values, s):
            return lax.dynamic_index_in_dim(values, lax.rem(z + s, n), 0, keepdims=False)

        g_all = jnp.stack(
            [piece(grad_att, 0)] + [shift_by(piece(grad_att, s), s) for s in range(1, n)]
        )

        tables = rope_lane_tables(length, depth, lanes)
        own = [lax.dynamic_slice_in_dim(b_in[:, t * width : (t + 1) * width], z * cz, cz, 1) for t in range(3)]
        b_own = jnp.concatenate(own, axis=1)
        bias_own = jnp.concatenate(
            [lax.dynamic_slice_in_dim(bias32, t * width + z * cz, cz, 0) for t in range(3)]
        ).reshape(1, 3 * cz)

        def block_of(s, z_ref):
            return lax.rem(z_ref[0] - s + n, n)

        table_spec = pl.BlockSpec((span, lanes), lambda s, q, z_ref: (block_of(s, z_ref), 0))
        head_spec = pl.BlockSpec((1, span, cz), lambda s, q, z_ref: (q, block_of(s, z_ref), 0))
        query, keys, values, first_all, mid_all = pl.pallas_call(
            qkv_kernel,
            grid_spec=pltpu.PrefetchScalarGridSpec(
                num_scalar_prefetch=1,
                grid=(n, seqs),
                in_specs=[
                    pl.BlockSpec((1, 1, span, width), lambda s, q, z_ref: (s, q, 0, 0)),
                    pl.BlockSpec((1, width), lambda s, q, z_ref: (0, 0)),
                    pl.BlockSpec((1, width), lambda s, q, z_ref: (0, 0)),
                    pl.BlockSpec((width, cz), lambda s, q, z_ref: (0, z_ref[0])),
                    pl.BlockSpec((width, cz), lambda s, q, z_ref: (0, n + z_ref[0])),
                    pl.BlockSpec((width, cz), lambda s, q, z_ref: (0, 2 * n + z_ref[0])),
                    pl.BlockSpec((width, rank), lambda s, q, z_ref: (0, a_at // rank)),
                    pl.BlockSpec((rank, 3 * cz), lambda s, q, z_ref: (0, 0)),
                    pl.BlockSpec((1, 3 * cz), lambda s, q, z_ref: (0, 0)),
                    table_spec,
                    table_spec,
                    table_spec,
                ],
                out_specs=[
                    head_spec,
                    head_spec,
                    head_spec,
                    pl.BlockSpec((1, 1, span, width), lambda s, q, z_ref: (block_of(s, z_ref), q, 0, 0)),
                    pl.BlockSpec((1, 1, span, rank), lambda s, q, z_ref: (block_of(s, z_ref), q, 0, 0)),
                ],
            ),
            out_shape=[jax.ShapeDtypeStruct((seqs, length, cz), bf16)] * 3
            + [
                jax.ShapeDtypeStruct((n, seqs, span, width), bf16),
                jax.ShapeDtypeStruct((n, seqs, span, rank), bf16),
            ],
            compiler_params=pltpu.CompilerParams(vmem_limit_bytes=48 << 20),
            cost_estimate=pl.CostEstimate(
                flops=2 * n * rows * width * 4 * cz, bytes_accessed=6 * n * rows * width, transcendentals=0
            ),
            name="qkv",
        )(
            z_arr, x_all, norm_gain[0:1], norm_shift[0:1], one, one, one, one, b_own, bias_own, *tables
        )

        input_rows = tokens.astype(f32).reshape(rows, width)
        centre = input_rows - jnp.mean(input_rows, axis=-1, keepdims=True)
        inv = lax.rsqrt(jnp.mean(centre * centre, axis=-1, keepdims=True) + norm_eps)
        second = (centre * inv * norm_gain[1] + norm_shift[1]).astype(bf16)
        a_up = a_all[:, 2 * rank :]
        mid_up = nn(second, a_up).astype(bf16)
        dmid_ff = (adapter_scale * nt(grad_low, b_ff)).astype(bf16)
        g_pos = jnp.concatenate([g_all, g_all])
        g_pos = lax.rev(g_pos, (0,))
        g_pos = lax.dynamic_slice_in_dim(g_pos, lax.rem(n - 1 - z + n, n), n, 0)
        g_pos = jnp.transpose(g_pos, (1, 0, 2, 3)).reshape(seqs, length, cz)

        first_pos = jnp.transpose(first_all, (1, 0, 2, 3))
        mid_pos = jnp.transpose(mid_all, (1, 0, 2, 3))
        w_in = jnp.concatenate([one[:, :a_at], two], axis=1)
        mid_up_t, dmid_ff_t, dmid_out_t = (
            jnp.transpose(v.reshape(seqs, span, rank), (0, 2, 1)) for v in (mid_up, dmid_ff, dmid_out)
        )

    pairs = cz // lanes
    steps = seqs * pairs
    inner_block = min(512, inner)
    def one_buffer(shape):
        zeros = (0,) * len(shape)
        return pl.BlockSpec(shape, lambda s: zeros, pipeline_mode=pl.Buffered(1))

    def seq_pair(s):
        s = jnp.minimum(s, steps - 1)
        return s // pairs, lax.rem(s, pairs)

    def head_map(s):
        seq, pair = seq_pair(s)
        return seq, 0, pair

    def inner_at(s):
        return jnp.maximum(s - steps, 0)

    head = pl.BlockSpec((1, length, lanes), head_map)
    early = whole_front
    dma = pltpu.SemaphoreType.DMA
    half_rank = rank // 2

    def wide(*dims, dtype=bf16):
        return jax.ShapeDtypeStruct(dims, dtype)

    in_specs = (
        [head] * 4
        + [one_buffer((length, lanes))] * 3
        + [one_buffer((rows, width))] * 2
        + [one_buffer((rows, rank)), one_buffer((seqs, rank, span))] * 2
        + [
            pl.BlockSpec((width, inner_block), lambda s: (0, 4 * width // inner_block + inner_at(s))),
            pl.BlockSpec((inner_block, width), lambda s: (inner_at(s), 0)),
            pl.BlockSpec((inner_block, rank), lambda s: (inner_at(s), 0)),
            one_buffer((rank, 8 * width))
            if early
            else pl.BlockSpec((rank, inner_block), lambda s: (0, 4 * width // inner_block + inner_at(s))),
            pl.BlockSpec((1, inner_block), lambda s: (0, 4 * width // inner_block + inner_at(s))),
        ]
    )
    operands = [
        query, keys, values, g_pos, *tables, second, grad_low, mid_up, mid_up_t, dmid_ff, dmid_ff_t,
        w_in, w_down, a_ff, b_in, bias32.reshape(1, -1),
    ]
    partial_specs = [one_buffer((rows, width))] * 2 + [one_buffer((rows, rank))] * 2
    partial_shapes = [wide(rows, width, dtype=f32)] * 2 + [wide(rows, rank)] * 2
    local_spec, local_shape = pl.BlockSpec(memory_space=pl.ANY), wide(seqs, 4, span, width)
    scratch = [
        pltpu.VMEM((steps, n, 4, span, lanes), bf16),
        pltpu.VMEM((length, lanes), f32),
        pltpu.VMEM((length, lanes), f32),
        pltpu.VMEM((rows, rank), f32),
        pltpu.VMEM((rows, rank), f32),
        dma((steps, n)),
        dma((steps, n)),
        dma((steps,)),
    ]
    if early:
        in_specs += [
            pl.BlockSpec((1, length, width), lambda s: (seq_pair(s)[0], 0, 0)),
            pl.BlockSpec((1, length, rank), lambda s: (seq_pair(s)[0], 0, 0)),
        ]
        operands += [first_pos, mid_pos]
        out_specs = [local_spec] + partial_specs + [one_buffer((rank, early_end))]
        out_shapes = [local_shape] + partial_shapes + [wide(rank, early_end)]
        cuts = len(early_cuts)
        scratch += [
            pltpu.VMEM((2, 2, 2, rank, early_end), bf16),
            pltpu.VMEM((length, rank), f32),
            pltpu.VMEM((3, pairs, rank, lanes), f32),
            pltpu.VMEM((rank, width), f32),
            pltpu.VMEM((2, 2, rank, early_end), bf16),
            pltpu.VMEM((2, half_rank, early_end), bf16),
            pltpu.VMEM((2, half_rank, early_end), bf16),
            pltpu.VMEM((half_rank, early_end), bf16),
            pltpu.VMEM((half_rank, early_end), bf16),
            dma((5,)), dma((5,)), dma((2, cuts)), dma((2, cuts)), dma((2, cuts)), dma((2, cuts)),
        ]
    else:
        out_specs = (
            [local_spec, pl.BlockSpec((1, 3, length, lanes), lambda s: (seq_pair(s)[0], 0, 0, seq_pair(s)[1]))]
            + partial_specs
            + [pl.BlockSpec((rank, inner_block), lambda s: (0, inner_at(s)))] * 2
        )
        out_shapes = (
            [local_shape, wide(seqs, 3, length, cz)] + partial_shapes + [wide(rank, inner, dtype=f32)] * 2
        )
    middle = pl.pallas_call(
        functools.partial(middle_kernel, n=n, pairs=pairs, steps=steps, depth=depth, early=early),
        grid=(steps + inner // inner_block,),
        in_specs=in_specs,
        out_specs=out_specs,
        out_shape=out_shapes,
        scratch_shapes=scratch,
        compiler_params=pltpu.CompilerParams(
            collective_id=0, has_side_effects=True, vmem_limit_bytes=60 << 20
        ),
        name="middle",
    )(*operands)

    if early:
        local, ff, grad_second, mid_ff, dmid_up, summed = middle
        part = rank // n

        def single(shape, *at):
            return pl.BlockSpec(shape, lambda s: at, pipeline_mode=pl.Buffered(1))

        wide_block = width // 2

        def of_out(s):
            return jnp.minimum(s, 1)

        def of_grad(s):
            return jnp.clip(s - 2, 0, 1)

        def of_seq(s):
            return jnp.maximum(s - 4, 0)

        def piece_spec(kind, at):
            return pl.BlockSpec((seqs, 1, span, wide_block), lambda s: (0, kind, 0, at(s)))

        def columns(kind, height):
            return pl.BlockSpec((height, wide_block), lambda s: (0, kind * 2 + of_grad(s)))

        full = pl.BlockSpec((1, span, width), lambda s: (of_seq(s), 0, 0))
        flat = pl.BlockSpec((span, width), lambda s: (of_seq(s), 0))
        cuts = len(early_cuts)
        b_here = [adapt_b, mean_b, square_b, adapt_b_ff, mean_b_ff, square_b_ff]
        mixed, grad_tokens, reduced, norm_sum, fresh = pl.pallas_call(
            functools.partial(tail_kernel, n=n),
            grid=(4 + seqs,),
            in_specs=[
                piece_spec(0, of_out), piece_spec(1, of_grad), piece_spec(2, of_grad), piece_spec(3, of_grad),
                pl.BlockSpec((wide_block, width), lambda s: (of_out(s), 3)),
                columns(0, width), columns(1, width), columns(2, width),
                pl.BlockSpec((wide_block, rank), lambda s: (of_out(s), 1)),
                single((width, rank), 0, 0),
                single((rank, width), 0, 3),
                columns(0, rank), columns(1, rank), columns(2, rank),
                single((1, width), 0, 3),
                full, full,
                single((rows, 1), 0, 0),
                flat,
                single((1, width), 0, 0),
                single((rows, rank), 0, 0),
                single((rank, width), 0, 0),
                flat,
                single((rows, rank), 0, 0),
                single((width, rank), 0, 2),
                single((2, width), 0, 0),
                single((seqs, rank, span), 0, 0, 0),
                single((rows, width), 0, 0),
                single((rank, early_end), 0, 0),
            ]
            + [single(v.shape, 0, 0) for v in b_here],
            out_specs=[
                full, full, pl.BlockSpec(memory_space=pl.ANY), single((4, width), 0, 0),
                pl.BlockSpec(memory_space=pl.ANY),
            ],
            out_shape=[
                wide(seqs, span, width), wide(seqs, span, width), wide(rank, 2048), wide(4, width, dtype=f32),
                wide(dp_n, rank, b_cols),
            ],
            scratch_shapes=[
                pltpu.VMEM((rank, 2048), bf16),
                pltpu.VMEM((dp_n, rank, b_cols), bf16),
                pltpu.VMEM((rows, width), f32),
                pltpu.VMEM((rows, rank), f32),
                pltpu.VMEM((rows, width), f32),
                pltpu.VMEM((rows, rank), f32),
                pltpu.VMEM((n, part, early_end), bf16),
                pltpu.VMEM((2, 2, 2, rank, lanes), bf16),
                pltpu.VMEM((rank, width), bf16),
                pltpu.VMEM((2, 2, rank, lanes), bf16),
                pltpu.VMEM((2, rank, lanes), bf16),
                pltpu.VMEM((rank, lanes), bf16),
                pltpu.VMEM((3, rank, width), bf16),
                pltpu.VMEM((rank, lanes), bf16),
                pltpu.VMEM((n, part, lanes), bf16),
                pltpu.VMEM((n, part, width), bf16),
                pltpu.VMEM((rank, width), bf16),
                pltpu.VMEM((2 + n, 4, width), f32),
                pltpu.VMEM((4, 4, width), f32),
                dma((n, cuts)), dma((n, cuts)), dma((n, cuts)), dma((n, cuts)),
                dma((2, 3)), dma((2, 3)), dma((2, n)), dma((2, n)), dma((2, n)), dma((2, n)),
                dma((2 + n,)), dma((2 + n,)), dma((7,)), dma((7,)), dma((2,)),
            ],
            compiler_params=pltpu.CompilerParams(
                collective_id=1, has_side_effects=True, vmem_limit_bytes=58 << 20
            ),
            name="tail",
        )(
            local, local, local, local, w_in, w_in, w_in, w_in, a_all, a_all, b_in, b_in, b_in, b_in,
            bias32.reshape(1, -1), tokens, cotangent, row_weight, ff, bias_ff.astype(f32).reshape(1, -1), mid_ff, b_ff,
            grad_second, dmid_up, a_all, norm_gain, dmid_out_t, grad_low, summed, *b_here,
        )
    else:
        local, own, ff, grad_second, mid_ff, dmid_up, grad_a_ff_t, grad_b_up = middle
        grad_b_up = adapter_scale * grad_b_up
        first_pos = first_pos.reshape(seqs * length, width)
        mid_pos = mid_pos.reshape(seqs * length, rank)
        b_own = jnp.concatenate(
            [lax.dynamic_slice_in_dim(b_in[:, t * width : (t + 1) * width], z * cz, cz, 1) for t in range(3)], axis=1
        )
        djoint_own = [own[:, t].reshape(seqs * length, cz) for t in range(3)]
        dmid_own = sum(nt(djoint_own[t], b_own[:, t * cz : (t + 1) * cz]) for t in range(3))
        dmid_own = (adapter_scale * dmid_own).astype(bf16)
        grad_a_qkv_t = tn(dmid_own, first_pos)
        mine = (jnp.arange(n, dtype=jnp.int32) == z)[None, :, None]
        grad_b_qkv = jnp.concatenate(
            [
                jnp.where(mine, adapter_scale * tn(mid_pos, part)[:, None, :], 0.0).reshape(rank, width)
                for part in djoint_own
            ],
            axis=1,
        )
        grad_a_up_t = tn(dmid_up, second)
        grad_b_ffp = adapter_scale * tn(mid_ff, grad_low)

        def fixed(shape, *at):
            return pl.BlockSpec(shape, lambda t: at, pipeline_mode=pl.Buffered(1))

        def column(at, height):
            return pl.BlockSpec((height, cz), lambda t: (0, at * n + t))

        mixed, grad_tokens, norm_part, grad_a_out_t, grad_b_out = pl.pallas_call(
            finish_kernel,
            grid=(n,),
            in_specs=[
                pl.BlockSpec((seqs, 4, span, cz), lambda t: (0, 0, 0, t)),
                pl.BlockSpec((cz, width), lambda t: (t, 3)),
                column(0, width), column(1, width), column(2, width),
                pl.BlockSpec((cz, rank), lambda t: (t, 1)),
                fixed((width, rank), 0, 0),
                fixed((rank, width), 0, 3),
                column(0, rank), column(1, rank), column(2, rank),
                fixed((1, width), 0, 3),
                fixed((seqs, span, width), 0, 0, 0),
                fixed((seqs, span, width), 0, 0, 0),
                fixed((rows, 1), 0, 0),
                fixed((rows, width), 0, 0),
                fixed((1, width), 0, 0),
                fixed((rows, rank), 0, 0),
                fixed((rank, width), 0, 0),
                fixed((rows, width), 0, 0),
                fixed((rows, rank), 0, 0),
                fixed((width, rank), 0, 2),
                fixed((2, width), 0, 0),
                fixed((seqs, rank, span), 0, 0, 0),
                fixed((rows, width), 0, 0),
            ],
            out_specs=[
                fixed((seqs, span, width), 0, 0, 0),
                fixed((seqs, span, width), 0, 0, 0),
                fixed((4, width), 0, 0),
                pl.BlockSpec((rank, cz), lambda t: (0, t)),
                fixed((rank, width), 0, 0),
            ],
            out_shape=[
                jax.ShapeDtypeStruct((seqs, span, width), bf16),
                jax.ShapeDtypeStruct((seqs, span, width), bf16),
                jax.ShapeDtypeStruct((4, width), f32),
                jax.ShapeDtypeStruct((rank, width), f32),
                jax.ShapeDtypeStruct((rank, width), f32),
            ],
            scratch_shapes=[
                pltpu.VMEM((rows, width), f32),
                pltpu.VMEM((rows, rank), f32),
                pltpu.VMEM((rows, width), f32),
                pltpu.VMEM((rows, rank), f32),
            ],
            compiler_params=pltpu.CompilerParams(vmem_limit_bytes=56 << 20),
            name="finish",
        )(
            local, w_in, w_in, w_in, w_in, a_all, a_all, b_in, b_in, b_in, b_in, bias32.reshape(1, -1),
            tokens, cotangent, row_weight, ff, bias_ff.astype(f32).reshape(1, -1), mid_ff, b_ff,
            grad_second, dmid_up, a_all, norm_gain, dmid_out_t, grad_low,
        )
        grad_b_out = adapter_scale * grad_b_out

        def by_owner(values):
            return values.reshape(rank, dp_n, -1)

        parts = [
            by_owner(grad_a_up_t), by_owner(grad_b_ffp), by_owner(grad_a_qkv_t), by_owner(grad_a_ff_t),
            by_owner(jnp.concatenate([grad_b_qkv, grad_b_out, grad_b_up], axis=1)), by_owner(grad_a_out_t),
        ]
        widths = [p.shape[2] for p in parts]
        owned = jnp.transpose(jnp.concatenate([p.astype(bf16) for p in parts], axis=2), (1, 0, 2))
        b_at = sum(widths[:4])
        reduced = lax.psum_scatter(owned.astype(f32), "dp", scatter_dimension=0, tiled=True)
        reduced = lax.psum(reduced[0], "blk").astype(bf16)
        norm_sum = lax.psum(norm_part, ("dp", "blk"))
        grads_b = reduced[:, b_at : b_at + adapt_b.shape[1]].astype(f32)
        grads_f = reduced[:, widths[0] : widths[0] + widths[1]].astype(f32)
        fresh = jnp.concatenate(
            [
                adam_fresh(adapt_b, grads_b, mean_b, square_b),
                adam_fresh(adapt_b_ff, grads_f, mean_b_ff, square_b_ff),
            ],
            axis=1,
        ).astype(bf16)
        fresh = lax.all_gather(fresh, "dp", axis=0, tiled=False)
    grad_gain, grad_shift = norm_sum[:2], norm_sum[2:]

    state = [
        adapt_a, mean_a, square_a, keep_a,
        adapt_a_ff, mean_a_ff, square_a_ff, keep_a_ff,
        adapt_b, mean_b, square_b, keep_b,
        adapt_b_ff, mean_b_ff, square_b_ff, keep_b_ff,
    ]

    def all_of(value):
        zeros = (0,) * value.ndim
        return pl.BlockSpec(value.shape, lambda j: zeros, pipeline_mode=pl.Buffered(1))

    four = [adapt_a, adapt_a_ff, adapt_b, adapt_b_ff]
    results = [v for v in four] + [v for v in four for _ in range(2)]
    b_w, f_w = adapt_b.shape[1], adapt_b_ff.shape[1]
    owners = max(1, lanes // f_w)
    w_spec = pl.BlockSpec((kr, owners * b_w), lambda j: (0, j))
    wd_spec = pl.BlockSpec((down_rows, owners * f_w), lambda j: (0, j))
    updated = pl.pallas_call(
        functools.partial(update_kernel, rank=rank, width=width),
        grid=(dp_n // owners,),
        in_specs=[all_of(reduced), pl.BlockSpec((owners, rank, b_cols), lambda j: (j, 0, 0)), w_spec, wd_spec]
        + [all_of(v) for v in state],
        out_specs=[all_of(v) for v in results] + [w_spec, wd_spec],
        out_shape=[jax.ShapeDtypeStruct(v.shape, f32) for v in results]
        + [
            jax.ShapeDtypeStruct(frozen_input_weights.shape, bf16),
            jax.ShapeDtypeStruct(frozen_down_weight.shape, bf16),
        ],
        scratch_shapes=[pltpu.VMEM((3, kr, rank), bf16), pltpu.VMEM((down_rows, rank), bf16)],
        compiler_params=pltpu.CompilerParams(vmem_limit_bytes=48 << 20),
        name="update",
    )(reduced, fresh, frozen_input_weights, frozen_down_weight, *state)
    grad_a, grad_a_ff, grad_b, grad_b_ff = updated[:4]
    new_mean_a, new_square_a, new_mean_a_ff, new_square_a_ff = updated[4:8]
    new_mean_b, new_square_b, new_mean_b_ff, new_square_b_ff = updated[8:12]
    folded_input_weights, folded_down_weight = updated[12:]
    return (
        mixed,
        grad_tokens,
        grad_gain,
        grad_shift,
        grad_a,
        grad_a_ff,
        grad_b,
        grad_b_ff,
        new_mean_a,
        new_square_a,
        new_mean_a_ff,
        new_square_a_ff,
        new_mean_b,
        new_square_b,
        new_mean_b_ff,
        new_square_b_ff,
        folded_input_weights,
        folded_down_weight,
    )


def solution(mesh):
    in_specs = (
        P("dp", "blk", None),
        P("dp", "blk", None),
        P("dp", "blk"),
        P(),
        P("dp", None),
        P(),
        P("dp", None),
        P(),
        P(),
        P(),
        P("dp", None),
        P("dp", None),
        P(None, "dp"),
        P(None, "dp"),
        P("dp", None),
        P("dp", None),
        P(None, "dp"),
        P(None, "dp"),
        P("dp", None),
        P("dp", None),
        P(None, "dp"),
        P(None, "dp"),
        P("dp", None),
        P("dp", None),
        P(None, "dp"),
        P(None, "dp"),
    )
    out_specs = (
        P("dp", "blk", None),
        P("dp", "blk", None),
        P(),
        P(),
        P("dp", None),
        P("dp", None),
        P(None, "dp"),
        P(None, "dp"),
        P("dp", None),
        P("dp", None),
        P("dp", None),
        P("dp", None),
        P(None, "dp"),
        P(None, "dp"),
        P(None, "dp"),
        P(None, "dp"),
        P("dp", None),
        P("dp", None),
    )
    return jax.shard_map(
        functools.partial(body, mesh.shape["dp"], mesh.shape["blk"]), mesh=mesh, in_specs=in_specs, out_specs=out_specs, check_vma=False)
```

```python
import functools
import math

import jax
import jax.numpy as jnp
import numpy as np
from jax import lax
from jax.experimental import pallas as pl
from jax.experimental.pallas import tpu as pltpu
from jax.sharding import PartitionSpec as P

HEADS = 16
ROTARY = 16
DOMAINS = 22

adapter_scale = 0.25
rope_base = 10000.0
norm_eps = 1e-05
masked_score = -1e30
first_fix = 1.0 - (0.9**10) ** 10
second_fix = 1.0 - (0.999**10) ** 10

f32 = jnp.float32
bf16 = jnp.bfloat16


def nn(left, right):
    return lax.dot_general(left, right, (((1,), (0,)), ((), ())), preferred_element_type=f32)


def nt(left, right):
    return lax.dot_general(left, right, (((1,), (1,)), ((), ())), preferred_element_type=f32)


def tn(left, right):
    return lax.dot_general(left, right, (((0,), (0,)), ((), ())), preferred_element_type=f32)


def rope_lane_tables(length, depth, lanes):
    half = ROTARY // 2
    freqs = rope_base ** (-(jnp.arange(half, dtype=f32) * 2.0) / ROTARY)
    angles = jnp.arange(length, dtype=f32)[:, None] * freqs[None, :]
    cosine, sine = jnp.cos(angles), jnp.sin(angles)
    rest = depth - ROTARY
    ones, zero_half = jnp.ones((length, rest), f32), jnp.zeros((length, half), f32)
    zero_rest = jnp.zeros((length, rest), f32)
    keep = jnp.concatenate([cosine, cosine, ones], axis=1)
    from_above = jnp.concatenate([-sine, zero_half, zero_rest], axis=1)
    from_below = jnp.concatenate([zero_half, sine, zero_rest], axis=1)
    times = lanes // depth
    return tuple(jnp.tile(table, (1, times)) for table in (keep, from_above, from_below))


def turn(values, keep, above, below, sign):
    lanes = values.shape[-1]
    half = ROTARY // 2
    up = pltpu.roll(values, lanes - half, 1)
    down = pltpu.roll(values, half, 1)
    return values * keep + sign * (up * above + down * below)


def qkv_kernel(
    z_ref, x_ref, gain_ref, shift_ref, wq_ref, wk_ref, wv_ref, a_ref, b_ref, bias_ref,
    keep_ref, above_ref, below_ref, q_ref, k_ref, v_ref, first_ref, mid_ref,
):
    cols = wq_ref.shape[1]
    x = x_ref[...].reshape(x_ref.shape[2:]).astype(f32)
    centre = x - jnp.mean(x, axis=-1, keepdims=True)
    spread = jnp.mean(centre * centre, axis=-1, keepdims=True)
    first = (centre * lax.rsqrt(spread + norm_eps) * gain_ref[...] + shift_ref[...]).astype(bf16)
    mid = nn(first, a_ref[...]).astype(bf16)
    first_ref[...] = first.reshape(first_ref.shape)
    mid_ref[...] = mid.reshape(mid_ref.shape)
    low = adapter_scale * nn(mid, b_ref[...]) + bias_ref[...]
    lanes = keep_ref.shape[1]
    tables = keep_ref[...], above_ref[...], below_ref[...]
    query = nn(first, wq_ref[...]) + low[:, :cols]
    keys = nn(first, wk_ref[...]) + low[:, cols : 2 * cols]
    values = nn(first, wv_ref[...]) + low[:, 2 * cols :]
    for at in range(0, cols, lanes):
        part = slice(at, at + lanes)
        q_ref[0, :, part] = turn(query[:, part], *tables, 1.0).astype(bf16)
        k_ref[0, :, part] = turn(keys[:, part], *tables, 1.0).astype(bf16)
    v_ref[0] = values.astype(bf16)


MESH = pl.DeviceIdType.MESH


def attend_pair(query, keys, values, grad, tables, dk_ref, dv_ref, depth, blocks, store):
    lanes = keys.shape[1]
    span = keys.shape[0] // blocks
    scale = 1.0 / math.sqrt(depth)
    lane = lax.broadcasted_iota(jnp.int32, (1, lanes), 1)
    heads = lanes // depth
    masks = [jnp.where(lane // depth == h, 1.0, 0.0).astype(bf16) for h in range(heads)]
    scaled = [jnp.where(lane // depth == h, scale, 0.0).astype(bf16) for h in range(heads)]
    diagonal = lax.broadcasted_iota(jnp.int32, (span, span), 0) <= lax.broadcasted_iota(
        jnp.int32, (span, span), 1
    )
    keys_t, values_t = keys.T, values.T
    for i in range(blocks):
        done, end = i * span, (i + 1) * span
        rows = slice(done, end)
        q_i, g_i = query[rows], grad[rows]
        g_t = g_i.T
        outs, grads, lows, grads_s, q_parts, g_parts = [], [], [], [], [], []
        for h in range(heads):
            part = slice(h * depth, (h + 1) * depth)
            q_h, g_h = q_i * scaled[h], g_i * masks[h]
            last = jnp.where(diagonal, nt(keys[rows], q_h), masked_score)
            top = jnp.max(last, axis=0, keepdims=True)
            if i:
                scores = nt(keys[:done], q_h)
                top = jnp.maximum(top, jnp.max(scores, axis=0, keepdims=True))
            weights = jnp.exp(last - top)
            total = jnp.sum(weights, axis=0, keepdims=True)
            if i:
                before = jnp.exp(scores - top)
                total += jnp.sum(before, axis=0, keepdims=True)
                weights = jnp.concatenate([before, weights], axis=0)
            weights = weights * (1.0 / total)
            low = weights.astype(bf16)
            out_t = nn(values_t[part, :end], low)
            grad_p = nt(values[:end], g_h)
            delta = jnp.sum(out_t * g_t[part].astype(f32), axis=0, keepdims=True)
            grad_s = (weights * (grad_p - delta)).astype(bf16)
            outs.append(out_t)
            grads.append(nn(keys_t[part, :end], grad_s))
            lows.append(low)
            grads_s.append(grad_s)
            q_parts.append(q_h)
            g_parts.append(g_h)
        dk = nn(jnp.concatenate(grads_s, axis=1), jnp.concatenate(q_parts, axis=0))
        dv = nn(jnp.concatenate(lows, axis=1), jnp.concatenate(g_parts, axis=0))
        if i:
            dk_ref[:done] += dk[:done]
            dv_ref[:done] += dv[:done]
        dk_ref[rows] = dk[done:]
        dv_ref[rows] = dv[done:]
        store(i, 0, jnp.concatenate(outs, axis=0).T.astype(bf16))
        dq = jnp.concatenate(grads, axis=0).T * scale
        store(i, 1, turn(dq, *[t[rows] for t in tables], -1.0).astype(bf16))
    for i in range(blocks):
        rows = slice(i * span, (i + 1) * span)
        store(i, 2, turn(dk_ref[rows], *[t[rows] for t in tables], -1.0).astype(bf16))
        store(i, 3, dv_ref[rows].astype(bf16))


def normal(x):
    centre = x - jnp.mean(x, axis=-1, keepdims=True)
    return centre * lax.rsqrt(jnp.mean(centre * centre, axis=-1, keepdims=True) + norm_eps)


def front_kernel(
    tokens_ref, win_ref, wdown_ref, a_wide, aff_wide, b_wide, bff_wide,
    cot_ref, ids_ref, domain_ref, gain_ref, shift_ref, bias_ref, freq_ref,
    win_out, wdown_out, a_out, aff_out, b_out, bff_out,
    q_out, k_out, v_out, first_out, mid_out, g_out,
    low_ref, second_ref, mid_up_ref, mid_up_t_ref, dmid_ff_ref, dmid_ff_t_ref, dmid_out_t_ref,
    keep_ref, above_ref, below_ref, weight_ref,
    a_ref, aff_ref, b_ref, bff_ref, x_all, q_s, k_s, v_s, first_s, mid_s, ga, wout_v, wqkv_v, a_v, b_v, bff_v,
    sx, qx, own_sem, sr, qr, sl, ql, sd, qd, load_sem, store_sem, token_sem,
    *, n, depth,
):
    z = lax.axis_index("blk")
    dp = lax.axis_index("dp")
    y, x, c = dp // 4, lax.rem(dp // 2, 2), lax.rem(dp, 2)
    core = (dp + 1 - 2 * c, z)
    along_x = (dp + 2 - 4 * x, z)
    along_y = (dp + 4 - 8 * y, z)
    peers = [(dp, lax.rem(z + t, n)) for t in range(1, n)]
    seqs, span, width = tokens_ref.shape
    kr, down_rows, rank = win_ref.shape[0], wdown_ref.shape[0], b_ref.shape[0]
    b_w, f_w = b_ref.shape[1], bff_ref.shape[1]
    cz = q_s.shape[2]
    lanes = keep_ref.shape[1]
    four = 4 * width

    barrier = pltpu.get_barrier_semaphore()
    for peer in [core, along_x, along_y] + peers:
        pl.semaphore_signal(barrier, inc=1, device_id=peer, device_id_type=MESH)
    pl.semaphore_wait(barrier, 2 + n)

    def remote(src, dst, send, recv, peer):
        return pltpu.make_async_remote_copy(
            src_ref=src, dst_ref=dst, send_sem=send, recv_sem=recv, device_id=peer, device_id_type=MESH
        )

    shards = [
        (win_ref.at[:, :four], lambda d: win_out.at[pl.ds(pl.multiple_of(d * kr, kr), kr), :four]),
        (a_ref, lambda d: a_out.at[pl.ds(pl.multiple_of(d * kr, kr), kr), :]),
        (b_ref, lambda d: b_out.at[:, pl.ds(pl.multiple_of(d * b_w, b_w), b_w)]),
        (bff_ref, lambda d: bff_out.at[:, pl.ds(pl.multiple_of(d * f_w, f_w), f_w)]),
        (win_ref.at[:, four:], lambda d: win_out.at[pl.ds(pl.multiple_of(d * kr, kr), kr), four:]),
        (wdown_ref, lambda d: wdown_out.at[pl.ds(pl.multiple_of(d * down_rows, down_rows), down_rows), :]),
        (aff_ref, lambda d: aff_out.at[pl.ds(pl.multiple_of(d * down_rows, down_rows), down_rows), :]),
    ]
    groups = [(0, 1, 2, 3), (4,), (5, 6)]
    from_x, from_y = dp + 2 - 4 * x, dp + 4 - 8 * y
    across = dp + 2 - 4 * x + 4 - 8 * y
    onward = jnp.where(c == 0, from_y, from_x)
    target = (jnp.where(c == 0, along_x[0], along_y[0]), z)

    def hop(i, kind):
        shard, there = shards[i]
        src, dst, peer = {
            0: (shard, there(dp), along_x),
            1: (shard, there(dp), along_y),
            2: (shard, there(dp), core),
            3: (there(onward), there(onward), target),
            4: (there(from_x), there(from_x), core),
            5: (there(from_y), there(from_y), core),
            6: (there(across), there(across), core),
        }[kind]
        return remote(src, dst, sx.at[i, kind], qx.at[i, kind], peer)

    def own_copy(i):
        return pltpu.make_async_copy(shards[i][0], shards[i][1](dp), own_sem.at[i])

    def start_own(group):
        for kind in (0, 1, 2):
            for i in groups[group]:
                hop(i, kind).start()
        for i in groups[group]:
            own_copy(i).start()

    def pass_on(group):
        for i in groups[group]:
            hop(i, 0).wait_recv()
            hop(i, 1).wait_recv()
        for kind in (3, 4, 5):
            for i in groups[group]:
                hop(i, kind).start()

    def close(group):
        for i in groups[group]:
            hop(i, 3).wait_recv()
            hop(i, 6).start()

    def arrived(group):
        for i in groups[group]:
            own_copy(i).wait()
            for kind in (2, 4, 5, 6):
                hop(i, kind).wait_recv()

    def rightward(s):
        return remote(x_all.at[z - s + 1], x_all.at[z - s + 1], sr.at[s], qr.at[s], (dp, z + 1))

    def leftward(s):
        return remote(x_all.at[z + s - 1], x_all.at[z + s - 1], sl.at[s], ql.at[s], (dp, z - 1))

    def from_left(s):
        return remote(x_all.at[z - s], x_all.at[z - s], sr.at[s], qr.at[s], (dp, z - 1))

    def from_right(s):
        return remote(x_all.at[z + s], x_all.at[z + s], sl.at[s], ql.at[s], (dp, z + 1))

    def ring_start(s):
        pl.when((z < n - 1) & (z - s + 1 >= 0))(lambda: rightward(s).start())
        pl.when((z > 0) & (z + s - 1 < n))(lambda: leftward(s).start())

    def ring_wait(s):
        pl.when(z - s >= 0)(lambda: from_left(s).wait_recv())
        pl.when(z + s < n)(lambda: from_right(s).wait_recv())

    def ring_end(s):
        pl.when((z < n - 1) & (z - s + 1 >= 0))(lambda: rightward(s).wait_send())
        pl.when((z > 0) & (z + s - 1 < n))(lambda: leftward(s).wait_send())

    for low, values in ((a_ref, a_wide), (aff_ref, aff_wide), (b_ref, b_wide), (bff_ref, bff_wide)):
        low[...] = values[...].astype(bf16)
    token_copy = pltpu.make_async_copy(tokens_ref, x_all.at[z], token_sem.at[0])
    token_copy.start()
    start_own(0)
    token_copy.wait()
    ring_start(1)

    unit_lane = lax.rem(lax.broadcasted_iota(jnp.int32, (1, lanes), 1), depth)
    half = ROTARY // 2
    for b in range(n):
        rows = slice(b * span, (b + 1) * span)
        place = (lax.broadcasted_iota(jnp.int32, (span, lanes), 0) + b * span).astype(f32)
        angle = place * freq_ref[...]
        cosine, sine = jnp.cos(angle), jnp.sin(angle)
        keep_ref[rows] = jnp.where(unit_lane < ROTARY, cosine, 1.0)
        above_ref[rows] = jnp.where(unit_lane < half, -sine, 0.0)
        below_ref[rows] = jnp.where((unit_lane >= half) & (unit_lane < ROTARY), sine, 0.0)
    for q in range(seqs):
        part = slice(q * span, (q + 1) * span)
        ids = ids_ref[q : q + 1, :]
        found = jnp.zeros((1, span), f32)
        for k in range(DOMAINS):
            found = jnp.where(ids == k, domain_ref[k], found)
        weight = jnp.broadcast_to(found, (8, span)).T[:, :1]
        weight_ref[part] = weight
        low_ref[part] = (cot_ref[q].astype(f32) * weight).astype(bf16)
        unit = normal(x_all[z, q].astype(f32))
        second_ref[part] = (unit * gain_ref[1:2] + shift_ref[1:2]).astype(bf16)

    pass_on(0)
    start_own(1)
    ring_wait(1)
    if n > 2:
        ring_start(2)
    close(0)
    arrived(0)

    loads = [
        pltpu.make_async_copy(win_out.at[:, 3 * width : four], wout_v, load_sem.at[0]),
        pltpu.make_async_copy(a_out, a_v, load_sem.at[1]),
        pltpu.make_async_copy(b_out, b_v, load_sem.at[2]),
        pltpu.make_async_copy(bff_out, bff_v, load_sem.at[3]),
    ] + [
        pltpu.make_async_copy(
            win_out.at[:, pl.ds(pl.multiple_of(t * width + z * cz, cz), cz)], wqkv_v.at[t], load_sem.at[4 + t]
        )
        for t in range(3)
    ]
    for copy in loads:
        copy.start()
    for copy in loads:
        copy.wait()

    def grad_out(q, _):
        part = pl.ds(pl.multiple_of(q * span, span), span)
        low = low_ref[part, :]
        dmid = (adapter_scale * nt(low, b_v[:, 3 * width : four])).astype(bf16)
        dmid_out_t_ref[q] = dmid.T
        for g in range(n):
            rows = slice(g * cz, (g + 1) * cz)
            value = nt(low, wout_v[rows]) + nt(dmid, a_v[rows, rank : 2 * rank])
            ga[g, q] = value.astype(bf16)
        return 0

    lax.fori_loop(0, seqs, grad_out, 0)
    place_own = pl.ds(pl.multiple_of(z * span, span), span)

    def grad_send(t):
        return remote(ga.at[lax.rem(z + t, n)], g_out.at[:, place_own, :], sd.at[t], qd.at[t], peers[t - 1])

    grad_own = pltpu.make_async_copy(ga.at[z], g_out.at[:, place_own, :], token_sem.at[1])
    grad_own.start()
    for t in range(1, n):
        grad_send(t).start()

    def stores(b):
        rows = pl.ds(pl.multiple_of(b * span, span), span)
        return [
            pltpu.make_async_copy(src.at[:, rows, :], dst.at[:, rows, :], store_sem.at[i, b])
            for i, (src, dst) in enumerate(
                ((q_s, q_out), (k_s, k_out), (v_s, v_out), (first_s, first_out), (mid_s, mid_out))
            )
        ]

    def project_block(b):
        rows = pl.ds(pl.multiple_of(b * span, span), span)

        def one(q, _):
            first = (normal(x_all[b, q].astype(f32)) * gain_ref[0:1] + shift_ref[0:1]).astype(bf16)
            mid = nn(first, a_v[:, 0:rank]).astype(bf16)
            first_s[q, rows, :] = first
            mid_s[q, rows, :] = mid
            for t, kept in enumerate((q_s, k_s, v_s)):
                at = pl.ds(pl.multiple_of(t * width + z * cz, cz), cz)
                value = nn(first, wqkv_v[t]) + adapter_scale * nn(mid, b_v[:, at]) + bias_ref[:, at]
                if t < 2:
                    value = jnp.concatenate(
                        [
                            turn(value[:, i : i + lanes], keep_ref[rows, :], above_ref[rows, :], below_ref[rows, :], 1.0)
                            for i in range(0, cz, lanes)
                        ],
                        axis=1,
                    )
                kept[q, rows, :] = value.astype(bf16)
            return 0

        lax.fori_loop(0, seqs, one, 0)
        for copy in stores(b):
            copy.start()

    def project_near(s):
        def side(i, _):
            b = z + s * (2 * i - 1)
            pl.when((b >= 0) & (b < n) & ((s > 0) | (i == 0)))(lambda: project_block(b))
            return 0

        lax.fori_loop(0, 2, side, 0)

    def local_products(q, _):
        part = pl.ds(pl.multiple_of(q * span, span), span)
        mid = nn(second_ref[part, :], a_v[:, 2 * rank : 3 * rank]).astype(bf16)
        mid_up_ref[part, :] = mid
        mid_up_t_ref[q] = mid.T
        dmid = (adapter_scale * nt(low_ref[part, :], bff_v[...])).astype(bf16)
        dmid_ff_ref[part, :] = dmid
        dmid_ff_t_ref[q] = dmid.T
        return 0

    def walk(s, _):
        @pl.when(s == 1)
        def _():
            pass_on(1)
            start_own(2)

        @pl.when((s > 1) & (s < n))
        def _():
            ring_wait(s)
            pl.when(s + 1 < n)(lambda: ring_start(s + 1))

        project_near(s - 1)

        @pl.when(s == 2)
        def _():
            close(1)
            lax.fori_loop(0, seqs, local_products, 0)
            pass_on(2)

        return 0

    lax.fori_loop(1, n + 1, walk, 0)
    close(2)
    arrived(1)
    arrived(2)
    for i in range(len(shards)):
        for kind in range(7):
            hop(i, kind).wait_send()
    for s in range(1, n):
        ring_end(s)
    grad_own.wait()
    for t in range(1, n):
        grad_send(t).wait()
    for b in range(n):
        for copy in stores(b):
            copy.wait()


def remote(src, dst, send, recv, peer):
    return pltpu.make_async_remote_copy(
        src_ref=src, dst_ref=dst, send_sem=send, recv_sem=recv, device_id=peer, device_id_type=MESH
    )


def add_low(a, b):
    return (a.astype(f32) + b.astype(f32)).astype(bf16)


def plane():
    dp, z = lax.axis_index("dp"), lax.axis_index("blk")
    y, x, c = dp // 4, lax.rem(dp // 2, 2), lax.rem(dp, 2)
    return dp, z, y, x, c, (dp + 1 - 2 * c, z), (dp + 2 - 4 * x, z), (dp + 4 - 8 * y, z)


def greet(peers):
    barrier = pltpu.get_barrier_semaphore()
    for peer in peers:
        pl.semaphore_signal(barrier, inc=1, device_id=peer, device_id_type=MESH)
    pl.semaphore_wait(barrier, len(peers))


early_cuts = ((0, 512), (512, 1024), (1024, 1536), (1536, 2048))
late_end, a_out_at, a_ff_at, b_at_col, early_end = 256, 384, 512, 1024, 2048


class PlaneSum:
    def __init__(self, e, r1, r2a, r2b, r3a, r3b, s1, q1, s2, q2, s3, q3):
        self.refs = e, r1, r2a, r2b, r3a, r3b
        self.sems = s1, q1, s2, q2, s3, q3
        self.at = plane()
        self.half = e.shape[3] // 2

    def first(self, m):
        e, r1 = self.refs[:2]
        c, core = self.at[4], self.at[5]
        s1, q1 = self.sems[:2]
        if m < 4:
            cut = slice(late_end, early_end)
            return remote(e.at[m // 2, m % 2, 1 - c, :, cut], r1.at[m // 2, m % 2, :, cut], s1.at[m], q1.at[m], core)
        cut = slice(0, late_end)
        return remote(e.at[:, :, 1 - c, :, cut], r1.at[:, :, :, cut], s1.at[m], q1.at[m], core)

    def take_first(self, m):
        e, r1 = self.refs[:2]
        c = self.at[4]
        self.first(m).wait()
        for i in (m,) if m < 4 else range(4):
            yy, xx = i // 2, i % 2
            cut = slice(late_end, early_end) if m < 4 else slice(0, late_end)
            e[yy, xx, c, :, cut] = add_low(e[yy, xx, c, :, cut], r1[yy, xx, :, cut])

    def finish(self, out):
        e, r1, r2a, r2b, r3a, r3b = self.refs
        dp, z, y, x, c, core, along_x, along_y = self.at
        s1, q1, s2, q2, s3, q3 = self.sems
        half = self.half

        def second(k):
            cut = slice(*early_cuts[k])
            return [
                remote(e.at[:, 1 - x, c, 0:half, cut], r2a.at[:, :, cut], s2.at[0, k], q2.at[0, k], along_x),
                remote(e.at[1 - y, :, c, half:, cut], r2b.at[:, :, cut], s2.at[1, k], q2.at[1, k], along_y),
            ]

        def third(k):
            cut = slice(*early_cuts[k])
            return [
                remote(e.at[1 - y, x, c, 0:half, cut], r3a.at[:, cut], s3.at[0, k], q3.at[0, k], along_y),
                remote(e.at[y, 1 - x, c, half:, cut], r3b.at[:, cut], s3.at[1, k], q3.at[1, k], along_x),
            ]

        def after_second(k):
            cut = slice(*early_cuts[k])
            for copy in second(k):
                copy.wait()
            for i in range(2):
                e[i, x, c, 0:half, cut] = add_low(e[i, x, c, 0:half, cut], r2a[i, :, cut])
                e[y, i, c, half:, cut] = add_low(e[y, i, c, half:, cut], r2b[i, :, cut])
            for copy in third(k):
                copy.start()

        def after_third(k):
            cut = slice(*early_cuts[k])
            for copy in third(k):
                copy.wait()
            out[0:half, cut] = add_low(e[y, x, c, 0:half, cut], r3a[:, cut])
            out[half:, cut] = add_low(e[y, x, c, half:, cut], r3b[:, cut])

        count = len(early_cuts)
        for k in range(count):
            for copy in second(k):
                copy.start()
        for k in range(count + 1):
            if k < count:
                after_second(k)
            if k:
                after_third(k - 1)


def middle_kernel(
    q_ref, k_ref, v_ref, g_ref, keep_ref, above_ref, below_ref,
    second_ref, low_ref, mid_ref, mid_t_ref, dmid_ref, dmid_t_ref,
    up_ref, down_ref, a_ref, b_ref, bias_ref, *refs,
    n, pairs, steps, depth, early,
):
    if early:
        first_ref, mid_qkv_ref, a_out_ref, dmid_out_t_ref = refs[:4]
        refs = refs[4:]
        local_ref, ff_ref, back_ref, mid_ff_ref, dmid_up_ref, sum_ref = refs[:6]
        buffer, dk_ref, dv_ref, mid_acc, dmid_acc, send_sem, recv_sem, own_sem = refs[6:14]
        e_ref, dmid_seq, gb_acc, ga_acc, o_here, load_sem = refs[14:20]
        plane_refs = refs[20:]
    else:
        local_ref, own_ref, ff_ref, back_ref, mid_ff_ref, dmid_up_ref, ga_ref, gb_ref = refs[:8]
        buffer, dk_ref, dv_ref, mid_acc, dmid_acc, send_sem, recv_sem, own_sem = refs[8:]
    step = pl.program_id(0)
    z = lax.axis_index("blk")
    dp = lax.axis_index("dp")
    lanes = q_ref.shape[2]
    length = q_ref.shape[1]
    inner_block = up_ref.shape[1]
    width = up_ref.shape[0]
    cz = pairs * lanes
    if early:
        plane_sum = PlaneSum(e_ref, *plane_refs)

    def copies(kind, s):
        seq, pair = s // pairs, lax.rem(s, pairs)
        what = slice(1, 4) if kind else slice(0, 1)
        at = pl.ds(pl.multiple_of((z * pairs + pair) * lanes, lanes), lanes)
        target = local_ref.at[seq, what, :, at]
        own = pltpu.make_async_copy(buffer.at[s, z, what], target, own_sem.at[kind, s])
        away = []
        for t in range(1, n):
            peer = lax.rem(z + t, n)
            away.append(
                remote(
                    buffer.at[s, peer, what], target, send_sem.at[kind, s, t], recv_sem.at[kind, s, t], (dp, peer)
                )
            )
        return [own] + away

    def send(kind, s):
        for copy in copies(kind, s):
            copy.start()

    def receive(kind):
        for s in range(steps):
            for copy in copies(kind, s):
                copy.wait()

    @pl.when(step == 0)
    def _():
        peers = [(dp, lax.rem(z + t, n)) for t in range(1, n)]
        greet((list(plane()[5:]) if early else []) + peers)

    @pl.when(step < steps)
    def _():
        def store(i, kind, value):
            buffer[step, i, kind] = value
            if kind and not early:
                own_ref[0, kind - 1, i * value.shape[0] : (i + 1) * value.shape[0], :] = value

        tables = keep_ref[...], above_ref[...], below_ref[...]
        attend_pair(q_ref[0], k_ref[0], v_ref[0], g_ref[0], tables, dk_ref, dv_ref, depth, n, store)
        send(0, step)
        pl.when(step == 0)(lambda: send(1, 0))
        pl.when(step == steps - 2)(lambda: send(1, 1))
        if early:
            seq, pair = step // pairs, lax.rem(step, pairs)
            mid_t = mid_qkv_ref[0].T
            dmid = jnp.zeros((length, lanes), f32)
            for t in range(3):
                grad = buffer[step, :, t + 1].reshape(length, lanes)
                at = pl.ds(pl.multiple_of(t * width + z * cz + pair * lanes, lanes), lanes)
                dmid += nt(grad, b_ref[:, at])
                product = nn(mid_t, grad)
                gb_acc[t, pair] = jnp.where(seq == 0, product, gb_acc[t, pair] + product)
            dmid = jnp.where(pair == 0, dmid, dmid_seq[...] + dmid)
            dmid_seq[...] = dmid

            @pl.when(pair == pairs - 1)
            def _():
                product = nn((adapter_scale * dmid_seq[...]).astype(bf16).T, first_ref[0])
                ga_acc[...] = jnp.where(seq == 0, product, ga_acc[...] + product)

    @pl.when(step == steps)
    def _():
        for s in range(2, steps):
            send(1, s)
        ff_ref[...] = jnp.zeros_like(ff_ref)
        back_ref[...] = jnp.zeros_like(back_ref)
        mid_acc[...] = jnp.zeros_like(mid_acc)
        dmid_acc[...] = jnp.zeros_like(dmid_acc)
        if early:
            for owner in range(8):
                place = (owner // 4, owner // 2 % 2, owner % 2)
                e_ref[place + (slice(None), slice(late_end, a_out_at))] = ga_acc[
                    :, owner * lanes : (owner + 1) * lanes
                ].astype(bf16)
                if owner < 3:
                    e_ref[place + (slice(None), slice(b_at_col, early_end))] = jnp.zeros((lanes, 1024), bf16)
            for t in range(3):
                for pair in range(pairs):
                    at = pl.ds(pl.multiple_of(b_at_col + z * cz + pair * lanes, lanes), lanes)
                    e_ref[0, t // 2, t % 2, :, at] = (adapter_scale * gb_acc[t, pair]).astype(bf16)

    @pl.when(step >= steps)
    def _():
        count, size = mid_t_ref.shape[0], mid_t_ref.shape[2]
        j = step - steps
        if early:
            up_b = b_ref[:, pl.ds(pl.multiple_of(4 * width + j * inner_block, inner_block), inner_block)]
        else:
            up_b = b_ref[...]
        ga, gb = None, None
        for at in range(count):
            rows = slice(at * size, (at + 1) * size)
            pre = nn(second_ref[rows], up_ref[...]) + bias_ref[...] + adapter_scale * nn(mid_ref[rows], up_b)
            cdf = 0.5 + 0.5 * lax.erf(pre * (1.0 / math.sqrt(2.0)))
            hidden = (pre * cdf).astype(bf16)
            slope = cdf + pre * (jnp.exp(-0.5 * pre * pre) * (1.0 / math.sqrt(2.0 * math.pi)))
            grad_hidden = nt(low_ref[rows], down_ref[...]) + nt(dmid_ref[rows], a_ref[...])
            dup = (slope * grad_hidden).astype(bf16)
            ff_ref[rows] += nn(hidden, down_ref[...])
            back_ref[rows] += nt(dup, up_ref[...])
            mid_acc[rows] += nn(hidden, a_ref[...])
            dmid_acc[rows] += nt(dup, up_b)
            ga_part = nn(dmid_t_ref[at], hidden)
            gb_part = nn(mid_t_ref[at], dup)
            ga = ga_part if ga is None else ga + ga_part
            gb = gb_part if gb is None else gb + gb_part
        if early:
            e_ref[j // 4, lax.rem(j // 2, 2), lax.rem(j, 2), :, a_ff_at:b_at_col] = ga.astype(bf16)
            at = pl.ds(pl.multiple_of(b_at_col + lax.rem(j, 2) * inner_block, lanes), inner_block)
            e_ref[1, j // 4, lax.rem(j // 2, 2), :, at] = (adapter_scale * gb).astype(bf16)

            @pl.when(j == 2)
            def _():
                receive(0)
                load = pltpu.make_async_copy(local_ref.at[:, 0], o_here, load_sem.at[0])
                load.start()
                load.wait()
                ga_out, gb_out = None, None
                for q in range(count):
                    rows = slice(q * size, (q + 1) * size)
                    out = o_here[q]
                    mid = nn(out, a_out_ref[...]).astype(bf16)
                    ga_part = nn(dmid_out_t_ref[q], out)
                    gb_part = nn(mid.T, low_ref[rows])
                    ga_out = ga_part if ga_out is None else ga_out + ga_part
                    gb_out = gb_part if gb_out is None else gb_out + gb_part
                e_ref[0, 1, 1, :, b_at_col:early_end] = (adapter_scale * gb_out).astype(bf16)
                for owner in range(8):
                    at = slice(owner * lanes, (owner + 1) * lanes)
                    e_ref[owner // 4, owner // 2 % 2, owner % 2, :, a_out_at:a_ff_at] = ga_out[:, at].astype(bf16)

            for m, (begin, take) in enumerate(((3, 5), (4, 6), (5, 7))):
                pl.when(j == begin)(lambda m=m: plane_sum.first(m).start())
                pl.when(j == take)(lambda m=m: plane_sum.take_first(m))
            pl.when(j == 7)(lambda: plane_sum.first(3).start())
        else:
            ga_ref[...] = ga
            gb_ref[...] = gb

    @pl.when(step == pl.num_programs(0) - 1)
    def _():
        mid_ff_ref[...] = mid_acc[...].astype(bf16)
        dmid_up_ref[...] = (adapter_scale * dmid_acc[...]).astype(bf16)
        if early:
            count, size = mid_t_ref.shape[0], mid_t_ref.shape[2]
            ga, gb = None, None
            for at in range(count):
                rows = slice(at * size, (at + 1) * size)
                ga_part = nn(dmid_up_ref[rows].T, second_ref[rows])
                gb_part = nn(mid_ff_ref[rows].T, low_ref[rows])
                ga = ga_part if ga is None else ga + ga_part
                gb = gb_part if gb is None else gb + gb_part
            for owner in range(8):
                place = (owner // 4, owner // 2 % 2, owner % 2, slice(None))
                at = slice(owner * lanes, (owner + 1) * lanes)
                e_ref[place + (slice(0, lanes),)] = ga[:, at].astype(bf16)
                e_ref[place + (slice(lanes, late_end),)] = (adapter_scale * gb[:, at]).astype(bf16)
            plane_sum.first(4).start()
            plane_sum.take_first(3)
            plane_sum.take_first(4)
            plane_sum.finish(sum_ref)
        if not early:
            receive(0)
        receive(1)


def finish_kernel(
    local_ref, wo_ref, wq_ref, wk_ref, wv_ref, a_out_ref, a_qkv_ref, b_out_ref, bq_ref, bk_ref, bv_ref,
    bias_ref, x_ref, cot_ref, weight_ref, ff_ref, bias_ff_ref, mid_ff_ref, b_ff_ref,
    second_ref, dmid_up_ref, a_up_ref, gain_ref, dmid_out_t_ref, low_ref,
    mixed_ref, tokens_ref, norm_ref, ga_ref, gb_ref,
    att_acc, mid_acc, first_acc, dmid_acc,
):
    t = pl.program_id(0)
    rows = x_ref.shape[0] * x_ref.shape[1]
    cols = wq_ref.shape[1]

    @pl.when(t == 0)
    def _():
        att_acc[...] = jnp.zeros_like(att_acc)
        mid_acc[...] = jnp.zeros_like(mid_acc)
        first_acc[...] = jnp.zeros_like(first_acc)
        dmid_acc[...] = jnp.zeros_like(dmid_acc)

    out, dq, dk, dv = (local_ref[:, i].reshape(rows, cols) for i in range(4))
    att_acc[...] += nn(out, wo_ref[...])
    mid_acc[...] += nn(out, a_out_ref[...])
    first_acc[...] += nt(dq, wq_ref[...]) + nt(dk, wk_ref[...]) + nt(dv, wv_ref[...])
    dmid_acc[...] += nt(dq, bq_ref[...]) + nt(dk, bk_ref[...]) + nt(dv, bv_ref[...])
    size = x_ref.shape[1]
    ga_ref[...] = sum(nn(dmid_out_t_ref[q], out[q * size : (q + 1) * size]) for q in range(x_ref.shape[0]))

    @pl.when(t == pl.num_programs(0) - 1)
    def _():
        size = x_ref.shape[1]
        norm = [jnp.zeros((1, first_acc.shape[1]), f32) for _ in range(4)]
        for q in range(x_ref.shape[0]):
            part = slice(q * size, (q + 1) * size)
            x = x_ref[q].astype(f32)
            mid = mid_acc[part].astype(bf16)
            gb = tn(mid, low_ref[part])
            gb_ref[...] = gb if q == 0 else gb_ref[...] + gb
            att = att_acc[part] + bias_ref[...] + adapter_scale * nn(mid, b_out_ref[...])
            ff = ff_ref[part] + bias_ff_ref[...] + adapter_scale * nn(mid_ff_ref[part], b_ff_ref[...])
            mixed_ref[q] = (x + att + ff).astype(bf16)
            dmid = (adapter_scale * dmid_acc[part]).astype(bf16)
            grad_first = first_acc[part] + nt(dmid, a_qkv_ref[...])
            grad_second = second_ref[part] + nt(dmid_up_ref[part], a_up_ref[...])
            centre = x - jnp.mean(x, axis=-1, keepdims=True)
            inv = lax.rsqrt(jnp.mean(centre * centre, axis=-1, keepdims=True) + norm_eps)
            unit = centre * inv
            pulled = grad_first * gain_ref[0:1] + grad_second * gain_ref[1:2]
            back = inv * (
                pulled
                - jnp.mean(pulled, axis=-1, keepdims=True)
                - unit * jnp.mean(pulled * unit, axis=-1, keepdims=True)
            )
            row_grad = cot_ref[q].astype(f32) * weight_ref[part]
            tokens_ref[q] = (row_grad + back).astype(bf16)
            for k, value in enumerate((grad_first * unit, grad_second * unit, grad_first, grad_second)):
                norm[k] += jnp.sum(value, axis=0, keepdims=True)
        norm_ref[...] = jnp.concatenate(norm, axis=0)


def tail_kernel(
    o_ref, dq_ref, dk_ref, dv_ref, wo_ref, wq_ref, wk_ref, wv_ref, a_out_ref, a_qkv_ref, b_out_ref,
    bq_ref, bk_ref, bv_ref, bias_ref, x_ref, cot_ref, weight_ref, ff_ref, bias_ff_ref, mid_ff_ref, b_ff_ref,
    second_ref, dmid_up_ref, a_up_ref, gain_ref,
    e_ref, b_ref, mean_ref, square_ref, bf_ref, mean_f_ref, square_f_ref,
    mixed_ref, tokens_ref, out_hbm, norm_ref, fresh_hbm,
    out_ref, fresh_ref, att_acc, mid_acc, first_acc, dmid_acc,
    r4, nr, nsum,
    s4, q4, s5, q5, sf, qf, sn, qn, sg, qg, done_sem,
    *, n,
):
    step = pl.program_id(0)
    dp, z, y, x, c, core, along_x, along_y = plane()
    peers = [(dp, lax.rem(z + t, n)) for t in range(1, n)]
    seqs, size, width = o_ref.shape[0], o_ref.shape[2], x_ref.shape[2]
    rows, cols = seqs * size, o_ref.shape[3]
    outs = width // cols
    grads = width // dq_ref.shape[3]
    first_seq = outs + grads
    rank = e_ref.shape[0]
    part = rank // n
    lanes = 128
    mine = pl.ds(pl.multiple_of(z * part, part), part)

    def to_part(t):
        return pl.ds(pl.multiple_of(lax.rem(z + t, n) * part, part), part)

    def e_out(k, t):
        cut = slice(*early_cuts[k])
        return remote(e_ref.at[to_part(t), cut], r4.at[t, :, cut], s4.at[t, k], q4.at[t, k], peers[t - 1])

    def e_back(k, t):
        cut = slice(*early_cuts[k])
        return remote(out_ref.at[mine, cut], out_ref.at[mine, cut], s5.at[t, k], q5.at[t, k], peers[t - 1])

    count = len(early_cuts)

    def fresh_back(t):
        return remote(fresh_ref.at[dp, mine, :], fresh_ref.at[dp, mine, :], sf.at[t], qf.at[t], peers[t - 1])

    from_x, from_y, from_c = along_x[0], along_y[0], core[0]
    across = from_x + from_y - dp
    onward = jnp.where(c == 0, from_y, from_x)
    target = (jnp.where(c == 0, from_x, from_y), z)
    other = 1 - 2 * c
    hops = [
        (dp, from_x, along_x), (dp, from_y, along_y), (dp, from_c, core), (onward, across, target),
        (from_x, from_x + other, core), (from_y, from_y + other, core), (across, across + other, core),
    ]

    middle_row = rank // 2
    parts = (slice(0, middle_row), slice(middle_row, rank))

    def gather(kind, p):
        slot, _, peer = hops[kind]
        there = fresh_ref.at[slot, parts[p], :]
        return remote(there, there, sg.at[p, kind], qg.at[p, kind], peer)

    def fresh_rows(value, grad_b):
        cut = b_ref.shape[1]
        new_b = adam_fresh(b_ref[mine, :], grad_b, mean_ref[mine, :], square_ref[mine, :])
        new_f = adam_fresh(bf_ref[mine, :], value, mean_f_ref[mine, :], square_f_ref[mine, :])
        fresh_ref[dp, mine, :] = jnp.concatenate([new_b, new_f], axis=1).astype(bf16)

    def norm_copy(i, peer):
        return remote(nsum.at[i], nr.at[i], sn.at[i], qn.at[i], peer)

    norm_stages = [norm_copy(0, core), norm_copy(1, along_x), norm_copy(2, along_y)]
    norm_last = [
        remote(nsum.at[3], nr.at[2 + t], sn.at[2 + t], qn.at[2 + t], peers[t - 1]) for t in range(1, n)
    ]

    def norm_take(i):
        norm_stages[i].wait()
        nsum[i + 1] = nsum[i] + nr[i]

    @pl.when(step == 0)
    def _():
        greet([core, along_x, along_y] + peers)
        for k in range(count):
            for t in range(1, n):
                e_out(k, t).start()
        att_acc[...] = jnp.zeros_like(att_acc)
        mid_acc[...] = jnp.zeros_like(mid_acc)
        first_acc[...] = jnp.zeros_like(first_acc)
        dmid_acc[...] = jnp.zeros_like(dmid_acc)

    @pl.when(step < outs)
    def _():
        out = o_ref[...].reshape(rows, cols)
        att_acc[...] += nn(out, wo_ref[...])
        mid_acc[...] += nn(out, a_out_ref[...])

    @pl.when((step >= outs) & (step < first_seq))
    def _():
        dq, dk, dv = (r[...].reshape(rows, r.shape[3]) for r in (dq_ref, dk_ref, dv_ref))
        first_acc[...] += nt(dq, wq_ref[...]) + nt(dk, wk_ref[...]) + nt(dv, wv_ref[...])
        dmid_acc[...] += nt(dq, bq_ref[...]) + nt(dk, bk_ref[...]) + nt(dv, bv_ref[...])

    @pl.when(step == outs)
    def _():
        for k in range(count):
            cut = slice(*early_cuts[k])
            for t in range(1, n):
                e_out(k, t).wait()
            value = e_ref[mine, cut].astype(f32)
            for t in range(1, n):
                value += r4[t, :, cut].astype(f32)
            out_ref[mine, cut] = value.astype(bf16)
        fresh_rows(out_ref[mine, lanes:late_end].astype(f32), out_ref[mine, b_at_col:early_end].astype(f32))
        for t in range(1, n):
            fresh_back(t).start()

    @pl.when(step == first_seq - 1)
    def _():
        for t in range(1, n):
            fresh_back(t).wait()
        for p in range(2):
            for kind in (0, 1, 2):
                gather(kind, p).start()
        for k in range(count):
            for t in range(1, n):
                e_back(k, t).start()

    @pl.when(step >= first_seq)
    def _():
        q = step - first_seq
        at = pl.ds(pl.multiple_of(q * size, size), size)
        x_in = x_ref[0].astype(f32)
        mid = mid_acc[at, :].astype(bf16)
        att = att_acc[at, :] + bias_ref[...] + adapter_scale * nn(mid, b_out_ref[...])
        ff = ff_ref[...] + bias_ff_ref[...] + adapter_scale * nn(mid_ff_ref[at, :], b_ff_ref[...])
        mixed_ref[0] = (x_in + att + ff).astype(bf16)
        dmid = (adapter_scale * dmid_acc[at, :]).astype(bf16)
        grad_first = first_acc[at, :] + nt(dmid, a_qkv_ref[...])
        grad_second = second_ref[...] + nt(dmid_up_ref[at, :], a_up_ref[...])
        centre = x_in - jnp.mean(x_in, axis=-1, keepdims=True)
        inv = lax.rsqrt(jnp.mean(centre * centre, axis=-1, keepdims=True) + norm_eps)
        unit = centre * inv
        pulled = grad_first * gain_ref[0:1] + grad_second * gain_ref[1:2]
        back = inv * (
            pulled
            - jnp.mean(pulled, axis=-1, keepdims=True)
            - unit * jnp.mean(pulled * unit, axis=-1, keepdims=True)
        )
        row_grad = cot_ref[0].astype(f32) * weight_ref[at, :]
        tokens_ref[0] = (row_grad + back).astype(bf16)
        norm = [
            jnp.sum(value, axis=0, keepdims=True)
            for value in (grad_first * unit, grad_second * unit, grad_first, grad_second)
        ]
        norm = jnp.concatenate(norm, axis=0)
        nsum[0] = jnp.where(q == 0, norm, nsum[0] + norm)

    @pl.when(step == pl.num_programs(0) - 1)
    def _():
        norm_stages[0].start()
        for p in range(2):
            gather(0, p).wait_recv()
            gather(1, p).wait_recv()
            for kind in (3, 4, 5):
                gather(kind, p).start()
            norm_take(p)
            norm_stages[p + 1].start()
        for p in range(2):
            gather(3, p).wait_recv()
            gather(6, p).start()
        norm_take(2)
        for copy in norm_last:
            copy.start()
        for k in range(count):
            for t in range(1, n):
                e_back(k, t).wait()

        keep_out = pltpu.make_async_copy(out_ref, out_hbm, done_sem.at[0])
        keep_out.start()
        for p in range(2):
            for kind in (2, 4, 5, 6):
                gather(kind, p).wait_recv()
        keep_fresh = pltpu.make_async_copy(fresh_ref, fresh_hbm, done_sem.at[1])
        keep_fresh.start()
        for p in range(2):
            for kind in range(7):
                gather(kind, p).wait_send()
        for copy in norm_last:
            copy.wait()
        keep_out.wait()
        keep_fresh.wait()
        value = jnp.zeros_like(nsum[3])
        for blk in range(n):
            there = lax.rem(z - blk + n, n)
            value += jnp.where(there == 0, nsum[3], nr[2 + jnp.maximum(there, 1)])
        norm_ref[...] = value


def update_kernel(
    g_ref, fresh_ref, w_ref, wd_ref, *refs, rank, width,
):
    params, outs = refs[:16], refs[16:30]
    a_new, aff_new = refs[30:]
    j = pl.program_id(0)
    cols = w_ref.shape[1]

    @pl.when(j == 0)
    def _():
        rows, inner = params[0].shape[0], params[4].shape[0]
        got = g_ref[...].astype(f32)
        cut, cut_f = params[8].shape[1], params[12].shape[1]
        up = got[:, :rows]
        qkv = got[:, rows + cut_f : 2 * rows + cut_f]
        out = got[:, 2 * rows + cut_f : 3 * rows + cut_f]
        at = 3 * rows + cut_f
        grads = [
            jnp.concatenate([part.T for part in (qkv, out, up)], axis=1),
            got[:, at : at + inner].T,
            got[:, at + inner : at + inner + cut],
            got[:, rows : rows + cut_f],
        ]
        for i, grad in enumerate(grads):
            param, mean, square, keep = (r[...] for r in params[4 * i : 4 * i + 4])
            mean_new = 0.9 * mean + 0.1 * grad
            square_new = 0.999 * square + 0.001 * grad * grad
            kept = keep.astype(f32)
            outs[i][...] = grad
            outs[4 + 2 * i][...] = mean_new * kept
            outs[5 + 2 * i][...] = square_new * kept
            if i < 2:
                fresh = param - 0.01 * (mean_new / first_fix) / (jnp.sqrt(square_new / second_fix) + 1e-08)
                if i == 0:
                    for k in range(3):
                        a_new[k] = fresh[:, k * rank : (k + 1) * rank].astype(bf16)
                else:
                    aff_new[...] = fresh.astype(bf16)

    cut = params[8].shape[1]
    fresh = [fresh_ref[i] for i in range(fresh_ref.shape[0])]
    update = []
    for i, part in enumerate(fresh):
        at = j * cols + i * cut
        block = jnp.where(at < 3 * width, 0, jnp.where(at < 4 * width, 1, 2))
        update.append(nn(a_new[block], part[:, :cut]))
    update = jnp.concatenate(update, axis=1)
    outs[12][...] = (w_ref[...].astype(f32) + adapter_scale * update).astype(bf16)
    update = nn(aff_new[...], jnp.concatenate([f[:, cut:] for f in fresh], axis=1))
    outs[13][...] = (wd_ref[...].astype(f32) + adapter_scale * update).astype(bf16)


def adam_fresh(param, grad, mean, square):
    mean_new = 0.9 * mean + 0.1 * grad
    square_new = 0.999 * square + 0.001 * grad * grad
    return param - 0.01 * (mean_new / first_fix) / (jnp.sqrt(square_new / second_fix) + 1e-08)


def body(
    dp_n,
    n,
    tokens,
    cotangent,
    domain_ids,
    domain_weight,
    frozen_input_weights,
    bias_in,
    frozen_down_weight,
    bias_ff,
    norm_gain,
    norm_shift,
    adapt_a,
    adapt_a_ff,
    adapt_b,
    adapt_b_ff,
    mean_a,
    mean_a_ff,
    mean_b,
    mean_b_ff,
    square_a,
    square_a_ff,
    square_b,
    square_b_ff,
    keep_a,
    keep_a_ff,
    keep_b,
    keep_b_ff,
):
    seqs, span, width = tokens.shape
    rows = seqs * span
    rank = adapt_b.shape[0]
    depth = width // HEADS
    cz = width // n
    length = n * span
    z = lax.axis_index("blk")
    z_arr = jnp.full((1,), z, jnp.int32)
    kr = frozen_input_weights.shape[0]
    down_rows, inner = frozen_down_weight.shape[0], frozen_down_weight.shape[0] * dp_n
    lanes = 128

    def shift_by(values, s):
        return lax.ppermute(values, "blk", [(i, (i + s) % n) for i in range(n)])

    b_cols = adapt_b.shape[1] + adapt_b_ff.shape[1]
    bias32 = bias_in.astype(f32)
    whole_front = dp_n == 8 and n == 4 and seqs > 1 and (rank, width, inner) == (128, 1024, 4096)
    if whole_front:
        vmem = pl.BlockSpec(memory_space=pltpu.VMEM)
        hbm = pl.BlockSpec(memory_space=pl.ANY)
        dma = pltpu.SemaphoreType.DMA
        half = ROTARY // 2
        freq = [rope_base ** (-(k * 2.0) / ROTARY) for k in range(half)]
        freq = np.tile(np.array(freq + freq + [0.0] * (depth - ROTARY), np.float32), lanes // depth)

        def shape(*dims, dtype=bf16):
            return jax.ShapeDtypeStruct(dims, dtype)

        (
            w_in, w_down, a_all, a_ff, b_in, b_ff, query, keys, values, first_pos, mid_pos, g_pos,
            grad_low, second, mid_up, mid_up_t, dmid_ff, dmid_ff_t, dmid_out_t, *tables, row_weight,
        ) = pl.pallas_call(
            functools.partial(front_kernel, n=n, depth=depth),
            in_specs=[hbm] * 3 + [vmem] * 6 + [pl.BlockSpec(memory_space=pltpu.SMEM)] + [vmem] * 4,
            out_specs=[hbm] * 12 + [vmem] * 11,
            out_shape=[
                shape(width, 8 * width), shape(inner, width), shape(width, 3 * rank), shape(inner, rank),
                shape(rank, 8 * width), shape(rank, width),
                shape(seqs, length, cz), shape(seqs, length, cz), shape(seqs, length, cz),
                shape(seqs, length, width), shape(seqs, length, rank), shape(seqs, length, cz),
                shape(rows, width), shape(rows, width),
                shape(rows, rank), shape(seqs, rank, span), shape(rows, rank), shape(seqs, rank, span),
                shape(seqs, rank, span),
                shape(length, lanes, dtype=f32), shape(length, lanes, dtype=f32), shape(length, lanes, dtype=f32),
                shape(rows, 1, dtype=f32),
            ],
            scratch_shapes=[
                pltpu.VMEM(adapt_a.shape, bf16),
                pltpu.VMEM(adapt_a_ff.shape, bf16),
                pltpu.VMEM(adapt_b.shape, bf16),
                pltpu.VMEM(adapt_b_ff.shape, bf16),
                pltpu.VMEM((n, seqs, span, width), bf16),
                pltpu.VMEM((seqs, length, cz), bf16),
                pltpu.VMEM((seqs, length, cz), bf16),
                pltpu.VMEM((seqs, length, cz), bf16),
                pltpu.VMEM((seqs, length, width), bf16),
                pltpu.VMEM((seqs, length, rank), bf16),
                pltpu.VMEM((n, seqs, span, cz), bf16),
                pltpu.VMEM((width, width), bf16),
                pltpu.VMEM((3, width, cz), bf16),
                pltpu.VMEM((width, 3 * rank), bf16),
                pltpu.VMEM((rank, 8 * width), bf16),
                pltpu.VMEM((rank, width), bf16),
                dma((7, 7)), dma((7, 7)), dma((7,)),
                dma((n,)), dma((n,)), dma((n,)), dma((n,)), dma((n,)), dma((n,)),
                dma((7,)), dma((5, n)), dma((2,)),
            ],
            compiler_params=pltpu.CompilerParams(
                collective_id=2, has_side_effects=True, vmem_limit_bytes=58 << 20
            ),
            name="front",
        )(
            tokens, frozen_input_weights, frozen_down_weight,
            adapt_a, adapt_a_ff, adapt_b, adapt_b_ff,
            cotangent, domain_ids, domain_weight, norm_gain, norm_shift, bias32.reshape(1, -1), freq.reshape(1, -1),
        )
    else:
        lookup = (domain_ids[..., None] == jnp.arange(DOMAINS, dtype=jnp.int32)).astype(f32)
        row_weight = jnp.sum(lookup * domain_weight, axis=-1).reshape(rows, 1)
        row_grad = cotangent.astype(f32).reshape(rows, width) * row_weight
        grad_low = row_grad.astype(bf16)
        b_shard = jnp.concatenate([adapt_b, adapt_b_ff], axis=1).astype(bf16)
        one = jnp.concatenate(
            [frozen_input_weights[:, : 4 * width], adapt_a.astype(bf16), b_shard.reshape(kr, -1)], axis=1
        )
        one = lax.all_gather(one, "dp", axis=0, tiled=True)
        two = lax.all_gather(frozen_input_weights[:, 4 * width :], "dp", axis=0, tiled=True)
        three = jnp.concatenate([frozen_down_weight, adapt_a_ff.astype(bf16)], axis=1)
        three = lax.all_gather(three, "dp", axis=0, tiled=True)
        a_at = 4 * width
        b_at = a_at + 3 * rank
        a_all = one[:, a_at:b_at]
        b_all = one[:, b_at:].reshape(dp_n, rank, b_cols)
        b_in = jnp.transpose(b_all[:, :, : adapt_b.shape[1]], (1, 0, 2)).reshape(rank, -1)
        b_ff = jnp.transpose(b_all[:, :, adapt_b.shape[1] :], (1, 0, 2)).reshape(rank, width)
        w_out = one[:, 3 * width : 4 * width]
        w_up = two
        w_down, a_ff = three[:, :width], three[:, width:]

        right, left = tokens, tokens
        rights, lefts = [None], [None]
        for s in range(1, n):
            right = lax.ppermute(right, "blk", [(i, i + 1) for i in range(n - 1)])
            left = lax.ppermute(left, "blk", [(i + 1, i) for i in range(n - 1)])
            rights.append(right)
            lefts.append(left)
        x_all = jnp.stack(
            [tokens] + [jnp.where(z >= s, rights[s], lefts[n - s]) for s in range(1, n)]
        )

        b_out = b_in[:, 3 * width : 4 * width]
        a_out = a_all[:, rank : 2 * rank]
        dmid_out = (adapter_scale * nt(grad_low, b_out)).astype(bf16)
        grad_att = (nt(grad_low, w_out) + nt(dmid_out, a_out)).astype(bf16)
        grad_att = jnp.transpose(grad_att.reshape(seqs, span, n, cz), (2, 0, 1, 3))

        def piece(values, s):
            return lax.dynamic_index_in_dim(values, lax.rem(z + s, n), 0, keepdims=False)

        g_all = jnp.stack(
            [piece(grad_att, 0)] + [shift_by(piece(grad_att, s), s) for s in range(1, n)]
        )

        tables = rope_lane_tables(length, depth, lanes)
        own = [lax.dynamic_slice_in_dim(b_in[:, t * width : (t + 1) * width], z * cz, cz, 1) for t in range(3)]
        b_own = jnp.concatenate(own, axis=1)
        bias_own = jnp.concatenate(
            [lax.dynamic_slice_in_dim(bias32, t * width + z * cz, cz, 0) for t in range(3)]
        ).reshape(1, 3 * cz)

        def block_of(s, z_ref):
            return lax.rem(z_ref[0] - s + n, n)

        table_spec = pl.BlockSpec((span, lanes), lambda s, q, z_ref: (block_of(s, z_ref), 0))
        head_spec = pl.BlockSpec((1, span, cz), lambda s, q, z_ref: (q, block_of(s, z_ref), 0))
        query, keys, values, first_all, mid_all = pl.pallas_call(
            qkv_kernel,
            grid_spec=pltpu.PrefetchScalarGridSpec(
                num_scalar_prefetch=1,
                grid=(n, seqs),
                in_specs=[
                    pl.BlockSpec((1, 1, span, width), lambda s, q, z_ref: (s, q, 0, 0)),
                    pl.BlockSpec((1, width), lambda s, q, z_ref: (0, 0)),
                    pl.BlockSpec((1, width), lambda s, q, z_ref: (0, 0)),
                    pl.BlockSpec((width, cz), lambda s, q, z_ref: (0, z_ref[0])),
                    pl.BlockSpec((width, cz), lambda s, q, z_ref: (0, n + z_ref[0])),
                    pl.BlockSpec((width, cz), lambda s, q, z_ref: (0, 2 * n + z_ref[0])),
                    pl.BlockSpec((width, rank), lambda s, q, z_ref: (0, a_at // rank)),
                    pl.BlockSpec((rank, 3 * cz), lambda s, q, z_ref: (0, 0)),
                    pl.BlockSpec((1, 3 * cz), lambda s, q, z_ref: (0, 0)),
                    table_spec,
                    table_spec,
                    table_spec,
                ],
                out_specs=[
                    head_spec,
                    head_spec,
                    head_spec,
                    pl.BlockSpec((1, 1, span, width), lambda s, q, z_ref: (block_of(s, z_ref), q, 0, 0)),
                    pl.BlockSpec((1, 1, span, rank), lambda s, q, z_ref: (block_of(s, z_ref), q, 0, 0)),
                ],
            ),
            out_shape=[jax.ShapeDtypeStruct((seqs, length, cz), bf16)] * 3
            + [
                jax.ShapeDtypeStruct((n, seqs, span, width), bf16),
                jax.ShapeDtypeStruct((n, seqs, span, rank), bf16),
            ],
            compiler_params=pltpu.CompilerParams(vmem_limit_bytes=48 << 20),
            cost_estimate=pl.CostEstimate(
                flops=2 * n * rows * width * 4 * cz, bytes_accessed=6 * n * rows * width, transcendentals=0
            ),
            name="qkv",
        )(
            z_arr, x_all, norm_gain[0:1], norm_shift[0:1], one, one, one, one, b_own, bias_own, *tables
        )

        input_rows = tokens.astype(f32).reshape(rows, width)
        centre = input_rows - jnp.mean(input_rows, axis=-1, keepdims=True)
        inv = lax.rsqrt(jnp.mean(centre * centre, axis=-1, keepdims=True) + norm_eps)
        second = (centre * inv * norm_gain[1] + norm_shift[1]).astype(bf16)
        a_up = a_all[:, 2 * rank :]
        mid_up = nn(second, a_up).astype(bf16)
        dmid_ff = (adapter_scale * nt(grad_low, b_ff)).astype(bf16)
        g_pos = jnp.concatenate([g_all, g_all])
        g_pos = lax.rev(g_pos, (0,))
        g_pos = lax.dynamic_slice_in_dim(g_pos, lax.rem(n - 1 - z + n, n), n, 0)
        g_pos = jnp.transpose(g_pos, (1, 0, 2, 3)).reshape(seqs, length, cz)

        first_pos = jnp.transpose(first_all, (1, 0, 2, 3))
        mid_pos = jnp.transpose(mid_all, (1, 0, 2, 3))
        w_in = jnp.concatenate([one[:, :a_at], two], axis=1)
        mid_up_t, dmid_ff_t, dmid_out_t = (
            jnp.transpose(v.reshape(seqs, span, rank), (0, 2, 1)) for v in (mid_up, dmid_ff, dmid_out)
        )

    pairs = cz // lanes
    steps = seqs * pairs
    inner_block = min(512, inner)
    def one_buffer(shape):
        zeros = (0,) * len(shape)
        return pl.BlockSpec(shape, lambda s: zeros, pipeline_mode=pl.Buffered(1))

    def seq_pair(s):
        s = jnp.minimum(s, steps - 1)
        return s // pairs, lax.rem(s, pairs)

    def head_map(s):
        seq, pair = seq_pair(s)
        return seq, 0, pair

    def inner_at(s):
        return jnp.maximum(s - steps, 0)

    head = pl.BlockSpec((1, length, lanes), head_map)
    early = whole_front
    dma = pltpu.SemaphoreType.DMA
    half_rank = rank // 2

    def wide(*dims, dtype=bf16):
        return jax.ShapeDtypeStruct(dims, dtype)

    in_specs = (
        [head] * 4
        + [one_buffer((length, lanes))] * 3
        + [one_buffer((rows, width))] * 2
        + [one_buffer((rows, rank)), one_buffer((seqs, rank, span))] * 2
        + [
            pl.BlockSpec((width, inner_block), lambda s: (0, 4 * width // inner_block + inner_at(s))),
            pl.BlockSpec((inner_block, width), lambda s: (inner_at(s), 0)),
            pl.BlockSpec((inner_block, rank), lambda s: (inner_at(s), 0)),
            one_buffer((rank, 8 * width))
            if early
            else pl.BlockSpec((rank, inner_block), lambda s: (0, 4 * width // inner_block + inner_at(s))),
            pl.BlockSpec((1, inner_block), lambda s: (0, 4 * width // inner_block + inner_at(s))),
        ]
    )
    operands = [
        query, keys, values, g_pos, *tables, second, grad_low, mid_up, mid_up_t, dmid_ff, dmid_ff_t,
        w_in, w_down, a_ff, b_in, bias32.reshape(1, -1),
    ]
    partial_specs = [one_buffer((rows, width))] * 2 + [one_buffer((rows, rank))] * 2
    partial_shapes = [wide(rows, width, dtype=f32)] * 2 + [wide(rows, rank)] * 2
    local_spec, local_shape = pl.BlockSpec(memory_space=pl.ANY), wide(seqs, 4, span, width)
    scratch = [
        pltpu.VMEM((steps, n, 4, span, lanes), bf16),
        pltpu.VMEM((length, lanes), f32),
        pltpu.VMEM((length, lanes), f32),
        pltpu.VMEM((rows, rank), f32),
        pltpu.VMEM((rows, rank), f32),
        dma((2, steps, n)),
        dma((2, steps, n)),
        dma((2, steps)),
    ]
    if early:
        in_specs += [
            pl.BlockSpec((1, length, width), lambda s: (seq_pair(s)[0], 0, 0)),
            pl.BlockSpec((1, length, rank), lambda s: (seq_pair(s)[0], 0, 0)),
        ]
        in_specs += [
            pl.BlockSpec((width, rank), lambda s: (0, 1), pipeline_mode=pl.Buffered(1)),
            one_buffer((seqs, rank, span)),
        ]
        operands += [first_pos, mid_pos, a_all, dmid_out_t]
        out_specs = [local_spec] + partial_specs + [one_buffer((rank, early_end))]
        out_shapes = [local_shape] + partial_shapes + [wide(rank, early_end)]
        cuts = len(early_cuts)
        scratch += [
            pltpu.VMEM((2, 2, 2, rank, early_end), bf16),
            pltpu.VMEM((length, rank), f32),
            pltpu.VMEM((3, pairs, rank, lanes), f32),
            pltpu.VMEM((rank, width), f32),
            pltpu.VMEM((seqs, span, width), bf16),
            dma((1,)),
            pltpu.VMEM((2, 2, rank, early_end), bf16),
            pltpu.VMEM((2, half_rank, early_end), bf16),
            pltpu.VMEM((2, half_rank, early_end), bf16),
            pltpu.VMEM((half_rank, early_end), bf16),
            pltpu.VMEM((half_rank, early_end), bf16),
            dma((5,)), dma((5,)), dma((2, cuts)), dma((2, cuts)), dma((2, cuts)), dma((2, cuts)),
        ]
    else:
        out_specs = (
            [local_spec, pl.BlockSpec((1, 3, length, lanes), lambda s: (seq_pair(s)[0], 0, 0, seq_pair(s)[1]))]
            + partial_specs
            + [pl.BlockSpec((rank, inner_block), lambda s: (0, inner_at(s)))] * 2
        )
        out_shapes = (
            [local_shape, wide(seqs, 3, length, cz)] + partial_shapes + [wide(rank, inner, dtype=f32)] * 2
        )
    middle = pl.pallas_call(
        functools.partial(middle_kernel, n=n, pairs=pairs, steps=steps, depth=depth, early=early),
        grid=(steps + inner // inner_block,),
        in_specs=in_specs,
        out_specs=out_specs,
        out_shape=out_shapes,
        scratch_shapes=scratch,
        compiler_params=pltpu.CompilerParams(
            collective_id=0, has_side_effects=True, vmem_limit_bytes=60 << 20
        ),
        name="middle",
    )(*operands)

    if early:
        local, ff, grad_second, mid_ff, dmid_up, summed = middle
        part = rank // n

        def single(shape, *at):
            return pl.BlockSpec(shape, lambda s: at, pipeline_mode=pl.Buffered(1))

        wide_block = width // 2

        def of_out(s):
            return jnp.minimum(s, 1)

        def of_grad(s):
            return jnp.clip(s - 2, 0, n - 1)

        def of_seq(s):
            return jnp.maximum(s - 2 - n, 0)

        def piece_spec(kind):
            return pl.BlockSpec((seqs, 1, span, cz), lambda s: (0, kind, 0, of_grad(s)))

        def columns(kind, height):
            return pl.BlockSpec((height, cz), lambda s: (0, kind * n + of_grad(s)))

        full = pl.BlockSpec((1, span, width), lambda s: (of_seq(s), 0, 0))
        flat = pl.BlockSpec((span, width), lambda s: (of_seq(s), 0))
        cuts = len(early_cuts)
        b_here = [adapt_b, mean_b, square_b, adapt_b_ff, mean_b_ff, square_b_ff]
        mixed, grad_tokens, reduced, norm_sum, fresh = pl.pallas_call(
            functools.partial(tail_kernel, n=n),
            grid=(2 + n + seqs,),
            in_specs=[
                pl.BlockSpec((seqs, 1, span, wide_block), lambda s: (0, 0, 0, of_out(s))),
                piece_spec(1), piece_spec(2), piece_spec(3),
                pl.BlockSpec((wide_block, width), lambda s: (of_out(s), 3)),
                columns(0, width), columns(1, width), columns(2, width),
                pl.BlockSpec((wide_block, rank), lambda s: (of_out(s), 1)),
                single((width, rank), 0, 0),
                single((rank, width), 0, 3),
                columns(0, rank), columns(1, rank), columns(2, rank),
                single((1, width), 0, 3),
                full, full,
                single((rows, 1), 0, 0),
                flat,
                single((1, width), 0, 0),
                single((rows, rank), 0, 0),
                single((rank, width), 0, 0),
                flat,
                single((rows, rank), 0, 0),
                single((width, rank), 0, 2),
                single((2, width), 0, 0),
                single((rank, early_end), 0, 0),
            ]
            + [single(v.shape, 0, 0) for v in b_here],
            out_specs=[
                full, full, pl.BlockSpec(memory_space=pl.ANY), single((4, width), 0, 0),
                pl.BlockSpec(memory_space=pl.ANY),
            ],
            out_shape=[
                wide(seqs, span, width), wide(seqs, span, width), wide(rank, 2048), wide(4, width, dtype=f32),
                wide(dp_n, rank, b_cols),
            ],
            scratch_shapes=[
                pltpu.VMEM((rank, 2048), bf16),
                pltpu.VMEM((dp_n, rank, b_cols), bf16),
                pltpu.VMEM((rows, width), f32),
                pltpu.VMEM((rows, rank), f32),
                pltpu.VMEM((rows, width), f32),
                pltpu.VMEM((rows, rank), f32),
                pltpu.VMEM((n, part, early_end), bf16),
                pltpu.VMEM((2 + n, 4, width), f32),
                pltpu.VMEM((4, 4, width), f32),
                dma((n, cuts)), dma((n, cuts)), dma((n, cuts)), dma((n, cuts)), dma((n,)), dma((n,)),
                dma((2 + n,)), dma((2 + n,)), dma((2, 7)), dma((2, 7)), dma((2,)),
            ],
            compiler_params=pltpu.CompilerParams(
                collective_id=1, has_side_effects=True, vmem_limit_bytes=58 << 20
            ),
            name="tail",
        )(
            local, local, local, local, w_in, w_in, w_in, w_in, a_all, a_all, b_in, b_in, b_in, b_in,
            bias32.reshape(1, -1), tokens, cotangent, row_weight, ff, bias_ff.astype(f32).reshape(1, -1), mid_ff, b_ff,
            grad_second, dmid_up, a_all, norm_gain, summed, *b_here,
        )
    else:
        local, own, ff, grad_second, mid_ff, dmid_up, grad_a_ff_t, grad_b_up = middle
        grad_b_up = adapter_scale * grad_b_up
        first_pos = first_pos.reshape(seqs * length, width)
        mid_pos = mid_pos.reshape(seqs * length, rank)
        b_own = jnp.concatenate(
            [lax.dynamic_slice_in_dim(b_in[:, t * width : (t + 1) * width], z * cz, cz, 1) for t in range(3)], axis=1
        )
        djoint_own = [own[:, t].reshape(seqs * length, cz) for t in range(3)]
        dmid_own = sum(nt(djoint_own[t], b_own[:, t * cz : (t + 1) * cz]) for t in range(3))
        dmid_own = (adapter_scale * dmid_own).astype(bf16)
        grad_a_qkv_t = tn(dmid_own, first_pos)
        mine = (jnp.arange(n, dtype=jnp.int32) == z)[None, :, None]
        grad_b_qkv = jnp.concatenate(
            [
                jnp.where(mine, adapter_scale * tn(mid_pos, part)[:, None, :], 0.0).reshape(rank, width)
                for part in djoint_own
            ],
            axis=1,
        )
        grad_a_up_t = tn(dmid_up, second)
        grad_b_ffp = adapter_scale * tn(mid_ff, grad_low)

        def fixed(shape, *at):
            return pl.BlockSpec(shape, lambda t: at, pipeline_mode=pl.Buffered(1))

        def column(at, height):
            return pl.BlockSpec((height, cz), lambda t: (0, at * n + t))

        mixed, grad_tokens, norm_part, grad_a_out_t, grad_b_out = pl.pallas_call(
            finish_kernel,
            grid=(n,),
            in_specs=[
                pl.BlockSpec((seqs, 4, span, cz), lambda t: (0, 0, 0, t)),
                pl.BlockSpec((cz, width), lambda t: (t, 3)),
                column(0, width), column(1, width), column(2, width),
                pl.BlockSpec((cz, rank), lambda t: (t, 1)),
                fixed((width, rank), 0, 0),
                fixed((rank, width), 0, 3),
                column(0, rank), column(1, rank), column(2, rank),
                fixed((1, width), 0, 3),
                fixed((seqs, span, width), 0, 0, 0),
                fixed((seqs, span, width), 0, 0, 0),
                fixed((rows, 1), 0, 0),
                fixed((rows, width), 0, 0),
                fixed((1, width), 0, 0),
                fixed((rows, rank), 0, 0),
                fixed((rank, width), 0, 0),
                fixed((rows, width), 0, 0),
                fixed((rows, rank), 0, 0),
                fixed((width, rank), 0, 2),
                fixed((2, width), 0, 0),
                fixed((seqs, rank, span), 0, 0, 0),
                fixed((rows, width), 0, 0),
            ],
            out_specs=[
                fixed((seqs, span, width), 0, 0, 0),
                fixed((seqs, span, width), 0, 0, 0),
                fixed((4, width), 0, 0),
                pl.BlockSpec((rank, cz), lambda t: (0, t)),
                fixed((rank, width), 0, 0),
            ],
            out_shape=[
                jax.ShapeDtypeStruct((seqs, span, width), bf16),
                jax.ShapeDtypeStruct((seqs, span, width), bf16),
                jax.ShapeDtypeStruct((4, width), f32),
                jax.ShapeDtypeStruct((rank, width), f32),
                jax.ShapeDtypeStruct((rank, width), f32),
            ],
            scratch_shapes=[
                pltpu.VMEM((rows, width), f32),
                pltpu.VMEM((rows, rank), f32),
                pltpu.VMEM((rows, width), f32),
                pltpu.VMEM((rows, rank), f32),
            ],
            compiler_params=pltpu.CompilerParams(vmem_limit_bytes=56 << 20),
            name="finish",
        )(
            local, w_in, w_in, w_in, w_in, a_all, a_all, b_in, b_in, b_in, b_in, bias32.reshape(1, -1),
            tokens, cotangent, row_weight, ff, bias_ff.astype(f32).reshape(1, -1), mid_ff, b_ff,
            grad_second, dmid_up, a_all, norm_gain, dmid_out_t, grad_low,
        )
        grad_b_out = adapter_scale * grad_b_out

        def by_owner(values):
            return values.reshape(rank, dp_n, -1)

        parts = [
            by_owner(grad_a_up_t), by_owner(grad_b_ffp), by_owner(grad_a_qkv_t), by_owner(grad_a_out_t),
            by_owner(grad_a_ff_t), by_owner(jnp.concatenate([grad_b_qkv, grad_b_out, grad_b_up], axis=1)),
        ]
        widths = [p.shape[2] for p in parts]
        owned = jnp.transpose(jnp.concatenate([p.astype(bf16) for p in parts], axis=2), (1, 0, 2))
        b_at = sum(widths[:5])
        reduced = lax.psum_scatter(owned.astype(f32), "dp", scatter_dimension=0, tiled=True)
        reduced = lax.psum(reduced[0], "blk").astype(bf16)
        norm_sum = lax.psum(norm_part, ("dp", "blk"))
        grads_b = reduced[:, b_at : b_at + adapt_b.shape[1]].astype(f32)
        grads_f = reduced[:, widths[0] : widths[0] + widths[1]].astype(f32)
        fresh = jnp.concatenate(
            [
                adam_fresh(adapt_b, grads_b, mean_b, square_b),
                adam_fresh(adapt_b_ff, grads_f, mean_b_ff, square_b_ff),
            ],
            axis=1,
        ).astype(bf16)
        fresh = lax.all_gather(fresh, "dp", axis=0, tiled=False)
    grad_gain, grad_shift = norm_sum[:2], norm_sum[2:]

    state = [
        adapt_a, mean_a, square_a, keep_a,
        adapt_a_ff, mean_a_ff, square_a_ff, keep_a_ff,
        adapt_b, mean_b, square_b, keep_b,
        adapt_b_ff, mean_b_ff, square_b_ff, keep_b_ff,
    ]

    def all_of(value):
        zeros = (0,) * value.ndim
        return pl.BlockSpec(value.shape, lambda j: zeros, pipeline_mode=pl.Buffered(1))

    four = [adapt_a, adapt_a_ff, adapt_b, adapt_b_ff]
    results = [v for v in four] + [v for v in four for _ in range(2)]
    b_w, f_w = adapt_b.shape[1], adapt_b_ff.shape[1]
    owners = max(4, lanes // f_w)
    w_spec = pl.BlockSpec((kr, owners * b_w), lambda j: (0, j))
    wd_spec = pl.BlockSpec((down_rows, owners * f_w), lambda j: (0, j))
    updated = pl.pallas_call(
        functools.partial(update_kernel, rank=rank, width=width),
        grid=(dp_n // owners,),
        in_specs=[all_of(reduced), pl.BlockSpec((owners, rank, b_cols), lambda j: (j, 0, 0)), w_spec, wd_spec]
        + [all_of(v) for v in state],
        out_specs=[all_of(v) for v in results] + [w_spec, wd_spec],
        out_shape=[jax.ShapeDtypeStruct(v.shape, f32) for v in results]
        + [
            jax.ShapeDtypeStruct(frozen_input_weights.shape, bf16),
            jax.ShapeDtypeStruct(frozen_down_weight.shape, bf16),
        ],
        scratch_shapes=[pltpu.VMEM((3, kr, rank), bf16), pltpu.VMEM((down_rows, rank), bf16)],
        compiler_params=pltpu.CompilerParams(vmem_limit_bytes=48 << 20),
        name="update",
    )(reduced, fresh, frozen_input_weights, frozen_down_weight, *state)
    grad_a, grad_a_ff, grad_b, grad_b_ff = updated[:4]
    new_mean_a, new_square_a, new_mean_a_ff, new_square_a_ff = updated[4:8]
    new_mean_b, new_square_b, new_mean_b_ff, new_square_b_ff = updated[8:12]
    folded_input_weights, folded_down_weight = updated[12:]
    return (
        mixed,
        grad_tokens,
        grad_gain,
        grad_shift,
        grad_a,
        grad_a_ff,
        grad_b,
        grad_b_ff,
        new_mean_a,
        new_square_a,
        new_mean_a_ff,
        new_square_a_ff,
        new_mean_b,
        new_square_b,
        new_mean_b_ff,
        new_square_b_ff,
        folded_input_weights,
        folded_down_weight,
    )


def solution(mesh):
    in_specs = (
        P("dp", "blk", None),
        P("dp", "blk", None),
        P("dp", "blk"),
        P(),
        P("dp", None),
        P(),
        P("dp", None),
        P(),
        P(),
        P(),
        P("dp", None),
        P("dp", None),
        P(None, "dp"),
        P(None, "dp"),
        P("dp", None),
        P("dp", None),
        P(None, "dp"),
        P(None, "dp"),
        P("dp", None),
        P("dp", None),
        P(None, "dp"),
        P(None, "dp"),
        P("dp", None),
        P("dp", None),
        P(None, "dp"),
        P(None, "dp"),
    )
    out_specs = (
        P("dp", "blk", None),
        P("dp", "blk", None),
        P(),
        P(),
        P("dp", None),
        P("dp", None),
        P(None, "dp"),
        P(None, "dp"),
        P("dp", None),
        P("dp", None),
        P("dp", None),
        P("dp", None),
        P(None, "dp"),
        P(None, "dp"),
        P(None, "dp"),
        P(None, "dp"),
        P("dp", None),
        P("dp", None),
    )
    return jax.shard_map(
        functools.partial(body, mesh.shape["dp"], mesh.shape["blk"]), mesh=mesh, in_specs=in_specs, out_specs=out_specs, check_vma=False)
```

```python
import functools
import math

import jax
import jax.numpy as jnp
import numpy as np
from jax import lax
from jax.experimental import pallas as pl
from jax.experimental.pallas import tpu as pltpu
from jax.sharding import PartitionSpec as P

HEADS = 16
ROTARY = 16
DOMAINS = 22

adapter_scale = 0.25
rope_base = 10000.0
norm_eps = 1e-05
masked_score = -1e30
first_fix = 1.0 - (0.9**10) ** 10
second_fix = 1.0 - (0.999**10) ** 10

f32 = jnp.float32
bf16 = jnp.bfloat16


def nn(left, right):
    return lax.dot_general(left, right, (((1,), (0,)), ((), ())), preferred_element_type=f32)


def nt(left, right):
    return lax.dot_general(left, right, (((1,), (1,)), ((), ())), preferred_element_type=f32)


def tn(left, right):
    return lax.dot_general(left, right, (((0,), (0,)), ((), ())), preferred_element_type=f32)


def rope_lane_tables(length, depth, lanes):
    half = ROTARY // 2
    freqs = rope_base ** (-(jnp.arange(half, dtype=f32) * 2.0) / ROTARY)
    angles = jnp.arange(length, dtype=f32)[:, None] * freqs[None, :]
    cosine, sine = jnp.cos(angles), jnp.sin(angles)
    rest = depth - ROTARY
    ones, zero_half = jnp.ones((length, rest), f32), jnp.zeros((length, half), f32)
    zero_rest = jnp.zeros((length, rest), f32)
    keep = jnp.concatenate([cosine, cosine, ones], axis=1)
    from_above = jnp.concatenate([-sine, zero_half, zero_rest], axis=1)
    from_below = jnp.concatenate([zero_half, sine, zero_rest], axis=1)
    times = lanes // depth
    return tuple(jnp.tile(table, (1, times)) for table in (keep, from_above, from_below))


def turn(values, keep, above, below, sign):
    lanes = values.shape[-1]
    half = ROTARY // 2
    up = pltpu.roll(values, lanes - half, 1)
    down = pltpu.roll(values, half, 1)
    return values * keep + sign * (up * above + down * below)


def qkv_kernel(
    z_ref, x_ref, gain_ref, shift_ref, wq_ref, wk_ref, wv_ref, a_ref, b_ref, bias_ref,
    keep_ref, above_ref, below_ref, q_ref, k_ref, v_ref, first_ref, mid_ref,
):
    cols = wq_ref.shape[1]
    x = x_ref[...].reshape(x_ref.shape[2:]).astype(f32)
    centre = x - jnp.mean(x, axis=-1, keepdims=True)
    spread = jnp.mean(centre * centre, axis=-1, keepdims=True)
    first = (centre * lax.rsqrt(spread + norm_eps) * gain_ref[...] + shift_ref[...]).astype(bf16)
    mid = nn(first, a_ref[...]).astype(bf16)
    first_ref[...] = first.reshape(first_ref.shape)
    mid_ref[...] = mid.reshape(mid_ref.shape)
    low = adapter_scale * nn(mid, b_ref[...]) + bias_ref[...]
    lanes = keep_ref.shape[1]
    tables = keep_ref[...], above_ref[...], below_ref[...]
    query = nn(first, wq_ref[...]) + low[:, :cols]
    keys = nn(first, wk_ref[...]) + low[:, cols : 2 * cols]
    values = nn(first, wv_ref[...]) + low[:, 2 * cols :]
    for at in range(0, cols, lanes):
        part = slice(at, at + lanes)
        q_ref[0, :, part] = turn(query[:, part], *tables, 1.0).astype(bf16)
        k_ref[0, :, part] = turn(keys[:, part], *tables, 1.0).astype(bf16)
    v_ref[0] = values.astype(bf16)


MESH = pl.DeviceIdType.MESH


def attend_pair(query, keys, values, grad, tables, dk_ref, dv_ref, depth, blocks, store, block_done):
    lanes = keys.shape[1]
    span = keys.shape[0] // blocks
    scale = 1.0 / math.sqrt(depth)
    lane = lax.broadcasted_iota(jnp.int32, (1, lanes), 1)
    heads = lanes // depth
    masks = [jnp.where(lane // depth == h, 1.0, 0.0).astype(bf16) for h in range(heads)]
    scaled = [jnp.where(lane // depth == h, scale, 0.0).astype(bf16) for h in range(heads)]
    diagonal = lax.broadcasted_iota(jnp.int32, (span, span), 0) <= lax.broadcasted_iota(
        jnp.int32, (span, span), 1
    )
    keys_t, values_t = keys.T, values.T
    for i in range(blocks):
        done, end = i * span, (i + 1) * span
        rows = slice(done, end)
        q_i, g_i = query[rows], grad[rows]
        g_t = g_i.T
        outs, grads, lows, grads_s, q_parts, g_parts = [], [], [], [], [], []
        for h in range(heads):
            part = slice(h * depth, (h + 1) * depth)
            q_h, g_h = q_i * scaled[h], g_i * masks[h]
            last = jnp.where(diagonal, nt(keys[rows], q_h), masked_score)
            top = jnp.max(last, axis=0, keepdims=True)
            if i:
                scores = nt(keys[:done], q_h)
                top = jnp.maximum(top, jnp.max(scores, axis=0, keepdims=True))
            weights = jnp.exp(last - top)
            total = jnp.sum(weights, axis=0, keepdims=True)
            if i:
                before = jnp.exp(scores - top)
                total += jnp.sum(before, axis=0, keepdims=True)
                weights = jnp.concatenate([before, weights], axis=0)
            weights = weights * (1.0 / total)
            low = weights.astype(bf16)
            out_t = nn(values_t[part, :end], low)
            grad_p = nt(values[:end], g_h)
            delta = jnp.sum(out_t * g_t[part].astype(f32), axis=0, keepdims=True)
            grad_s = (weights * (grad_p - delta)).astype(bf16)
            outs.append(out_t)
            grads.append(nn(keys_t[part, :end], grad_s))
            lows.append(low)
            grads_s.append(grad_s)
            q_parts.append(q_h)
            g_parts.append(g_h)
        dk = nn(jnp.concatenate(grads_s, axis=1), jnp.concatenate(q_parts, axis=0))
        dv = nn(jnp.concatenate(lows, axis=1), jnp.concatenate(g_parts, axis=0))
        if i:
            dk_ref[:done] += dk[:done]
            dv_ref[:done] += dv[:done]
        dk_ref[rows] = dk[done:]
        dv_ref[rows] = dv[done:]
        store(i, 0, jnp.concatenate(outs, axis=0).T.astype(bf16))
        dq = jnp.concatenate(grads, axis=0).T * scale
        store(i, 1, turn(dq, *[t[rows] for t in tables], -1.0).astype(bf16))
        block_done(i)
    for i in range(blocks):
        rows = slice(i * span, (i + 1) * span)
        store(i, 2, turn(dk_ref[rows], *[t[rows] for t in tables], -1.0).astype(bf16))
        store(i, 3, dv_ref[rows].astype(bf16))


def normal(x):
    centre = x - jnp.mean(x, axis=-1, keepdims=True)
    return centre * lax.rsqrt(jnp.mean(centre * centre, axis=-1, keepdims=True) + norm_eps)


def front_kernel(
    tokens_ref, win_ref, wdown_ref, a_wide, aff_wide, b_wide, bff_wide,
    cot_ref, ids_ref, domain_ref, gain_ref, shift_ref, bias_ref, freq_ref,
    win_out, wdown_out, a_out, aff_out, b_out, bff_out,
    q_out, k_out, v_out, first_out, mid_out, g_out,
    low_ref, second_ref, mid_up_ref, mid_up_t_ref, dmid_ff_ref, dmid_ff_t_ref, dmid_out_t_ref,
    keep_ref, above_ref, below_ref, weight_ref,
    a_ref, aff_ref, b_ref, bff_ref, x_all, q_s, k_s, v_s, first_s, mid_s, ga, wout_v, wqkv_v, a_v, b_v, bff_v,
    sx, qx, own_sem, sr, qr, sl, ql, sd, qd, load_sem, store_sem, token_sem,
    *, n, depth,
):
    z = lax.axis_index("blk")
    dp = lax.axis_index("dp")
    y, x, c = dp // 4, lax.rem(dp // 2, 2), lax.rem(dp, 2)
    core = (dp + 1 - 2 * c, z)
    along_x = (dp + 2 - 4 * x, z)
    along_y = (dp + 4 - 8 * y, z)
    peers = [(dp, lax.rem(z + t, n)) for t in range(1, n)]
    seqs, span, width = tokens_ref.shape
    kr, down_rows, rank = win_ref.shape[0], wdown_ref.shape[0], b_ref.shape[0]
    b_w, f_w = b_ref.shape[1], bff_ref.shape[1]
    cz = q_s.shape[2]
    lanes = keep_ref.shape[1]
    four = 4 * width

    barrier = pltpu.get_barrier_semaphore()
    for peer in [core, along_x, along_y] + peers:
        pl.semaphore_signal(barrier, inc=1, device_id=peer, device_id_type=MESH)
    pl.semaphore_wait(barrier, 2 + n)

    def remote(src, dst, send, recv, peer):
        return pltpu.make_async_remote_copy(
            src_ref=src, dst_ref=dst, send_sem=send, recv_sem=recv, device_id=peer, device_id_type=MESH
        )

    shards = [
        (win_ref.at[:, :four], lambda d: win_out.at[pl.ds(pl.multiple_of(d * kr, kr), kr), :four]),
        (a_ref, lambda d: a_out.at[pl.ds(pl.multiple_of(d * kr, kr), kr), :]),
        (b_ref, lambda d: b_out.at[:, pl.ds(pl.multiple_of(d * b_w, b_w), b_w)]),
        (bff_ref, lambda d: bff_out.at[:, pl.ds(pl.multiple_of(d * f_w, f_w), f_w)]),
        (win_ref.at[:, four:], lambda d: win_out.at[pl.ds(pl.multiple_of(d * kr, kr), kr), four:]),
        (wdown_ref, lambda d: wdown_out.at[pl.ds(pl.multiple_of(d * down_rows, down_rows), down_rows), :]),
        (aff_ref, lambda d: aff_out.at[pl.ds(pl.multiple_of(d * down_rows, down_rows), down_rows), :]),
    ]
    groups = [(0, 1, 2, 3), (4,), (5, 6)]
    from_x, from_y = dp + 2 - 4 * x, dp + 4 - 8 * y
    across = dp + 2 - 4 * x + 4 - 8 * y
    onward = jnp.where(c == 0, from_y, from_x)
    target = (jnp.where(c == 0, along_x[0], along_y[0]), z)

    def hop(i, kind):
        shard, there = shards[i]
        src, dst, peer = {
            0: (shard, there(dp), along_x),
            1: (shard, there(dp), along_y),
            2: (shard, there(dp), core),
            3: (there(onward), there(onward), target),
            4: (there(from_x), there(from_x), core),
            5: (there(from_y), there(from_y), core),
            6: (there(across), there(across), core),
        }[kind]
        return remote(src, dst, sx.at[i, kind], qx.at[i, kind], peer)

    def own_copy(i):
        return pltpu.make_async_copy(shards[i][0], shards[i][1](dp), own_sem.at[i])

    def start_own(group):
        for kind in (0, 1, 2):
            for i in groups[group]:
                hop(i, kind).start()
        for i in groups[group]:
            own_copy(i).start()

    def pass_on(group):
        for i in groups[group]:
            hop(i, 0).wait_recv()
            hop(i, 1).wait_recv()
        for kind in (3, 4, 5):
            for i in groups[group]:
                hop(i, kind).start()

    def close(group):
        for i in groups[group]:
            hop(i, 3).wait_recv()
            hop(i, 6).start()

    def arrived(group):
        for i in groups[group]:
            own_copy(i).wait()
            for kind in (2, 4, 5, 6):
                hop(i, kind).wait_recv()

    def rightward(s):
        return remote(x_all.at[z - s + 1], x_all.at[z - s + 1], sr.at[s], qr.at[s], (dp, z + 1))

    def leftward(s):
        return remote(x_all.at[z + s - 1], x_all.at[z + s - 1], sl.at[s], ql.at[s], (dp, z - 1))

    def from_left(s):
        return remote(x_all.at[z - s], x_all.at[z - s], sr.at[s], qr.at[s], (dp, z - 1))

    def from_right(s):
        return remote(x_all.at[z + s], x_all.at[z + s], sl.at[s], ql.at[s], (dp, z + 1))

    def ring_start(s):
        pl.when((z < n - 1) & (z - s + 1 >= 0))(lambda: rightward(s).start())
        pl.when((z > 0) & (z + s - 1 < n))(lambda: leftward(s).start())

    def ring_wait(s):
        pl.when(z - s >= 0)(lambda: from_left(s).wait_recv())
        pl.when(z + s < n)(lambda: from_right(s).wait_recv())

    def ring_end(s):
        pl.when((z < n - 1) & (z - s + 1 >= 0))(lambda: rightward(s).wait_send())
        pl.when((z > 0) & (z + s - 1 < n))(lambda: leftward(s).wait_send())

    for low, values in ((a_ref, a_wide), (aff_ref, aff_wide), (b_ref, b_wide), (bff_ref, bff_wide)):
        low[...] = values[...].astype(bf16)
    token_copy = pltpu.make_async_copy(tokens_ref, x_all.at[z], token_sem.at[0])
    token_copy.start()
    start_own(0)
    token_copy.wait()
    ring_start(1)

    unit_lane = lax.rem(lax.broadcasted_iota(jnp.int32, (1, lanes), 1), depth)
    half = ROTARY // 2
    for b in range(n):
        rows = slice(b * span, (b + 1) * span)
        place = (lax.broadcasted_iota(jnp.int32, (span, lanes), 0) + b * span).astype(f32)
        angle = place * freq_ref[...]
        cosine, sine = jnp.cos(angle), jnp.sin(angle)
        keep_ref[rows] = jnp.where(unit_lane < ROTARY, cosine, 1.0)
        above_ref[rows] = jnp.where(unit_lane < half, -sine, 0.0)
        below_ref[rows] = jnp.where((unit_lane >= half) & (unit_lane < ROTARY), sine, 0.0)
    for q in range(seqs):
        part = slice(q * span, (q + 1) * span)
        ids = ids_ref[q : q + 1, :]
        found = jnp.zeros((1, span), f32)
        for k in range(DOMAINS):
            found = jnp.where(ids == k, domain_ref[k], found)
        weight = jnp.broadcast_to(found, (8, span)).T[:, :1]
        weight_ref[part] = weight
        low_ref[part] = (cot_ref[q].astype(f32) * weight).astype(bf16)
        unit = normal(x_all[z, q].astype(f32))
        second_ref[part] = (unit * gain_ref[1:2] + shift_ref[1:2]).astype(bf16)

    pass_on(0)
    start_own(1)
    ring_wait(1)
    if n > 2:
        ring_start(2)
    close(0)
    arrived(0)

    loads = [
        pltpu.make_async_copy(win_out.at[:, 3 * width : four], wout_v, load_sem.at[0]),
        pltpu.make_async_copy(a_out, a_v, load_sem.at[1]),
        pltpu.make_async_copy(b_out, b_v, load_sem.at[2]),
        pltpu.make_async_copy(bff_out, bff_v, load_sem.at[3]),
    ] + [
        pltpu.make_async_copy(
            win_out.at[:, pl.ds(pl.multiple_of(t * width + z * cz, cz), cz)], wqkv_v.at[t], load_sem.at[4 + t]
        )
        for t in range(3)
    ]
    for copy in loads:
        copy.start()
    for copy in loads:
        copy.wait()

    def grad_out(q, _):
        part = pl.ds(pl.multiple_of(q * span, span), span)
        low = low_ref[part, :]
        dmid = (adapter_scale * nt(low, b_v[:, 3 * width : four])).astype(bf16)
        dmid_out_t_ref[q] = dmid.T
        for g in range(n):
            rows = slice(g * cz, (g + 1) * cz)
            value = nt(low, wout_v[rows]) + nt(dmid, a_v[rows, rank : 2 * rank])
            ga[g, q] = value.astype(bf16)
        return 0

    lax.fori_loop(0, seqs, grad_out, 0)
    place_own = pl.ds(pl.multiple_of(z * span, span), span)

    def grad_send(t):
        return remote(ga.at[lax.rem(z + t, n)], g_out.at[:, place_own, :], sd.at[t], qd.at[t], peers[t - 1])

    grad_own = pltpu.make_async_copy(ga.at[z], g_out.at[:, place_own, :], token_sem.at[1])
    grad_own.start()

    def stores(b):
        rows = pl.ds(pl.multiple_of(b * span, span), span)
        return [
            pltpu.make_async_copy(src.at[:, rows, :], dst.at[:, rows, :], store_sem.at[i, b])
            for i, (src, dst) in enumerate(
                ((q_s, q_out), (k_s, k_out), (v_s, v_out), (first_s, first_out), (mid_s, mid_out))
            )
        ]

    def project_block(b):
        rows = pl.ds(pl.multiple_of(b * span, span), span)

        def one(q, _):
            first = (normal(x_all[b, q].astype(f32)) * gain_ref[0:1] + shift_ref[0:1]).astype(bf16)
            mid = nn(first, a_v[:, 0:rank]).astype(bf16)
            first_s[q, rows, :] = first
            mid_s[q, rows, :] = mid
            for t, kept in enumerate((q_s, k_s, v_s)):
                at = pl.ds(pl.multiple_of(t * width + z * cz, cz), cz)
                value = nn(first, wqkv_v[t]) + adapter_scale * nn(mid, b_v[:, at]) + bias_ref[:, at]
                if t < 2:
                    value = jnp.concatenate(
                        [
                            turn(value[:, i : i + lanes], keep_ref[rows, :], above_ref[rows, :], below_ref[rows, :], 1.0)
                            for i in range(0, cz, lanes)
                        ],
                        axis=1,
                    )
                kept[q, rows, :] = value.astype(bf16)
            return 0

        lax.fori_loop(0, seqs, one, 0)
        for copy in stores(b):
            copy.start()

    def project_near(s):
        def side(i, _):
            b = z + s * (2 * i - 1)
            pl.when((b >= 0) & (b < n) & ((s > 0) | (i == 0)))(lambda: project_block(b))
            return 0

        lax.fori_loop(0, 2, side, 0)

    def local_products(q, _):
        part = pl.ds(pl.multiple_of(q * span, span), span)
        mid = nn(second_ref[part, :], a_v[:, 2 * rank : 3 * rank]).astype(bf16)
        mid_up_ref[part, :] = mid
        mid_up_t_ref[q] = mid.T
        dmid = (adapter_scale * nt(low_ref[part, :], bff_v[...])).astype(bf16)
        dmid_ff_ref[part, :] = dmid
        dmid_ff_t_ref[q] = dmid.T
        return 0

    def walk(s, _):
        @pl.when(s == 1)
        def _():
            pass_on(1)
            start_own(2)

        @pl.when((s > 1) & (s < n))
        def _():
            ring_wait(s)
            pl.when(s + 1 < n)(lambda: ring_start(s + 1))

        @pl.when(s == 2)
        def _():
            for t in range(1, n):
                grad_send(t).start()

        project_near(s - 1)

        @pl.when(s == 2)
        def _():
            close(1)
            lax.fori_loop(0, seqs, local_products, 0)
            pass_on(2)

        return 0

    lax.fori_loop(1, n + 1, walk, 0)
    close(2)
    arrived(1)
    arrived(2)
    for i in range(len(shards)):
        for kind in range(7):
            hop(i, kind).wait_send()
    for s in range(1, n):
        ring_end(s)
    grad_own.wait()
    for t in range(1, n):
        grad_send(t).wait()
    for b in range(n):
        for copy in stores(b):
            copy.wait()


def remote(src, dst, send, recv, peer):
    return pltpu.make_async_remote_copy(
        src_ref=src, dst_ref=dst, send_sem=send, recv_sem=recv, device_id=peer, device_id_type=MESH
    )


def add_low(a, b):
    return (a.astype(f32) + b.astype(f32)).astype(bf16)


def plane():
    dp, z = lax.axis_index("dp"), lax.axis_index("blk")
    y, x, c = dp // 4, lax.rem(dp // 2, 2), lax.rem(dp, 2)
    return dp, z, y, x, c, (dp + 1 - 2 * c, z), (dp + 2 - 4 * x, z), (dp + 4 - 8 * y, z)


def greet(peers):
    barrier = pltpu.get_barrier_semaphore()
    for peer in peers:
        pl.semaphore_signal(barrier, inc=1, device_id=peer, device_id_type=MESH)
    pl.semaphore_wait(barrier, len(peers))


early_cuts = ((0, 512), (512, 1024), (1024, 1536), (1536, 2048))
late_end, a_out_at, a_ff_at, b_at_col, early_end = 256, 384, 512, 1024, 2048


class PlaneSum:
    def __init__(self, e, r1, r2a, r2b, r3a, r3b, s1, q1, s2, q2, s3, q3):
        self.refs = e, r1, r2a, r2b, r3a, r3b
        self.sems = s1, q1, s2, q2, s3, q3
        self.at = plane()
        self.half = e.shape[3] // 2

    def first(self, m):
        e, r1 = self.refs[:2]
        c, core = self.at[4], self.at[5]
        s1, q1 = self.sems[:2]
        if m < 4:
            cut = slice(late_end, early_end)
            return remote(e.at[m // 2, m % 2, 1 - c, :, cut], r1.at[m // 2, m % 2, :, cut], s1.at[m], q1.at[m], core)
        cut = slice(0, late_end)
        return remote(e.at[:, :, 1 - c, :, cut], r1.at[:, :, :, cut], s1.at[m], q1.at[m], core)

    def take_first(self, m):
        e, r1 = self.refs[:2]
        c = self.at[4]
        self.first(m).wait()
        for i in (m,) if m < 4 else range(4):
            yy, xx = i // 2, i % 2
            cut = slice(late_end, early_end) if m < 4 else slice(0, late_end)
            e[yy, xx, c, :, cut] = add_low(e[yy, xx, c, :, cut], r1[yy, xx, :, cut])

    def finish(self, out):
        e, r1, r2a, r2b, r3a, r3b = self.refs
        dp, z, y, x, c, core, along_x, along_y = self.at
        s1, q1, s2, q2, s3, q3 = self.sems
        half = self.half

        def second(k):
            cut = slice(*early_cuts[k])
            return [
                remote(e.at[:, 1 - x, c, 0:half, cut], r2a.at[:, :, cut], s2.at[0, k], q2.at[0, k], along_x),
                remote(e.at[1 - y, :, c, half:, cut], r2b.at[:, :, cut], s2.at[1, k], q2.at[1, k], along_y),
            ]

        def third(k):
            cut = slice(*early_cuts[k])
            return [
                remote(e.at[1 - y, x, c, 0:half, cut], r3a.at[:, cut], s3.at[0, k], q3.at[0, k], along_y),
                remote(e.at[y, 1 - x, c, half:, cut], r3b.at[:, cut], s3.at[1, k], q3.at[1, k], along_x),
            ]

        def after_second(k):
            cut = slice(*early_cuts[k])
            for copy in second(k):
                copy.wait()
            for i in range(2):
                e[i, x, c, 0:half, cut] = add_low(e[i, x, c, 0:half, cut], r2a[i, :, cut])
                e[y, i, c, half:, cut] = add_low(e[y, i, c, half:, cut], r2b[i, :, cut])
            for copy in third(k):
                copy.start()

        def after_third(k):
            cut = slice(*early_cuts[k])
            for copy in third(k):
                copy.wait()
            out[0:half, cut] = add_low(e[y, x, c, 0:half, cut], r3a[:, cut])
            out[half:, cut] = add_low(e[y, x, c, half:, cut], r3b[:, cut])

        count = len(early_cuts)
        for k in range(count):
            for copy in second(k):
                copy.start()
        for k in range(count + 1):
            if k < count:
                after_second(k)
            if k:
                after_third(k - 1)


def middle_kernel(
    q_ref, k_ref, v_ref, g_ref, keep_ref, above_ref, below_ref,
    second_ref, low_ref, mid_ref, mid_t_ref, dmid_ref, dmid_t_ref,
    up_ref, down_ref, a_ref, b_ref, bias_ref, *refs,
    n, pairs, steps, depth, early,
):
    if early:
        first_ref, mid_qkv_ref, a_out_ref, dmid_out_t_ref = refs[:4]
        refs = refs[4:]
        local_ref, ff_ref, back_ref, mid_ff_ref, dmid_up_ref, sum_ref = refs[:6]
        buffer, dk_ref, dv_ref, mid_acc, dmid_acc, send_sem, recv_sem, own_sem = refs[6:14]
        e_ref, dmid_seq, gb_acc, ga_acc, o_here, load_sem = refs[14:20]
        plane_refs = refs[20:]
    else:
        local_ref, own_ref, ff_ref, back_ref, mid_ff_ref, dmid_up_ref, ga_ref, gb_ref = refs[:8]
        buffer, dk_ref, dv_ref, mid_acc, dmid_acc, send_sem, recv_sem, own_sem = refs[8:]
    step = pl.program_id(0)
    z = lax.axis_index("blk")
    dp = lax.axis_index("dp")
    lanes = q_ref.shape[2]
    length = q_ref.shape[1]
    inner_block = up_ref.shape[1]
    width = up_ref.shape[0]
    cz = pairs * lanes
    if early:
        plane_sum = PlaneSum(e_ref, *plane_refs)

    def pair_place(kind, s):
        seq, pair = s // pairs, lax.rem(s, pairs)
        what = slice(2, 4) if kind else slice(0, 2)
        at = pl.ds(pl.multiple_of((z * pairs + pair) * lanes, lanes), lanes)
        return what, local_ref.at[seq, what, :, at]

    def own_copy(kind, s):
        what, target = pair_place(kind, s)
        return pltpu.make_async_copy(buffer.at[s, z, what], target, own_sem.at[kind, s])

    def away_copy(kind, s, t):
        what, target = pair_place(kind, s)
        peer = lax.rem(z + t, n)
        return remote(buffer.at[s, peer, what], target, send_sem.at[kind, s, t], recv_sem.at[kind, s, t], (dp, peer))

    def copies(kind, s):
        return [own_copy(kind, s)] + [away_copy(kind, s, t) for t in range(1, n)]

    def receive(kind):
        for s in range(steps):
            for copy in copies(kind, s):
                copy.wait()

    @pl.when(step == 0)
    def _():
        peers = [(dp, lax.rem(z + t, n)) for t in range(1, n)]
        greet((list(plane()[5:]) if early else []) + peers)

    @pl.when(step < steps)
    def _():
        def store(i, kind, value):
            buffer[step, i, kind] = value
            if kind and not early:
                own_ref[0, kind - 1, i * value.shape[0] : (i + 1) * value.shape[0], :] = value

        tables = keep_ref[...], above_ref[...], below_ref[...]

        def block_done(i):
            pl.when(i == z)(lambda: own_copy(0, step).start())
            pl.when(i != z)(lambda: away_copy(0, step, lax.rem(i - z + n, n)).start())

        attend_pair(
            q_ref[0], k_ref[0], v_ref[0], g_ref[0], tables, dk_ref, dv_ref, depth, n, store, block_done
        )
        if early:
            seq, pair = step // pairs, lax.rem(step, pairs)
            mid_t = mid_qkv_ref[0].T
            dmid = jnp.zeros((length, lanes), f32)
            for t in range(3):
                grad = buffer[step, :, t + 1].reshape(length, lanes)
                at = pl.ds(pl.multiple_of(t * width + z * cz + pair * lanes, lanes), lanes)
                dmid += nt(grad, b_ref[:, at])
                product = nn(mid_t, grad)
                gb_acc[t, pair] = jnp.where(seq == 0, product, gb_acc[t, pair] + product)
            dmid = jnp.where(pair == 0, dmid, dmid_seq[...] + dmid)
            dmid_seq[...] = dmid

            @pl.when(pair == pairs - 1)
            def _():
                product = nn((adapter_scale * dmid_seq[...]).astype(bf16).T, first_ref[0])
                ga_acc[...] = jnp.where(seq == 0, product, ga_acc[...] + product)

    @pl.when(step == steps)
    def _():
        for s in range(steps):
            own_copy(1, s).start()
            for t in range(1, n) if s % 2 else range(n - 1, 0, -1):
                away_copy(1, s, t).start()
        ff_ref[...] = jnp.zeros_like(ff_ref)
        back_ref[...] = jnp.zeros_like(back_ref)
        mid_acc[...] = jnp.zeros_like(mid_acc)
        dmid_acc[...] = jnp.zeros_like(dmid_acc)
        if early:
            for owner in range(8):
                place = (owner // 4, owner // 2 % 2, owner % 2)
                e_ref[place + (slice(None), slice(late_end, a_out_at))] = ga_acc[
                    :, owner * lanes : (owner + 1) * lanes
                ].astype(bf16)
                if owner < 3:
                    e_ref[place + (slice(None), slice(b_at_col, early_end))] = jnp.zeros((lanes, 1024), bf16)
            for t in range(3):
                for pair in range(pairs):
                    at = pl.ds(pl.multiple_of(b_at_col + z * cz + pair * lanes, lanes), lanes)
                    e_ref[0, t // 2, t % 2, :, at] = (adapter_scale * gb_acc[t, pair]).astype(bf16)

    @pl.when(step >= steps)
    def _():
        count, size = mid_t_ref.shape[0], mid_t_ref.shape[2]
        j = step - steps
        if early:
            up_b = b_ref[:, pl.ds(pl.multiple_of(4 * width + j * inner_block, inner_block), inner_block)]
        else:
            up_b = b_ref[...]
        ga, gb = None, None
        for at in range(count):
            rows = slice(at * size, (at + 1) * size)
            pre = nn(second_ref[rows], up_ref[...]) + bias_ref[...] + adapter_scale * nn(mid_ref[rows], up_b)
            cdf = 0.5 + 0.5 * lax.erf(pre * (1.0 / math.sqrt(2.0)))
            hidden = (pre * cdf).astype(bf16)
            slope = cdf + pre * (jnp.exp(-0.5 * pre * pre) * (1.0 / math.sqrt(2.0 * math.pi)))
            grad_hidden = nt(low_ref[rows], down_ref[...]) + nt(dmid_ref[rows], a_ref[...])
            dup = (slope * grad_hidden).astype(bf16)
            ff_ref[rows] += nn(hidden, down_ref[...])
            back_ref[rows] += nt(dup, up_ref[...])
            mid_acc[rows] += nn(hidden, a_ref[...])
            dmid_acc[rows] += nt(dup, up_b)
            ga_part = nn(dmid_t_ref[at], hidden)
            gb_part = nn(mid_t_ref[at], dup)
            ga = ga_part if ga is None else ga + ga_part
            gb = gb_part if gb is None else gb + gb_part
        if early:
            e_ref[j // 4, lax.rem(j // 2, 2), lax.rem(j, 2), :, a_ff_at:b_at_col] = ga.astype(bf16)
            at = pl.ds(pl.multiple_of(b_at_col + lax.rem(j, 2) * inner_block, lanes), inner_block)
            e_ref[1, j // 4, lax.rem(j // 2, 2), :, at] = (adapter_scale * gb).astype(bf16)

            @pl.when(j == 2)
            def _():
                receive(0)
                load = pltpu.make_async_copy(local_ref.at[:, 0], o_here, load_sem.at[0])
                load.start()
                load.wait()
                ga_out, gb_out = None, None
                for q in range(count):
                    rows = slice(q * size, (q + 1) * size)
                    out = o_here[q]
                    mid = nn(out, a_out_ref[...]).astype(bf16)
                    ga_part = nn(dmid_out_t_ref[q], out)
                    gb_part = nn(mid.T, low_ref[rows])
                    ga_out = ga_part if ga_out is None else ga_out + ga_part
                    gb_out = gb_part if gb_out is None else gb_out + gb_part
                e_ref[0, 1, 1, :, b_at_col:early_end] = (adapter_scale * gb_out).astype(bf16)
                for owner in range(8):
                    at = slice(owner * lanes, (owner + 1) * lanes)
                    e_ref[owner // 4, owner // 2 % 2, owner % 2, :, a_out_at:a_ff_at] = ga_out[:, at].astype(bf16)

            for m, (begin, take) in enumerate(((3, 5), (4, 6), (5, 7))):
                pl.when(j == begin)(lambda m=m: plane_sum.first(m).start())
                pl.when(j == take)(lambda m=m: plane_sum.take_first(m))
            pl.when(j == 7)(lambda: plane_sum.first(3).start())
        else:
            ga_ref[...] = ga
            gb_ref[...] = gb

    @pl.when(step == pl.num_programs(0) - 1)
    def _():
        mid_ff_ref[...] = mid_acc[...].astype(bf16)
        dmid_up_ref[...] = (adapter_scale * dmid_acc[...]).astype(bf16)
        if early:
            count, size = mid_t_ref.shape[0], mid_t_ref.shape[2]
            ga, gb = None, None
            for at in range(count):
                rows = slice(at * size, (at + 1) * size)
                ga_part = nn(dmid_up_ref[rows].T, second_ref[rows])
                gb_part = nn(mid_ff_ref[rows].T, low_ref[rows])
                ga = ga_part if ga is None else ga + ga_part
                gb = gb_part if gb is None else gb + gb_part
            for owner in range(8):
                place = (owner // 4, owner // 2 % 2, owner % 2, slice(None))
                at = slice(owner * lanes, (owner + 1) * lanes)
                e_ref[place + (slice(0, lanes),)] = ga[:, at].astype(bf16)
                e_ref[place + (slice(lanes, late_end),)] = (adapter_scale * gb[:, at]).astype(bf16)
            plane_sum.first(4).start()
            plane_sum.take_first(3)
            plane_sum.take_first(4)
            plane_sum.finish(sum_ref)
        if not early:
            receive(0)
        receive(1)


def finish_kernel(
    local_ref, wo_ref, wq_ref, wk_ref, wv_ref, a_out_ref, a_qkv_ref, b_out_ref, bq_ref, bk_ref, bv_ref,
    bias_ref, x_ref, cot_ref, weight_ref, ff_ref, bias_ff_ref, mid_ff_ref, b_ff_ref,
    second_ref, dmid_up_ref, a_up_ref, gain_ref, dmid_out_t_ref, low_ref,
    mixed_ref, tokens_ref, norm_ref, ga_ref, gb_ref,
    att_acc, mid_acc, first_acc, dmid_acc,
):
    t = pl.program_id(0)
    rows = x_ref.shape[0] * x_ref.shape[1]
    cols = wq_ref.shape[1]

    @pl.when(t == 0)
    def _():
        att_acc[...] = jnp.zeros_like(att_acc)
        mid_acc[...] = jnp.zeros_like(mid_acc)
        first_acc[...] = jnp.zeros_like(first_acc)
        dmid_acc[...] = jnp.zeros_like(dmid_acc)

    out, dq, dk, dv = (local_ref[:, i].reshape(rows, cols) for i in range(4))
    att_acc[...] += nn(out, wo_ref[...])
    mid_acc[...] += nn(out, a_out_ref[...])
    first_acc[...] += nt(dq, wq_ref[...]) + nt(dk, wk_ref[...]) + nt(dv, wv_ref[...])
    dmid_acc[...] += nt(dq, bq_ref[...]) + nt(dk, bk_ref[...]) + nt(dv, bv_ref[...])
    size = x_ref.shape[1]
    ga_ref[...] = sum(nn(dmid_out_t_ref[q], out[q * size : (q + 1) * size]) for q in range(x_ref.shape[0]))

    @pl.when(t == pl.num_programs(0) - 1)
    def _():
        size = x_ref.shape[1]
        norm = [jnp.zeros((1, first_acc.shape[1]), f32) for _ in range(4)]
        for q in range(x_ref.shape[0]):
            part = slice(q * size, (q + 1) * size)
            x = x_ref[q].astype(f32)
            mid = mid_acc[part].astype(bf16)
            gb = tn(mid, low_ref[part])
            gb_ref[...] = gb if q == 0 else gb_ref[...] + gb
            att = att_acc[part] + bias_ref[...] + adapter_scale * nn(mid, b_out_ref[...])
            ff = ff_ref[part] + bias_ff_ref[...] + adapter_scale * nn(mid_ff_ref[part], b_ff_ref[...])
            mixed_ref[q] = (x + att + ff).astype(bf16)
            dmid = (adapter_scale * dmid_acc[part]).astype(bf16)
            grad_first = first_acc[part] + nt(dmid, a_qkv_ref[...])
            grad_second = second_ref[part] + nt(dmid_up_ref[part], a_up_ref[...])
            centre = x - jnp.mean(x, axis=-1, keepdims=True)
            inv = lax.rsqrt(jnp.mean(centre * centre, axis=-1, keepdims=True) + norm_eps)
            unit = centre * inv
            pulled = grad_first * gain_ref[0:1] + grad_second * gain_ref[1:2]
            back = inv * (
                pulled
                - jnp.mean(pulled, axis=-1, keepdims=True)
                - unit * jnp.mean(pulled * unit, axis=-1, keepdims=True)
            )
            row_grad = cot_ref[q].astype(f32) * weight_ref[part]
            tokens_ref[q] = (row_grad + back).astype(bf16)
            for k, value in enumerate((grad_first * unit, grad_second * unit, grad_first, grad_second)):
                norm[k] += jnp.sum(value, axis=0, keepdims=True)
        norm_ref[...] = jnp.concatenate(norm, axis=0)


def tail_kernel(
    o_ref, dq_ref, dk_ref, dv_ref, wo_ref, wq_ref, wk_ref, wv_ref, a_out_ref, a_qkv_ref, b_out_ref,
    bq_ref, bk_ref, bv_ref, bias_ref, x_ref, cot_ref, weight_ref, ff_ref, bias_ff_ref, mid_ff_ref, b_ff_ref,
    second_ref, dmid_up_ref, a_up_ref, gain_ref,
    e_ref, b_ref, mean_ref, square_ref, bf_ref, mean_f_ref, square_f_ref,
    mixed_ref, tokens_ref, out_hbm, norm_ref, fresh_hbm,
    out_ref, fresh_ref, att_acc, mid_acc, first_acc, dmid_acc,
    r4, nr, nsum,
    s4, q4, s5, q5, sf, qf, sn, qn, sg, qg, done_sem,
    *, n,
):
    step = pl.program_id(0)
    dp, z, y, x, c, core, along_x, along_y = plane()
    peers = [(dp, lax.rem(z + t, n)) for t in range(1, n)]
    seqs, size, width = o_ref.shape[0], o_ref.shape[2], x_ref.shape[2]
    rows, cols = seqs * size, o_ref.shape[3]
    outs = width // cols
    grads = width // dq_ref.shape[3]
    first_seq = outs + grads
    rank = e_ref.shape[0]
    part = rank // n
    lanes = 128
    mine = pl.ds(pl.multiple_of(z * part, part), part)

    def to_part(t):
        return pl.ds(pl.multiple_of(lax.rem(z + t, n) * part, part), part)

    def e_out(k, t):
        cut = slice(*early_cuts[k])
        return remote(e_ref.at[to_part(t), cut], r4.at[t, :, cut], s4.at[t, k], q4.at[t, k], peers[t - 1])

    def e_back(k, t):
        cut = slice(*early_cuts[k])
        return remote(out_ref.at[mine, cut], out_ref.at[mine, cut], s5.at[t, k], q5.at[t, k], peers[t - 1])

    count = len(early_cuts)

    def fresh_back(t):
        return remote(fresh_ref.at[dp, mine, :], fresh_ref.at[dp, mine, :], sf.at[t], qf.at[t], peers[t - 1])

    from_x, from_y, from_c = along_x[0], along_y[0], core[0]
    across = from_x + from_y - dp
    onward = jnp.where(c == 0, from_y, from_x)
    target = (jnp.where(c == 0, from_x, from_y), z)
    other = 1 - 2 * c
    hops = [
        (dp, from_x, along_x), (dp, from_y, along_y), (dp, from_c, core), (onward, across, target),
        (from_x, from_x + other, core), (from_y, from_y + other, core), (across, across + other, core),
    ]

    middle_row = rank // 2
    parts = (slice(0, middle_row), slice(middle_row, rank))

    def gather(kind, p):
        slot, _, peer = hops[kind]
        there = fresh_ref.at[slot, parts[p], :]
        return remote(there, there, sg.at[p, kind], qg.at[p, kind], peer)

    def fresh_rows(value, grad_b):
        cut = b_ref.shape[1]
        new_b = adam_fresh(b_ref[mine, :], grad_b, mean_ref[mine, :], square_ref[mine, :])
        new_f = adam_fresh(bf_ref[mine, :], value, mean_f_ref[mine, :], square_f_ref[mine, :])
        fresh_ref[dp, mine, :] = jnp.concatenate([new_b, new_f], axis=1).astype(bf16)

    def norm_copy(i, peer):
        return remote(nsum.at[i], nr.at[i], sn.at[i], qn.at[i], peer)

    norm_stages = [norm_copy(0, core), norm_copy(1, along_x), norm_copy(2, along_y)]
    norm_last = [
        remote(nsum.at[3], nr.at[2 + t], sn.at[2 + t], qn.at[2 + t], peers[t - 1]) for t in range(1, n)
    ]

    def norm_take(i):
        norm_stages[i].wait()
        nsum[i + 1] = nsum[i] + nr[i]

    @pl.when(step == 0)
    def _():
        greet([core, along_x, along_y] + peers)
        for k in range(count):
            for t in range(1, n):
                e_out(k, t).start()
        att_acc[...] = jnp.zeros_like(att_acc)
        mid_acc[...] = jnp.zeros_like(mid_acc)
        first_acc[...] = jnp.zeros_like(first_acc)
        dmid_acc[...] = jnp.zeros_like(dmid_acc)

    @pl.when(step < outs)
    def _():
        out = o_ref[...].reshape(rows, cols)
        att_acc[...] += nn(out, wo_ref[...])
        mid_acc[...] += nn(out, a_out_ref[...])

    @pl.when((step >= outs) & (step < first_seq))
    def _():
        dq, dk, dv = (r[...].reshape(rows, r.shape[3]) for r in (dq_ref, dk_ref, dv_ref))
        first_acc[...] += nt(dq, wq_ref[...]) + nt(dk, wk_ref[...]) + nt(dv, wv_ref[...])
        dmid_acc[...] += nt(dq, bq_ref[...]) + nt(dk, bk_ref[...]) + nt(dv, bv_ref[...])

    @pl.when(step == outs)
    def _():
        for k in range(count):
            cut = slice(*early_cuts[k])
            for t in range(1, n):
                e_out(k, t).wait()
            value = e_ref[mine, cut].astype(f32)
            for t in range(1, n):
                value += r4[t, :, cut].astype(f32)
            out_ref[mine, cut] = value.astype(bf16)
        fresh_rows(out_ref[mine, lanes:late_end].astype(f32), out_ref[mine, b_at_col:early_end].astype(f32))
        for t in range(1, n):
            fresh_back(t).start()

    @pl.when(step == first_seq - 1)
    def _():
        for t in range(1, n):
            fresh_back(t).wait()
        for p in range(2):
            for kind in (0, 1, 2):
                gather(kind, p).start()
        for k in range(count):
            for t in range(1, n):
                e_back(k, t).start()

    @pl.when(step >= first_seq)
    def _():
        q = step - first_seq
        at = pl.ds(pl.multiple_of(q * size, size), size)
        x_in = x_ref[0].astype(f32)
        mid = mid_acc[at, :].astype(bf16)
        att = att_acc[at, :] + bias_ref[...] + adapter_scale * nn(mid, b_out_ref[...])
        ff = ff_ref[...] + bias_ff_ref[...] + adapter_scale * nn(mid_ff_ref[at, :], b_ff_ref[...])
        mixed_ref[0] = (x_in + att + ff).astype(bf16)
        dmid = (adapter_scale * dmid_acc[at, :]).astype(bf16)
        grad_first = first_acc[at, :] + nt(dmid, a_qkv_ref[...])
        grad_second = second_ref[...] + nt(dmid_up_ref[at, :], a_up_ref[...])
        centre = x_in - jnp.mean(x_in, axis=-1, keepdims=True)
        inv = lax.rsqrt(jnp.mean(centre * centre, axis=-1, keepdims=True) + norm_eps)
        unit = centre * inv
        pulled = grad_first * gain_ref[0:1] + grad_second * gain_ref[1:2]
        back = inv * (
            pulled
            - jnp.mean(pulled, axis=-1, keepdims=True)
            - unit * jnp.mean(pulled * unit, axis=-1, keepdims=True)
        )
        row_grad = cot_ref[0].astype(f32) * weight_ref[at, :]
        tokens_ref[0] = (row_grad + back).astype(bf16)
        norm = [
            jnp.sum(value, axis=0, keepdims=True)
            for value in (grad_first * unit, grad_second * unit, grad_first, grad_second)
        ]
        norm = jnp.concatenate(norm, axis=0)
        nsum[0] = jnp.where(q == 0, norm, nsum[0] + norm)

    @pl.when(step == pl.num_programs(0) - 1)
    def _():
        norm_stages[0].start()
        for p in range(2):
            gather(0, p).wait_recv()
            gather(1, p).wait_recv()
            for kind in (3, 4, 5):
                gather(kind, p).start()
            norm_take(p)
            norm_stages[p + 1].start()
        for p in range(2):
            gather(3, p).wait_recv()
            gather(6, p).start()
        norm_take(2)
        for copy in norm_last:
            copy.start()
        for k in range(count):
            for t in range(1, n):
                e_back(k, t).wait()

        keep_out = pltpu.make_async_copy(out_ref, out_hbm, done_sem.at[0])
        keep_out.start()
        for p in range(2):
            for kind in (2, 4, 5, 6):
                gather(kind, p).wait_recv()
        keep_fresh = pltpu.make_async_copy(fresh_ref, fresh_hbm, done_sem.at[1])
        keep_fresh.start()
        for p in range(2):
            for kind in range(7):
                gather(kind, p).wait_send()
        for copy in norm_last:
            copy.wait()
        keep_out.wait()
        keep_fresh.wait()
        value = jnp.zeros_like(nsum[3])
        for blk in range(n):
            there = lax.rem(z - blk + n, n)
            value += jnp.where(there == 0, nsum[3], nr[2 + jnp.maximum(there, 1)])
        norm_ref[...] = value


def update_kernel(
    g_ref, fresh_ref, w_ref, wd_ref, *refs, rank, width,
):
    params, outs = refs[:16], refs[16:30]
    a_new, aff_new = refs[30:]
    j = pl.program_id(0)
    cols = w_ref.shape[1]

    @pl.when(j == 0)
    def _():
        rows, inner = params[0].shape[0], params[4].shape[0]
        got = g_ref[...].astype(f32)
        cut, cut_f = params[8].shape[1], params[12].shape[1]
        up = got[:, :rows]
        qkv = got[:, rows + cut_f : 2 * rows + cut_f]
        out = got[:, 2 * rows + cut_f : 3 * rows + cut_f]
        at = 3 * rows + cut_f
        grads = [
            jnp.concatenate([part.T for part in (qkv, out, up)], axis=1),
            got[:, at : at + inner].T,
            got[:, at + inner : at + inner + cut],
            got[:, rows : rows + cut_f],
        ]
        for i, grad in enumerate(grads):
            param, mean, square, keep = (r[...] for r in params[4 * i : 4 * i + 4])
            mean_new = 0.9 * mean + 0.1 * grad
            square_new = 0.999 * square + 0.001 * grad * grad
            kept = keep.astype(f32)
            outs[i][...] = grad
            outs[4 + 2 * i][...] = mean_new * kept
            outs[5 + 2 * i][...] = square_new * kept
            if i < 2:
                fresh = param - 0.01 * (mean_new / first_fix) / (jnp.sqrt(square_new / second_fix) + 1e-08)
                if i == 0:
                    for k in range(3):
                        a_new[k] = fresh[:, k * rank : (k + 1) * rank].astype(bf16)
                else:
                    aff_new[...] = fresh.astype(bf16)

    cut = params[8].shape[1]
    fresh = [fresh_ref[i] for i in range(fresh_ref.shape[0])]
    update = []
    for i, part in enumerate(fresh):
        at = j * cols + i * cut
        block = jnp.where(at < 3 * width, 0, jnp.where(at < 4 * width, 1, 2))
        update.append(nn(a_new[block], part[:, :cut]))
    update = jnp.concatenate(update, axis=1)
    outs[12][...] = (w_ref[...].astype(f32) + adapter_scale * update).astype(bf16)
    update = nn(aff_new[...], jnp.concatenate([f[:, cut:] for f in fresh], axis=1))
    outs[13][...] = (wd_ref[...].astype(f32) + adapter_scale * update).astype(bf16)


def adam_fresh(param, grad, mean, square):
    mean_new = 0.9 * mean + 0.1 * grad
    square_new = 0.999 * square + 0.001 * grad * grad
    return param - 0.01 * (mean_new / first_fix) / (jnp.sqrt(square_new / second_fix) + 1e-08)


def body(
    dp_n,
    n,
    tokens,
    cotangent,
    domain_ids,
    domain_weight,
    frozen_input_weights,
    bias_in,
    frozen_down_weight,
    bias_ff,
    norm_gain,
    norm_shift,
    adapt_a,
    adapt_a_ff,
    adapt_b,
    adapt_b_ff,
    mean_a,
    mean_a_ff,
    mean_b,
    mean_b_ff,
    square_a,
    square_a_ff,
    square_b,
    square_b_ff,
    keep_a,
    keep_a_ff,
    keep_b,
    keep_b_ff,
):
    seqs, span, width = tokens.shape
    rows = seqs * span
    rank = adapt_b.shape[0]
    depth = width // HEADS
    cz = width // n
    length = n * span
    z = lax.axis_index("blk")
    z_arr = jnp.full((1,), z, jnp.int32)
    kr = frozen_input_weights.shape[0]
    down_rows, inner = frozen_down_weight.shape[0], frozen_down_weight.shape[0] * dp_n
    lanes = 128

    def shift_by(values, s):
        return lax.ppermute(values, "blk", [(i, (i + s) % n) for i in range(n)])

    b_cols = adapt_b.shape[1] + adapt_b_ff.shape[1]
    bias32 = bias_in.astype(f32)
    whole_front = dp_n == 8 and n == 4 and seqs > 1 and (rank, width, inner) == (128, 1024, 4096)
    if whole_front:
        vmem = pl.BlockSpec(memory_space=pltpu.VMEM)
        hbm = pl.BlockSpec(memory_space=pl.ANY)
        dma = pltpu.SemaphoreType.DMA
        half = ROTARY // 2
        freq = [rope_base ** (-(k * 2.0) / ROTARY) for k in range(half)]
        freq = np.tile(np.array(freq + freq + [0.0] * (depth - ROTARY), np.float32), lanes // depth)

        def shape(*dims, dtype=bf16):
            return jax.ShapeDtypeStruct(dims, dtype)

        (
            w_in, w_down, a_all, a_ff, b_in, b_ff, query, keys, values, first_pos, mid_pos, g_pos,
            grad_low, second, mid_up, mid_up_t, dmid_ff, dmid_ff_t, dmid_out_t, *tables, row_weight,
        ) = pl.pallas_call(
            functools.partial(front_kernel, n=n, depth=depth),
            in_specs=[hbm] * 3 + [vmem] * 6 + [pl.BlockSpec(memory_space=pltpu.SMEM)] + [vmem] * 4,
            out_specs=[hbm] * 12 + [vmem] * 11,
            out_shape=[
                shape(width, 8 * width), shape(inner, width), shape(width, 3 * rank), shape(inner, rank),
                shape(rank, 8 * width), shape(rank, width),
                shape(seqs, length, cz), shape(seqs, length, cz), shape(seqs, length, cz),
                shape(seqs, length, width), shape(seqs, length, rank), shape(seqs, length, cz),
                shape(rows, width), shape(rows, width),
                shape(rows, rank), shape(seqs, rank, span), shape(rows, rank), shape(seqs, rank, span),
                shape(seqs, rank, span),
                shape(length, lanes, dtype=f32), shape(length, lanes, dtype=f32), shape(length, lanes, dtype=f32),
                shape(rows, 1, dtype=f32),
            ],
            scratch_shapes=[
                pltpu.VMEM(adapt_a.shape, bf16),
                pltpu.VMEM(adapt_a_ff.shape, bf16),
                pltpu.VMEM(adapt_b.shape, bf16),
                pltpu.VMEM(adapt_b_ff.shape, bf16),
                pltpu.VMEM((n, seqs, span, width), bf16),
                pltpu.VMEM((seqs, length, cz), bf16),
                pltpu.VMEM((seqs, length, cz), bf16),
                pltpu.VMEM((seqs, length, cz), bf16),
                pltpu.VMEM((seqs, length, width), bf16),
                pltpu.VMEM((seqs, length, rank), bf16),
                pltpu.VMEM((n, seqs, span, cz), bf16),
                pltpu.VMEM((width, width), bf16),
                pltpu.VMEM((3, width, cz), bf16),
                pltpu.VMEM((width, 3 * rank), bf16),
                pltpu.VMEM((rank, 8 * width), bf16),
                pltpu.VMEM((rank, width), bf16),
                dma((7, 7)), dma((7, 7)), dma((7,)),
                dma((n,)), dma((n,)), dma((n,)), dma((n,)), dma((n,)), dma((n,)),
                dma((7,)), dma((5, n)), dma((2,)),
            ],
            compiler_params=pltpu.CompilerParams(
                collective_id=2, has_side_effects=True, vmem_limit_bytes=58 << 20
            ),
            name="front",
        )(
            tokens, frozen_input_weights, frozen_down_weight,
            adapt_a, adapt_a_ff, adapt_b, adapt_b_ff,
            cotangent, domain_ids, domain_weight, norm_gain, norm_shift, bias32.reshape(1, -1), freq.reshape(1, -1),
        )
    else:
        lookup = (domain_ids[..., None] == jnp.arange(DOMAINS, dtype=jnp.int32)).astype(f32)
        row_weight = jnp.sum(lookup * domain_weight, axis=-1).reshape(rows, 1)
        row_grad = cotangent.astype(f32).reshape(rows, width) * row_weight
        grad_low = row_grad.astype(bf16)
        b_shard = jnp.concatenate([adapt_b, adapt_b_ff], axis=1).astype(bf16)
        one = jnp.concatenate(
            [frozen_input_weights[:, : 4 * width], adapt_a.astype(bf16), b_shard.reshape(kr, -1)], axis=1
        )
        one = lax.all_gather(one, "dp", axis=0, tiled=True)
        two = lax.all_gather(frozen_input_weights[:, 4 * width :], "dp", axis=0, tiled=True)
        three = jnp.concatenate([frozen_down_weight, adapt_a_ff.astype(bf16)], axis=1)
        three = lax.all_gather(three, "dp", axis=0, tiled=True)
        a_at = 4 * width
        b_at = a_at + 3 * rank
        a_all = one[:, a_at:b_at]
        b_all = one[:, b_at:].reshape(dp_n, rank, b_cols)
        b_in = jnp.transpose(b_all[:, :, : adapt_b.shape[1]], (1, 0, 2)).reshape(rank, -1)
        b_ff = jnp.transpose(b_all[:, :, adapt_b.shape[1] :], (1, 0, 2)).reshape(rank, width)
        w_out = one[:, 3 * width : 4 * width]
        w_up = two
        w_down, a_ff = three[:, :width], three[:, width:]

        right, left = tokens, tokens
        rights, lefts = [None], [None]
        for s in range(1, n):
            right = lax.ppermute(right, "blk", [(i, i + 1) for i in range(n - 1)])
            left = lax.ppermute(left, "blk", [(i + 1, i) for i in range(n - 1)])
            rights.append(right)
            lefts.append(left)
        x_all = jnp.stack(
            [tokens] + [jnp.where(z >= s, rights[s], lefts[n - s]) for s in range(1, n)]
        )

        b_out = b_in[:, 3 * width : 4 * width]
        a_out = a_all[:, rank : 2 * rank]
        dmid_out = (adapter_scale * nt(grad_low, b_out)).astype(bf16)
        grad_att = (nt(grad_low, w_out) + nt(dmid_out, a_out)).astype(bf16)
        grad_att = jnp.transpose(grad_att.reshape(seqs, span, n, cz), (2, 0, 1, 3))

        def piece(values, s):
            return lax.dynamic_index_in_dim(values, lax.rem(z + s, n), 0, keepdims=False)

        g_all = jnp.stack(
            [piece(grad_att, 0)] + [shift_by(piece(grad_att, s), s) for s in range(1, n)]
        )

        tables = rope_lane_tables(length, depth, lanes)
        own = [lax.dynamic_slice_in_dim(b_in[:, t * width : (t + 1) * width], z * cz, cz, 1) for t in range(3)]
        b_own = jnp.concatenate(own, axis=1)
        bias_own = jnp.concatenate(
            [lax.dynamic_slice_in_dim(bias32, t * width + z * cz, cz, 0) for t in range(3)]
        ).reshape(1, 3 * cz)

        def block_of(s, z_ref):
            return lax.rem(z_ref[0] - s + n, n)

        table_spec = pl.BlockSpec((span, lanes), lambda s, q, z_ref: (block_of(s, z_ref), 0))
        head_spec = pl.BlockSpec((1, span, cz), lambda s, q, z_ref: (q, block_of(s, z_ref), 0))
        query, keys, values, first_all, mid_all = pl.pallas_call(
            qkv_kernel,
            grid_spec=pltpu.PrefetchScalarGridSpec(
                num_scalar_prefetch=1,
                grid=(n, seqs),
                in_specs=[
                    pl.BlockSpec((1, 1, span, width), lambda s, q, z_ref: (s, q, 0, 0)),
                    pl.BlockSpec((1, width), lambda s, q, z_ref: (0, 0)),
                    pl.BlockSpec((1, width), lambda s, q, z_ref: (0, 0)),
                    pl.BlockSpec((width, cz), lambda s, q, z_ref: (0, z_ref[0])),
                    pl.BlockSpec((width, cz), lambda s, q, z_ref: (0, n + z_ref[0])),
                    pl.BlockSpec((width, cz), lambda s, q, z_ref: (0, 2 * n + z_ref[0])),
                    pl.BlockSpec((width, rank), lambda s, q, z_ref: (0, a_at // rank)),
                    pl.BlockSpec((rank, 3 * cz), lambda s, q, z_ref: (0, 0)),
                    pl.BlockSpec((1, 3 * cz), lambda s, q, z_ref: (0, 0)),
                    table_spec,
                    table_spec,
                    table_spec,
                ],
                out_specs=[
                    head_spec,
                    head_spec,
                    head_spec,
                    pl.BlockSpec((1, 1, span, width), lambda s, q, z_ref: (block_of(s, z_ref), q, 0, 0)),
                    pl.BlockSpec((1, 1, span, rank), lambda s, q, z_ref: (block_of(s, z_ref), q, 0, 0)),
                ],
            ),
            out_shape=[jax.ShapeDtypeStruct((seqs, length, cz), bf16)] * 3
            + [
                jax.ShapeDtypeStruct((n, seqs, span, width), bf16),
                jax.ShapeDtypeStruct((n, seqs, span, rank), bf16),
            ],
            compiler_params=pltpu.CompilerParams(vmem_limit_bytes=48 << 20),
            cost_estimate=pl.CostEstimate(
                flops=2 * n * rows * width * 4 * cz, bytes_accessed=6 * n * rows * width, transcendentals=0
            ),
            name="qkv",
        )(
            z_arr, x_all, norm_gain[0:1], norm_shift[0:1], one, one, one, one, b_own, bias_own, *tables
        )

        input_rows = tokens.astype(f32).reshape(rows, width)
        centre = input_rows - jnp.mean(input_rows, axis=-1, keepdims=True)
        inv = lax.rsqrt(jnp.mean(centre * centre, axis=-1, keepdims=True) + norm_eps)
        second = (centre * inv * norm_gain[1] + norm_shift[1]).astype(bf16)
        a_up = a_all[:, 2 * rank :]
        mid_up = nn(second, a_up).astype(bf16)
        dmid_ff = (adapter_scale * nt(grad_low, b_ff)).astype(bf16)
        g_pos = jnp.concatenate([g_all, g_all])
        g_pos = lax.rev(g_pos, (0,))
        g_pos = lax.dynamic_slice_in_dim(g_pos, lax.rem(n - 1 - z + n, n), n, 0)
        g_pos = jnp.transpose(g_pos, (1, 0, 2, 3)).reshape(seqs, length, cz)

        first_pos = jnp.transpose(first_all, (1, 0, 2, 3))
        mid_pos = jnp.transpose(mid_all, (1, 0, 2, 3))
        w_in = jnp.concatenate([one[:, :a_at], two], axis=1)
        mid_up_t, dmid_ff_t, dmid_out_t = (
            jnp.transpose(v.reshape(seqs, span, rank), (0, 2, 1)) for v in (mid_up, dmid_ff, dmid_out)
        )

    pairs = cz // lanes
    steps = seqs * pairs
    inner_block = min(512, inner)
    def one_buffer(shape):
        zeros = (0,) * len(shape)
        return pl.BlockSpec(shape, lambda s: zeros, pipeline_mode=pl.Buffered(1))

    def seq_pair(s):
        s = jnp.minimum(s, steps - 1)
        return s // pairs, lax.rem(s, pairs)

    def head_map(s):
        seq, pair = seq_pair(s)
        return seq, 0, pair

    def inner_at(s):
        return jnp.maximum(s - steps, 0)

    head = pl.BlockSpec((1, length, lanes), head_map)
    early = whole_front
    dma = pltpu.SemaphoreType.DMA
    half_rank = rank // 2

    def wide(*dims, dtype=bf16):
        return jax.ShapeDtypeStruct(dims, dtype)

    in_specs = (
        [head] * 4
        + [one_buffer((length, lanes))] * 3
        + [one_buffer((rows, width))] * 2
        + [one_buffer((rows, rank)), one_buffer((seqs, rank, span))] * 2
        + [
            pl.BlockSpec((width, inner_block), lambda s: (0, 4 * width // inner_block + inner_at(s))),
            pl.BlockSpec((inner_block, width), lambda s: (inner_at(s), 0)),
            pl.BlockSpec((inner_block, rank), lambda s: (inner_at(s), 0)),
            one_buffer((rank, 8 * width))
            if early
            else pl.BlockSpec((rank, inner_block), lambda s: (0, 4 * width // inner_block + inner_at(s))),
            pl.BlockSpec((1, inner_block), lambda s: (0, 4 * width // inner_block + inner_at(s))),
        ]
    )
    operands = [
        query, keys, values, g_pos, *tables, second, grad_low, mid_up, mid_up_t, dmid_ff, dmid_ff_t,
        w_in, w_down, a_ff, b_in, bias32.reshape(1, -1),
    ]
    partial_specs = [one_buffer((rows, width))] * 2 + [one_buffer((rows, rank))] * 2
    partial_shapes = [wide(rows, width, dtype=f32)] * 2 + [wide(rows, rank)] * 2
    local_spec, local_shape = pl.BlockSpec(memory_space=pl.ANY), wide(seqs, 4, span, width)
    scratch = [
        pltpu.VMEM((steps, n, 4, span, lanes), bf16),
        pltpu.VMEM((length, lanes), f32),
        pltpu.VMEM((length, lanes), f32),
        pltpu.VMEM((rows, rank), f32),
        pltpu.VMEM((rows, rank), f32),
        dma((2, steps, n)),
        dma((2, steps, n)),
        dma((2, steps)),
    ]
    if early:
        in_specs += [
            pl.BlockSpec((1, length, width), lambda s: (seq_pair(s)[0], 0, 0)),
            pl.BlockSpec((1, length, rank), lambda s: (seq_pair(s)[0], 0, 0)),
        ]
        in_specs += [
            pl.BlockSpec((width, rank), lambda s: (0, 1), pipeline_mode=pl.Buffered(1)),
            one_buffer((seqs, rank, span)),
        ]
        operands += [first_pos, mid_pos, a_all, dmid_out_t]
        out_specs = [local_spec] + partial_specs + [one_buffer((rank, early_end))]
        out_shapes = [local_shape] + partial_shapes + [wide(rank, early_end)]
        cuts = len(early_cuts)
        scratch += [
            pltpu.VMEM((2, 2, 2, rank, early_end), bf16),
            pltpu.VMEM((length, rank), f32),
            pltpu.VMEM((3, pairs, rank, lanes), f32),
            pltpu.VMEM((rank, width), f32),
            pltpu.VMEM((seqs, span, width), bf16),
            dma((1,)),
            pltpu.VMEM((2, 2, rank, early_end), bf16),
            pltpu.VMEM((2, half_rank, early_end), bf16),
            pltpu.VMEM((2, half_rank, early_end), bf16),
            pltpu.VMEM((half_rank, early_end), bf16),
            pltpu.VMEM((half_rank, early_end), bf16),
            dma((5,)), dma((5,)), dma((2, cuts)), dma((2, cuts)), dma((2, cuts)), dma((2, cuts)),
        ]
    else:
        out_specs = (
            [local_spec, pl.BlockSpec((1, 3, length, lanes), lambda s: (seq_pair(s)[0], 0, 0, seq_pair(s)[1]))]
            + partial_specs
            + [pl.BlockSpec((rank, inner_block), lambda s: (0, inner_at(s)))] * 2
        )
        out_shapes = (
            [local_shape, wide(seqs, 3, length, cz)] + partial_shapes + [wide(rank, inner, dtype=f32)] * 2
        )
    middle = pl.pallas_call(
        functools.partial(middle_kernel, n=n, pairs=pairs, steps=steps, depth=depth, early=early),
        grid=(steps + inner // inner_block,),
        in_specs=in_specs,
        out_specs=out_specs,
        out_shape=out_shapes,
        scratch_shapes=scratch,
        compiler_params=pltpu.CompilerParams(
            collective_id=0, has_side_effects=True, vmem_limit_bytes=60 << 20
        ),
        name="middle",
    )(*operands)

    if early:
        local, ff, grad_second, mid_ff, dmid_up, summed = middle
        part = rank // n

        def single(shape, *at):
            return pl.BlockSpec(shape, lambda s: at, pipeline_mode=pl.Buffered(1))

        wide_block = width // 2

        def of_out(s):
            return jnp.minimum(s, 1)

        def of_grad(s):
            return jnp.clip(s - 2, 0, n - 1)

        def of_seq(s):
            return jnp.maximum(s - 2 - n, 0)

        def piece_spec(kind):
            return pl.BlockSpec((seqs, 1, span, cz), lambda s: (0, kind, 0, of_grad(s)))

        def columns(kind, height):
            return pl.BlockSpec((height, cz), lambda s: (0, kind * n + of_grad(s)))

        full = pl.BlockSpec((1, span, width), lambda s: (of_seq(s), 0, 0))
        flat = pl.BlockSpec((span, width), lambda s: (of_seq(s), 0))
        cuts = len(early_cuts)
        b_here = [adapt_b, mean_b, square_b, adapt_b_ff, mean_b_ff, square_b_ff]
        mixed, grad_tokens, reduced, norm_sum, fresh = pl.pallas_call(
            functools.partial(tail_kernel, n=n),
            grid=(2 + n + seqs,),
            in_specs=[
                pl.BlockSpec((seqs, 1, span, wide_block), lambda s: (0, 0, 0, of_out(s))),
                piece_spec(1), piece_spec(2), piece_spec(3),
                pl.BlockSpec((wide_block, width), lambda s: (of_out(s), 3)),
                columns(0, width), columns(1, width), columns(2, width),
                pl.BlockSpec((wide_block, rank), lambda s: (of_out(s), 1)),
                single((width, rank), 0, 0),
                single((rank, width), 0, 3),
                columns(0, rank), columns(1, rank), columns(2, rank),
                single((1, width), 0, 3),
                full, full,
                single((rows, 1), 0, 0),
                flat,
                single((1, width), 0, 0),
                single((rows, rank), 0, 0),
                single((rank, width), 0, 0),
                flat,
                single((rows, rank), 0, 0),
                single((width, rank), 0, 2),
                single((2, width), 0, 0),
                single((rank, early_end), 0, 0),
            ]
            + [single(v.shape, 0, 0) for v in b_here],
            out_specs=[
                full, full, pl.BlockSpec(memory_space=pl.ANY), single((4, width), 0, 0),
                pl.BlockSpec(memory_space=pl.ANY),
            ],
            out_shape=[
                wide(seqs, span, width), wide(seqs, span, width), wide(rank, 2048), wide(4, width, dtype=f32),
                wide(dp_n, rank, b_cols),
            ],
            scratch_shapes=[
                pltpu.VMEM((rank, 2048), bf16),
                pltpu.VMEM((dp_n, rank, b_cols), bf16),
                pltpu.VMEM((rows, width), f32),
                pltpu.VMEM((rows, rank), f32),
                pltpu.VMEM((rows, width), f32),
                pltpu.VMEM((rows, rank), f32),
                pltpu.VMEM((n, part, early_end), bf16),
                pltpu.VMEM((2 + n, 4, width), f32),
                pltpu.VMEM((4, 4, width), f32),
                dma((n, cuts)), dma((n, cuts)), dma((n, cuts)), dma((n, cuts)), dma((n,)), dma((n,)),
                dma((2 + n,)), dma((2 + n,)), dma((2, 7)), dma((2, 7)), dma((2,)),
            ],
            compiler_params=pltpu.CompilerParams(
                collective_id=1, has_side_effects=True, vmem_limit_bytes=58 << 20
            ),
            name="tail",
        )(
            local, local, local, local, w_in, w_in, w_in, w_in, a_all, a_all, b_in, b_in, b_in, b_in,
            bias32.reshape(1, -1), tokens, cotangent, row_weight, ff, bias_ff.astype(f32).reshape(1, -1), mid_ff, b_ff,
            grad_second, dmid_up, a_all, norm_gain, summed, *b_here,
        )
    else:
        local, own, ff, grad_second, mid_ff, dmid_up, grad_a_ff_t, grad_b_up = middle
        grad_b_up = adapter_scale * grad_b_up
        first_pos = first_pos.reshape(seqs * length, width)
        mid_pos = mid_pos.reshape(seqs * length, rank)
        b_own = jnp.concatenate(
            [lax.dynamic_slice_in_dim(b_in[:, t * width : (t + 1) * width], z * cz, cz, 1) for t in range(3)], axis=1
        )
        djoint_own = [own[:, t].reshape(seqs * length, cz) for t in range(3)]
        dmid_own = sum(nt(djoint_own[t], b_own[:, t * cz : (t + 1) * cz]) for t in range(3))
        dmid_own = (adapter_scale * dmid_own).astype(bf16)
        grad_a_qkv_t = tn(dmid_own, first_pos)
        mine = (jnp.arange(n, dtype=jnp.int32) == z)[None, :, None]
        grad_b_qkv = jnp.concatenate(
            [
                jnp.where(mine, adapter_scale * tn(mid_pos, part)[:, None, :], 0.0).reshape(rank, width)
                for part in djoint_own
            ],
            axis=1,
        )
        grad_a_up_t = tn(dmid_up, second)
        grad_b_ffp = adapter_scale * tn(mid_ff, grad_low)

        def fixed(shape, *at):
            return pl.BlockSpec(shape, lambda t: at, pipeline_mode=pl.Buffered(1))

        def column(at, height):
            return pl.BlockSpec((height, cz), lambda t: (0, at * n + t))

        mixed, grad_tokens, norm_part, grad_a_out_t, grad_b_out = pl.pallas_call(
            finish_kernel,
            grid=(n,),
            in_specs=[
                pl.BlockSpec((seqs, 4, span, cz), lambda t: (0, 0, 0, t)),
                pl.BlockSpec((cz, width), lambda t: (t, 3)),
                column(0, width), column(1, width), column(2, width),
                pl.BlockSpec((cz, rank), lambda t: (t, 1)),
                fixed((width, rank), 0, 0),
                fixed((rank, width), 0, 3),
                column(0, rank), column(1, rank), column(2, rank),
                fixed((1, width), 0, 3),
                fixed((seqs, span, width), 0, 0, 0),
                fixed((seqs, span, width), 0, 0, 0),
                fixed((rows, 1), 0, 0),
                fixed((rows, width), 0, 0),
                fixed((1, width), 0, 0),
                fixed((rows, rank), 0, 0),
                fixed((rank, width), 0, 0),
                fixed((rows, width), 0, 0),
                fixed((rows, rank), 0, 0),
                fixed((width, rank), 0, 2),
                fixed((2, width), 0, 0),
                fixed((seqs, rank, span), 0, 0, 0),
                fixed((rows, width), 0, 0),
            ],
            out_specs=[
                fixed((seqs, span, width), 0, 0, 0),
                fixed((seqs, span, width), 0, 0, 0),
                fixed((4, width), 0, 0),
                pl.BlockSpec((rank, cz), lambda t: (0, t)),
                fixed((rank, width), 0, 0),
            ],
            out_shape=[
                jax.ShapeDtypeStruct((seqs, span, width), bf16),
                jax.ShapeDtypeStruct((seqs, span, width), bf16),
                jax.ShapeDtypeStruct((4, width), f32),
                jax.ShapeDtypeStruct((rank, width), f32),
                jax.ShapeDtypeStruct((rank, width), f32),
            ],
            scratch_shapes=[
                pltpu.VMEM((rows, width), f32),
                pltpu.VMEM((rows, rank), f32),
                pltpu.VMEM((rows, width), f32),
                pltpu.VMEM((rows, rank), f32),
            ],
            compiler_params=pltpu.CompilerParams(vmem_limit_bytes=56 << 20),
            name="finish",
        )(
            local, w_in, w_in, w_in, w_in, a_all, a_all, b_in, b_in, b_in, b_in, bias32.reshape(1, -1),
            tokens, cotangent, row_weight, ff, bias_ff.astype(f32).reshape(1, -1), mid_ff, b_ff,
            grad_second, dmid_up, a_all, norm_gain, dmid_out_t, grad_low,
        )
        grad_b_out = adapter_scale * grad_b_out

        def by_owner(values):
            return values.reshape(rank, dp_n, -1)

        parts = [
            by_owner(grad_a_up_t), by_owner(grad_b_ffp), by_owner(grad_a_qkv_t), by_owner(grad_a_out_t),
            by_owner(grad_a_ff_t), by_owner(jnp.concatenate([grad_b_qkv, grad_b_out, grad_b_up], axis=1)),
        ]
        widths = [p.shape[2] for p in parts]
        owned = jnp.transpose(jnp.concatenate([p.astype(bf16) for p in parts], axis=2), (1, 0, 2))
        b_at = sum(widths[:5])
        reduced = lax.psum_scatter(owned.astype(f32), "dp", scatter_dimension=0, tiled=True)
        reduced = lax.psum(reduced[0], "blk").astype(bf16)
        norm_sum = lax.psum(norm_part, ("dp", "blk"))
        grads_b = reduced[:, b_at : b_at + adapt_b.shape[1]].astype(f32)
        grads_f = reduced[:, widths[0] : widths[0] + widths[1]].astype(f32)
        fresh = jnp.concatenate(
            [
                adam_fresh(adapt_b, grads_b, mean_b, square_b),
                adam_fresh(adapt_b_ff, grads_f, mean_b_ff, square_b_ff),
            ],
            axis=1,
        ).astype(bf16)
        fresh = lax.all_gather(fresh, "dp", axis=0, tiled=False)
    grad_gain, grad_shift = norm_sum[:2], norm_sum[2:]

    state = [
        adapt_a, mean_a, square_a, keep_a,
        adapt_a_ff, mean_a_ff, square_a_ff, keep_a_ff,
        adapt_b, mean_b, square_b, keep_b,
        adapt_b_ff, mean_b_ff, square_b_ff, keep_b_ff,
    ]

    def all_of(value):
        zeros = (0,) * value.ndim
        return pl.BlockSpec(value.shape, lambda j: zeros, pipeline_mode=pl.Buffered(1))

    four = [adapt_a, adapt_a_ff, adapt_b, adapt_b_ff]
    results = [v for v in four] + [v for v in four for _ in range(2)]
    b_w, f_w = adapt_b.shape[1], adapt_b_ff.shape[1]
    owners = max(4, lanes // f_w)
    w_spec = pl.BlockSpec((kr, owners * b_w), lambda j: (0, j))
    wd_spec = pl.BlockSpec((down_rows, owners * f_w), lambda j: (0, j))
    updated = pl.pallas_call(
        functools.partial(update_kernel, rank=rank, width=width),
        grid=(dp_n // owners,),
        in_specs=[all_of(reduced), pl.BlockSpec((owners, rank, b_cols), lambda j: (j, 0, 0)), w_spec, wd_spec]
        + [all_of(v) for v in state],
        out_specs=[all_of(v) for v in results] + [w_spec, wd_spec],
        out_shape=[jax.ShapeDtypeStruct(v.shape, f32) for v in results]
        + [
            jax.ShapeDtypeStruct(frozen_input_weights.shape, bf16),
            jax.ShapeDtypeStruct(frozen_down_weight.shape, bf16),
        ],
        scratch_shapes=[pltpu.VMEM((3, kr, rank), bf16), pltpu.VMEM((down_rows, rank), bf16)],
        compiler_params=pltpu.CompilerParams(vmem_limit_bytes=48 << 20),
        name="update",
    )(reduced, fresh, frozen_input_weights, frozen_down_weight, *state)
    grad_a, grad_a_ff, grad_b, grad_b_ff = updated[:4]
    new_mean_a, new_square_a, new_mean_a_ff, new_square_a_ff = updated[4:8]
    new_mean_b, new_square_b, new_mean_b_ff, new_square_b_ff = updated[8:12]
    folded_input_weights, folded_down_weight = updated[12:]
    return (
        mixed,
        grad_tokens,
        grad_gain,
        grad_shift,
        grad_a,
        grad_a_ff,
        grad_b,
        grad_b_ff,
        new_mean_a,
        new_square_a,
        new_mean_a_ff,
        new_square_a_ff,
        new_mean_b,
        new_square_b,
        new_mean_b_ff,
        new_square_b_ff,
        folded_input_weights,
        folded_down_weight,
    )


def solution(mesh):
    in_specs = (
        P("dp", "blk", None),
        P("dp", "blk", None),
        P("dp", "blk"),
        P(),
        P("dp", None),
        P(),
        P("dp", None),
        P(),
        P(),
        P(),
        P("dp", None),
        P("dp", None),
        P(None, "dp"),
        P(None, "dp"),
        P("dp", None),
        P("dp", None),
        P(None, "dp"),
        P(None, "dp"),
        P("dp", None),
        P("dp", None),
        P(None, "dp"),
        P(None, "dp"),
        P("dp", None),
        P("dp", None),
        P(None, "dp"),
        P(None, "dp"),
    )
    out_specs = (
        P("dp", "blk", None),
        P("dp", "blk", None),
        P(),
        P(),
        P("dp", None),
        P("dp", None),
        P(None, "dp"),
        P(None, "dp"),
        P("dp", None),
        P("dp", None),
        P("dp", None),
        P("dp", None),
        P(None, "dp"),
        P(None, "dp"),
        P(None, "dp"),
        P(None, "dp"),
        P("dp", None),
        P("dp", None),
    )
    return jax.shard_map(
        functools.partial(body, mesh.shape["dp"], mesh.shape["blk"]), mesh=mesh, in_specs=in_specs, out_specs=out_specs, check_vma=False)
```

```python
import functools
import math

import jax
import jax.numpy as jnp
import numpy as np
from jax import lax
from jax.experimental import pallas as pl
from jax.experimental.pallas import tpu as pltpu
from jax.sharding import PartitionSpec as P

HEADS = 16
ROTARY = 16
DOMAINS = 22

adapter_scale = 0.25
rope_base = 10000.0
norm_eps = 1e-05
masked_score = -1e30
first_fix = 1.0 - (0.9**10) ** 10
second_fix = 1.0 - (0.999**10) ** 10

f32 = jnp.float32
bf16 = jnp.bfloat16


def nn(left, right):
    return lax.dot_general(left, right, (((1,), (0,)), ((), ())), preferred_element_type=f32)


def nt(left, right):
    return lax.dot_general(left, right, (((1,), (1,)), ((), ())), preferred_element_type=f32)


def tn(left, right):
    return lax.dot_general(left, right, (((0,), (0,)), ((), ())), preferred_element_type=f32)


def rope_lane_tables(length, depth, lanes):
    half = ROTARY // 2
    freqs = rope_base ** (-(jnp.arange(half, dtype=f32) * 2.0) / ROTARY)
    angles = jnp.arange(length, dtype=f32)[:, None] * freqs[None, :]
    cosine, sine = jnp.cos(angles), jnp.sin(angles)
    rest = depth - ROTARY
    ones, zero_half = jnp.ones((length, rest), f32), jnp.zeros((length, half), f32)
    zero_rest = jnp.zeros((length, rest), f32)
    keep = jnp.concatenate([cosine, cosine, ones], axis=1)
    from_above = jnp.concatenate([-sine, zero_half, zero_rest], axis=1)
    from_below = jnp.concatenate([zero_half, sine, zero_rest], axis=1)
    times = lanes // depth
    return tuple(jnp.tile(table, (1, times)) for table in (keep, from_above, from_below))


def turn(values, keep, above, below, sign):
    lanes = values.shape[-1]
    half = ROTARY // 2
    up = pltpu.roll(values, lanes - half, 1)
    down = pltpu.roll(values, half, 1)
    return values * keep + sign * (up * above + down * below)


def qkv_kernel(
    z_ref, x_ref, gain_ref, shift_ref, wq_ref, wk_ref, wv_ref, a_ref, b_ref, bias_ref,
    keep_ref, above_ref, below_ref, q_ref, k_ref, v_ref, first_ref, mid_ref,
):
    cols = wq_ref.shape[1]
    x = x_ref[...].reshape(x_ref.shape[2:]).astype(f32)
    centre = x - jnp.mean(x, axis=-1, keepdims=True)
    spread = jnp.mean(centre * centre, axis=-1, keepdims=True)
    first = (centre * lax.rsqrt(spread + norm_eps) * gain_ref[...] + shift_ref[...]).astype(bf16)
    mid = nn(first, a_ref[...]).astype(bf16)
    first_ref[...] = first.reshape(first_ref.shape)
    mid_ref[...] = mid.reshape(mid_ref.shape)
    low = adapter_scale * nn(mid, b_ref[...]) + bias_ref[...]
    lanes = keep_ref.shape[1]
    tables = keep_ref[...], above_ref[...], below_ref[...]
    query = nn(first, wq_ref[...]) + low[:, :cols]
    keys = nn(first, wk_ref[...]) + low[:, cols : 2 * cols]
    values = nn(first, wv_ref[...]) + low[:, 2 * cols :]
    for at in range(0, cols, lanes):
        part = slice(at, at + lanes)
        q_ref[0, :, part] = turn(query[:, part], *tables, 1.0).astype(bf16)
        k_ref[0, :, part] = turn(keys[:, part], *tables, 1.0).astype(bf16)
    v_ref[0] = values.astype(bf16)


MESH = pl.DeviceIdType.MESH


def attend_pair(query, keys, values, grad, tables, dk_ref, dv_ref, depth, blocks, store, block_done):
    lanes = keys.shape[1]
    span = keys.shape[0] // blocks
    scale = 1.0 / math.sqrt(depth)
    lane = lax.broadcasted_iota(jnp.int32, (1, lanes), 1)
    heads = lanes // depth
    masks = [jnp.where(lane // depth == h, 1.0, 0.0).astype(bf16) for h in range(heads)]
    scaled = [jnp.where(lane // depth == h, scale, 0.0).astype(bf16) for h in range(heads)]
    diagonal = lax.broadcasted_iota(jnp.int32, (span, span), 0) <= lax.broadcasted_iota(
        jnp.int32, (span, span), 1
    )
    keys_t, values_t = keys.T, values.T
    for i in range(blocks):
        done, end = i * span, (i + 1) * span
        rows = slice(done, end)
        q_i, g_i = query[rows], grad[rows]
        g_t = g_i.T
        outs, grads, lows, grads_s, q_parts, g_parts = [], [], [], [], [], []
        for h in range(heads):
            part = slice(h * depth, (h + 1) * depth)
            q_h, g_h = q_i * scaled[h], g_i * masks[h]
            last = jnp.where(diagonal, nt(keys[rows], q_h), masked_score)
            top = jnp.max(last, axis=0, keepdims=True)
            if i:
                scores = nt(keys[:done], q_h)
                top = jnp.maximum(top, jnp.max(scores, axis=0, keepdims=True))
            weights = jnp.exp(last - top)
            total = jnp.sum(weights, axis=0, keepdims=True)
            if i:
                before = jnp.exp(scores - top)
                total += jnp.sum(before, axis=0, keepdims=True)
                weights = jnp.concatenate([before, weights], axis=0)
            weights = weights * (1.0 / total)
            low = weights.astype(bf16)
            out_t = nn(values_t[part, :end], low)
            grad_p = nt(values[:end], g_h)
            delta = jnp.sum(out_t * g_t[part].astype(f32), axis=0, keepdims=True)
            grad_s = (weights * (grad_p - delta)).astype(bf16)
            outs.append(out_t)
            grads.append(nn(keys_t[part, :end], grad_s))
            lows.append(low)
            grads_s.append(grad_s)
            q_parts.append(q_h)
            g_parts.append(g_h)
        dk = nn(jnp.concatenate(grads_s, axis=1), jnp.concatenate(q_parts, axis=0))
        dv = nn(jnp.concatenate(lows, axis=1), jnp.concatenate(g_parts, axis=0))
        if i:
            dk_ref[:done] += dk[:done]
            dv_ref[:done] += dv[:done]
        dk_ref[rows] = dk[done:]
        dv_ref[rows] = dv[done:]
        store(i, 0, jnp.concatenate(outs, axis=0).T.astype(bf16))
        dq = jnp.concatenate(grads, axis=0).T * scale
        store(i, 1, turn(dq, *[t[rows] for t in tables], -1.0).astype(bf16))
        block_done(i)
    for i in range(blocks):
        rows = slice(i * span, (i + 1) * span)
        store(i, 2, turn(dk_ref[rows], *[t[rows] for t in tables], -1.0).astype(bf16))
        store(i, 3, dv_ref[rows].astype(bf16))


def normal(x):
    centre = x - jnp.mean(x, axis=-1, keepdims=True)
    return centre * lax.rsqrt(jnp.mean(centre * centre, axis=-1, keepdims=True) + norm_eps)


def front_kernel(
    tokens_ref, win_ref, wdown_ref, a_wide, aff_wide, b_wide, bff_wide,
    cot_ref, ids_ref, domain_ref, gain_ref, shift_ref, bias_ref, freq_ref,
    win_out, wdown_out, a_out, aff_out, b_out, bff_out,
    q_out, k_out, v_out, first_out, mid_out, g_out,
    low_ref, second_ref, mid_up_ref, mid_up_t_ref, dmid_ff_ref, dmid_ff_t_ref, dmid_out_t_ref,
    keep_ref, above_ref, below_ref, weight_ref,
    a_ref, aff_ref, b_ref, bff_ref, x_all, q_s, k_s, v_s, first_s, mid_s, ga, wout_v, wqkv_v, a_v, b_v, bff_v,
    sx, qx, own_sem, sr, qr, sl, ql, sd, qd, load_sem, store_sem, token_sem,
    *, n, depth,
):
    z = lax.axis_index("blk")
    dp = lax.axis_index("dp")
    y, x, c = dp // 4, lax.rem(dp // 2, 2), lax.rem(dp, 2)
    core = (dp + 1 - 2 * c, z)
    along_x = (dp + 2 - 4 * x, z)
    along_y = (dp + 4 - 8 * y, z)
    peers = [(dp, lax.rem(z + t, n)) for t in range(1, n)]
    seqs, span, width = tokens_ref.shape
    kr, down_rows, rank = win_ref.shape[0], wdown_ref.shape[0], b_ref.shape[0]
    b_w, f_w = b_ref.shape[1], bff_ref.shape[1]
    cz = q_s.shape[2]
    lanes = keep_ref.shape[1]
    four = 4 * width

    barrier = pltpu.get_barrier_semaphore()
    for peer in [core, along_x, along_y] + peers:
        pl.semaphore_signal(barrier, inc=1, device_id=peer, device_id_type=MESH)
    pl.semaphore_wait(barrier, 2 + n)

    def remote(src, dst, send, recv, peer):
        return pltpu.make_async_remote_copy(
            src_ref=src, dst_ref=dst, send_sem=send, recv_sem=recv, device_id=peer, device_id_type=MESH
        )

    shards = [
        (win_ref.at[:, :four], lambda d: win_out.at[pl.ds(pl.multiple_of(d * kr, kr), kr), :four]),
        (a_ref, lambda d: a_out.at[pl.ds(pl.multiple_of(d * kr, kr), kr), :]),
        (b_ref, lambda d: b_out.at[:, pl.ds(pl.multiple_of(d * b_w, b_w), b_w)]),
        (bff_ref, lambda d: bff_out.at[:, pl.ds(pl.multiple_of(d * f_w, f_w), f_w)]),
        (win_ref.at[:, four:], lambda d: win_out.at[pl.ds(pl.multiple_of(d * kr, kr), kr), four:]),
        (wdown_ref, lambda d: wdown_out.at[pl.ds(pl.multiple_of(d * down_rows, down_rows), down_rows), :]),
        (aff_ref, lambda d: aff_out.at[pl.ds(pl.multiple_of(d * down_rows, down_rows), down_rows), :]),
    ]
    groups = [(0, 1, 2, 3), (4,), (5, 6)]
    from_x, from_y = dp + 2 - 4 * x, dp + 4 - 8 * y
    across = dp + 2 - 4 * x + 4 - 8 * y
    onward = jnp.where(c == 0, from_y, from_x)
    target = (jnp.where(c == 0, along_x[0], along_y[0]), z)

    def hop(i, kind):
        shard, there = shards[i]
        src, dst, peer = {
            0: (shard, there(dp), along_x),
            1: (shard, there(dp), along_y),
            2: (shard, there(dp), core),
            3: (there(onward), there(onward), target),
            4: (there(from_x), there(from_x), core),
            5: (there(from_y), there(from_y), core),
            6: (there(across), there(across), core),
        }[kind]
        return remote(src, dst, sx.at[i, kind], qx.at[i, kind], peer)

    def own_copy(i):
        return pltpu.make_async_copy(shards[i][0], shards[i][1](dp), own_sem.at[i])

    def start_own(group):
        for kind in (0, 1, 2):
            for i in groups[group]:
                hop(i, kind).start()
        for i in groups[group]:
            own_copy(i).start()

    def pass_on(group):
        for i in groups[group]:
            hop(i, 0).wait_recv()
            hop(i, 1).wait_recv()
        for kind in (3, 4, 5):
            for i in groups[group]:
                hop(i, kind).start()

    def close(group):
        for i in groups[group]:
            hop(i, 3).wait_recv()
            hop(i, 6).start()

    def arrived(group):
        for i in groups[group]:
            own_copy(i).wait()
            for kind in (2, 4, 5, 6):
                hop(i, kind).wait_recv()

    def token_hop(block, q, send, recv, s, to):
        return remote(x_all.at[block, q], x_all.at[block, q], send.at[s, q], recv.at[s, q], (dp, to))

    def rightward(s, q):
        return token_hop(z - s + 1, q, sr, qr, s, z + 1)

    def leftward(s, q):
        return token_hop(z + s - 1, q, sl, ql, s, z - 1)

    def from_left(s, q):
        return token_hop(z - s, q, sr, qr, s, z - 1)

    def from_right(s, q):
        return token_hop(z + s, q, sl, ql, s, z + 1)

    def ring_start(s):
        for q in range(seqs):
            pl.when((z < n - 1) & (z - s + 1 >= 0))(lambda q=q: rightward(s, q).start())
            pl.when((z > 0) & (z + s - 1 < n))(lambda q=q: leftward(s, q).start())

    def ring_wait(s):
        for q in range(seqs):
            pl.when(z - s >= 0)(lambda q=q: from_left(s, q).wait_recv())
            pl.when(z + s < n)(lambda q=q: from_right(s, q).wait_recv())

    def ring_end(s):
        for q in range(seqs):
            pl.when((z < n - 1) & (z - s + 1 >= 0))(lambda q=q: rightward(s, q).wait_send())
            pl.when((z > 0) & (z + s - 1 < n))(lambda q=q: leftward(s, q).wait_send())

    for low, values in ((a_ref, a_wide), (aff_ref, aff_wide), (b_ref, b_wide), (bff_ref, bff_wide)):
        low[...] = values[...].astype(bf16)
    token_copy = pltpu.make_async_copy(tokens_ref, x_all.at[z], token_sem.at[0])
    token_copy.start()
    start_own(0)
    token_copy.wait()
    ring_start(1)

    unit_lane = lax.rem(lax.broadcasted_iota(jnp.int32, (1, lanes), 1), depth)
    half = ROTARY // 2
    for b in range(n):
        rows = slice(b * span, (b + 1) * span)
        place = (lax.broadcasted_iota(jnp.int32, (span, lanes), 0) + b * span).astype(f32)
        angle = place * freq_ref[...]
        cosine, sine = jnp.cos(angle), jnp.sin(angle)
        keep_ref[rows] = jnp.where(unit_lane < ROTARY, cosine, 1.0)
        above_ref[rows] = jnp.where(unit_lane < half, -sine, 0.0)
        below_ref[rows] = jnp.where((unit_lane >= half) & (unit_lane < ROTARY), sine, 0.0)
    for q in range(seqs):
        part = slice(q * span, (q + 1) * span)
        ids = ids_ref[q : q + 1, :]
        found = jnp.zeros((1, span), f32)
        for k in range(DOMAINS):
            found = jnp.where(ids == k, domain_ref[k], found)
        weight = jnp.broadcast_to(found, (8, span)).T[:, :1]
        weight_ref[part] = weight
        low_ref[part] = (cot_ref[q].astype(f32) * weight).astype(bf16)
        unit = normal(x_all[z, q].astype(f32))
        second_ref[part] = (unit * gain_ref[1:2] + shift_ref[1:2]).astype(bf16)

    pass_on(0)
    start_own(1)
    ring_wait(1)
    if n > 2:
        ring_start(2)
    close(0)
    arrived(0)

    loads = [
        pltpu.make_async_copy(win_out.at[:, 3 * width : four], wout_v, load_sem.at[0]),
        pltpu.make_async_copy(a_out, a_v, load_sem.at[1]),
        pltpu.make_async_copy(b_out, b_v, load_sem.at[2]),
        pltpu.make_async_copy(bff_out, bff_v, load_sem.at[3]),
    ] + [
        pltpu.make_async_copy(
            win_out.at[:, pl.ds(pl.multiple_of(t * width + z * cz, cz), cz)], wqkv_v.at[t], load_sem.at[4 + t]
        )
        for t in range(3)
    ]
    for copy in loads:
        copy.start()
    for copy in loads:
        copy.wait()

    def grad_out(q, _):
        part = pl.ds(pl.multiple_of(q * span, span), span)
        low = low_ref[part, :]
        dmid = (adapter_scale * nt(low, b_v[:, 3 * width : four])).astype(bf16)
        dmid_out_t_ref[q] = dmid.T
        for g in range(n):
            rows = slice(g * cz, (g + 1) * cz)
            value = nt(low, wout_v[rows]) + nt(dmid, a_v[rows, rank : 2 * rank])
            ga[g, q] = value.astype(bf16)
        return 0

    lax.fori_loop(0, seqs, grad_out, 0)
    place_own = pl.ds(pl.multiple_of(z * span, span), span)

    def grad_send(t):
        return remote(ga.at[lax.rem(z + t, n)], g_out.at[:, place_own, :], sd.at[t], qd.at[t], peers[t - 1])

    grad_own = pltpu.make_async_copy(ga.at[z], g_out.at[:, place_own, :], token_sem.at[1])
    grad_own.start()

    def stores(b):
        rows = pl.ds(pl.multiple_of(b * span, span), span)
        return [
            pltpu.make_async_copy(src.at[:, rows, :], dst.at[:, rows, :], store_sem.at[i, b])
            for i, (src, dst) in enumerate(
                ((q_s, q_out), (k_s, k_out), (v_s, v_out), (first_s, first_out), (mid_s, mid_out))
            )
        ]

    def project_block(b):
        rows = pl.ds(pl.multiple_of(b * span, span), span)

        def one(q, _):
            pl.when(b == z - n + 1)(lambda: from_left(n - 1, q).wait_recv())
            pl.when(b == z + n - 1)(lambda: from_right(n - 1, q).wait_recv())
            first = (normal(x_all[b, q].astype(f32)) * gain_ref[0:1] + shift_ref[0:1]).astype(bf16)
            mid = nn(first, a_v[:, 0:rank]).astype(bf16)
            first_s[q, rows, :] = first
            mid_s[q, rows, :] = mid
            for t, kept in enumerate((q_s, k_s, v_s)):
                at = pl.ds(pl.multiple_of(t * width + z * cz, cz), cz)
                value = nn(first, wqkv_v[t]) + adapter_scale * nn(mid, b_v[:, at]) + bias_ref[:, at]
                if t < 2:
                    value = jnp.concatenate(
                        [
                            turn(value[:, i : i + lanes], keep_ref[rows, :], above_ref[rows, :], below_ref[rows, :], 1.0)
                            for i in range(0, cz, lanes)
                        ],
                        axis=1,
                    )
                kept[q, rows, :] = value.astype(bf16)
            return 0

        lax.fori_loop(0, seqs, one, 0)
        for copy in stores(b):
            copy.start()

    def project_near(s):
        def side(i, _):
            b = z + s * (2 * i - 1)
            pl.when((b >= 0) & (b < n) & ((s > 0) | (i == 0)))(lambda: project_block(b))
            return 0

        lax.fori_loop(0, 2, side, 0)

    def local_products(q, _):
        part = pl.ds(pl.multiple_of(q * span, span), span)
        mid = nn(second_ref[part, :], a_v[:, 2 * rank : 3 * rank]).astype(bf16)
        mid_up_ref[part, :] = mid
        mid_up_t_ref[q] = mid.T
        dmid = (adapter_scale * nt(low_ref[part, :], bff_v[...])).astype(bf16)
        dmid_ff_ref[part, :] = dmid
        dmid_ff_t_ref[q] = dmid.T
        return 0

    def walk(s, _):
        @pl.when(s == 1)
        def _():
            pass_on(1)
            start_own(2)

        @pl.when((s > 1) & (s < n - 1))
        def _():
            ring_wait(s)
            ring_start(s + 1)

        @pl.when(s == 2)
        def _():
            for t in range(1, n):
                grad_send(t).start()

        project_near(s - 1)

        @pl.when(s == 2)
        def _():
            close(1)
            lax.fori_loop(0, seqs, local_products, 0)
            pass_on(2)

        return 0

    lax.fori_loop(1, n + 1, walk, 0)
    close(2)
    arrived(1)
    arrived(2)
    for i in range(len(shards)):
        for kind in range(7):
            hop(i, kind).wait_send()
    for s in range(1, n):
        ring_end(s)
    grad_own.wait()
    for t in range(1, n):
        grad_send(t).wait()
    for b in range(n):
        for copy in stores(b):
            copy.wait()


def remote(src, dst, send, recv, peer):
    return pltpu.make_async_remote_copy(
        src_ref=src, dst_ref=dst, send_sem=send, recv_sem=recv, device_id=peer, device_id_type=MESH
    )


def add_low(a, b):
    return (a.astype(f32) + b.astype(f32)).astype(bf16)


def plane():
    dp, z = lax.axis_index("dp"), lax.axis_index("blk")
    y, x, c = dp // 4, lax.rem(dp // 2, 2), lax.rem(dp, 2)
    return dp, z, y, x, c, (dp + 1 - 2 * c, z), (dp + 2 - 4 * x, z), (dp + 4 - 8 * y, z)


def greet(peers):
    barrier = pltpu.get_barrier_semaphore()
    for peer in peers:
        pl.semaphore_signal(barrier, inc=1, device_id=peer, device_id_type=MESH)
    pl.semaphore_wait(barrier, len(peers))


early_cuts = ((0, 512), (512, 1024), (1024, 1536), (1536, 2048))
late_end, a_out_at, a_ff_at, b_at_col, early_end = 256, 384, 512, 1024, 2048


class PlaneSum:
    def __init__(self, e, r1, r2a, r2b, r3a, r3b, s1, q1, s2, q2, s3, q3):
        self.refs = e, r1, r2a, r2b, r3a, r3b
        self.sems = s1, q1, s2, q2, s3, q3
        self.at = plane()
        self.half = e.shape[3] // 2

    def first(self, m):
        e, r1 = self.refs[:2]
        c, core = self.at[4], self.at[5]
        s1, q1 = self.sems[:2]
        if m < 4:
            cut = slice(late_end, early_end)
            return remote(e.at[m // 2, m % 2, 1 - c, :, cut], r1.at[m // 2, m % 2, :, cut], s1.at[m], q1.at[m], core)
        cut = slice(0, late_end)
        return remote(e.at[:, :, 1 - c, :, cut], r1.at[:, :, :, cut], s1.at[m], q1.at[m], core)

    def take_first(self, m):
        e, r1 = self.refs[:2]
        c = self.at[4]
        self.first(m).wait()
        for i in (m,) if m < 4 else range(4):
            yy, xx = i // 2, i % 2
            cut = slice(late_end, early_end) if m < 4 else slice(0, late_end)
            e[yy, xx, c, :, cut] = add_low(e[yy, xx, c, :, cut], r1[yy, xx, :, cut])

    def finish(self, out):
        e, r1, r2a, r2b, r3a, r3b = self.refs
        dp, z, y, x, c, core, along_x, along_y = self.at
        s1, q1, s2, q2, s3, q3 = self.sems
        half = self.half

        def second(k):
            cut = slice(*early_cuts[k])
            return [
                remote(e.at[:, 1 - x, c, 0:half, cut], r2a.at[:, :, cut], s2.at[0, k], q2.at[0, k], along_x),
                remote(e.at[1 - y, :, c, half:, cut], r2b.at[:, :, cut], s2.at[1, k], q2.at[1, k], along_y),
            ]

        def third(k):
            cut = slice(*early_cuts[k])
            return [
                remote(e.at[1 - y, x, c, 0:half, cut], r3a.at[:, cut], s3.at[0, k], q3.at[0, k], along_y),
                remote(e.at[y, 1 - x, c, half:, cut], r3b.at[:, cut], s3.at[1, k], q3.at[1, k], along_x),
            ]

        def after_second(k):
            cut = slice(*early_cuts[k])
            for copy in second(k):
                copy.wait()
            for i in range(2):
                e[i, x, c, 0:half, cut] = add_low(e[i, x, c, 0:half, cut], r2a[i, :, cut])
                e[y, i, c, half:, cut] = add_low(e[y, i, c, half:, cut], r2b[i, :, cut])
            for copy in third(k):
                copy.start()

        def after_third(k):
            cut = slice(*early_cuts[k])
            for copy in third(k):
                copy.wait()
            out[0:half, cut] = add_low(e[y, x, c, 0:half, cut], r3a[:, cut])
            out[half:, cut] = add_low(e[y, x, c, half:, cut], r3b[:, cut])

        count = len(early_cuts)
        for k in range(count):
            for copy in second(k):
                copy.start()
        for k in range(count + 1):
            if k < count:
                after_second(k)
            if k:
                after_third(k - 1)


def middle_kernel(
    q_ref, k_ref, v_ref, g_ref, keep_ref, above_ref, below_ref,
    second_ref, low_ref, mid_ref, mid_t_ref, dmid_ref, dmid_t_ref,
    up_ref, down_ref, a_ref, b_ref, bias_ref, *refs,
    n, pairs, steps, depth, early,
):
    if early:
        first_ref, mid_qkv_ref, a_out_ref, dmid_out_t_ref = refs[:4]
        refs = refs[4:]
        local_ref, ff_ref, back_ref, mid_ff_ref, dmid_up_ref, sum_ref = refs[:6]
        buffer, dk_ref, dv_ref, mid_acc, dmid_acc, send_sem, recv_sem, own_sem = refs[6:14]
        e_ref, dmid_seq, gb_acc, ga_acc, o_here, load_sem = refs[14:20]
        plane_refs = refs[20:]
    else:
        local_ref, own_ref, ff_ref, back_ref, mid_ff_ref, dmid_up_ref, ga_ref, gb_ref = refs[:8]
        buffer, dk_ref, dv_ref, mid_acc, dmid_acc, send_sem, recv_sem, own_sem = refs[8:]
    step = pl.program_id(0)
    z = lax.axis_index("blk")
    dp = lax.axis_index("dp")
    lanes = q_ref.shape[2]
    length = q_ref.shape[1]
    inner_block = up_ref.shape[1]
    width = up_ref.shape[0]
    cz = pairs * lanes
    if early:
        plane_sum = PlaneSum(e_ref, *plane_refs)

    def pair_place(kind, s):
        seq, pair = s // pairs, lax.rem(s, pairs)
        what = slice(2, 4) if kind else slice(0, 2)
        at = pl.ds(pl.multiple_of((z * pairs + pair) * lanes, lanes), lanes)
        return what, local_ref.at[seq, what, :, at]

    def own_copy(kind, s):
        what, target = pair_place(kind, s)
        return pltpu.make_async_copy(buffer.at[s, z, what], target, own_sem.at[kind, s])

    def away_copy(kind, s, t):
        what, target = pair_place(kind, s)
        peer = lax.rem(z + t, n)
        return remote(buffer.at[s, peer, what], target, send_sem.at[kind, s, t], recv_sem.at[kind, s, t], (dp, peer))

    def copies(kind, s):
        return [own_copy(kind, s)] + [away_copy(kind, s, t) for t in range(1, n)]

    def receive(kind):
        for s in range(steps):
            for copy in copies(kind, s):
                copy.wait()

    @pl.when(step == 0)
    def _():
        peers = [(dp, lax.rem(z + t, n)) for t in range(1, n)]
        greet((list(plane()[5:]) if early else []) + peers)

    @pl.when(step < steps)
    def _():
        def store(i, kind, value):
            buffer[step, i, kind] = value
            if kind and not early:
                own_ref[0, kind - 1, i * value.shape[0] : (i + 1) * value.shape[0], :] = value

        tables = keep_ref[...], above_ref[...], below_ref[...]

        def block_done(i):
            pl.when(i == z)(lambda: own_copy(0, step).start())
            pl.when(i != z)(lambda: away_copy(0, step, lax.rem(i - z + n, n)).start())

        attend_pair(
            q_ref[0], k_ref[0], v_ref[0], g_ref[0], tables, dk_ref, dv_ref, depth, n, store, block_done
        )
        if early:
            seq, pair = step // pairs, lax.rem(step, pairs)
            mid_t = mid_qkv_ref[0].T
            dmid = jnp.zeros((length, lanes), f32)
            for t in range(3):
                grad = buffer[step, :, t + 1].reshape(length, lanes)
                at = pl.ds(pl.multiple_of(t * width + z * cz + pair * lanes, lanes), lanes)
                dmid += nt(grad, b_ref[:, at])
                product = nn(mid_t, grad)
                gb_acc[t, pair] = jnp.where(seq == 0, product, gb_acc[t, pair] + product)
            dmid = jnp.where(pair == 0, dmid, dmid_seq[...] + dmid)
            dmid_seq[...] = dmid

            @pl.when(pair == pairs - 1)
            def _():
                product = nn((adapter_scale * dmid_seq[...]).astype(bf16).T, first_ref[0])
                ga_acc[...] = jnp.where(seq == 0, product, ga_acc[...] + product)

    @pl.when(step == steps)
    def _():
        for s in range(steps):
            own_copy(1, s).start()
            for t in range(1, n) if s % 2 else range(n - 1, 0, -1):
                away_copy(1, s, t).start()
        ff_ref[...] = jnp.zeros_like(ff_ref)
        back_ref[...] = jnp.zeros_like(back_ref)
        mid_acc[...] = jnp.zeros_like(mid_acc)
        dmid_acc[...] = jnp.zeros_like(dmid_acc)
        if early:
            for owner in range(8):
                place = (owner // 4, owner // 2 % 2, owner % 2)
                e_ref[place + (slice(None), slice(late_end, a_out_at))] = ga_acc[
                    :, owner * lanes : (owner + 1) * lanes
                ].astype(bf16)
                if owner < 3:
                    e_ref[place + (slice(None), slice(b_at_col, early_end))] = jnp.zeros((lanes, 1024), bf16)
            for t in range(3):
                for pair in range(pairs):
                    at = pl.ds(pl.multiple_of(b_at_col + z * cz + pair * lanes, lanes), lanes)
                    e_ref[0, t // 2, t % 2, :, at] = (adapter_scale * gb_acc[t, pair]).astype(bf16)

    @pl.when(step >= steps)
    def _():
        count, size = mid_t_ref.shape[0], mid_t_ref.shape[2]
        j = step - steps
        if early:
            up_b = b_ref[:, pl.ds(pl.multiple_of(4 * width + j * inner_block, inner_block), inner_block)]
        else:
            up_b = b_ref[...]
        ga, gb = None, None
        for at in range(count):
            rows = slice(at * size, (at + 1) * size)
            pre = nn(second_ref[rows], up_ref[...]) + bias_ref[...] + adapter_scale * nn(mid_ref[rows], up_b)
            cdf = 0.5 + 0.5 * lax.erf(pre * (1.0 / math.sqrt(2.0)))
            hidden = (pre * cdf).astype(bf16)
            slope = cdf + pre * (jnp.exp(-0.5 * pre * pre) * (1.0 / math.sqrt(2.0 * math.pi)))
            grad_hidden = nt(low_ref[rows], down_ref[...]) + nt(dmid_ref[rows], a_ref[...])
            dup = (slope * grad_hidden).astype(bf16)
            ff_ref[rows] += nn(hidden, down_ref[...])
            back_ref[rows] += nt(dup, up_ref[...])
            mid_acc[rows] += nn(hidden, a_ref[...])
            dmid_acc[rows] += nt(dup, up_b)
            ga_part = nn(dmid_t_ref[at], hidden)
            gb_part = nn(mid_t_ref[at], dup)
            ga = ga_part if ga is None else ga + ga_part
            gb = gb_part if gb is None else gb + gb_part
        if early:
            e_ref[j // 4, lax.rem(j // 2, 2), lax.rem(j, 2), :, a_ff_at:b_at_col] = ga.astype(bf16)
            at = pl.ds(pl.multiple_of(b_at_col + lax.rem(j, 2) * inner_block, lanes), inner_block)
            e_ref[1, j // 4, lax.rem(j // 2, 2), :, at] = (adapter_scale * gb).astype(bf16)

            @pl.when(j == 2)
            def _():
                receive(0)
                load = pltpu.make_async_copy(local_ref.at[:, 0], o_here, load_sem.at[0])
                load.start()
                load.wait()
                ga_out, gb_out = None, None
                for q in range(count):
                    rows = slice(q * size, (q + 1) * size)
                    out = o_here[q]
                    mid = nn(out, a_out_ref[...]).astype(bf16)
                    ga_part = nn(dmid_out_t_ref[q], out)
                    gb_part = nn(mid.T, low_ref[rows])
                    ga_out = ga_part if ga_out is None else ga_out + ga_part
                    gb_out = gb_part if gb_out is None else gb_out + gb_part
                e_ref[0, 1, 1, :, b_at_col:early_end] = (adapter_scale * gb_out).astype(bf16)
                for owner in range(8):
                    at = slice(owner * lanes, (owner + 1) * lanes)
                    e_ref[owner // 4, owner // 2 % 2, owner % 2, :, a_out_at:a_ff_at] = ga_out[:, at].astype(bf16)

            for m, (begin, take) in enumerate(((3, 5), (4, 6), (5, 7))):
                pl.when(j == begin)(lambda m=m: plane_sum.first(m).start())
                pl.when(j == take)(lambda m=m: plane_sum.take_first(m))
            pl.when(j == 7)(lambda: plane_sum.first(3).start())
        else:
            ga_ref[...] = ga
            gb_ref[...] = gb

    @pl.when(step == pl.num_programs(0) - 1)
    def _():
        mid_ff_ref[...] = mid_acc[...].astype(bf16)
        dmid_up_ref[...] = (adapter_scale * dmid_acc[...]).astype(bf16)
        if early:
            count, size = mid_t_ref.shape[0], mid_t_ref.shape[2]
            ga, gb = None, None
            for at in range(count):
                rows = slice(at * size, (at + 1) * size)
                ga_part = nn(dmid_up_ref[rows].T, second_ref[rows])
                gb_part = nn(mid_ff_ref[rows].T, low_ref[rows])
                ga = ga_part if ga is None else ga + ga_part
                gb = gb_part if gb is None else gb + gb_part
            for owner in range(8):
                place = (owner // 4, owner // 2 % 2, owner % 2, slice(None))
                at = slice(owner * lanes, (owner + 1) * lanes)
                e_ref[place + (slice(0, lanes),)] = ga[:, at].astype(bf16)
                e_ref[place + (slice(lanes, late_end),)] = (adapter_scale * gb[:, at]).astype(bf16)
            plane_sum.first(4).start()
            plane_sum.take_first(3)
            plane_sum.take_first(4)
            plane_sum.finish(sum_ref)
        if not early:
            receive(0)
        receive(1)


def finish_kernel(
    local_ref, wo_ref, wq_ref, wk_ref, wv_ref, a_out_ref, a_qkv_ref, b_out_ref, bq_ref, bk_ref, bv_ref,
    bias_ref, x_ref, cot_ref, weight_ref, ff_ref, bias_ff_ref, mid_ff_ref, b_ff_ref,
    second_ref, dmid_up_ref, a_up_ref, gain_ref, dmid_out_t_ref, low_ref,
    mixed_ref, tokens_ref, norm_ref, ga_ref, gb_ref,
    att_acc, mid_acc, first_acc, dmid_acc,
):
    t = pl.program_id(0)
    rows = x_ref.shape[0] * x_ref.shape[1]
    cols = wq_ref.shape[1]

    @pl.when(t == 0)
    def _():
        att_acc[...] = jnp.zeros_like(att_acc)
        mid_acc[...] = jnp.zeros_like(mid_acc)
        first_acc[...] = jnp.zeros_like(first_acc)
        dmid_acc[...] = jnp.zeros_like(dmid_acc)

    out, dq, dk, dv = (local_ref[:, i].reshape(rows, cols) for i in range(4))
    att_acc[...] += nn(out, wo_ref[...])
    mid_acc[...] += nn(out, a_out_ref[...])
    first_acc[...] += nt(dq, wq_ref[...]) + nt(dk, wk_ref[...]) + nt(dv, wv_ref[...])
    dmid_acc[...] += nt(dq, bq_ref[...]) + nt(dk, bk_ref[...]) + nt(dv, bv_ref[...])
    size = x_ref.shape[1]
    ga_ref[...] = sum(nn(dmid_out_t_ref[q], out[q * size : (q + 1) * size]) for q in range(x_ref.shape[0]))

    @pl.when(t == pl.num_programs(0) - 1)
    def _():
        size = x_ref.shape[1]
        norm = [jnp.zeros((1, first_acc.shape[1]), f32) for _ in range(4)]
        for q in range(x_ref.shape[0]):
            part = slice(q * size, (q + 1) * size)
            x = x_ref[q].astype(f32)
            mid = mid_acc[part].astype(bf16)
            gb = tn(mid, low_ref[part])
            gb_ref[...] = gb if q == 0 else gb_ref[...] + gb
            att = att_acc[part] + bias_ref[...] + adapter_scale * nn(mid, b_out_ref[...])
            ff = ff_ref[part] + bias_ff_ref[...] + adapter_scale * nn(mid_ff_ref[part], b_ff_ref[...])
            mixed_ref[q] = (x + att + ff).astype(bf16)
            dmid = (adapter_scale * dmid_acc[part]).astype(bf16)
            grad_first = first_acc[part] + nt(dmid, a_qkv_ref[...])
            grad_second = second_ref[part] + nt(dmid_up_ref[part], a_up_ref[...])
            centre = x - jnp.mean(x, axis=-1, keepdims=True)
            inv = lax.rsqrt(jnp.mean(centre * centre, axis=-1, keepdims=True) + norm_eps)
            unit = centre * inv
            pulled = grad_first * gain_ref[0:1] + grad_second * gain_ref[1:2]
            back = inv * (
                pulled
                - jnp.mean(pulled, axis=-1, keepdims=True)
                - unit * jnp.mean(pulled * unit, axis=-1, keepdims=True)
            )
            row_grad = cot_ref[q].astype(f32) * weight_ref[part]
            tokens_ref[q] = (row_grad + back).astype(bf16)
            for k, value in enumerate((grad_first * unit, grad_second * unit, grad_first, grad_second)):
                norm[k] += jnp.sum(value, axis=0, keepdims=True)
        norm_ref[...] = jnp.concatenate(norm, axis=0)


def tail_kernel(
    o_ref, dq_ref, dk_ref, dv_ref, wo_ref, wq_ref, wk_ref, wv_ref, a_out_ref, a_qkv_ref, b_out_ref,
    bq_ref, bk_ref, bv_ref, bias_ref, x_ref, cot_ref, weight_ref, ff_ref, bias_ff_ref, mid_ff_ref, b_ff_ref,
    second_ref, dmid_up_ref, a_up_ref, gain_ref,
    e_ref, b_ref, mean_ref, square_ref, bf_ref, mean_f_ref, square_f_ref,
    mixed_ref, tokens_ref, out_hbm, norm_ref, fresh_hbm,
    out_ref, fresh_ref, att_acc, mid_acc, first_acc, dmid_acc,
    r4, nr, nsum,
    s4, q4, s5, q5, sf, qf, sn, qn, sg, qg, done_sem,
    *, n,
):
    step = pl.program_id(0)
    dp, z, y, x, c, core, along_x, along_y = plane()
    peers = [(dp, lax.rem(z + t, n)) for t in range(1, n)]
    seqs, size, width = o_ref.shape[0], o_ref.shape[2], x_ref.shape[2]
    rows, cols = seqs * size, o_ref.shape[3]
    outs = width // cols
    grads = width // dq_ref.shape[3]
    first_seq = outs + grads
    rank = e_ref.shape[0]
    part = rank // n
    lanes = 128
    mine = pl.ds(pl.multiple_of(z * part, part), part)

    def to_part(t):
        return pl.ds(pl.multiple_of(lax.rem(z + t, n) * part, part), part)

    def e_out(k, t):
        cut = slice(*early_cuts[k])
        return remote(e_ref.at[to_part(t), cut], r4.at[t, :, cut], s4.at[t, k], q4.at[t, k], peers[t - 1])

    def e_back(k, t):
        cut = slice(*early_cuts[k])
        return remote(out_ref.at[mine, cut], out_ref.at[mine, cut], s5.at[t, k], q5.at[t, k], peers[t - 1])

    count = len(early_cuts)

    def fresh_back(t):
        return remote(fresh_ref.at[dp, mine, :], fresh_ref.at[dp, mine, :], sf.at[t], qf.at[t], peers[t - 1])

    from_x, from_y, from_c = along_x[0], along_y[0], core[0]
    across = from_x + from_y - dp
    onward = jnp.where(c == 0, from_y, from_x)
    target = (jnp.where(c == 0, from_x, from_y), z)
    other = 1 - 2 * c
    hops = [
        (dp, from_x, along_x), (dp, from_y, along_y), (dp, from_c, core), (onward, across, target),
        (from_x, from_x + other, core), (from_y, from_y + other, core), (across, across + other, core),
    ]

    middle_row = rank // 2
    parts = (slice(0, middle_row), slice(middle_row, rank))

    def gather(kind, p):
        slot, _, peer = hops[kind]
        there = fresh_ref.at[slot, parts[p], :]
        return remote(there, there, sg.at[p, kind], qg.at[p, kind], peer)

    def fresh_rows(value, grad_b):
        cut = b_ref.shape[1]
        new_b = adam_fresh(b_ref[mine, :], grad_b, mean_ref[mine, :], square_ref[mine, :])
        new_f = adam_fresh(bf_ref[mine, :], value, mean_f_ref[mine, :], square_f_ref[mine, :])
        fresh_ref[dp, mine, :] = jnp.concatenate([new_b, new_f], axis=1).astype(bf16)

    def norm_copy(i, peer):
        return remote(nsum.at[i], nr.at[i], sn.at[i], qn.at[i], peer)

    norm_stages = [norm_copy(0, core), norm_copy(1, along_x), norm_copy(2, along_y)]
    norm_last = [
        remote(nsum.at[3], nr.at[2 + t], sn.at[2 + t], qn.at[2 + t], peers[t - 1]) for t in range(1, n)
    ]

    def norm_take(i):
        norm_stages[i].wait()
        nsum[i + 1] = nsum[i] + nr[i]

    @pl.when(step == 0)
    def _():
        greet([core, along_x, along_y] + peers)
        for k in range(count):
            for t in range(1, n):
                e_out(k, t).start()
        att_acc[...] = jnp.zeros_like(att_acc)
        mid_acc[...] = jnp.zeros_like(mid_acc)
        first_acc[...] = jnp.zeros_like(first_acc)
        dmid_acc[...] = jnp.zeros_like(dmid_acc)

    @pl.when(step < outs)
    def _():
        out = o_ref[...].reshape(rows, cols)
        att_acc[...] += nn(out, wo_ref[...])
        mid_acc[...] += nn(out, a_out_ref[...])

    @pl.when((step >= outs) & (step < first_seq))
    def _():
        dq, dk, dv = (r[...].reshape(rows, r.shape[3]) for r in (dq_ref, dk_ref, dv_ref))
        first_acc[...] += nt(dq, wq_ref[...]) + nt(dk, wk_ref[...]) + nt(dv, wv_ref[...])
        dmid_acc[...] += nt(dq, bq_ref[...]) + nt(dk, bk_ref[...]) + nt(dv, bv_ref[...])

    @pl.when(step == outs)
    def _():
        for k in range(count):
            cut = slice(*early_cuts[k])
            for t in range(1, n):
                e_out(k, t).wait()
            value = e_ref[mine, cut].astype(f32)
            for t in range(1, n):
                value += r4[t, :, cut].astype(f32)
            out_ref[mine, cut] = value.astype(bf16)
        fresh_rows(out_ref[mine, lanes:late_end].astype(f32), out_ref[mine, b_at_col:early_end].astype(f32))
        for t in range(1, n):
            fresh_back(t).start()

    @pl.when(step == first_seq - 1)
    def _():
        for t in range(1, n):
            fresh_back(t).wait()
        for p in range(2):
            for kind in (0, 1, 2):
                gather(kind, p).start()
        for k in range(count):
            for t in range(1, n):
                e_back(k, t).start()

    @pl.when(step >= first_seq)
    def _():
        q = step - first_seq
        at = pl.ds(pl.multiple_of(q * size, size), size)
        x_in = x_ref[0].astype(f32)
        mid = mid_acc[at, :].astype(bf16)
        att = att_acc[at, :] + bias_ref[...] + adapter_scale * nn(mid, b_out_ref[...])
        ff = ff_ref[...] + bias_ff_ref[...] + adapter_scale * nn(mid_ff_ref[at, :], b_ff_ref[...])
        mixed_ref[0] = (x_in + att + ff).astype(bf16)
        dmid = (adapter_scale * dmid_acc[at, :]).astype(bf16)
        grad_first = first_acc[at, :] + nt(dmid, a_qkv_ref[...])
        grad_second = second_ref[...] + nt(dmid_up_ref[at, :], a_up_ref[...])
        centre = x_in - jnp.mean(x_in, axis=-1, keepdims=True)
        inv = lax.rsqrt(jnp.mean(centre * centre, axis=-1, keepdims=True) + norm_eps)
        unit = centre * inv
        pulled = grad_first * gain_ref[0:1] + grad_second * gain_ref[1:2]
        back = inv * (
            pulled
            - jnp.mean(pulled, axis=-1, keepdims=True)
            - unit * jnp.mean(pulled * unit, axis=-1, keepdims=True)
        )
        row_grad = cot_ref[0].astype(f32) * weight_ref[at, :]
        tokens_ref[0] = (row_grad + back).astype(bf16)
        norm = [
            jnp.sum(value, axis=0, keepdims=True)
            for value in (grad_first * unit, grad_second * unit, grad_first, grad_second)
        ]
        norm = jnp.concatenate(norm, axis=0)
        nsum[0] = jnp.where(q == 0, norm, nsum[0] + norm)

    @pl.when(step == pl.num_programs(0) - 1)
    def _():
        norm_stages[0].start()
        for p in range(2):
            gather(0, p).wait_recv()
            gather(1, p).wait_recv()
            for kind in (3, 4, 5):
                gather(kind, p).start()
            norm_take(p)
            norm_stages[p + 1].start()
        for p in range(2):
            gather(3, p).wait_recv()
            gather(6, p).start()
        norm_take(2)
        for copy in norm_last:
            copy.start()
        for k in range(count):
            for t in range(1, n):
                e_back(k, t).wait()

        keep_out = pltpu.make_async_copy(out_ref, out_hbm, done_sem.at[0])
        keep_out.start()
        for p in range(2):
            for kind in (2, 4, 5, 6):
                gather(kind, p).wait_recv()
        keep_fresh = pltpu.make_async_copy(fresh_ref, fresh_hbm, done_sem.at[1])
        keep_fresh.start()
        for p in range(2):
            for kind in range(7):
                gather(kind, p).wait_send()
        for copy in norm_last:
            copy.wait()
        keep_out.wait()
        keep_fresh.wait()
        value = jnp.zeros_like(nsum[3])
        for blk in range(n):
            there = lax.rem(z - blk + n, n)
            value += jnp.where(there == 0, nsum[3], nr[2 + jnp.maximum(there, 1)])
        norm_ref[...] = value


def update_kernel(
    g_ref, fresh_ref, w_ref, wd_ref, *refs, rank, width,
):
    params, outs = refs[:16], refs[16:30]
    a_new, aff_new = refs[30:]
    j = pl.program_id(0)
    cols = w_ref.shape[1]

    @pl.when(j == 0)
    def _():
        rows, inner = params[0].shape[0], params[4].shape[0]
        got = g_ref[...].astype(f32)
        cut, cut_f = params[8].shape[1], params[12].shape[1]
        up = got[:, :rows]
        qkv = got[:, rows + cut_f : 2 * rows + cut_f]
        out = got[:, 2 * rows + cut_f : 3 * rows + cut_f]
        at = 3 * rows + cut_f
        grads = [
            jnp.concatenate([part.T for part in (qkv, out, up)], axis=1),
            got[:, at : at + inner].T,
            got[:, at + inner : at + inner + cut],
            got[:, rows : rows + cut_f],
        ]
        for i, grad in enumerate(grads):
            param, mean, square, keep = (r[...] for r in params[4 * i : 4 * i + 4])
            mean_new = 0.9 * mean + 0.1 * grad
            square_new = 0.999 * square + 0.001 * grad * grad
            kept = keep.astype(f32)
            outs[i][...] = grad
            outs[4 + 2 * i][...] = mean_new * kept
            outs[5 + 2 * i][...] = square_new * kept
            if i < 2:
                fresh = param - 0.01 * (mean_new / first_fix) / (jnp.sqrt(square_new / second_fix) + 1e-08)
                if i == 0:
                    for k in range(3):
                        a_new[k] = fresh[:, k * rank : (k + 1) * rank].astype(bf16)
                else:
                    aff_new[...] = fresh.astype(bf16)

    cut = params[8].shape[1]
    fresh = [fresh_ref[i] for i in range(fresh_ref.shape[0])]
    update = []
    for i, part in enumerate(fresh):
        at = j * cols + i * cut
        block = jnp.where(at < 3 * width, 0, jnp.where(at < 4 * width, 1, 2))
        update.append(nn(a_new[block], part[:, :cut]))
    update = jnp.concatenate(update, axis=1)
    outs[12][...] = (w_ref[...].astype(f32) + adapter_scale * update).astype(bf16)
    update = nn(aff_new[...], jnp.concatenate([f[:, cut:] for f in fresh], axis=1))
    outs[13][...] = (wd_ref[...].astype(f32) + adapter_scale * update).astype(bf16)


def adam_fresh(param, grad, mean, square):
    mean_new = 0.9 * mean + 0.1 * grad
    square_new = 0.999 * square + 0.001 * grad * grad
    return param - 0.01 * (mean_new / first_fix) / (jnp.sqrt(square_new / second_fix) + 1e-08)


def body(
    dp_n,
    n,
    tokens,
    cotangent,
    domain_ids,
    domain_weight,
    frozen_input_weights,
    bias_in,
    frozen_down_weight,
    bias_ff,
    norm_gain,
    norm_shift,
    adapt_a,
    adapt_a_ff,
    adapt_b,
    adapt_b_ff,
    mean_a,
    mean_a_ff,
    mean_b,
    mean_b_ff,
    square_a,
    square_a_ff,
    square_b,
    square_b_ff,
    keep_a,
    keep_a_ff,
    keep_b,
    keep_b_ff,
):
    seqs, span, width = tokens.shape
    rows = seqs * span
    rank = adapt_b.shape[0]
    depth = width // HEADS
    cz = width // n
    length = n * span
    z = lax.axis_index("blk")
    z_arr = jnp.full((1,), z, jnp.int32)
    kr = frozen_input_weights.shape[0]
    down_rows, inner = frozen_down_weight.shape[0], frozen_down_weight.shape[0] * dp_n
    lanes = 128

    def shift_by(values, s):
        return lax.ppermute(values, "blk", [(i, (i + s) % n) for i in range(n)])

    b_cols = adapt_b.shape[1] + adapt_b_ff.shape[1]
    bias32 = bias_in.astype(f32)
    whole_front = dp_n == 8 and n == 4 and seqs > 1 and (rank, width, inner) == (128, 1024, 4096)
    if whole_front:
        vmem = pl.BlockSpec(memory_space=pltpu.VMEM)
        hbm = pl.BlockSpec(memory_space=pl.ANY)
        dma = pltpu.SemaphoreType.DMA
        half = ROTARY // 2
        freq = [rope_base ** (-(k * 2.0) / ROTARY) for k in range(half)]
        freq = np.tile(np.array(freq + freq + [0.0] * (depth - ROTARY), np.float32), lanes // depth)

        def shape(*dims, dtype=bf16):
            return jax.ShapeDtypeStruct(dims, dtype)

        (
            w_in, w_down, a_all, a_ff, b_in, b_ff, query, keys, values, first_pos, mid_pos, g_pos,
            grad_low, second, mid_up, mid_up_t, dmid_ff, dmid_ff_t, dmid_out_t, *tables, row_weight,
        ) = pl.pallas_call(
            functools.partial(front_kernel, n=n, depth=depth),
            in_specs=[hbm] * 3 + [vmem] * 6 + [pl.BlockSpec(memory_space=pltpu.SMEM)] + [vmem] * 4,
            out_specs=[hbm] * 12 + [vmem] * 11,
            out_shape=[
                shape(width, 8 * width), shape(inner, width), shape(width, 3 * rank), shape(inner, rank),
                shape(rank, 8 * width), shape(rank, width),
                shape(seqs, length, cz), shape(seqs, length, cz), shape(seqs, length, cz),
                shape(seqs, length, width), shape(seqs, length, rank), shape(seqs, length, cz),
                shape(rows, width), shape(rows, width),
                shape(rows, rank), shape(seqs, rank, span), shape(rows, rank), shape(seqs, rank, span),
                shape(seqs, rank, span),
                shape(length, lanes, dtype=f32), shape(length, lanes, dtype=f32), shape(length, lanes, dtype=f32),
                shape(rows, 1, dtype=f32),
            ],
            scratch_shapes=[
                pltpu.VMEM(adapt_a.shape, bf16),
                pltpu.VMEM(adapt_a_ff.shape, bf16),
                pltpu.VMEM(adapt_b.shape, bf16),
                pltpu.VMEM(adapt_b_ff.shape, bf16),
                pltpu.VMEM((n, seqs, span, width), bf16),
                pltpu.VMEM((seqs, length, cz), bf16),
                pltpu.VMEM((seqs, length, cz), bf16),
                pltpu.VMEM((seqs, length, cz), bf16),
                pltpu.VMEM((seqs, length, width), bf16),
                pltpu.VMEM((seqs, length, rank), bf16),
                pltpu.VMEM((n, seqs, span, cz), bf16),
                pltpu.VMEM((width, width), bf16),
                pltpu.VMEM((3, width, cz), bf16),
                pltpu.VMEM((width, 3 * rank), bf16),
                pltpu.VMEM((rank, 8 * width), bf16),
                pltpu.VMEM((rank, width), bf16),
                dma((7, 7)), dma((7, 7)), dma((7,)),
                dma((n, seqs)), dma((n, seqs)), dma((n, seqs)), dma((n, seqs)), dma((n,)), dma((n,)),
                dma((7,)), dma((5, n)), dma((2,)),
            ],
            compiler_params=pltpu.CompilerParams(
                collective_id=2, has_side_effects=True, vmem_limit_bytes=58 << 20
            ),
            name="front",
        )(
            tokens, frozen_input_weights, frozen_down_weight,
            adapt_a, adapt_a_ff, adapt_b, adapt_b_ff,
            cotangent, domain_ids, domain_weight, norm_gain, norm_shift, bias32.reshape(1, -1), freq.reshape(1, -1),
        )
    else:
        lookup = (domain_ids[..., None] == jnp.arange(DOMAINS, dtype=jnp.int32)).astype(f32)
        row_weight = jnp.sum(lookup * domain_weight, axis=-1).reshape(rows, 1)
        row_grad = cotangent.astype(f32).reshape(rows, width) * row_weight
        grad_low = row_grad.astype(bf16)
        b_shard = jnp.concatenate([adapt_b, adapt_b_ff], axis=1).astype(bf16)
        one = jnp.concatenate(
            [frozen_input_weights[:, : 4 * width], adapt_a.astype(bf16), b_shard.reshape(kr, -1)], axis=1
        )
        one = lax.all_gather(one, "dp", axis=0, tiled=True)
        two = lax.all_gather(frozen_input_weights[:, 4 * width :], "dp", axis=0, tiled=True)
        three = jnp.concatenate([frozen_down_weight, adapt_a_ff.astype(bf16)], axis=1)
        three = lax.all_gather(three, "dp", axis=0, tiled=True)
        a_at = 4 * width
        b_at = a_at + 3 * rank
        a_all = one[:, a_at:b_at]
        b_all = one[:, b_at:].reshape(dp_n, rank, b_cols)
        b_in = jnp.transpose(b_all[:, :, : adapt_b.shape[1]], (1, 0, 2)).reshape(rank, -1)
        b_ff = jnp.transpose(b_all[:, :, adapt_b.shape[1] :], (1, 0, 2)).reshape(rank, width)
        w_out = one[:, 3 * width : 4 * width]
        w_up = two
        w_down, a_ff = three[:, :width], three[:, width:]

        right, left = tokens, tokens
        rights, lefts = [None], [None]
        for s in range(1, n):
            right = lax.ppermute(right, "blk", [(i, i + 1) for i in range(n - 1)])
            left = lax.ppermute(left, "blk", [(i + 1, i) for i in range(n - 1)])
            rights.append(right)
            lefts.append(left)
        x_all = jnp.stack(
            [tokens] + [jnp.where(z >= s, rights[s], lefts[n - s]) for s in range(1, n)]
        )

        b_out = b_in[:, 3 * width : 4 * width]
        a_out = a_all[:, rank : 2 * rank]
        dmid_out = (adapter_scale * nt(grad_low, b_out)).astype(bf16)
        grad_att = (nt(grad_low, w_out) + nt(dmid_out, a_out)).astype(bf16)
        grad_att = jnp.transpose(grad_att.reshape(seqs, span, n, cz), (2, 0, 1, 3))

        def piece(values, s):
            return lax.dynamic_index_in_dim(values, lax.rem(z + s, n), 0, keepdims=False)

        g_all = jnp.stack(
            [piece(grad_att, 0)] + [shift_by(piece(grad_att, s), s) for s in range(1, n)]
        )

        tables = rope_lane_tables(length, depth, lanes)
        own = [lax.dynamic_slice_in_dim(b_in[:, t * width : (t + 1) * width], z * cz, cz, 1) for t in range(3)]
        b_own = jnp.concatenate(own, axis=1)
        bias_own = jnp.concatenate(
            [lax.dynamic_slice_in_dim(bias32, t * width + z * cz, cz, 0) for t in range(3)]
        ).reshape(1, 3 * cz)

        def block_of(s, z_ref):
            return lax.rem(z_ref[0] - s + n, n)

        table_spec = pl.BlockSpec((span, lanes), lambda s, q, z_ref: (block_of(s, z_ref), 0))
        head_spec = pl.BlockSpec((1, span, cz), lambda s, q, z_ref: (q, block_of(s, z_ref), 0))
        query, keys, values, first_all, mid_all = pl.pallas_call(
            qkv_kernel,
            grid_spec=pltpu.PrefetchScalarGridSpec(
                num_scalar_prefetch=1,
                grid=(n, seqs),
                in_specs=[
                    pl.BlockSpec((1, 1, span, width), lambda s, q, z_ref: (s, q, 0, 0)),
                    pl.BlockSpec((1, width), lambda s, q, z_ref: (0, 0)),
                    pl.BlockSpec((1, width), lambda s, q, z_ref: (0, 0)),
                    pl.BlockSpec((width, cz), lambda s, q, z_ref: (0, z_ref[0])),
                    pl.BlockSpec((width, cz), lambda s, q, z_ref: (0, n + z_ref[0])),
                    pl.BlockSpec((width, cz), lambda s, q, z_ref: (0, 2 * n + z_ref[0])),
                    pl.BlockSpec((width, rank), lambda s, q, z_ref: (0, a_at // rank)),
                    pl.BlockSpec((rank, 3 * cz), lambda s, q, z_ref: (0, 0)),
                    pl.BlockSpec((1, 3 * cz), lambda s, q, z_ref: (0, 0)),
                    table_spec,
                    table_spec,
                    table_spec,
                ],
                out_specs=[
                    head_spec,
                    head_spec,
                    head_spec,
                    pl.BlockSpec((1, 1, span, width), lambda s, q, z_ref: (block_of(s, z_ref), q, 0, 0)),
                    pl.BlockSpec((1, 1, span, rank), lambda s, q, z_ref: (block_of(s, z_ref), q, 0, 0)),
                ],
            ),
            out_shape=[jax.ShapeDtypeStruct((seqs, length, cz), bf16)] * 3
            + [
                jax.ShapeDtypeStruct((n, seqs, span, width), bf16),
                jax.ShapeDtypeStruct((n, seqs, span, rank), bf16),
            ],
            compiler_params=pltpu.CompilerParams(vmem_limit_bytes=48 << 20),
            cost_estimate=pl.CostEstimate(
                flops=2 * n * rows * width * 4 * cz, bytes_accessed=6 * n * rows * width, transcendentals=0
            ),
            name="qkv",
        )(
            z_arr, x_all, norm_gain[0:1], norm_shift[0:1], one, one, one, one, b_own, bias_own, *tables
        )

        input_rows = tokens.astype(f32).reshape(rows, width)
        centre = input_rows - jnp.mean(input_rows, axis=-1, keepdims=True)
        inv = lax.rsqrt(jnp.mean(centre * centre, axis=-1, keepdims=True) + norm_eps)
        second = (centre * inv * norm_gain[1] + norm_shift[1]).astype(bf16)
        a_up = a_all[:, 2 * rank :]
        mid_up = nn(second, a_up).astype(bf16)
        dmid_ff = (adapter_scale * nt(grad_low, b_ff)).astype(bf16)
        g_pos = jnp.concatenate([g_all, g_all])
        g_pos = lax.rev(g_pos, (0,))
        g_pos = lax.dynamic_slice_in_dim(g_pos, lax.rem(n - 1 - z + n, n), n, 0)
        g_pos = jnp.transpose(g_pos, (1, 0, 2, 3)).reshape(seqs, length, cz)

        first_pos = jnp.transpose(first_all, (1, 0, 2, 3))
        mid_pos = jnp.transpose(mid_all, (1, 0, 2, 3))
        w_in = jnp.concatenate([one[:, :a_at], two], axis=1)
        mid_up_t, dmid_ff_t, dmid_out_t = (
            jnp.transpose(v.reshape(seqs, span, rank), (0, 2, 1)) for v in (mid_up, dmid_ff, dmid_out)
        )

    pairs = cz // lanes
    steps = seqs * pairs
    inner_block = min(512, inner)
    def one_buffer(shape):
        zeros = (0,) * len(shape)
        return pl.BlockSpec(shape, lambda s: zeros, pipeline_mode=pl.Buffered(1))

    def seq_pair(s):
        s = jnp.minimum(s, steps - 1)
        return s // pairs, lax.rem(s, pairs)

    def head_map(s):
        seq, pair = seq_pair(s)
        return seq, 0, pair

    def inner_at(s):
        return jnp.maximum(s - steps, 0)

    head = pl.BlockSpec((1, length, lanes), head_map)
    early = whole_front
    dma = pltpu.SemaphoreType.DMA
    half_rank = rank // 2

    def wide(*dims, dtype=bf16):
        return jax.ShapeDtypeStruct(dims, dtype)

    in_specs = (
        [head] * 4
        + [one_buffer((length, lanes))] * 3
        + [one_buffer((rows, width))] * 2
        + [one_buffer((rows, rank)), one_buffer((seqs, rank, span))] * 2
        + [
            pl.BlockSpec((width, inner_block), lambda s: (0, 4 * width // inner_block + inner_at(s))),
            pl.BlockSpec((inner_block, width), lambda s: (inner_at(s), 0)),
            pl.BlockSpec((inner_block, rank), lambda s: (inner_at(s), 0)),
            one_buffer((rank, 8 * width))
            if early
            else pl.BlockSpec((rank, inner_block), lambda s: (0, 4 * width // inner_block + inner_at(s))),
            pl.BlockSpec((1, inner_block), lambda s: (0, 4 * width // inner_block + inner_at(s))),
        ]
    )
    operands = [
        query, keys, values, g_pos, *tables, second, grad_low, mid_up, mid_up_t, dmid_ff, dmid_ff_t,
        w_in, w_down, a_ff, b_in, bias32.reshape(1, -1),
    ]
    partial_specs = [one_buffer((rows, width))] * 2 + [one_buffer((rows, rank))] * 2
    partial_shapes = [wide(rows, width, dtype=f32)] * 2 + [wide(rows, rank)] * 2
    local_spec, local_shape = pl.BlockSpec(memory_space=pl.ANY), wide(seqs, 4, span, width)
    scratch = [
        pltpu.VMEM((steps, n, 4, span, lanes), bf16),
        pltpu.VMEM((length, lanes), f32),
        pltpu.VMEM((length, lanes), f32),
        pltpu.VMEM((rows, rank), f32),
        pltpu.VMEM((rows, rank), f32),
        dma((2, steps, n)),
        dma((2, steps, n)),
        dma((2, steps)),
    ]
    if early:
        in_specs += [
            pl.BlockSpec((1, length, width), lambda s: (seq_pair(s)[0], 0, 0)),
            pl.BlockSpec((1, length, rank), lambda s: (seq_pair(s)[0], 0, 0)),
        ]
        in_specs += [
            pl.BlockSpec((width, rank), lambda s: (0, 1), pipeline_mode=pl.Buffered(1)),
            one_buffer((seqs, rank, span)),
        ]
        operands += [first_pos, mid_pos, a_all, dmid_out_t]
        out_specs = [local_spec] + partial_specs + [one_buffer((rank, early_end))]
        out_shapes = [local_shape] + partial_shapes + [wide(rank, early_end)]
        cuts = len(early_cuts)
        scratch += [
            pltpu.VMEM((2, 2, 2, rank, early_end), bf16),
            pltpu.VMEM((length, rank), f32),
            pltpu.VMEM((3, pairs, rank, lanes), f32),
            pltpu.VMEM((rank, width), f32),
            pltpu.VMEM((seqs, span, width), bf16),
            dma((1,)),
            pltpu.VMEM((2, 2, rank, early_end), bf16),
            pltpu.VMEM((2, half_rank, early_end), bf16),
            pltpu.VMEM((2, half_rank, early_end), bf16),
            pltpu.VMEM((half_rank, early_end), bf16),
            pltpu.VMEM((half_rank, early_end), bf16),
            dma((5,)), dma((5,)), dma((2, cuts)), dma((2, cuts)), dma((2, cuts)), dma((2, cuts)),
        ]
    else:
        out_specs = (
            [local_spec, pl.BlockSpec((1, 3, length, lanes), lambda s: (seq_pair(s)[0], 0, 0, seq_pair(s)[1]))]
            + partial_specs
            + [pl.BlockSpec((rank, inner_block), lambda s: (0, inner_at(s)))] * 2
        )
        out_shapes = (
            [local_shape, wide(seqs, 3, length, cz)] + partial_shapes + [wide(rank, inner, dtype=f32)] * 2
        )
    middle = pl.pallas_call(
        functools.partial(middle_kernel, n=n, pairs=pairs, steps=steps, depth=depth, early=early),
        grid=(steps + inner // inner_block,),
        in_specs=in_specs,
        out_specs=out_specs,
        out_shape=out_shapes,
        scratch_shapes=scratch,
        compiler_params=pltpu.CompilerParams(
            collective_id=0, has_side_effects=True, vmem_limit_bytes=60 << 20
        ),
        name="middle",
    )(*operands)

    if early:
        local, ff, grad_second, mid_ff, dmid_up, summed = middle
        part = rank // n

        def single(shape, *at):
            return pl.BlockSpec(shape, lambda s: at, pipeline_mode=pl.Buffered(1))

        wide_block = width // 2

        def of_out(s):
            return jnp.minimum(s, 1)

        def of_grad(s):
            return jnp.clip(s - 2, 0, n - 1)

        def of_seq(s):
            return jnp.maximum(s - 2 - n, 0)

        def piece_spec(kind):
            return pl.BlockSpec((seqs, 1, span, cz), lambda s: (0, kind, 0, of_grad(s)))

        def columns(kind, height):
            return pl.BlockSpec((height, cz), lambda s: (0, kind * n + of_grad(s)))

        full = pl.BlockSpec((1, span, width), lambda s: (of_seq(s), 0, 0))
        flat = pl.BlockSpec((span, width), lambda s: (of_seq(s), 0))
        cuts = len(early_cuts)
        b_here = [adapt_b, mean_b, square_b, adapt_b_ff, mean_b_ff, square_b_ff]
        mixed, grad_tokens, reduced, norm_sum, fresh = pl.pallas_call(
            functools.partial(tail_kernel, n=n),
            grid=(2 + n + seqs,),
            in_specs=[
                pl.BlockSpec((seqs, 1, span, wide_block), lambda s: (0, 0, 0, of_out(s))),
                piece_spec(1), piece_spec(2), piece_spec(3),
                pl.BlockSpec((wide_block, width), lambda s: (of_out(s), 3)),
                columns(0, width), columns(1, width), columns(2, width),
                pl.BlockSpec((wide_block, rank), lambda s: (of_out(s), 1)),
                single((width, rank), 0, 0),
                single((rank, width), 0, 3),
                columns(0, rank), columns(1, rank), columns(2, rank),
                single((1, width), 0, 3),
                full, full,
                single((rows, 1), 0, 0),
                flat,
                single((1, width), 0, 0),
                single((rows, rank), 0, 0),
                single((rank, width), 0, 0),
                flat,
                single((rows, rank), 0, 0),
                single((width, rank), 0, 2),
                single((2, width), 0, 0),
                single((rank, early_end), 0, 0),
            ]
            + [single(v.shape, 0, 0) for v in b_here],
            out_specs=[
                full, full, pl.BlockSpec(memory_space=pl.ANY), single((4, width), 0, 0),
                pl.BlockSpec(memory_space=pl.ANY),
            ],
            out_shape=[
                wide(seqs, span, width), wide(seqs, span, width), wide(rank, 2048), wide(4, width, dtype=f32),
                wide(dp_n, rank, b_cols),
            ],
            scratch_shapes=[
                pltpu.VMEM((rank, 2048), bf16),
                pltpu.VMEM((dp_n, rank, b_cols), bf16),
                pltpu.VMEM((rows, width), f32),
                pltpu.VMEM((rows, rank), f32),
                pltpu.VMEM((rows, width), f32),
                pltpu.VMEM((rows, rank), f32),
                pltpu.VMEM((n, part, early_end), bf16),
                pltpu.VMEM((2 + n, 4, width), f32),
                pltpu.VMEM((4, 4, width), f32),
                dma((n, cuts)), dma((n, cuts)), dma((n, cuts)), dma((n, cuts)), dma((n,)), dma((n,)),
                dma((2 + n,)), dma((2 + n,)), dma((2, 7)), dma((2, 7)), dma((2,)),
            ],
            compiler_params=pltpu.CompilerParams(
                collective_id=1, has_side_effects=True, vmem_limit_bytes=58 << 20
            ),
            name="tail",
        )(
            local, local, local, local, w_in, w_in, w_in, w_in, a_all, a_all, b_in, b_in, b_in, b_in,
            bias32.reshape(1, -1), tokens, cotangent, row_weight, ff, bias_ff.astype(f32).reshape(1, -1), mid_ff, b_ff,
            grad_second, dmid_up, a_all, norm_gain, summed, *b_here,
        )
    else:
        local, own, ff, grad_second, mid_ff, dmid_up, grad_a_ff_t, grad_b_up = middle
        grad_b_up = adapter_scale * grad_b_up
        first_pos = first_pos.reshape(seqs * length, width)
        mid_pos = mid_pos.reshape(seqs * length, rank)
        b_own = jnp.concatenate(
            [lax.dynamic_slice_in_dim(b_in[:, t * width : (t + 1) * width], z * cz, cz, 1) for t in range(3)], axis=1
        )
        djoint_own = [own[:, t].reshape(seqs * length, cz) for t in range(3)]
        dmid_own = sum(nt(djoint_own[t], b_own[:, t * cz : (t + 1) * cz]) for t in range(3))
        dmid_own = (adapter_scale * dmid_own).astype(bf16)
        grad_a_qkv_t = tn(dmid_own, first_pos)
        mine = (jnp.arange(n, dtype=jnp.int32) == z)[None, :, None]
        grad_b_qkv = jnp.concatenate(
            [
                jnp.where(mine, adapter_scale * tn(mid_pos, part)[:, None, :], 0.0).reshape(rank, width)
                for part in djoint_own
            ],
            axis=1,
        )
        grad_a_up_t = tn(dmid_up, second)
        grad_b_ffp = adapter_scale * tn(mid_ff, grad_low)

        def fixed(shape, *at):
            return pl.BlockSpec(shape, lambda t: at, pipeline_mode=pl.Buffered(1))

        def column(at, height):
            return pl.BlockSpec((height, cz), lambda t: (0, at * n + t))

        mixed, grad_tokens, norm_part, grad_a_out_t, grad_b_out = pl.pallas_call(
            finish_kernel,
            grid=(n,),
            in_specs=[
                pl.BlockSpec((seqs, 4, span, cz), lambda t: (0, 0, 0, t)),
                pl.BlockSpec((cz, width), lambda t: (t, 3)),
                column(0, width), column(1, width), column(2, width),
                pl.BlockSpec((cz, rank), lambda t: (t, 1)),
                fixed((width, rank), 0, 0),
                fixed((rank, width), 0, 3),
                column(0, rank), column(1, rank), column(2, rank),
                fixed((1, width), 0, 3),
                fixed((seqs, span, width), 0, 0, 0),
                fixed((seqs, span, width), 0, 0, 0),
                fixed((rows, 1), 0, 0),
                fixed((rows, width), 0, 0),
                fixed((1, width), 0, 0),
                fixed((rows, rank), 0, 0),
                fixed((rank, width), 0, 0),
                fixed((rows, width), 0, 0),
                fixed((rows, rank), 0, 0),
                fixed((width, rank), 0, 2),
                fixed((2, width), 0, 0),
                fixed((seqs, rank, span), 0, 0, 0),
                fixed((rows, width), 0, 0),
            ],
            out_specs=[
                fixed((seqs, span, width), 0, 0, 0),
                fixed((seqs, span, width), 0, 0, 0),
                fixed((4, width), 0, 0),
                pl.BlockSpec((rank, cz), lambda t: (0, t)),
                fixed((rank, width), 0, 0),
            ],
            out_shape=[
                jax.ShapeDtypeStruct((seqs, span, width), bf16),
                jax.ShapeDtypeStruct((seqs, span, width), bf16),
                jax.ShapeDtypeStruct((4, width), f32),
                jax.ShapeDtypeStruct((rank, width), f32),
                jax.ShapeDtypeStruct((rank, width), f32),
            ],
            scratch_shapes=[
                pltpu.VMEM((rows, width), f32),
                pltpu.VMEM((rows, rank), f32),
                pltpu.VMEM((rows, width), f32),
                pltpu.VMEM((rows, rank), f32),
            ],
            compiler_params=pltpu.CompilerParams(vmem_limit_bytes=56 << 20),
            name="finish",
        )(
            local, w_in, w_in, w_in, w_in, a_all, a_all, b_in, b_in, b_in, b_in, bias32.reshape(1, -1),
            tokens, cotangent, row_weight, ff, bias_ff.astype(f32).reshape(1, -1), mid_ff, b_ff,
            grad_second, dmid_up, a_all, norm_gain, dmid_out_t, grad_low,
        )
        grad_b_out = adapter_scale * grad_b_out

        def by_owner(values):
            return values.reshape(rank, dp_n, -1)

        parts = [
            by_owner(grad_a_up_t), by_owner(grad_b_ffp), by_owner(grad_a_qkv_t), by_owner(grad_a_out_t),
            by_owner(grad_a_ff_t), by_owner(jnp.concatenate([grad_b_qkv, grad_b_out, grad_b_up], axis=1)),
        ]
        widths = [p.shape[2] for p in parts]
        owned = jnp.transpose(jnp.concatenate([p.astype(bf16) for p in parts], axis=2), (1, 0, 2))
        b_at = sum(widths[:5])
        reduced = lax.psum_scatter(owned.astype(f32), "dp", scatter_dimension=0, tiled=True)
        reduced = lax.psum(reduced[0], "blk").astype(bf16)
        norm_sum = lax.psum(norm_part, ("dp", "blk"))
        grads_b = reduced[:, b_at : b_at + adapt_b.shape[1]].astype(f32)
        grads_f = reduced[:, widths[0] : widths[0] + widths[1]].astype(f32)
        fresh = jnp.concatenate(
            [
                adam_fresh(adapt_b, grads_b, mean_b, square_b),
                adam_fresh(adapt_b_ff, grads_f, mean_b_ff, square_b_ff),
            ],
            axis=1,
        ).astype(bf16)
        fresh = lax.all_gather(fresh, "dp", axis=0, tiled=False)
    grad_gain, grad_shift = norm_sum[:2], norm_sum[2:]

    state = [
        adapt_a, mean_a, square_a, keep_a,
        adapt_a_ff, mean_a_ff, square_a_ff, keep_a_ff,
        adapt_b, mean_b, square_b, keep_b,
        adapt_b_ff, mean_b_ff, square_b_ff, keep_b_ff,
    ]

    def all_of(value):
        zeros = (0,) * value.ndim
        return pl.BlockSpec(value.shape, lambda j: zeros, pipeline_mode=pl.Buffered(1))

    four = [adapt_a, adapt_a_ff, adapt_b, adapt_b_ff]
    results = [v for v in four] + [v for v in four for _ in range(2)]
    b_w, f_w = adapt_b.shape[1], adapt_b_ff.shape[1]
    owners = max(4, lanes // f_w)
    w_spec = pl.BlockSpec((kr, owners * b_w), lambda j: (0, j))
    wd_spec = pl.BlockSpec((down_rows, owners * f_w), lambda j: (0, j))
    updated = pl.pallas_call(
        functools.partial(update_kernel, rank=rank, width=width),
        grid=(dp_n // owners,),
        in_specs=[all_of(reduced), pl.BlockSpec((owners, rank, b_cols), lambda j: (j, 0, 0)), w_spec, wd_spec]
        + [all_of(v) for v in state],
        out_specs=[all_of(v) for v in results] + [w_spec, wd_spec],
        out_shape=[jax.ShapeDtypeStruct(v.shape, f32) for v in results]
        + [
            jax.ShapeDtypeStruct(frozen_input_weights.shape, bf16),
            jax.ShapeDtypeStruct(frozen_down_weight.shape, bf16),
        ],
        scratch_shapes=[pltpu.VMEM((3, kr, rank), bf16), pltpu.VMEM((down_rows, rank), bf16)],
        compiler_params=pltpu.CompilerParams(vmem_limit_bytes=48 << 20),
        name="update",
    )(reduced, fresh, frozen_input_weights, frozen_down_weight, *state)
    grad_a, grad_a_ff, grad_b, grad_b_ff = updated[:4]
    new_mean_a, new_square_a, new_mean_a_ff, new_square_a_ff = updated[4:8]
    new_mean_b, new_square_b, new_mean_b_ff, new_square_b_ff = updated[8:12]
    folded_input_weights, folded_down_weight = updated[12:]
    return (
        mixed,
        grad_tokens,
        grad_gain,
        grad_shift,
        grad_a,
        grad_a_ff,
        grad_b,
        grad_b_ff,
        new_mean_a,
        new_square_a,
        new_mean_a_ff,
        new_square_a_ff,
        new_mean_b,
        new_square_b,
        new_mean_b_ff,
        new_square_b_ff,
        folded_input_weights,
        folded_down_weight,
    )


def solution(mesh):
    in_specs = (
        P("dp", "blk", None),
        P("dp", "blk", None),
        P("dp", "blk"),
        P(),
        P("dp", None),
        P(),
        P("dp", None),
        P(),
        P(),
        P(),
        P("dp", None),
        P("dp", None),
        P(None, "dp"),
        P(None, "dp"),
        P("dp", None),
        P("dp", None),
        P(None, "dp"),
        P(None, "dp"),
        P("dp", None),
        P("dp", None),
        P(None, "dp"),
        P(None, "dp"),
        P("dp", None),
        P("dp", None),
        P(None, "dp"),
        P(None, "dp"),
    )
    out_specs = (
        P("dp", "blk", None),
        P("dp", "blk", None),
        P(),
        P(),
        P("dp", None),
        P("dp", None),
        P(None, "dp"),
        P(None, "dp"),
        P("dp", None),
        P("dp", None),
        P("dp", None),
        P("dp", None),
        P(None, "dp"),
        P(None, "dp"),
        P(None, "dp"),
        P(None, "dp"),
        P("dp", None),
        P("dp", None),
    )
    return jax.shard_map(
        functools.partial(body, mesh.shape["dp"], mesh.shape["blk"]), mesh=mesh, in_specs=in_specs, out_specs=out_specs, check_vma=False)
```
